32 devices in a mesh: dp: 16 (over z, y, core), head: 2 (over x).
Axes of the slice: x: 2, y: 2, z: 4, core: 2. Of those that a mesh axis runs over, the one named last changes fastest.
Arguments:
- tokens: bfloat16 [49152, 512], P(('dp', 'head')), may hold values from -6 to 6
- ln1_gain: float32 [512], replicated, may hold values from 0.5 to 1.5
- qkv_weight: bfloat16 [3, 512, 512], P(None, 'dp', 'head'), may hold values from -0.25 to 0.25
- out_weight: bfloat16 [512, 512], P('head', 'dp'), may hold values from -0.75 to 0.75
- blend: float32 [3, 8], replicated, may hold values from 0.5 to 4
- ln2_gain: float32 [512], replicated, may hold values from 0.5 to 1.5
- in_weight: bfloat16 [2048, 512], P(('dp', 'head')), may hold values from -0.25 to 0.25
- down_weight: bfloat16 [2048, 512], P(('dp', 'head')), may hold values from -0.125 to 0.125
- cotangent: bfloat16 [49152, 512], P(('dp', 'head')), may hold values from -6 to 6
- lengths: int32 [16, 10], P('dp'), may hold values from 0 to 3072, as said below
Outputs:
- layer_out: bfloat16 [49152, 512], P(('dp', 'head'))
- input_grad: float32 [49152, 512], P(('dp', 'head'))
- ln1_gain_grad: float32 [512], replicated
- qkv_grad: float32 [3, 512, 512], P(None, 'dp', 'head')
- out_weight_grad: float32 [512, 512], P('head', 'dp')
- blend_grad: float32 [3, 8], replicated
- ln2_gain_grad: float32 [512], replicated
- in_weight_grad: float32 [2048, 512], P(('dp', 'head'))
- down_weight_grad: float32 [2048, 512], P(('dp', 'head'))
The draws below stay inside these ranges and needn't reach their ends.
Inputs may be any that keep to these rules, and one draw needn't show every extreme that they name: In each row of lengths the used slots come first and are followed by zeros; every nonzero length is at least 1; a row sums to at most 3072; in every draw some row sums to exactly 3072 and begins with an item of exactly 3072 tokens.
All inputs are finite; a program needn't handle non-finite values.
Results may differ from the reference program's by a relative error of at most 0.018.
Values may be sent and summed in bfloat16 or wider, within the bound.
No kernel may reach another device: no remote copies, remote signals or barrier semaphores. Data moves between devices by JAX's collectives and lax.ppermute only.
A program may use at most 192 MiB of HBM per device.

```python
import math
import jax
import jax.numpy as jnp
from jax import lax

D = 512
HEADS = 8
HEAD_DIM = 64
FF = 2048
BAND = 30
BLOCK = 512
TAIL = 32
CAP = 3072
MAXLEN = 3072
MINLEN = 384
ITEMS = 10
TOKENS = 49152
N_DP = 16


def draw_lengths(key, part):
    full_key, size_key, len_key = jax.random.split(key, 3)
    full_group = jax.random.randint(full_key, (), 0, N_DP)
    group_ids = jnp.arange(N_DP, dtype=jnp.int32)
    limits = jax.random.randint(size_key, (N_DP,), CAP // 2, CAP + 1)
    limits = jnp.where(group_ids == full_group, CAP, limits)
    drawn = jax.random.randint(len_key, (N_DP, ITEMS), MINLEN, MAXLEN + 1)
    first_item = jnp.where(group_ids == full_group, MAXLEN, drawn[:, 0])
    drawn = drawn.at[:, 0].set(first_item)
    running_ends = jnp.cumsum(drawn, axis=1)
    kept_mask = running_ends <= limits[:, None]
    kept = jnp.where(kept_mask, drawn, 0)
    remainder = limits - jnp.sum(kept, axis=1)
    next_slot = jnp.sum(kept_mask.astype(jnp.int32), axis=1)
    slot_ids = jnp.arange(ITEMS, dtype=jnp.int32)
    filled = slot_ids[None, :] == next_slot[:, None]
    return jnp.where(filled, remainder[:, None], kept).astype(jnp.int32)


def steps_of(own_key, dims, cuts, least, largest):
    level = 1.0
    for dim, parts in cuts:
        steps = jax.random.uniform(jax.random.fold_in(jax.random.fold_in(own_key, 6), dim), (parts,), jnp.float32, least / len(cuts), largest / len(cuts))
        level = level * jnp.repeat(jnp.exp(steps), dims[dim] // parts).reshape((-1,) + (1,) * (len(dims) - 1 - dim))
    return level


def normal_values(key, dims, scale, limit, cuts=(), kind=jnp.bfloat16):
    values = scale * jax.random.normal(key, dims, jnp.float32)
    if cuts:
        values = values * steps_of(key, dims, cuts, -0.22, 0.18)
    return jnp.clip(values, -limit, limit).astype(kind)


def setup_inputs(seed: int = 0) -> dict:
    seeds = jax.random.split(jax.random.key(seed), 11)
    return {
        "tokens": normal_values(seeds[0], (TOKENS, D), 1.0, 6.0, ((0, 32),)),
        "ln1_gain": jnp.clip(1.0 + 0.1 * jax.random.normal(seeds[1], (D,), jnp.float32), 0.5, 1.5),
        "qkv_weight": normal_values(seeds[2], (3, D, D), D ** -0.5, 0.25, ((1, 16), (2, 2))),
        "out_weight": normal_values(seeds[3], (D, D), (D // 8) ** -0.5, 0.75, ((0, 2), (1, 16))),
        "blend": jnp.clip(jnp.exp(jax.random.uniform(seeds[4], (3, HEADS), jnp.float32, math.log(0.5), math.log(4.0))), 0.5, 4.0),
        "ln2_gain": jnp.clip(1.0 + 0.1 * jax.random.normal(seeds[5], (D,), jnp.float32), 0.5, 1.5),
        "in_weight": normal_values(seeds[6], (FF, D), D ** -0.5, 0.25, ((0, 32),)),
        "down_weight": normal_values(seeds[7], (FF, D), FF ** -0.5, 0.125, ((0, 32),)),
        "cotangent": normal_values(seeds[8], (TOKENS, D), 1.0, 6.0, ((0, 32),)),
        "lengths": draw_lengths(jax.random.fold_in(seeds[10], 71), 0),
    }


EXACT = lax.Precision.HIGHEST

@jax.custom_vjp
def low(v):
    return lax.optimization_barrier(v.astype(jnp.bfloat16)).astype(jnp.float32)

@jax.custom_vjp
def low_back(v):
    return v

def low_keep(v):
    return (low(v), None)

def low_pass(kept, grad):
    return (grad,)

def back_keep(v):
    return (v, None)

def back_low(kept, grad):
    return (low(grad),)
low.defvjp(low_keep, low_pass)
low_back.defvjp(back_keep, back_low)

def layer_norm(source, gain_vec):
    centered = source - lax.optimization_barrier(jnp.mean(source, axis=-1, keepdims=True))
    spread = lax.optimization_barrier(jnp.mean(centered * centered, axis=-1, keepdims=True))
    return centered * lax.rsqrt(spread + 1e-05) * gain_vec

def layout(item_lengths, slot_count):
    places = jnp.arange(slot_count, dtype=jnp.int32)
    item_ends = jnp.cumsum(item_lengths).astype(jnp.int32)
    passed = item_ends[None, :] <= places[:, None]
    segment = lax.optimization_barrier(jnp.sum(passed.astype(jnp.int32), axis=1)).astype(jnp.int32)
    item_start = lax.optimization_barrier(jnp.sum(jnp.where(passed, item_lengths[None, :], 0), axis=1)).astype(jnp.int32)
    inside = places < item_ends[-1]
    segment = jnp.where(inside, segment, item_lengths.shape[0] + places).astype(jnp.int32)
    counted = jnp.where(inside, places - item_start + 1, 1).astype(jnp.float32)
    return (segment, places, counted, inside.astype(jnp.float32))

def blocked(source, block_rows, tail_rows, filler):
    pieces = source.reshape((source.shape[0] // block_rows, block_rows) + source.shape[1:])
    leading = jnp.full((1, tail_rows) + source.shape[1:], filler, source.dtype)
    return (pieces, jnp.concatenate([leading, pieces[:-1, block_rows - tail_rows:]], axis=0))

def block_mix(queries, key_rows, value_rows, key_tail, value_tail, blend_here, states, seg_rows, seg_tail, pos_rows, pos_tail, counted, inside, seg_before):
    elu_state, elu_total, tanh_state = states
    key_all = jnp.concatenate([key_tail, key_rows], axis=0)
    value_all = jnp.concatenate([value_tail, value_rows], axis=0)
    seg_keys = jnp.concatenate([seg_tail, seg_rows])
    pos_keys = jnp.concatenate([pos_tail, pos_rows])
    distance = pos_rows[:, None] - pos_keys[None, :]
    near_mask = (seg_rows[:, None] == seg_keys[None, :]) & (distance >= 0) & (distance < BAND)
    scores = jnp.einsum('ihd,jhd->hij', queries, key_all, precision=EXACT) * queries.shape[-1] ** (-0.5)
    scores = jnp.where(near_mask[None], scores, -1e+30)
    highest = lax.optimization_barrier(jnp.max(scores, axis=-1, keepdims=True))
    weights = jnp.exp(scores - highest)
    weights = weights / lax.optimization_barrier(jnp.sum(weights, axis=-1, keepdims=True))
    near = jnp.einsum('hij,jhd->ihd', weights, value_all, precision=EXACT)
    order = pos_rows[:, None] - pos_rows[None, :]
    far_mask = ((seg_rows[:, None] == seg_rows[None, :]) & (order >= 0)).astype(queries.dtype)
    carried = (seg_rows == seg_before).astype(queries.dtype)
    lift_q = jax.nn.elu(queries) + 1.0
    lift_k = jax.nn.elu(key_rows) + 1.0
    pair_weight = jnp.einsum('ihd,jhd->hij', lift_q, lift_k, precision=EXACT) * far_mask[None]
    numerator = jnp.einsum('hij,jhd->ihd', pair_weight, value_rows, precision=EXACT) + carried[:, None, None] * jnp.einsum('ihd,hde->ihe', lift_q, elu_state, precision=EXACT)
    denominator = jnp.transpose(lax.optimization_barrier(jnp.sum(pair_weight, axis=-1))) + carried[:, None] * jnp.einsum('ihd,hd->ih', lift_q, elu_total, precision=EXACT)
    far_elu = numerator / denominator[:, :, None]
    bend_q = jnp.tanh(queries)
    bend_k = jnp.tanh(key_rows)
    pair_bend = jnp.einsum('ihd,jhd->hij', bend_q, bend_k, precision=EXACT) * far_mask[None]
    far_tanh = (jnp.einsum('hij,jhd->ihd', pair_bend, value_rows, precision=EXACT) + carried[:, None, None] * jnp.einsum('ihd,hde->ihe', bend_q, tanh_state, precision=EXACT)) / counted[:, None, None]
    mixed = (blend_here[0][None, :, None] * near + blend_here[1][None, :, None] * far_elu + blend_here[2][None, :, None] * far_tanh) * inside[:, None, None]
    closing_seg = seg_rows[-1]
    continues = (seg_before == closing_seg).astype(queries.dtype)
    closing = (seg_rows == closing_seg).astype(queries.dtype)[:, None, None]
    elu_state = continues * elu_state + jnp.einsum('jhd,jhe->hde', lift_k * closing, value_rows, precision=EXACT)
    elu_total = continues * elu_total + lax.optimization_barrier(jnp.sum(lift_k * closing, axis=0))
    tanh_state = continues * tanh_state + jnp.einsum('jhd,jhe->hde', bend_k * closing, value_rows, precision=EXACT)
    return (mixed, (elu_state, elu_total, tanh_state))

def attention(queries, key_rows, value_rows, blend_all, segment, places, counted, inside):
    q_pieces, q_tails = blocked(queries, BLOCK, TAIL, 0.0)
    k_pieces, k_tails = blocked(key_rows, BLOCK, TAIL, 0.0)
    v_pieces, v_tails = blocked(value_rows, BLOCK, TAIL, 0.0)
    s_pieces, s_tails = blocked(segment, BLOCK, TAIL, -2)
    p_pieces, p_tails = blocked(places, BLOCK, TAIL, -4 * BAND)
    c_pieces, c_tails = blocked(counted, BLOCK, TAIL, 1.0)
    i_pieces, i_tails = blocked(inside, BLOCK, TAIL, 0.0)
    before = jnp.concatenate([jnp.full((1,), -1, jnp.int32), s_pieces[:-1, -1]]).astype(jnp.int32)
    head_count = queries.shape[1]
    width = queries.shape[2]
    start_states = (jnp.zeros((head_count, width, width), queries.dtype), jnp.zeros((head_count, width), queries.dtype), jnp.zeros((head_count, width, width), queries.dtype))

    def block_step(states, inputs):
        qb, kb, vb, ktb, vtb, sb, stb, pb, ptb, cb, ib, seg_prev = inputs
        mixed, states = jax.checkpoint(block_mix)(qb, kb, vb, ktb, vtb, blend_all, states, sb, stb, pb, ptb, cb, ib, seg_prev)
        return (states, mixed)
    _, mixed = lax.scan(block_step, start_states, (q_pieces, k_pieces, v_pieces, k_tails, v_tails, s_pieces, s_tails, p_pieces, p_tails, c_pieces, i_pieces, before))
    return mixed.reshape(queries.shape)

def group_forward(inputs, item_lengths, ln1_gain, qkv_weight, out_weight, blend, ln2_gain, in_weight, down_weight):
    segment, places, counted, inside = layout(item_lengths, CAP)
    normed = low(layer_norm(inputs, ln1_gain))
    projected = low(low_back(jnp.einsum('td,cde->tce', normed, qkv_weight, precision=EXACT)))
    shaped = projected.reshape(CAP, 3, HEADS, HEAD_DIM)
    mixed = attention(shaped[:, 0], shaped[:, 1], shaped[:, 2], blend, segment, places, counted, inside)
    mixed = low(low_back(mixed.reshape(CAP, D)))
    hidden = inputs + low_back(jnp.dot(mixed, out_weight, precision=EXACT, preferred_element_type=jnp.float32))
    normed_two = low(layer_norm(hidden, ln2_gain))
    inner = low_back(jnp.dot(normed_two, in_weight.T, precision=EXACT, preferred_element_type=jnp.float32))
    active = low(jax.nn.gelu(inner, approximate=True))
    return hidden + jnp.dot(active, down_weight, precision=EXACT, preferred_element_type=jnp.float32)

def reference(tokens, ln1_gain, qkv_weight, out_weight, blend, ln2_gain, in_weight, down_weight, cotangent, lengths):
    groups = tokens.astype(jnp.float32).reshape(N_DP, CAP, D)
    params = (ln1_gain.astype(jnp.float32), qkv_weight.astype(jnp.float32), out_weight.astype(jnp.float32), blend.astype(jnp.float32), ln2_gain.astype(jnp.float32), in_weight.astype(jnp.float32), down_weight.astype(jnp.float32))

    def layer_all(group_rows, *weights):

        def group_step(running, inputs):
            return (running, jax.checkpoint(group_forward)(inputs[0], inputs[1], *weights))
        _, results = lax.scan(group_step, jnp.zeros((), jnp.float32), (group_rows, lengths))
        return results
    results, pull_back = jax.vjp(layer_all, groups, *params)
    grads = pull_back(cotangent.astype(jnp.float32).reshape(N_DP, CAP, D))
    layer_out = results.reshape(TOKENS, D).astype(jnp.bfloat16)
    input_grad = grads[0].reshape(TOKENS, D)
    return (layer_out, input_grad, grads[1], grads[2], grads[3], grads[4], grads[5], grads[6], grads[7])
```

```python
import functools
import math

import jax
import jax.numpy as jnp
from jax import lax
from jax.experimental import pallas as pl
from jax.experimental.pallas import tpu as pltpu
from jax.sharding import PartitionSpec as P

HEAD_DIM = 64
BAND = 30
ROWS = 96
TAIL = 32
WIN = ROWS + TAIL
PAIR = 2 * HEAD_DIM
EPS = 1e-05
NEG = -1e30
F32 = jnp.float32
BF16 = jnp.bfloat16
NT = (((1,), (1,)), ((), ()))
TN = (((0,), (0,)), ((), ()))
NN = (((1,), (0,)), ((), ()))


def mm(left, right, dims=NN):
    return lax.dot_general(left, right, dims, preferred_element_type=F32)


def iota(shape, axis):
    return lax.broadcasted_iota(jnp.int32, shape, axis)


def lift(values):
    return jnp.where(values > 0, values + 1.0, jnp.exp(jnp.minimum(values, 0.0)))


def head_lanes(dtype):
    first = (iota((1, PAIR), 1) < HEAD_DIM).astype(F32)
    return first.astype(dtype), (1.0 - first).astype(dtype)


def split_heads(block):
    first, second = head_lanes(block.dtype)
    return jnp.concatenate([block * first, block * second], axis=0)


def same_head():
    return (iota((PAIR, PAIR), 0) < HEAD_DIM) == (iota((PAIR, PAIR), 1) < HEAD_DIM)


def block_only(wide):
    keep = same_head()
    parts = [
        jnp.where(keep, wide[:, p * PAIR : (p + 1) * PAIR], 0.0)
        for p in range(wide.shape[1] // PAIR)
    ]
    return jnp.concatenate(parts, axis=1)


def fold(tall):
    half = tall.shape[0] // 2
    lanes = iota((half, PAIR), 1) < HEAD_DIM
    return jnp.where(lanes, tall[:half], tall[half:])


def two(half):
    return jnp.concatenate([half, half], axis=1)


def masks(step, start):
    row = iota((ROWS, WIN), 0) + step * ROWS
    first = step * ROWS - TAIL
    key = iota((ROWS, WIN), 1) + first
    floor = jnp.maximum(first, 0)
    causal = key <= row
    near = causal & (key >= jnp.maximum(start, row - (BAND - 1)))
    far = causal & (key >= jnp.maximum(start, floor))
    return near, far, start < floor, row, floor, first


def near_weights(query, key_heads, near):
    scores = mm(query, key_heads, NT) * (HEAD_DIM**-0.5)
    parts = []
    for h in range(2):
        part = jnp.where(near, scores[:, h * WIN : (h + 1) * WIN], NEG)
        parts.append(jnp.exp(part - jnp.max(part, axis=1, keepdims=True)))
    return jnp.concatenate(parts, axis=1)


def spread(product):
    high = product.astype(BF16)
    low = (product - high.astype(F32)).astype(BF16)
    table = (
        ((iota((2 * PAIR, 2 * WIN), 0) % PAIR) < HEAD_DIM) == (iota((2 * PAIR, 2 * WIN), 1) < WIN)
    ).astype(F32)
    return mm(jnp.concatenate([high, low], axis=1), table.astype(BF16))


def load_keys(qkv_ref, tail_ref, keys, values):
    rows = qkv_ref.shape[1]
    keys[pl.ds(0, TAIL), :] = tail_ref[0]
    keys[pl.ds(TAIL, rows), :] = qkv_ref[1]
    values[pl.ds(0, TAIL), :] = tail_ref[1]
    values[pl.ds(TAIL, rows), :] = qkv_ref[2]


def ends_kernel(scalars, qkv_ref, out_ref):
    rows = qkv_ref.shape[1]
    step_rows = rows // 4
    last = jnp.maximum(scalars[scalars.shape[0] - 2], 0)
    out_ref[0] = jnp.zeros(out_ref.shape[1:], F32)

    def body(step, carry):
        at = pl.multiple_of(step * step_rows, 16)
        key = qkv_ref[1, pl.ds(at, step_rows), :].astype(F32)
        value = qkv_ref[2, pl.ds(at, step_rows), :]
        live = iota((step_rows, PAIR), 0) + at >= last
        lifted = jnp.where(live, lift(key), 0.0).astype(BF16)
        bent = jnp.where(live, jnp.tanh(key), 0.0).astype(BF16)
        ones = jnp.ones((step_rows, PAIR), BF16)
        out_ref[0, :, : 2 * PAIR] += mm(lifted, jnp.concatenate([value, ones], axis=1), TN)
        out_ref[0, :, 2 * PAIR :] += mm(bent, value, TN)
        return carry

    lax.fori_loop(0, 4, body, 0)
    out_ref[0] = block_only(out_ref[0])


def forward_kernel(
    scalars,
    qkv_ref,
    tail_ref,
    start_ref,
    blend_ref,
    state_in_ref,
    att_ref,
    near_ref,
    far1_ref,
    far2_ref,
    invl_ref,
    invd_ref,
    states_ref,
    keys,
    values,
    state,
):
    rows = qkv_ref.shape[1]
    load_keys(qkv_ref, tail_ref, keys, values)
    state[...] = state_in_ref[0].astype(F32)
    count_valid = scalars[scalars.shape[0] - 1]
    b0, b1, b2 = (blend_ref[pl.ds(f, 1), :] for f in range(3))

    def body(step, carry):
        at = pl.multiple_of(step * ROWS, 32)
        query = qkv_ref[0, pl.ds(at, ROWS), :]
        key = keys[pl.ds(at, WIN), :]
        value = values[pl.ds(at, WIN), :]
        start = start_ref[pl.ds(at, ROWS), :]
        near_mask, far_mask, carried, row, floor, first = masks(step, start)
        query_f = query.astype(F32)
        key_f = key.astype(F32)
        lift_q = lift(query_f).astype(BF16)
        bend_q = jnp.tanh(query_f).astype(BF16)
        lift_k = lift(key_f)
        bend_k = jnp.tanh(key_f)
        ones = jnp.ones((WIN, PAIR), BF16)
        value_heads = jnp.concatenate([split_heads(value), split_heads(ones)], axis=1)
        weights = near_weights(query, split_heads(key), near_mask).astype(BF16)
        near_out = mm(weights, value_heads)
        inv_l = 1.0 / near_out[:, PAIR:]
        near = near_out[:, :PAIR] * inv_l
        before = state[...]
        before_low = before.astype(BF16)
        states_ref[0, pl.ds(pl.multiple_of(step * PAIR, PAIR), PAIR), :] = before_low
        far_two = two(far_mask)
        pair_weight = jnp.where(far_two, mm(lift_q, split_heads(lift_k.astype(BF16)), NT), 0.0)
        elu_out = mm(pair_weight.astype(BF16), value_heads)
        elu_state = mm(lift_q, before_low[:, : 2 * PAIR])
        numerator = elu_out[:, :PAIR] + jnp.where(carried, elu_state[:, :PAIR], 0.0)
        inv_d = 1.0 / (elu_out[:, PAIR:] + jnp.where(carried, elu_state[:, PAIR:], 0.0))
        far1 = numerator * inv_d
        pair_bend = jnp.where(far_two, mm(bend_q, split_heads(bend_k.astype(BF16)), NT), 0.0)
        tanh_out = mm(pair_bend.astype(BF16), value_heads[:, :PAIR]) + jnp.where(
            carried, mm(bend_q, before_low[:, 2 * PAIR :]), 0.0
        )
        far2 = tanh_out / (row - start + 1).astype(F32)
        mixed = jnp.where(row < count_valid, b0 * near + b1 * far1 + b2 * far2, 0.0)
        att_ref[pl.ds(at, ROWS), :] = mixed.astype(BF16)
        near_ref[pl.ds(at, ROWS), :] = near
        far1_ref[pl.ds(at, ROWS), :] = far1
        far2_ref[pl.ds(at, ROWS), :] = far2
        invl_ref[pl.ds(at, ROWS), :] = inv_l
        invd_ref[pl.ds(at, ROWS), :] = inv_d
        closing = scalars[step]
        live = iota((ROWS, PAIR), 0) + first >= jnp.maximum(closing, floor)
        lifted = jnp.where(live, lift_k[:ROWS], 0.0).astype(BF16)
        bent = jnp.where(live, bend_k[:ROWS], 0.0).astype(BF16)
        with_ones = jnp.concatenate([value[:ROWS], ones[:ROWS]], axis=1)
        added = jnp.concatenate([mm(lifted, with_ones, TN), mm(bent, value[:ROWS], TN)], axis=1)
        keep = (closing < floor).astype(F32)
        state[...] = keep * before + block_only(added)
        return carry

    lax.fori_loop(0, rows // ROWS, body, 0, unroll=2)


def near_back(query, key_heads, grad_pair, near_mask, spread_near, scale_q, rows_q, rows_g):
    weights = near_weights(query, key_heads, near_mask)
    shifted = (weights * (grad_pair - spread_near)).astype(BF16)
    d_query = mm(shifted, key_heads) * scale_q
    d_key = fold(mm(shifted, rows_q, TN))
    return weights.astype(BF16), d_query, d_key


def prologue_kernel(
    scalars,
    qkv_ref,
    tail_ref,
    start_ref,
    blend_ref,
    grad_ref,
    near_ref,
    far1_ref,
    far2_ref,
    invl_ref,
    invd_ref,
    adjoint_ref,
    tail_grad_ref,
    sums_ref,
):
    rows = qkv_ref.shape[1]
    count_valid = scalars[scalars.shape[0] - 1]
    b0, b1, b2 = (blend_ref[pl.ds(f, 1), :] for f in range(3))
    adjoint_ref[0] = jnp.zeros(adjoint_ref.shape[1:], F32)
    sums_ref[...] = jnp.zeros(sums_ref.shape, F32)
    lanes = iota((ROWS, PAIR), 1) < HEAD_DIM

    key = jnp.concatenate([tail_ref[0], qkv_ref[1, pl.ds(0, ROWS), :]], axis=0)
    value = jnp.concatenate([tail_ref[1], qkv_ref[2, pl.ds(0, ROWS), :]], axis=0)
    start = start_ref[pl.ds(0, ROWS), :]
    near_mask, _, _, row, _, _ = masks(0, start)
    query = qkv_ref[0, pl.ds(0, ROWS), :]
    grad_f = jnp.where(row < count_valid, grad_ref[pl.ds(0, ROWS), :].astype(F32), 0.0)
    grad = grad_f.astype(BF16)
    scale = b0 * invl_ref[pl.ds(0, ROWS), :]
    rows_q = (query.astype(F32) * (scale * HEAD_DIM**-0.5)).astype(BF16)
    rows_g = (grad_f * scale).astype(BF16)
    weights, _, d_key = near_back(
        query,
        split_heads(key),
        mm(grad, split_heads(value), NT),
        near_mask,
        spread(grad_f * near_ref[pl.ds(0, ROWS), :]),
        scale * HEAD_DIM**-0.5,
        rows_q,
        rows_g,
    )
    tail_grad_ref[0] = d_key[:TAIL]
    tail_grad_ref[1] = fold(mm(weights, rows_g, TN))[:TAIL]

    def body(step, carry):
        at = pl.multiple_of(step * ROWS, 32)
        row = iota((ROWS, PAIR), 0) + at
        start = start_ref[pl.ds(at, ROWS), :]
        grad_f = jnp.where(row < count_valid, grad_ref[pl.ds(at, ROWS), :].astype(F32), 0.0)
        grad = grad_f.astype(BF16)
        far1 = grad_f * far1_ref[pl.ds(at, ROWS), :]
        sums_ref[pl.ds(0, 8), :] += jnp.sum(
            (grad_f * near_ref[pl.ds(at, ROWS), :]).reshape(ROWS // 8, 8, PAIR), axis=0
        )
        sums_ref[pl.ds(8, 8), :] += jnp.sum(far1.reshape(ROWS // 8, 8, PAIR), axis=0)
        sums_ref[pl.ds(16, 8), :] += jnp.sum(
            (grad_f * far2_ref[pl.ds(at, ROWS), :]).reshape(ROWS // 8, 8, PAIR), axis=0
        )

        @pl.when(scalars[scalars.shape[0] - 3] > at)
        def _():
            wide = spread(far1)
            along = jnp.where(lanes, wide[:, :WIN], wide[:, WIN:]).astype(BF16)
            query_f = qkv_ref[0, pl.ds(at, ROWS), :].astype(F32)
            live = start < 0
            scaled = jnp.where(live, lift(query_f) * (b1 * invd_ref[pl.ds(at, ROWS), :]), 0.0)
            bent = jnp.where(
                live, jnp.tanh(query_f) * (b2 / (row - start + 1).astype(F32)), 0.0
            )
            adjoint_ref[0, :, : 2 * PAIR] += mm(
                scaled.astype(BF16), jnp.concatenate([grad, along], axis=1), TN
            )
            adjoint_ref[0, :, 2 * PAIR :] += mm(bent.astype(BF16), grad, TN)

        return carry

    lax.fori_loop(0, rows // ROWS, body, 0)
    adjoint_ref[0] = block_only(adjoint_ref[0])


def key_side(adjoint_low, lift_k, bend_k, value):
    ones = jnp.full(value.shape, -1.0 / HEAD_DIM, BF16)
    d_lift = mm(jnp.concatenate([value, ones], axis=1), adjoint_low[:, : 2 * PAIR], NT)
    d_bend = mm(value, adjoint_low[:, 2 * PAIR :], NT)
    both = jnp.concatenate([adjoint_low[:, :PAIR], adjoint_low[:, 2 * PAIR :]], axis=0)
    d_value = mm(jnp.concatenate([lift_k, bend_k], axis=1), both)
    return d_lift, d_bend, d_value


def backward_kernel(
    scalars,
    qkv_ref,
    tail_ref,
    start_ref,
    blend_ref,
    grad_ref,
    near_ref,
    far1_ref,
    invl_ref,
    invd_ref,
    states_ref,
    adjoint_in_ref,
    tail_grad_ref,
    out_ref,
    keys,
    values,
    adjoint,
    key_carry,
    value_carry,
):
    rows = qkv_ref.shape[1]
    steps = rows // ROWS
    load_keys(qkv_ref, tail_ref, keys, values)
    count_valid = scalars[scalars.shape[0] - 1]
    last = scalars[scalars.shape[0] - 2]
    b0, b1, b2 = (blend_ref[pl.ds(f, 1), :] for f in range(3))
    lanes = iota((ROWS, PAIR), 1) < HEAD_DIM

    arrived = adjoint_in_ref[0].astype(F32)
    end_key = keys[pl.ds(rows, TAIL), :].astype(F32)
    end_lift, end_bend = lift(end_key), jnp.tanh(end_key)
    end_parts = key_side(
        arrived.astype(BF16), end_lift.astype(BF16), end_bend.astype(BF16), values[pl.ds(rows, TAIL), :]
    )
    live = iota((TAIL, PAIR), 0) + (rows - TAIL) >= last
    key_carry[...] = tail_grad_ref[0] + jnp.where(
        live,
        end_parts[0] * jnp.minimum(end_lift, 1.0) + end_parts[1] * (1.0 - end_bend * end_bend),
        0.0,
    )
    value_carry[...] = tail_grad_ref[1] + jnp.where(live, end_parts[2], 0.0)
    adjoint[...] = jnp.where(last < rows - TAIL, 1.0, 0.0) * arrived

    def body(back, carry):
        step = steps - 1 - back
        at = pl.multiple_of(step * ROWS, 32)
        query = qkv_ref[0, pl.ds(at, ROWS), :]
        key = keys[pl.ds(at, WIN), :]
        value = values[pl.ds(at, WIN), :]
        start = start_ref[pl.ds(at, ROWS), :]
        near_mask, far_mask, carried, row, floor, first = masks(step, start)
        far_two = two(far_mask)
        grad_f = jnp.where(row < count_valid, grad_ref[pl.ds(at, ROWS), :].astype(F32), 0.0)
        grad = grad_f.astype(BF16)
        query_f = query.astype(F32)
        key_f = key.astype(F32)
        lift_qf, bend_qf = lift(query_f), jnp.tanh(query_f)
        lift_kf, bend_kf = lift(key_f), jnp.tanh(key_f)
        lift_q, bend_q = lift_qf.astype(BF16), bend_qf.astype(BF16)
        lift_k, bend_k = lift_kf.astype(BF16), bend_kf.astype(BF16)
        lift_heads, bend_heads = split_heads(lift_k), split_heads(bend_k)
        r0 = b0 * invl_ref[pl.ds(at, ROWS), :]
        r1 = b1 * invd_ref[pl.ds(at, ROWS), :]
        r2 = b2 / (row - start + 1).astype(F32)
        grad_pair = mm(grad, split_heads(value), NT)
        rows_q = (query_f * (r0 * HEAD_DIM**-0.5)).astype(BF16)
        weights, d_query, d_key = near_back(
            query,
            split_heads(key),
            grad_pair,
            near_mask,
            spread(grad_f * near_ref[pl.ds(at, ROWS), :]),
            r0 * HEAD_DIM**-0.5,
            rows_q,
            None,
        )
        spread_far = spread(grad_f * far1_ref[pl.ds(at, ROWS), :])
        along = jnp.where(lanes, spread_far[:, :WIN], spread_far[:, WIN:])
        shifted = jnp.where(far_two, grad_pair - spread_far, 0.0).astype(BF16)
        plain = jnp.where(far_two, grad_pair, 0.0).astype(BF16)
        pair_weight = jnp.where(far_two, mm(lift_q, lift_heads, NT), 0.0).astype(BF16)
        pair_bend = jnp.where(far_two, mm(bend_q, bend_heads, NT), 0.0).astype(BF16)
        before = states_ref[0, pl.ds(pl.multiple_of(step * PAIR, PAIR), PAIR), :]
        scaled_along = (along * (-1.0 / HEAD_DIM)).astype(BF16)
        state_lift = mm(jnp.concatenate([grad, scaled_along], axis=1), before[:, : 2 * PAIR], NT)
        state_bend = mm(grad, before[:, 2 * PAIR :], NT)
        d_query = (
            d_query
            + (mm(shifted, lift_heads) + jnp.where(carried, state_lift, 0.0))
            * (r1 * jnp.minimum(lift_qf, 1.0))
            + (mm(plain, bend_heads) + jnp.where(carried, state_bend, 0.0))
            * (r2 * (1.0 - bend_qf * bend_qf))
        )
        out_ref[0, pl.ds(at, ROWS), :] = d_query.astype(BF16)
        rows_a = lift_qf * r1
        rows_t = bend_qf * r2
        d_lift = fold(mm(shifted, rows_a.astype(BF16), TN))
        d_bend = fold(mm(plain, rows_t.astype(BF16), TN))
        d_value = fold(
            mm(
                jnp.concatenate([weights, pair_weight, pair_bend], axis=0),
                jnp.concatenate([grad_f * r0, grad_f * r1, grad_f * r2], axis=0).astype(BF16),
                TN,
            )
        )
        after = adjoint[...]
        parts = key_side(after.astype(BF16), lift_k[:ROWS], bend_k[:ROWS], value[:ROWS])
        closing = scalars[step]
        live = iota((ROWS, PAIR), 0) + first >= jnp.maximum(closing, floor)
        pad = jnp.zeros((TAIL, PAIR), F32)
        d_lift = d_lift + jnp.concatenate([jnp.where(live, parts[0], 0.0), pad], axis=0)
        d_bend = d_bend + jnp.concatenate([jnp.where(live, parts[1], 0.0), pad], axis=0)
        d_value = d_value + jnp.concatenate([jnp.where(live, parts[2], 0.0), pad], axis=0)
        d_key = d_key + d_lift * jnp.minimum(lift_kf, 1.0) + d_bend * (1.0 - bend_kf * bend_kf)
        out_ref[1, pl.ds(at, ROWS), :] = jnp.concatenate(
            [d_key[TAIL:ROWS], d_key[ROWS:] + key_carry[...]], axis=0
        ).astype(BF16)
        out_ref[2, pl.ds(at, ROWS), :] = jnp.concatenate(
            [d_value[TAIL:ROWS], d_value[ROWS:] + value_carry[...]], axis=0
        ).astype(BF16)
        key_carry[...] = d_key[:TAIL]
        value_carry[...] = d_value[:TAIL]
        from_lift = mm(
            jnp.where(carried, rows_a, 0.0).astype(BF16),
            jnp.concatenate([grad, along.astype(BF16)], axis=1),
            TN,
        )
        from_bend = mm(jnp.where(carried, rows_t, 0.0).astype(BF16), grad, TN)
        keep = (closing < floor).astype(F32)
        adjoint[...] = keep * after + block_only(jnp.concatenate([from_lift, from_bend], axis=1))
        return carry

    lax.fori_loop(0, steps, body, 0)


def pair_specs(rows):
    column = pl.BlockSpec((rows, PAIR), lambda p, s: (0, p))
    return {
        "qkv": pl.BlockSpec((3, rows, PAIR), lambda p, s: (0, 0, p)),
        "tail": pl.BlockSpec((2, TAIL, PAIR), lambda p, s: (0, 0, p)),
        "start": pl.BlockSpec((rows, PAIR), lambda p, s: (0, 0)),
        "blend": pl.BlockSpec((3, PAIR), lambda p, s: (0, p)),
        "column": column,
        "state": pl.BlockSpec((1, PAIR, 3 * PAIR), lambda p, s: (p, 0, 0)),
        "states": pl.BlockSpec((1, rows // ROWS * PAIR, 3 * PAIR), lambda p, s: (p, 0, 0)),
        "sums": pl.BlockSpec((24, PAIR), lambda p, s: (0, p)),
    }


def call(kernel, ins, outs, out_shapes, scratch, pairs, name, flops, moved):
    return pl.pallas_call(
        kernel,
        out_shape=out_shapes,
        grid_spec=pltpu.PrefetchScalarGridSpec(
            num_scalar_prefetch=1,
            grid=(pairs,),
            in_specs=ins,
            out_specs=outs,
            scratch_shapes=scratch,
        ),
        compiler_params=pltpu.CompilerParams(
            dimension_semantics=("arbitrary",), vmem_limit_bytes=56 * 1024 * 1024
        ),
        cost_estimate=pl.CostEstimate(flops=flops, bytes_accessed=moved, transcendentals=0),
        name=name,
    )


def norm_parts(source):
    centered = source - jnp.mean(source, axis=-1, keepdims=True)
    spread_of = jnp.mean(centered * centered, axis=-1, keepdims=True)
    scale = lax.rsqrt(spread_of + EPS)
    return centered * scale, scale


def norm_back(d_out, gain, normal, scale):
    e = d_out * gain
    inner = jnp.mean(e, axis=-1, keepdims=True)
    along = jnp.mean(e * normal, axis=-1, keepdims=True)
    return scale * (e - inner - normal * along), jnp.sum(d_out * normal, axis=0)


def bits(size):
    return [1 << b for b in range(int(math.log2(size)))]


def swap(array, axis, mask):
    size = lax.axis_size(axis)
    return lax.ppermute(array, axis, [(i, i ^ mask) for i in range(size)])


def orders():
    dp = bits(lax.axis_size("dp"))
    core, rest = dp[:1], dp[1:]
    mid = len(rest) // 2
    y = [("dp", m) for m in rest[:mid]]
    z = [("dp", m) for m in reversed(rest[mid:])]
    x = [("head", m) for m in bits(lax.axis_size("head"))]
    core = [("dp", m) for m in core]
    return z + y + x + core, z + x + y + core


def my_bit(axis, mask):
    return (lax.axis_index(axis) & mask) > 0


def slot(order, axis, mask):
    main = orders()[0]
    here = main.index((axis, mask))
    return sum(1 for pair in order if main.index(pair) < here)


def gather_relative(shard, order):
    block = shard[None]
    for step, (axis, mask) in enumerate(order):
        inner = 1 << slot(order[:step], axis, mask)
        other = swap(block, axis, mask)
        shape = (block.shape[0] // inner, 1, inner) + shard.shape
        block = jnp.concatenate([block.reshape(shape), other.reshape(shape)], axis=1)
        block = block.reshape((-1,) + shard.shape)
    return block.reshape((-1,) + shard.shape[1:])


def scatter_relative(total, order):
    block = total.reshape((1 << len(order), -1) + total.shape[1:])
    for step in reversed(range(len(order))):
        axis, mask = order[step]
        inner = 1 << slot(order[:step], axis, mask)
        block = block.reshape((-1, 2, inner) + block.shape[1:])
        give = block[:, 1].astype(BF16)
        block = block[:, 0] + swap(give, axis, mask).astype(F32)
        block = block.reshape((-1,) + block.shape[2:])
    return block[0]


def gather_absolute(shard, order):
    block = shard[None]
    for axis, mask in order:
        other = swap(block, axis, mask)
        mine = my_bit(axis, mask)
        block = jnp.stack([jnp.where(mine, other, block), jnp.where(mine, block, other)])
        block = block.reshape((-1,) + shard.shape)
    sizes = (2,) * len(order)
    block = block.reshape(sizes + shard.shape)
    stacked = list(reversed(order))
    dp = [stacked.index(("dp", m)) for m in reversed(bits(lax.axis_size("dp")))]
    head = [stacked.index(("head", m)) for m in reversed(bits(lax.axis_size("head")))]
    rest = [len(order) + d for d in range(shard.ndim)]
    block = jnp.transpose(block, dp + head + rest)
    return block.reshape((lax.axis_size("dp"), lax.axis_size("head")) + shard.shape)


def scatter_absolute(total, order):
    n_dp, n_head = lax.axis_size("dp"), lax.axis_size("head")
    dp_bits = list(reversed(bits(n_dp)))
    head_bits = list(reversed(bits(n_head)))
    shard = total.shape[2:]
    block = total.reshape((2,) * (len(dp_bits) + len(head_bits)) + shard)
    left = [("dp", m) for m in dp_bits] + [("head", m) for m in head_bits]
    for axis, mask in reversed(order):
        at = left.index((axis, mask))
        mine = my_bit(axis, mask).astype(jnp.int32)
        keep = lax.dynamic_index_in_dim(block, mine, at, keepdims=False)
        give = lax.dynamic_index_in_dim(block, 1 - mine, at, keepdims=False)
        block = keep + swap(give.astype(BF16), axis, mask).astype(F32)
        left.pop(at)
    return block


def sum_everywhere(array, order):
    for axis, mask in order:
        array = array + swap(array, axis, mask)
    return array


def pass_along(local, keep, shift):
    size = lax.axis_size("head")
    pairs = [(i, i + shift) for i in range(size) if 0 <= i + shift < size]
    arrived = None
    for _ in range(size - 1):
        total = local if arrived is None else local + keep * arrived.astype(F32)
        arrived = lax.ppermute(total.astype(BF16), "head", pairs)
    return arrived


def per_device(
    tokens,
    ln1_gain,
    qkv_weight,
    out_weight,
    blend,
    ln2_gain,
    in_weight,
    down_weight,
    cotangent,
    lengths,
):
    rows, width = tokens.shape
    n_head = lax.axis_size("head")
    pairs = width // PAIR
    steps = rows // ROWS
    order_a, order_b = orders()
    shift_next = [(i, i + 1) for i in range(n_head - 1)]
    shift_back = [(i + 1, i) for i in range(n_head - 1)]

    qkv_all = gather_absolute(qkv_weight, order_a)
    qkv_all = jnp.transpose(qkv_all, (2, 0, 3, 1, 4)).reshape(3, width, width)
    out_all = gather_absolute(out_weight.T, order_b)
    out_all = jnp.transpose(out_all, (1, 3, 0, 2)).reshape(width, width)
    in_all = gather_relative(in_weight, order_a)
    down_all = gather_relative(down_weight, order_b)

    item_lengths = lengths[0]
    slots = item_lengths.shape[0]
    ends = jnp.sum(
        jnp.where(iota((slots, slots), 1) <= iota((slots, slots), 0), item_lengths[None, :], 0),
        axis=1,
    )
    offset = lax.axis_index("head") * rows
    local = jnp.arange(rows, dtype=jnp.int32)
    place = local + offset
    total = ends[slots - 1]
    item_start = jnp.max(
        jnp.where(ends[None, :] <= place[:, None], ends[None, :], 0), axis=1
    )
    start = jnp.where(place < total, item_start - offset, local)
    carried_rows = jnp.sum((start < 0).astype(jnp.int32))
    scalars = jnp.concatenate(
        [
            start.reshape(steps, ROWS)[:, ROWS - TAIL - 1],
            carried_rows[None],
            start[rows - 1 :],
            (total - offset)[None],
        ]
    )
    start_wide = jnp.broadcast_to(start[:, None], (rows, PAIR))
    keep_all = (start[rows - 1] < 0).astype(F32)
    blend_wide = jnp.repeat(blend, HEAD_DIM, axis=1)

    residual = tokens.astype(F32)
    normal_one, scale_one = norm_parts(residual)
    normed_one = (normal_one * ln1_gain).astype(BF16)
    qkv = jnp.einsum("td,cde->cte", normed_one, qkv_all, preferred_element_type=F32).astype(BF16)

    spec = pair_specs(rows)
    wide = jax.ShapeDtypeStruct((rows, width), F32)
    state_shape = jax.ShapeDtypeStruct((pairs, PAIR, 3 * PAIR), F32)
    states_shape = jax.ShapeDtypeStruct((pairs, steps * PAIR, 3 * PAIR), BF16)
    tail_shape = jax.ShapeDtypeStruct((2, TAIL, width), F32)
    big = rows * width

    ends_state = call(
        ends_kernel, [spec["qkv"]], spec["state"], state_shape, [], pairs, "ends", 400 * big, 6 * big
    )(scalars, qkv)
    tails = lax.ppermute(qkv[1:, rows - TAIL :], "head", shift_next)
    state_in = pass_along(ends_state, keep_all, 1)

    key_scratch = pltpu.VMEM((rows + TAIL, PAIR), BF16)
    state_scratch = pltpu.VMEM((PAIR, 3 * PAIR), F32)
    tail_scratch = pltpu.VMEM((TAIL, PAIR), F32)
    mixed, near, far1, far2, inv_l, inv_d, states = call(
        forward_kernel,
        [spec["qkv"], spec["tail"], spec["start"], spec["blend"], spec["state"]],
        [spec["column"]] * 6 + [spec["states"]],
        [jax.ShapeDtypeStruct((rows, width), BF16)] + [wide] * 5 + [states_shape],
        [key_scratch, key_scratch, state_scratch],
        pairs,
        "forward",
        8000 * big,
        40 * big,
    )(scalars, qkv, tails, start_wide, blend_wide, state_in)

    hidden = residual + jnp.dot(mixed, out_all, preferred_element_type=F32)
    normal_two, scale_two = norm_parts(hidden)
    normed_two = (normal_two * ln2_gain).astype(BF16)
    inner = lax.dot_general(normed_two, in_all, NT, preferred_element_type=F32)
    c0 = math.sqrt(2.0 / math.pi)
    bent = jnp.tanh(c0 * (inner + 0.044715 * (inner * inner * inner)))
    active = (0.5 * inner * (1.0 + bent)).astype(BF16)
    layer_out = (hidden + jnp.dot(active, down_all, preferred_element_type=F32)).astype(BF16)
    d_active = lax.dot_general(cotangent, down_all, NT, preferred_element_type=F32)
    down_grad = lax.dot_general(active, cotangent, TN, preferred_element_type=F32)
    slope = 0.5 * (1.0 + bent) + 0.5 * inner * (1.0 - bent * bent) * c0 * (
        1.0 + 3.0 * 0.044715 * inner * inner
    )
    d_inner = (d_active * slope).astype(BF16)
    in_grad = lax.dot_general(d_inner, normed_two, TN, preferred_element_type=F32)
    d_normed_two = jnp.dot(d_inner, in_all, preferred_element_type=F32)
    d_hidden_part, gain_two_part = norm_back(d_normed_two, ln2_gain, normal_two, scale_two)
    d_hidden = cotangent.astype(F32) + d_hidden_part
    d_branch = d_hidden.astype(BF16)
    d_mixed = lax.dot_general(d_branch, out_all, NT, preferred_element_type=F32).astype(BF16)
    out_grad = lax.dot_general(d_branch, mixed, TN, preferred_element_type=F32)

    in_share = scatter_relative(in_grad, order_a)
    down_share = scatter_relative(down_grad, order_b)
    n_dp = lax.axis_size("dp")
    out_share = scatter_absolute(
        jnp.transpose(
            out_grad.reshape(n_dp, width // n_dp, n_head, width // n_head), (0, 2, 1, 3)
        ),
        order_b,
    ).T

    adjoint, tail_grads, sums = call(
        prologue_kernel,
        [spec["qkv"], spec["tail"], spec["start"], spec["blend"]] + [spec["column"]] * 6,
        [spec["state"], spec["tail"], spec["sums"]],
        [state_shape, tail_shape, jax.ShapeDtypeStruct((24, width), F32)],
        [],
        pairs,
        "prologue",
        500 * big,
        28 * big,
    )(scalars, qkv, tails, start_wide, blend_wide, d_mixed, near, far1, far2, inv_l, inv_d)
    adjoint_in = pass_along(adjoint, keep_all, -1)
    tail_in = lax.ppermute(tail_grads, "head", shift_back)
    blend_part = jnp.sum(sums.reshape(3, 8, blend.shape[1], HEAD_DIM), axis=(1, 3))

    d_qkv = call(
        backward_kernel,
        [spec["qkv"], spec["tail"], spec["start"], spec["blend"]]
        + [spec["column"]] * 5
        + [spec["states"], spec["state"], spec["tail"]],
        spec["qkv"],
        jax.ShapeDtypeStruct((3, rows, width), BF16),
        [key_scratch, key_scratch, state_scratch, tail_scratch, tail_scratch],
        pairs,
        "backward",
        16000 * big,
        40 * big,
    )(
        scalars,
        qkv,
        tails,
        start_wide,
        blend_wide,
        d_mixed,
        near,
        far1,
        inv_l,
        inv_d,
        states,
        adjoint_in,
        tail_in,
    )

    qkv_grad = jnp.einsum("td,cte->cde", normed_one, d_qkv, preferred_element_type=F32)
    d_normed_one = jnp.einsum("cte,cde->td", d_qkv, qkv_all, preferred_element_type=F32)
    d_residual_part, gain_one_part = norm_back(d_normed_one, ln1_gain, normal_one, scale_one)
    input_grad = d_hidden + d_residual_part
    qkv_share = scatter_absolute(
        jnp.transpose(
            qkv_grad.reshape(3, n_dp, width // n_dp, n_head, width // n_head), (1, 3, 0, 2, 4)
        ),
        order_a,
    )
    early = sum_everywhere(
        jnp.concatenate([gain_two_part, blend_part.reshape(-1)])[None], order_b
    )[0]
    gain_two = early[:width]
    blend_sum = early[width:].reshape(blend.shape)
    gain_one = sum_everywhere(gain_one_part[None], order_a)[0]
    return (
        layer_out,
        input_grad,
        gain_one,
        qkv_share,
        out_share,
        blend_sum,
        gain_two,
        in_share,
        down_share,
    )


def solution(mesh):
    return jax.shard_map(
        per_device,
        mesh=mesh,
        in_specs=(
            P(("dp", "head"), None),
            P(),
            P(None, "dp", "head"),
            P("head", "dp"),
            P(),
            P(),
            P(("dp", "head"), None),
            P(("dp", "head"), None),
            P(("dp", "head"), None),
            P("dp", None),
        ),
        out_specs=(
            P(("dp", "head"), None),
            P(("dp", "head"), None),
            P(),
            P(None, "dp", "head"),
            P("head", "dp"),
            P(),
            P(),
            P(("dp", "head"), None),
            P(("dp", "head"), None),
        ),
        check_vma=False,
    )
```

```python
import functools
import math

import jax
import jax.numpy as jnp
from jax import lax
from jax.experimental import pallas as pl
from jax.experimental.pallas import tpu as pltpu
from jax.sharding import PartitionSpec as P

HEAD_DIM = 64
BAND = 30
ROWS = 96
TAIL = 32
WIN = ROWS + TAIL
PAIR = 2 * HEAD_DIM
EPS = 1e-05
NEG = -1e30
F32 = jnp.float32
BF16 = jnp.bfloat16
NT = (((1,), (1,)), ((), ()))
TN = (((0,), (0,)), ((), ()))
NN = (((1,), (0,)), ((), ()))


def mm(left, right, dims=NN):
    return lax.dot_general(left, right, dims, preferred_element_type=F32)


def iota(shape, axis):
    return lax.broadcasted_iota(jnp.int32, shape, axis)


def lift(values):
    return jnp.where(values > 0, values + 1.0, jnp.exp(jnp.minimum(values, 0.0)))


def head_lanes(dtype):
    first = (iota((1, PAIR), 1) < HEAD_DIM).astype(F32)
    return first.astype(dtype), (1.0 - first).astype(dtype)


def split_heads(block):
    first, second = head_lanes(block.dtype)
    return jnp.concatenate([block * first, block * second], axis=0)


def same_head():
    return (iota((PAIR, PAIR), 0) < HEAD_DIM) == (iota((PAIR, PAIR), 1) < HEAD_DIM)


def block_only(wide):
    keep = same_head()
    parts = [
        jnp.where(keep, wide[:, p * PAIR : (p + 1) * PAIR], 0.0)
        for p in range(wide.shape[1] // PAIR)
    ]
    return jnp.concatenate(parts, axis=1)


def fold(tall):
    half = tall.shape[0] // 2
    lanes = iota((half, PAIR), 1) < HEAD_DIM
    return jnp.where(lanes, tall[:half], tall[half:])


def two(half):
    return jnp.concatenate([half, half], axis=1)


def masks(step, start):
    row = iota((ROWS, WIN), 0) + step * ROWS
    first = step * ROWS - TAIL
    key = iota((ROWS, WIN), 1) + first
    floor = jnp.maximum(first, 0)
    causal = key <= row
    near = causal & (key >= jnp.maximum(start, row - (BAND - 1)))
    far = causal & (key >= jnp.maximum(start, floor))
    return near, far, start < floor, row, floor, first


def near_weights(query, key_heads, near):
    scores = mm(query, key_heads, NT) * (HEAD_DIM**-0.5)
    parts = []
    for h in range(2):
        part = jnp.where(near, scores[:, h * WIN : (h + 1) * WIN], NEG)
        parts.append(jnp.exp(part - jnp.max(part, axis=1, keepdims=True)))
    return jnp.concatenate(parts, axis=1)


def spread(product):
    high = product.astype(BF16)
    low = (product - high.astype(F32)).astype(BF16)
    table = (
        ((iota((2 * PAIR, 2 * WIN), 0) % PAIR) < HEAD_DIM) == (iota((2 * PAIR, 2 * WIN), 1) < WIN)
    ).astype(F32)
    return mm(jnp.concatenate([high, low], axis=1), table.astype(BF16))


def load_keys(qkv_ref, message_ref, keys, values):
    rows = qkv_ref.shape[1]
    keys[pl.ds(0, TAIL), :] = message_ref[0, pl.ds(HEAD_DIM, TAIL), :PAIR]
    keys[pl.ds(TAIL, rows), :] = qkv_ref[1]
    values[pl.ds(0, TAIL), :] = message_ref[0, pl.ds(HEAD_DIM, TAIL), PAIR : 2 * PAIR]
    values[pl.ds(TAIL, rows), :] = qkv_ref[2]


def fold_state(wide):
    kept = block_only(wide)
    return (kept[:HEAD_DIM] + kept[HEAD_DIM:]).astype(BF16)


def unfold_state(message):
    half = message[:HEAD_DIM].astype(F32)
    return block_only(jnp.concatenate([half, half], axis=0))


def project_kernel(
    scalars,
    tokens_ref,
    gain_ref,
    shards_ref,
    qkv_ref,
    normed_ref,
    weight_ref,
    out_weight_ref,
    message_ref,
    state,
    *,
    spots,
):
    step = pl.program_id(0)
    rows, width = tokens_ref.shape
    pairs = width // PAIR
    tall, wide = shards_ref.shape[2:]
    last = jnp.maximum(scalars[scalars.shape[0] - 3], 0)
    me = scalars[scalars.shape[0] - 1]

    @pl.when(step == 0)
    def _():
        for d, h, spot in spots:
            piece = shards_ref[me ^ spot]
            at = (pl.ds(d * tall, tall), pl.ds(h * wide, wide))
            weight_ref[(slice(None),) + at] = piece[:3]
            out_weight_ref[at] = piece[3]
        state[...] = jnp.zeros(state.shape, F32)

    normed = (norm_parts(tokens_ref[...].astype(F32))[0] * gain_ref[...]).astype(BF16)
    normed_ref[...] = normed
    for c in range(3):
        qkv_ref[c] = mm(normed, weight_ref[c]).astype(BF16)
    live = iota((rows, PAIR), 0) + step * rows >= last
    ones = jnp.ones((rows, PAIR), BF16)
    for p in range(pairs):
        at = pl.ds(p * PAIR, PAIR)
        key = qkv_ref[1, :, at].astype(F32)
        value = qkv_ref[2, :, at]
        lifted = jnp.where(live, lift(key), 0.0).astype(BF16)
        bent = jnp.where(live, jnp.tanh(key), 0.0).astype(BF16)
        state[p, :, : 2 * PAIR] += mm(lifted, jnp.concatenate([value, ones], axis=1), TN)
        state[p, :, 2 * PAIR :] += mm(bent, value, TN)

    @pl.when(step == pl.num_programs(0) - 1)
    def _():
        for p in range(pairs):
            at = pl.ds(p * PAIR, PAIR)
            message_ref[p, pl.ds(0, HEAD_DIM), :] = fold_state(state[p])
            message_ref[p, pl.ds(HEAD_DIM, TAIL), :] = jnp.concatenate(
                [
                    qkv_ref[1, pl.ds(rows - TAIL, TAIL), at],
                    qkv_ref[2, pl.ds(rows - TAIL, TAIL), at],
                    jnp.zeros((TAIL, PAIR), BF16),
                ],
                axis=1,
            )


def weight_grad_kernel(
    scalars, normed_ref, d_qkv_ref, out_grad_ref, keep_ref, give_ref, whole, *, spots, n_head
):
    c = pl.program_id(0)
    me = scalars[scalars.shape[0] - 1]
    tall, wide = keep_ref.shape[2:]
    half = keep_ref.shape[0]

    @pl.when(c < 3)
    def _():
        whole[...] = mm(normed_ref[...], d_qkv_ref[0], TN).reshape(whole.shape)

    @pl.when(c == 3)
    def _():
        whole[...] = out_grad_ref[...].reshape(whole.shape)

    for d, h, spot in spots:
        index = me ^ spot
        value = whole[d, :, pl.ds(h * wide, wide)]

        @pl.when(index < half)
        def _():
            keep_ref[index, 0] = value

        @pl.when(index >= half)
        def _():
            give_ref[index - half, 0] = value.astype(BF16)


def forward_kernel(
    scalars,
    qkv_ref,
    message_ref,
    start_ref,
    blend_ref,
    att_ref,
    near_ref,
    far1_ref,
    far2_ref,
    invl_ref,
    invd_ref,
    states_ref,
    keys,
    values,
    state,
):
    rows = qkv_ref.shape[1]
    load_keys(qkv_ref, message_ref, keys, values)
    state[...] = unfold_state(message_ref[0])
    count_valid = scalars[scalars.shape[0] - 2]
    b0, b1, b2 = (blend_ref[pl.ds(f, 1), :] for f in range(3))

    def body(step, carry):
        at = pl.multiple_of(step * ROWS, 32)
        query = qkv_ref[0, pl.ds(at, ROWS), :]
        key = keys[pl.ds(at, WIN), :]
        value = values[pl.ds(at, WIN), :]
        start = start_ref[pl.ds(at, ROWS), :]
        near_mask, far_mask, carried, row, floor, first = masks(step, start)
        query_f = query.astype(F32)
        key_f = key.astype(F32)
        lift_q = lift(query_f).astype(BF16)
        bend_q = jnp.tanh(query_f).astype(BF16)
        lift_k = lift(key_f)
        bend_k = jnp.tanh(key_f)
        ones = jnp.ones((WIN, PAIR), BF16)
        value_heads = jnp.concatenate([split_heads(value), split_heads(ones)], axis=1)
        weights = near_weights(query, split_heads(key), near_mask).astype(BF16)
        near_out = mm(weights, value_heads)
        inv_l = 1.0 / near_out[:, PAIR:]
        near = near_out[:, :PAIR] * inv_l
        before = state[...]
        before_low = before.astype(BF16)
        states_ref[0, pl.ds(pl.multiple_of(step * PAIR, PAIR), PAIR), :] = before_low
        far_two = two(far_mask)
        pair_weight = jnp.where(far_two, mm(lift_q, split_heads(lift_k.astype(BF16)), NT), 0.0)
        elu_out = mm(pair_weight.astype(BF16), value_heads)
        elu_state = mm(lift_q, before_low[:, : 2 * PAIR])
        numerator = elu_out[:, :PAIR] + jnp.where(carried, elu_state[:, :PAIR], 0.0)
        inv_d = 1.0 / (elu_out[:, PAIR:] + jnp.where(carried, elu_state[:, PAIR:], 0.0))
        far1 = numerator * inv_d
        pair_bend = jnp.where(far_two, mm(bend_q, split_heads(bend_k.astype(BF16)), NT), 0.0)
        tanh_out = mm(pair_bend.astype(BF16), value_heads[:, :PAIR]) + jnp.where(
            carried, mm(bend_q, before_low[:, 2 * PAIR :]), 0.0
        )
        far2 = tanh_out / (row - start + 1).astype(F32)
        mixed = jnp.where(row < count_valid, b0 * near + b1 * far1 + b2 * far2, 0.0)
        att_ref[pl.ds(at, ROWS), :] = mixed.astype(BF16)
        near_ref[pl.ds(at, ROWS), :] = near
        far1_ref[pl.ds(at, ROWS), :] = far1
        far2_ref[pl.ds(at, ROWS), :] = far2
        invl_ref[pl.ds(at, ROWS), :] = inv_l
        invd_ref[pl.ds(at, ROWS), :] = inv_d
        closing = scalars[step]
        live = iota((ROWS, PAIR), 0) + first >= jnp.maximum(closing, floor)
        lifted = jnp.where(live, lift_k[:ROWS], 0.0).astype(BF16)
        bent = jnp.where(live, bend_k[:ROWS], 0.0).astype(BF16)
        with_ones = jnp.concatenate([value[:ROWS], ones[:ROWS]], axis=1)
        added = jnp.concatenate([mm(lifted, with_ones, TN), mm(bent, value[:ROWS], TN)], axis=1)
        keep = (closing < floor).astype(F32)
        state[...] = keep * before + block_only(added)
        return carry

    lax.fori_loop(0, rows // ROWS, body, 0, unroll=2)


def near_back(query, key_heads, grad_pair, near_mask, spread_near, scale_q, rows_q, rows_g):
    weights = near_weights(query, key_heads, near_mask)
    shifted = (weights * (grad_pair - spread_near)).astype(BF16)
    d_query = mm(shifted, key_heads) * scale_q
    d_key = fold(mm(shifted, rows_q, TN))
    return weights.astype(BF16), d_query, d_key


def prologue_kernel(
    scalars,
    qkv_ref,
    message_ref,
    start_ref,
    blend_ref,
    grad_ref,
    near_ref,
    far1_ref,
    far2_ref,
    invl_ref,
    invd_ref,
    back_ref,
    sums_ref,
    adjoint,
):
    rows = qkv_ref.shape[1]
    count_valid = scalars[scalars.shape[0] - 2]
    b0, b1, b2 = (blend_ref[pl.ds(f, 1), :] for f in range(3))
    adjoint[...] = jnp.zeros(adjoint.shape, F32)
    sums_ref[...] = jnp.zeros(sums_ref.shape, F32)
    lanes = iota((ROWS, PAIR), 1) < HEAD_DIM

    tails = message_ref[0, pl.ds(HEAD_DIM, TAIL), :]
    key = jnp.concatenate([tails[:, :PAIR], qkv_ref[1, pl.ds(0, ROWS), :]], axis=0)
    value = jnp.concatenate([tails[:, PAIR : 2 * PAIR], qkv_ref[2, pl.ds(0, ROWS), :]], axis=0)
    start = start_ref[pl.ds(0, ROWS), :]
    near_mask, _, _, row, _, _ = masks(0, start)
    query = qkv_ref[0, pl.ds(0, ROWS), :]
    grad_f = jnp.where(row < count_valid, grad_ref[pl.ds(0, ROWS), :].astype(F32), 0.0)
    grad = grad_f.astype(BF16)
    scale = b0 * invl_ref[pl.ds(0, ROWS), :]
    rows_q = (query.astype(F32) * (scale * HEAD_DIM**-0.5)).astype(BF16)
    rows_g = (grad_f * scale).astype(BF16)
    weights, _, d_key = near_back(
        query,
        split_heads(key),
        mm(grad, split_heads(value), NT),
        near_mask,
        spread(grad_f * near_ref[pl.ds(0, ROWS), :]),
        scale * HEAD_DIM**-0.5,
        rows_q,
        rows_g,
    )
    back_ref[0, pl.ds(HEAD_DIM, TAIL), :] = jnp.concatenate(
        [d_key[:TAIL], fold(mm(weights, rows_g, TN))[:TAIL], jnp.zeros((TAIL, PAIR), F32)], axis=1
    ).astype(BF16)

    def body(step, carry):
        at = pl.multiple_of(step * ROWS, 32)
        row = iota((ROWS, PAIR), 0) + at
        start = start_ref[pl.ds(at, ROWS), :]
        grad_f = jnp.where(row < count_valid, grad_ref[pl.ds(at, ROWS), :].astype(F32), 0.0)
        grad = grad_f.astype(BF16)
        far1 = grad_f * far1_ref[pl.ds(at, ROWS), :]
        sums_ref[pl.ds(0, 8), :] += jnp.sum(
            (grad_f * near_ref[pl.ds(at, ROWS), :]).reshape(ROWS // 8, 8, PAIR), axis=0
        )
        sums_ref[pl.ds(8, 8), :] += jnp.sum(far1.reshape(ROWS // 8, 8, PAIR), axis=0)
        sums_ref[pl.ds(16, 8), :] += jnp.sum(
            (grad_f * far2_ref[pl.ds(at, ROWS), :]).reshape(ROWS // 8, 8, PAIR), axis=0
        )

        @pl.when(scalars[scalars.shape[0] - 4] > at)
        def _():
            wide = spread(far1)
            along = jnp.where(lanes, wide[:, :WIN], wide[:, WIN:]).astype(BF16)
            query_f = qkv_ref[0, pl.ds(at, ROWS), :].astype(F32)
            live = start < 0
            scaled = jnp.where(live, lift(query_f) * (b1 * invd_ref[pl.ds(at, ROWS), :]), 0.0)
            bent = jnp.where(
                live, jnp.tanh(query_f) * (b2 / (row - start + 1).astype(F32)), 0.0
            )
            adjoint[:, : 2 * PAIR] += mm(
                scaled.astype(BF16), jnp.concatenate([grad, along], axis=1), TN
            )
            adjoint[:, 2 * PAIR :] += mm(bent.astype(BF16), grad, TN)

        return carry

    lax.fori_loop(0, rows // ROWS, body, 0)
    back_ref[0, pl.ds(0, HEAD_DIM), :] = fold_state(adjoint[...])


def key_side(adjoint_low, lift_k, bend_k, value):
    ones = jnp.full(value.shape, -1.0 / HEAD_DIM, BF16)
    d_lift = mm(jnp.concatenate([value, ones], axis=1), adjoint_low[:, : 2 * PAIR], NT)
    d_bend = mm(value, adjoint_low[:, 2 * PAIR :], NT)
    both = jnp.concatenate([adjoint_low[:, :PAIR], adjoint_low[:, 2 * PAIR :]], axis=0)
    d_value = mm(jnp.concatenate([lift_k, bend_k], axis=1), both)
    return d_lift, d_bend, d_value


def backward_kernel(
    scalars,
    qkv_ref,
    message_ref,
    start_ref,
    blend_ref,
    grad_ref,
    near_ref,
    far1_ref,
    invl_ref,
    invd_ref,
    states_ref,
    back_ref,
    done_ref,
    out_ref,
    keys,
    values,
    adjoint,
    key_carry,
    value_carry,
):
    rows = qkv_ref.shape[1]
    steps = rows // ROWS
    load_keys(qkv_ref, message_ref, keys, values)
    count_valid = scalars[scalars.shape[0] - 2]
    last = scalars[scalars.shape[0] - 3]
    b0, b1, b2 = (blend_ref[pl.ds(f, 1), :] for f in range(3))
    lanes = iota((ROWS, PAIR), 1) < HEAD_DIM

    arrived = unfold_state(back_ref[0])
    tail_grads = back_ref[0, pl.ds(HEAD_DIM, TAIL), :].astype(F32)
    end_key = keys[pl.ds(rows, TAIL), :].astype(F32)
    end_lift, end_bend = lift(end_key), jnp.tanh(end_key)
    end_parts = key_side(
        arrived.astype(BF16), end_lift.astype(BF16), end_bend.astype(BF16), values[pl.ds(rows, TAIL), :]
    )
    live = iota((TAIL, PAIR), 0) + (rows - TAIL) >= last
    key_carry[...] = tail_grads[:, :PAIR] + jnp.where(
        live,
        end_parts[0] * jnp.minimum(end_lift, 1.0) + end_parts[1] * (1.0 - end_bend * end_bend),
        0.0,
    )
    value_carry[...] = tail_grads[:, PAIR : 2 * PAIR] + jnp.where(live, end_parts[2], 0.0)
    adjoint[...] = jnp.where(last < rows - TAIL, 1.0, 0.0) * arrived

    def body(back, carry):
        step = steps - 1 - back
        at = pl.multiple_of(step * ROWS, 32)
        query = qkv_ref[0, pl.ds(at, ROWS), :]
        key = keys[pl.ds(at, WIN), :]
        value = values[pl.ds(at, WIN), :]
        start = start_ref[pl.ds(at, ROWS), :]
        near_mask, far_mask, carried, row, floor, first = masks(step, start)
        far_two = two(far_mask)
        grad_f = jnp.where(row < count_valid, grad_ref[pl.ds(at, ROWS), :].astype(F32), 0.0)
        grad = grad_f.astype(BF16)
        query_f = query.astype(F32)
        key_f = key.astype(F32)
        lift_qf, bend_qf = lift(query_f), jnp.tanh(query_f)
        lift_kf, bend_kf = lift(key_f), jnp.tanh(key_f)
        lift_q, bend_q = lift_qf.astype(BF16), bend_qf.astype(BF16)
        lift_k, bend_k = lift_kf.astype(BF16), bend_kf.astype(BF16)
        lift_heads, bend_heads = split_heads(lift_k), split_heads(bend_k)
        r0 = b0 * invl_ref[pl.ds(at, ROWS), :]
        r1 = b1 * invd_ref[pl.ds(at, ROWS), :]
        r2 = b2 / (row - start + 1).astype(F32)
        grad_pair = mm(grad, split_heads(value), NT)
        rows_q = (query_f * (r0 * HEAD_DIM**-0.5)).astype(BF16)
        weights, d_query, d_key = near_back(
            query,
            split_heads(key),
            grad_pair,
            near_mask,
            spread(grad_f * near_ref[pl.ds(at, ROWS), :]),
            r0 * HEAD_DIM**-0.5,
            rows_q,
            None,
        )
        spread_far = spread(grad_f * far1_ref[pl.ds(at, ROWS), :])
        along = jnp.where(lanes, spread_far[:, :WIN], spread_far[:, WIN:])
        shifted = jnp.where(far_two, grad_pair - spread_far, 0.0).astype(BF16)
        plain = jnp.where(far_two, grad_pair, 0.0).astype(BF16)
        pair_weight = jnp.where(far_two, mm(lift_q, lift_heads, NT), 0.0).astype(BF16)
        pair_bend = jnp.where(far_two, mm(bend_q, bend_heads, NT), 0.0).astype(BF16)
        before = states_ref[0, pl.ds(pl.multiple_of(step * PAIR, PAIR), PAIR), :]
        scaled_along = (along * (-1.0 / HEAD_DIM)).astype(BF16)
        state_lift = mm(jnp.concatenate([grad, scaled_along], axis=1), before[:, : 2 * PAIR], NT)
        state_bend = mm(grad, before[:, 2 * PAIR :], NT)
        d_query = (
            d_query
            + (mm(shifted, lift_heads) + jnp.where(carried, state_lift, 0.0))
            * (r1 * jnp.minimum(lift_qf, 1.0))
            + (mm(plain, bend_heads) + jnp.where(carried, state_bend, 0.0))
            * (r2 * (1.0 - bend_qf * bend_qf))
        )
        out_ref[0, pl.ds(at, ROWS), :] = d_query.astype(BF16)
        rows_a = lift_qf * r1
        rows_t = bend_qf * r2
        d_lift = fold(mm(shifted, rows_a.astype(BF16), TN))
        d_bend = fold(mm(plain, rows_t.astype(BF16), TN))
        d_value = fold(
            mm(
                jnp.concatenate([weights, pair_weight, pair_bend], axis=0),
                jnp.concatenate([grad_f * r0, grad_f * r1, grad_f * r2], axis=0).astype(BF16),
                TN,
            )
        )
        after = adjoint[...]
        parts = key_side(after.astype(BF16), lift_k[:ROWS], bend_k[:ROWS], value[:ROWS])
        closing = scalars[step]
        live = iota((ROWS, PAIR), 0) + first >= jnp.maximum(closing, floor)
        pad = jnp.zeros((TAIL, PAIR), F32)
        d_lift = d_lift + jnp.concatenate([jnp.where(live, parts[0], 0.0), pad], axis=0)
        d_bend = d_bend + jnp.concatenate([jnp.where(live, parts[1], 0.0), pad], axis=0)
        d_value = d_value + jnp.concatenate([jnp.where(live, parts[2], 0.0), pad], axis=0)
        d_key = d_key + d_lift * jnp.minimum(lift_kf, 1.0) + d_bend * (1.0 - bend_kf * bend_kf)
        out_ref[1, pl.ds(at, ROWS), :] = jnp.concatenate(
            [d_key[TAIL:ROWS], d_key[ROWS:] + key_carry[...]], axis=0
        ).astype(BF16)
        out_ref[2, pl.ds(at, ROWS), :] = jnp.concatenate(
            [d_value[TAIL:ROWS], d_value[ROWS:] + value_carry[...]], axis=0
        ).astype(BF16)
        key_carry[...] = d_key[:TAIL]
        value_carry[...] = d_value[:TAIL]
        from_lift = mm(
            jnp.where(carried, rows_a, 0.0).astype(BF16),
            jnp.concatenate([grad, along.astype(BF16)], axis=1),
            TN,
        )
        from_bend = mm(jnp.where(carried, rows_t, 0.0).astype(BF16), grad, TN)
        keep = (closing < floor).astype(F32)
        adjoint[...] = keep * after + block_only(jnp.concatenate([from_lift, from_bend], axis=1))
        return carry

    lax.fori_loop(0, steps, body, 0)


def pair_specs(rows, first=0):
    return {
        "qkv": pl.BlockSpec((3, rows, PAIR), lambda p, s: (0, 0, p + first)),
        "message": pl.BlockSpec((1, HEAD_DIM + TAIL, 3 * PAIR), lambda p, s: (p + first, 0, 0)),
        "start": pl.BlockSpec((rows, PAIR), lambda p, s: (0, 0)),
        "blend": pl.BlockSpec((3, PAIR), lambda p, s: (0, p + first)),
        "column": pl.BlockSpec((rows, PAIR), lambda p, s: (0, p + first)),
        "states": pl.BlockSpec((1, rows // ROWS * PAIR, 3 * PAIR), lambda p, s: (p + first, 0, 0)),
        "sums": pl.BlockSpec((24, PAIR), lambda p, s: (0, p + first)),
    }


def call(kernel, ins, outs, out_shapes, scratch, grid, name, flops, moved, aliases={}):
    return pl.pallas_call(
        kernel,
        out_shape=out_shapes,
        grid_spec=pltpu.PrefetchScalarGridSpec(
            num_scalar_prefetch=1,
            grid=(grid,),
            in_specs=ins,
            out_specs=outs,
            scratch_shapes=scratch,
        ),
        input_output_aliases=aliases,
        compiler_params=pltpu.CompilerParams(
            dimension_semantics=("arbitrary",), vmem_limit_bytes=56 * 1024 * 1024
        ),
        cost_estimate=pl.CostEstimate(flops=flops, bytes_accessed=moved, transcendentals=0),
        name=name,
    )


def norm_parts(source):
    centered = source - jnp.mean(source, axis=-1, keepdims=True)
    spread_of = jnp.mean(centered * centered, axis=-1, keepdims=True)
    scale = lax.rsqrt(spread_of + EPS)
    return centered * scale, scale


def norm_back(d_out, gain, normal, scale):
    e = d_out * gain
    inner = jnp.mean(e, axis=-1, keepdims=True)
    along = jnp.mean(e * normal, axis=-1, keepdims=True)
    return scale * (e - inner - normal * along), jnp.sum(d_out * normal, axis=0)


def bits(size):
    return [1 << b for b in range(int(math.log2(size)))]


def phases():
    dp = bits(lax.axis_size("dp"))
    core, rest = dp[:1], dp[1:]
    mid = len(rest) // 2
    far = [("dp", m) for m in rest[mid:]]
    near = [("dp", m) for m in rest[:mid]] + [("head", m) for m in bits(lax.axis_size("head"))]
    groups = []
    for run in (far, near, [("dp", m) for m in core]):
        groups += [run[i : i + 2] for i in range(0, len(run), 2)]
    return groups


def relative_bits():
    return [pair for group in phases() for pair in group]


def relative_index(dp_index, head_index):
    index = 0
    for place, (axis, mask) in enumerate(relative_bits()):
        own = dp_index if axis == "dp" else head_index
        index = index | (((own // mask) & 1) << place)
    return index


def peer(array, group, combo):
    n_dp, n_head = lax.axis_size("dp"), lax.axis_size("head")
    chosen = [pair for place, pair in enumerate(group) if combo >> place & 1]
    flip_dp = sum(m for axis, m in chosen if axis == "dp")
    flip_head = sum(m for axis, m in chosen if axis == "head")
    pairs = [
        (d * n_head + h, (d ^ flip_dp) * n_head + (h ^ flip_head))
        for d in range(n_dp)
        for h in range(n_head)
    ]
    return lax.ppermute(array, ("dp", "head"), pairs)


def widen(block, group, axis):
    others = [peer(block, group, combo) for combo in range(1, 1 << len(group))]
    return jnp.concatenate([block] + others, axis=axis)


def narrow(keep, gives, group):
    total = keep.astype(F32)
    for combo, give in enumerate(gives, 1):
        total = total + peer(give.astype(BF16), group, combo).astype(F32)
    return total


def narrow_axis(total, group, axis):
    parts = jnp.split(total, 1 << len(group), axis=axis)
    return narrow(parts[0], parts[1:], group)


def sum_everywhere(array):
    for group in reversed(phases()):
        array = array + sum(peer(array, group, combo) for combo in range(1, 1 << len(group)))
    return array


def pass_along(local, keep, shift):
    size = lax.axis_size("head")
    pairs = [(i, i + shift) for i in range(size) if 0 <= i + shift < size]
    arrived = lax.ppermute(local, "head", pairs)
    for _ in range(size - 2):
        rows = iota(local.shape, 1) < HEAD_DIM
        total = local.astype(F32) + jnp.where(rows, keep * arrived.astype(F32), 0.0)
        arrived = lax.ppermute(total.astype(BF16), "head", pairs)
    return arrived


def per_device(
    tokens,
    ln1_gain,
    qkv_weight,
    out_weight,
    blend,
    ln2_gain,
    in_weight,
    down_weight,
    cotangent,
    lengths,
):
    rows, width = tokens.shape
    n_dp, n_head = lax.axis_size("dp"), lax.axis_size("head")
    pairs = width // PAIR
    steps = rows // ROWS
    groups = phases()
    spots = [(d, h, relative_index(d, h)) for d in range(n_dp) for h in range(n_head)]

    shards = jnp.concatenate([qkv_weight, out_weight.T[None]], axis=0)[None]
    feed = jnp.stack([in_weight, down_weight])
    for group in groups[:-1]:
        shards = widen(shards, group, 0)
    shards, feed = lax.optimization_barrier((shards, feed))
    shards = widen(shards, groups[-1], 0)
    for group in groups:
        feed = widen(feed, group, 1)
    in_all, down_all = feed[0], feed[1]

    item_lengths = lengths[0]
    slots = item_lengths.shape[0]
    ends = jnp.sum(
        jnp.where(iota((slots, slots), 1) <= iota((slots, slots), 0), item_lengths[None, :], 0),
        axis=1,
    )
    offset = lax.axis_index("head") * rows
    local = jnp.arange(rows, dtype=jnp.int32)
    place = local + offset
    total = ends[slots - 1]
    item_start = jnp.max(
        jnp.where(ends[None, :] <= place[:, None], ends[None, :], 0), axis=1
    )
    start = jnp.where(place < total, item_start - offset, local)
    carried_rows = jnp.sum((start < 0).astype(jnp.int32))
    scalars = jnp.concatenate(
        [
            start.reshape(steps, ROWS)[:, ROWS - TAIL - 1],
            carried_rows[None],
            start[rows - 1 :],
            (total - offset)[None],
            jnp.asarray(relative_index(lax.axis_index("dp"), lax.axis_index("head")), jnp.int32)[None],
        ]
    )
    start_wide = jnp.broadcast_to(start[:, None], (rows, PAIR))
    keep_all = (start[rows - 1] < 0).astype(F32)
    blend_wide = jnp.repeat(blend, HEAD_DIM, axis=1)

    spec = pair_specs(rows)
    wide = jax.ShapeDtypeStruct((rows, width), F32)
    states_shape = jax.ShapeDtypeStruct((pairs, steps * PAIR, 3 * PAIR), BF16)
    message_shape = jax.ShapeDtypeStruct((pairs, HEAD_DIM + TAIL, 3 * PAIR), BF16)
    big = rows * width
    part = rows // 3

    def whole_spec(shape):
        return pl.BlockSpec(shape, lambda p, s: (0,) * len(shape))

    qkv, normed_one, qkv_all, out_all, closing = call(
        functools.partial(project_kernel, spots=spots),
        [
            pl.BlockSpec((part, width), lambda p, s: (p, 0)),
            whole_spec((1, width)),
            whole_spec(shards.shape),
        ],
        [
            pl.BlockSpec((3, part, width), lambda p, s: (0, p, 0)),
            pl.BlockSpec((part, width), lambda p, s: (p, 0)),
            whole_spec((3, width, width)),
            whole_spec((width, width)),
            whole_spec(message_shape.shape),
        ],
        [
            jax.ShapeDtypeStruct((3, rows, width), BF16),
            jax.ShapeDtypeStruct((rows, width), BF16),
            jax.ShapeDtypeStruct((3, width, width), BF16),
            jax.ShapeDtypeStruct((width, width), BF16),
            message_shape,
        ],
        [pltpu.VMEM((pairs, PAIR, 3 * PAIR), F32)],
        3,
        "project",
        6 * big * width,
        12 * big,
    )(scalars, tokens, ln1_gain[None], shards)
    message = pass_along(closing, keep_all, 1)

    key_scratch = pltpu.VMEM((rows + TAIL, PAIR), BF16)
    state_scratch = pltpu.VMEM((PAIR, 3 * PAIR), F32)
    tail_scratch = pltpu.VMEM((TAIL, PAIR), F32)
    mixed, near, far1, far2, inv_l, inv_d, states = call(
        forward_kernel,
        [spec["qkv"], spec["message"], spec["start"], spec["blend"]],
        [spec["column"]] * 6 + [spec["states"]],
        [jax.ShapeDtypeStruct((rows, width), BF16)] + [wide] * 5 + [states_shape],
        [key_scratch, key_scratch, state_scratch],
        pairs,
        "forward",
        8000 * big,
        40 * big,
    )(scalars, qkv, message, start_wide, blend_wide)

    residual = tokens.astype(F32)
    hidden = residual + lax.dot_general(mixed, out_all, NT, preferred_element_type=F32)
    normal_two, scale_two = norm_parts(hidden)
    normed_two = (normal_two * ln2_gain).astype(BF16)
    inner = lax.dot_general(normed_two, in_all, NT, preferred_element_type=F32)
    c0 = math.sqrt(2.0 / math.pi)
    bent = jnp.tanh(c0 * (inner + 0.044715 * (inner * inner * inner)))
    active = (0.5 * inner * (1.0 + bent)).astype(BF16)
    layer_out = (hidden + jnp.dot(active, down_all, preferred_element_type=F32)).astype(BF16)
    d_active = lax.dot_general(cotangent, down_all, NT, preferred_element_type=F32)
    down_grad = lax.dot_general(active, cotangent, TN, preferred_element_type=F32)
    slope = 0.5 * (1.0 + bent) + 0.5 * inner * (1.0 - bent * bent) * c0 * (
        1.0 + 3.0 * 0.044715 * inner * inner
    )
    d_inner = (d_active * slope).astype(BF16)
    in_grad = lax.dot_general(d_inner, normed_two, TN, preferred_element_type=F32)
    d_normed_two = jnp.dot(d_inner, in_all, preferred_element_type=F32)
    d_hidden_part, gain_two_part = norm_back(d_normed_two, ln2_gain, normal_two, scale_two)
    d_hidden = cotangent.astype(F32) + d_hidden_part
    d_branch = d_hidden.astype(BF16)
    d_mixed = jnp.dot(d_branch, out_all, preferred_element_type=F32).astype(BF16)
    out_grad = lax.dot_general(d_branch, mixed, TN, preferred_element_type=F32)

    back, sums = call(
        prologue_kernel,
        [spec["qkv"], spec["message"], spec["start"], spec["blend"]] + [spec["column"]] * 6,
        [spec["message"], spec["sums"]],
        [message_shape, jax.ShapeDtypeStruct((24, width), F32)],
        [state_scratch],
        pairs,
        "prologue",
        500 * big,
        28 * big,
    )(scalars, qkv, message, start_wide, blend_wide, d_mixed, near, far1, far2, inv_l, inv_d)
    back_in = pass_along(back, keep_all, -1)
    blend_part = jnp.sum(sums.reshape(3, 8, blend.shape[1], HEAD_DIM), axis=(1, 3))

    half = in_grad.shape[0] // 2
    keep = jnp.stack([in_grad[:half], down_grad[:half]])
    give = jnp.stack([in_grad[half:], down_grad[half:]]).astype(BF16)
    feed_share = narrow(keep, [give], groups[-1])
    left = list(reversed(groups[:-1]))

    d_qkv = jnp.zeros((3, 8, PAIR), BF16)
    first = 0
    for count in (pairs // 4, pairs // 2, pairs // 4):
        spec = pair_specs(rows, first)
        more = {12: 0} if first else {}
        d_qkv = call(
            backward_kernel,
            [spec["qkv"], spec["message"], spec["start"], spec["blend"]]
            + [spec["column"]] * 5
            + [spec["states"], spec["message"], pl.BlockSpec(memory_space=pl.ANY)],
            spec["qkv"],
            jax.ShapeDtypeStruct((3, rows, width), BF16),
            [key_scratch, key_scratch, state_scratch, tail_scratch, tail_scratch],
            count,
            "backward",
            16000 * big * count // pairs,
            40 * big * count // pairs,
            more,
        )(
            scalars,
            qkv,
            message,
            start_wide,
            blend_wide,
            d_mixed,
            near,
            far1,
            inv_l,
            inv_d,
            states,
            back_in,
            d_qkv,
        )
        first += count
        if left and first < pairs:
            feed_share, back_in = lax.optimization_barrier((feed_share, back_in))
            feed_share = narrow_axis(feed_share, left.pop(0), 1)
    for group in left:
        feed_share = narrow_axis(feed_share, group, 1)

    shard_shape = (n_dp * n_head // 2, 4, width // n_dp, width // n_head)
    shard_spec = pl.BlockSpec((shard_shape[0], 1) + shard_shape[2:], lambda p, s: (0, p, 0, 0))
    keep, give = call(
        functools.partial(weight_grad_kernel, spots=spots, n_head=n_head),
        [
            whole_spec((rows, width)),
            pl.BlockSpec((1, rows, width), lambda p, s: (jnp.minimum(p, 2), 0, 0)),
            whole_spec((width, width)),
        ],
        [shard_spec, shard_spec],
        [jax.ShapeDtypeStruct(shard_shape, F32), jax.ShapeDtypeStruct(shard_shape, BF16)],
        [pltpu.VMEM((n_dp, width // n_dp, width), F32)],
        4,
        "weight_grad",
        6 * big * width,
        8 * big,
    )(scalars, normed_one, d_qkv, out_grad)
    share = narrow(keep, [give], groups[-1])
    for group in reversed(groups[:-1]):
        share = narrow_axis(share, group, 0)
    d_normed_one = jnp.einsum("cte,cde->td", d_qkv, qkv_all, preferred_element_type=F32)
    normal_one, scale_one = norm_parts(residual)
    d_residual_part, gain_one_part = norm_back(d_normed_one, ln1_gain, normal_one, scale_one)
    input_grad = d_hidden + d_residual_part
    gathered = jnp.concatenate([gain_one_part, gain_two_part, blend_part.reshape(-1)])
    total_sums = sum_everywhere(gathered[None])[0]
    gain_one, gain_two = total_sums[:width], total_sums[width : 2 * width]
    blend_sum = total_sums[2 * width :].reshape(blend.shape)
    qkv_share, out_share = share[0, :3], share[0, 3].T
    in_share, down_share = feed_share[0], feed_share[1]
    return (
        layer_out,
        input_grad,
        gain_one,
        qkv_share,
        out_share,
        blend_sum,
        gain_two,
        in_share,
        down_share,
    )


def solution(mesh):
    return jax.shard_map(
        per_device,
        mesh=mesh,
        in_specs=(
            P(("dp", "head"), None),
            P(),
            P(None, "dp", "head"),
            P("head", "dp"),
            P(),
            P(),
            P(("dp", "head"), None),
            P(("dp", "head"), None),
            P(("dp", "head"), None),
            P("dp", None),
        ),
        out_specs=(
            P(("dp", "head"), None),
            P(("dp", "head"), None),
            P(),
            P(None, "dp", "head"),
            P("head", "dp"),
            P(),
            P(),
            P(("dp", "head"), None),
            P(("dp", "head"), None),
        ),
        check_vma=False,
    )
```

```python
import functools
import math

import jax
import jax.numpy as jnp
from jax import lax
from jax.experimental import pallas as pl
from jax.experimental.pallas import tpu as pltpu
from jax.sharding import PartitionSpec as P

HEAD_DIM = 64
BAND = 30
ROWS = 96
TAIL = 32
WIN = ROWS + TAIL
PAIR = 2 * HEAD_DIM
EPS = 1e-05
NEG = -1e30
CARRIED, LAST, VALID, ROW_AT, COLUMN_AT = range(-5, 0)
F32 = jnp.float32
BF16 = jnp.bfloat16
NT = (((1,), (1,)), ((), ()))
TN = (((0,), (0,)), ((), ()))
NN = (((1,), (0,)), ((), ()))


def mm(left, right, dims=NN):
    return lax.dot_general(left, right, dims, preferred_element_type=F32)


def iota(shape, axis):
    return lax.broadcasted_iota(jnp.int32, shape, axis)


def lift(values):
    return jnp.where(values > 0, values + 1.0, jnp.exp(jnp.minimum(values, 0.0)))


def head_lanes(dtype):
    first = (iota((1, PAIR), 1) < HEAD_DIM).astype(F32)
    return first.astype(dtype), (1.0 - first).astype(dtype)


def split_heads(block):
    first, second = head_lanes(block.dtype)
    return jnp.concatenate([block * first, block * second], axis=0)


def same_head():
    return (iota((PAIR, PAIR), 0) < HEAD_DIM) == (iota((PAIR, PAIR), 1) < HEAD_DIM)


def block_only(wide):
    keep = same_head()
    parts = [
        jnp.where(keep, wide[:, p * PAIR : (p + 1) * PAIR], 0.0)
        for p in range(wide.shape[1] // PAIR)
    ]
    return jnp.concatenate(parts, axis=1)


def fold(tall):
    half = tall.shape[0] // 2
    lanes = iota((half, PAIR), 1) < HEAD_DIM
    return jnp.where(lanes, tall[:half], tall[half:])


def two(half):
    return jnp.concatenate([half, half], axis=1)


def masks(step, start):
    row = iota((ROWS, WIN), 0) + step * ROWS
    first = step * ROWS - TAIL
    key = iota((ROWS, WIN), 1) + first
    floor = jnp.maximum(first, 0)
    causal = key <= row
    near = causal & (key >= jnp.maximum(start, row - (BAND - 1)))
    far = causal & (key >= jnp.maximum(start, floor))
    return near, far, start < floor, row, floor, first


def near_weights(query, key_heads, near):
    scores = mm(query, key_heads, NT) * (HEAD_DIM**-0.5)
    parts = []
    for h in range(2):
        part = jnp.where(near, scores[:, h * WIN : (h + 1) * WIN], NEG)
        parts.append(jnp.exp(part - jnp.max(part, axis=1, keepdims=True)))
    return jnp.concatenate(parts, axis=1)


def spread(product):
    high = product.astype(BF16)
    low = (product - high.astype(F32)).astype(BF16)
    table = (
        ((iota((2 * PAIR, 2 * WIN), 0) % PAIR) < HEAD_DIM) == (iota((2 * PAIR, 2 * WIN), 1) < WIN)
    ).astype(F32)
    return mm(jnp.concatenate([high, low], axis=1), table.astype(BF16))


def load_keys(qkv_ref, message_ref, keys, values):
    rows = qkv_ref.shape[1]
    keys[pl.ds(0, TAIL), :] = message_ref[0, pl.ds(HEAD_DIM, TAIL), :PAIR]
    keys[pl.ds(TAIL, rows), :] = qkv_ref[1]
    values[pl.ds(0, TAIL), :] = message_ref[0, pl.ds(HEAD_DIM, TAIL), PAIR : 2 * PAIR]
    values[pl.ds(TAIL, rows), :] = qkv_ref[2]


def fold_state(wide):
    kept = block_only(wide)
    return (kept[:HEAD_DIM] + kept[HEAD_DIM:]).astype(BF16)


def unfold_state(message):
    half = message[:HEAD_DIM].astype(F32)
    return block_only(jnp.concatenate([half, half], axis=0))


def project_kernel(
    scalars,
    tokens_ref,
    gain_ref,
    own_ref,
    other_ref,
    qkv_ref,
    normed_ref,
    weight_ref,
    out_weight_ref,
    message_ref,
    state,
    placed,
    *,
    flips,
):
    step = pl.program_id(0)
    rows, width = tokens_ref.shape
    pairs = width // PAIR
    half, _, tall, wide = own_ref.shape
    last = jnp.maximum(scalars[scalars.shape[0] + LAST], 0)

    @pl.when(step == 0)
    def _():
        for index, (flip_row, flip_column) in enumerate(flips):
            row = scalars[scalars.shape[0] + ROW_AT] ^ flip_row
            column = scalars[scalars.shape[0] + COLUMN_AT] ^ flip_column
            piece = own_ref[index] if index < half else other_ref[index - half]
            for c in range(4):
                placed[column, c, row] = piece[c]
        for h in range(width // wide):
            at = pl.ds(h * wide, wide)
            weight_ref[:, :, at] = placed[h, :3].reshape(3, width, wide)
            out_weight_ref[:, at] = placed[h, 3].reshape(width, wide)
        state[...] = jnp.zeros(state.shape, F32)

    normed = (norm_parts(tokens_ref[...].astype(F32))[0] * gain_ref[...]).astype(BF16)
    normed_ref[...] = normed
    for c in range(3):
        qkv_ref[c] = mm(normed, weight_ref[c]).astype(BF16)
    live = iota((rows, PAIR), 0) + step * rows >= last
    ones = jnp.ones((rows, PAIR), BF16)
    for p in range(pairs):
        at = pl.ds(p * PAIR, PAIR)
        key = qkv_ref[1, :, at].astype(F32)
        value = qkv_ref[2, :, at]
        lifted = jnp.where(live, lift(key), 0.0).astype(BF16)
        bent = jnp.where(live, jnp.tanh(key), 0.0).astype(BF16)
        state[p, :, : 2 * PAIR] += mm(lifted, jnp.concatenate([value, ones], axis=1), TN)
        state[p, :, 2 * PAIR :] += mm(bent, value, TN)

    @pl.when(step == pl.num_programs(0) - 1)
    def _():
        for p in range(pairs):
            at = pl.ds(p * PAIR, PAIR)
            message_ref[p, pl.ds(0, HEAD_DIM), :] = fold_state(state[p])
            message_ref[p, pl.ds(HEAD_DIM, TAIL), :] = jnp.concatenate(
                [
                    qkv_ref[1, pl.ds(rows - TAIL, TAIL), at],
                    qkv_ref[2, pl.ds(rows - TAIL, TAIL), at],
                    jnp.zeros((TAIL, PAIR), BF16),
                ],
                axis=1,
            )


def weight_grad_kernel(
    scalars, normed_ref, d_qkv_ref, out_grad_ref, keep_ref, give_ref, whole, *, flips
):
    c = pl.program_id(0)
    half, _, tall, wide = keep_ref.shape

    def place(total):
        for h in range(total.shape[1] // wide):
            part = total[:, h * wide : (h + 1) * wide]
            whole[h] = part.reshape(whole.shape[1:])

    @pl.when(c < 3)
    def _():
        place(mm(normed_ref[...], d_qkv_ref[0], TN))

    @pl.when(c == 3)
    def _():
        place(out_grad_ref[...])

    for index, (flip_row, flip_column) in enumerate(flips):
        row = scalars[scalars.shape[0] + ROW_AT] ^ flip_row
        column = scalars[scalars.shape[0] + COLUMN_AT] ^ flip_column
        if index < half:
            keep_ref[index, 0] = whole[column, row]
        else:
            give_ref[index - half, 0] = whole[column, row].astype(BF16)


def forward_kernel(
    scalars,
    qkv_ref,
    message_ref,
    start_ref,
    blend_ref,
    att_ref,
    near_ref,
    far1_ref,
    far2_ref,
    invl_ref,
    invd_ref,
    states_ref,
    keys,
    values,
    state,
):
    rows = qkv_ref.shape[1]
    load_keys(qkv_ref, message_ref, keys, values)
    state[...] = unfold_state(message_ref[0])
    count_valid = scalars[scalars.shape[0] + VALID]
    b0, b1, b2 = (blend_ref[pl.ds(f, 1), :] for f in range(3))

    def body(step, carry):
        at = pl.multiple_of(step * ROWS, 32)
        query = qkv_ref[0, pl.ds(at, ROWS), :]
        key = keys[pl.ds(at, WIN), :]
        value = values[pl.ds(at, WIN), :]
        start = start_ref[pl.ds(at, ROWS), :]
        near_mask, far_mask, carried, row, floor, first = masks(step, start)
        query_f = query.astype(F32)
        key_f = key.astype(F32)
        lift_q = lift(query_f).astype(BF16)
        bend_q = jnp.tanh(query_f).astype(BF16)
        lift_k = lift(key_f)
        bend_k = jnp.tanh(key_f)
        ones = jnp.ones((WIN, PAIR), BF16)
        value_heads = jnp.concatenate([split_heads(value), split_heads(ones)], axis=1)
        weights = near_weights(query, split_heads(key), near_mask).astype(BF16)
        near_out = mm(weights, value_heads)
        inv_l = 1.0 / near_out[:, PAIR:]
        near = near_out[:, :PAIR] * inv_l
        before = state[...]
        before_low = before.astype(BF16)
        states_ref[0, pl.ds(pl.multiple_of(step * PAIR, PAIR), PAIR), :] = before_low
        far_two = two(far_mask)
        pair_weight = jnp.where(far_two, mm(lift_q, split_heads(lift_k.astype(BF16)), NT), 0.0)
        elu_out = mm(pair_weight.astype(BF16), value_heads)
        elu_state = mm(lift_q, before_low[:, : 2 * PAIR])
        numerator = elu_out[:, :PAIR] + jnp.where(carried, elu_state[:, :PAIR], 0.0)
        inv_d = 1.0 / (elu_out[:, PAIR:] + jnp.where(carried, elu_state[:, PAIR:], 0.0))
        far1 = numerator * inv_d
        pair_bend = jnp.where(far_two, mm(bend_q, split_heads(bend_k.astype(BF16)), NT), 0.0)
        tanh_out = mm(pair_bend.astype(BF16), value_heads[:, :PAIR]) + jnp.where(
            carried, mm(bend_q, before_low[:, 2 * PAIR :]), 0.0
        )
        far2 = tanh_out / (row - start + 1).astype(F32)
        mixed = jnp.where(row < count_valid, b0 * near + b1 * far1 + b2 * far2, 0.0)
        att_ref[pl.ds(at, ROWS), :] = mixed.astype(BF16)
        near_ref[pl.ds(at, ROWS), :] = near
        far1_ref[pl.ds(at, ROWS), :] = far1
        far2_ref[pl.ds(at, ROWS), :] = far2
        invl_ref[pl.ds(at, ROWS), :] = inv_l
        invd_ref[pl.ds(at, ROWS), :] = inv_d
        closing = scalars[step]
        live = iota((ROWS, PAIR), 0) + first >= jnp.maximum(closing, floor)
        lifted = jnp.where(live, lift_k[:ROWS], 0.0).astype(BF16)
        bent = jnp.where(live, bend_k[:ROWS], 0.0).astype(BF16)
        with_ones = jnp.concatenate([value[:ROWS], ones[:ROWS]], axis=1)
        added = jnp.concatenate([mm(lifted, with_ones, TN), mm(bent, value[:ROWS], TN)], axis=1)
        keep = (closing < floor).astype(F32)
        state[...] = keep * before + block_only(added)
        return carry

    lax.fori_loop(0, rows // ROWS, body, 0, unroll=2)


def near_back(query, key_heads, grad_pair, near_mask, spread_near, scale_q, rows_q, rows_g):
    weights = near_weights(query, key_heads, near_mask)
    shifted = (weights * (grad_pair - spread_near)).astype(BF16)
    d_query = mm(shifted, key_heads) * scale_q
    d_key = fold(mm(shifted, rows_q, TN))
    return weights.astype(BF16), d_query, d_key


def prologue_kernel(
    scalars,
    query_ref,
    key_ref,
    message_ref,
    start_ref,
    blend_ref,
    grad_ref,
    near_ref,
    far1_ref,
    invl_ref,
    invd_ref,
    back_ref,
    adjoint,
):
    rows = query_ref.shape[1]
    step_rows = rows // 3
    count_valid = scalars[scalars.shape[0] + VALID]
    b0, b1, b2 = (blend_ref[pl.ds(f, 1), :] for f in range(3))
    adjoint[...] = jnp.zeros(adjoint.shape, F32)

    tails = message_ref[0, pl.ds(HEAD_DIM, TAIL), :]
    key = jnp.concatenate([tails[:, :PAIR], key_ref[0]], axis=0)
    value = jnp.concatenate([tails[:, PAIR : 2 * PAIR], key_ref[1]], axis=0)
    start = start_ref[pl.ds(0, ROWS), :]
    near_mask, _, _, row, _, _ = masks(0, start)
    query = query_ref[0, pl.ds(0, ROWS), :]
    grad_f = jnp.where(row < count_valid, grad_ref[pl.ds(0, ROWS), :].astype(F32), 0.0)
    grad = grad_f.astype(BF16)
    scale = b0 * invl_ref[...]
    rows_q = (query.astype(F32) * (scale * HEAD_DIM**-0.5)).astype(BF16)
    rows_g = (grad_f * scale).astype(BF16)
    weights, _, d_key = near_back(
        query,
        split_heads(key),
        mm(grad, split_heads(value), NT),
        near_mask,
        spread(grad_f * near_ref[...]),
        scale * HEAD_DIM**-0.5,
        rows_q,
        rows_g,
    )
    back_ref[0, pl.ds(HEAD_DIM, TAIL), :] = jnp.concatenate(
        [d_key[:TAIL], fold(mm(weights, rows_g, TN))[:TAIL], jnp.zeros((TAIL, PAIR), F32)], axis=1
    ).astype(BF16)
    heads = same_head().astype(F32).astype(BF16)
    heads = jnp.concatenate([heads, heads], axis=0)

    for step in range(3):
        at = step * step_rows

        @pl.when(scalars[scalars.shape[0] + CARRIED] > at)
        def _():
            here = pl.ds(at, step_rows)
            row = iota((step_rows, PAIR), 0) + at
            start = start_ref[here, :]
            grad_f = jnp.where(row < count_valid, grad_ref[here, :].astype(F32), 0.0)
            grad = grad_f.astype(BF16)
            product = grad_f * far1_ref[here, :]
            high = product.astype(BF16)
            low = (product - high.astype(F32)).astype(BF16)
            along = mm(jnp.concatenate([high, low], axis=1), heads).astype(BF16)
            query_f = query_ref[0, here, :].astype(F32)
            live = start < 0
            scaled = jnp.where(live, lift(query_f) * (b1 * invd_ref[here, :]), 0.0)
            bent = jnp.where(
                live, jnp.tanh(query_f) * (b2 / (row - start + 1).astype(F32)), 0.0
            )
            adjoint[:, : 2 * PAIR] += mm(
                scaled.astype(BF16), jnp.concatenate([grad, along], axis=1), TN
            )
            adjoint[:, 2 * PAIR :] += mm(bent.astype(BF16), grad, TN)

    back_ref[0, pl.ds(0, HEAD_DIM), :] = fold_state(adjoint[...])


def key_side(adjoint_low, lift_k, bend_k, value):
    ones = jnp.full(value.shape, -1.0 / HEAD_DIM, BF16)
    d_lift = mm(jnp.concatenate([value, ones], axis=1), adjoint_low[:, : 2 * PAIR], NT)
    d_bend = mm(value, adjoint_low[:, 2 * PAIR :], NT)
    both = jnp.concatenate([adjoint_low[:, :PAIR], adjoint_low[:, 2 * PAIR :]], axis=0)
    d_value = mm(jnp.concatenate([lift_k, bend_k], axis=1), both)
    return d_lift, d_bend, d_value


def backward_kernel(
    scalars,
    qkv_ref,
    message_ref,
    start_ref,
    blend_ref,
    grad_ref,
    near_ref,
    far1_ref,
    far2_ref,
    invl_ref,
    invd_ref,
    states_ref,
    back_ref,
    done_ref,
    out_ref,
    sums_ref,
    keys,
    values,
    adjoint,
    key_carry,
    value_carry,
):
    rows = qkv_ref.shape[1]
    steps = rows // ROWS
    load_keys(qkv_ref, message_ref, keys, values)
    count_valid = scalars[scalars.shape[0] + VALID]
    last = scalars[scalars.shape[0] + LAST]
    b0, b1, b2 = (blend_ref[pl.ds(f, 1), :] for f in range(3))
    lanes = iota((ROWS, PAIR), 1) < HEAD_DIM

    arrived = unfold_state(back_ref[0])
    tail_grads = back_ref[0, pl.ds(HEAD_DIM, TAIL), :].astype(F32)
    end_key = keys[pl.ds(rows, TAIL), :].astype(F32)
    end_lift, end_bend = lift(end_key), jnp.tanh(end_key)
    end_parts = key_side(
        arrived.astype(BF16), end_lift.astype(BF16), end_bend.astype(BF16), values[pl.ds(rows, TAIL), :]
    )
    live = iota((TAIL, PAIR), 0) + (rows - TAIL) >= last
    key_carry[...] = tail_grads[:, :PAIR] + jnp.where(
        live,
        end_parts[0] * jnp.minimum(end_lift, 1.0) + end_parts[1] * (1.0 - end_bend * end_bend),
        0.0,
    )
    value_carry[...] = tail_grads[:, PAIR : 2 * PAIR] + jnp.where(live, end_parts[2], 0.0)
    adjoint[...] = jnp.where(last < rows - TAIL, 1.0, 0.0) * arrived
    sums_ref[...] = jnp.zeros(sums_ref.shape, F32)

    def add_up(place, product):
        sums_ref[pl.ds(place, 8), :] += jnp.sum(product.reshape(ROWS // 8, 8, PAIR), axis=0)

    def body(back, carry):
        step = steps - 1 - back
        at = pl.multiple_of(step * ROWS, 32)
        query = qkv_ref[0, pl.ds(at, ROWS), :]
        key = keys[pl.ds(at, WIN), :]
        value = values[pl.ds(at, WIN), :]
        start = start_ref[pl.ds(at, ROWS), :]
        near_mask, far_mask, carried, row, floor, first = masks(step, start)
        far_two = two(far_mask)
        grad_f = jnp.where(row < count_valid, grad_ref[pl.ds(at, ROWS), :].astype(F32), 0.0)
        grad = grad_f.astype(BF16)
        query_f = query.astype(F32)
        key_f = key.astype(F32)
        lift_qf, bend_qf = lift(query_f), jnp.tanh(query_f)
        lift_kf, bend_kf = lift(key_f), jnp.tanh(key_f)
        lift_q, bend_q = lift_qf.astype(BF16), bend_qf.astype(BF16)
        lift_k, bend_k = lift_kf.astype(BF16), bend_kf.astype(BF16)
        lift_heads, bend_heads = split_heads(lift_k), split_heads(bend_k)
        r0 = b0 * invl_ref[pl.ds(at, ROWS), :]
        r1 = b1 * invd_ref[pl.ds(at, ROWS), :]
        r2 = b2 / (row - start + 1).astype(F32)
        grad_pair = mm(grad, split_heads(value), NT)
        rows_q = (query_f * (r0 * HEAD_DIM**-0.5)).astype(BF16)
        near_product = grad_f * near_ref[pl.ds(at, ROWS), :]
        weights, d_query, d_key = near_back(
            query,
            split_heads(key),
            grad_pair,
            near_mask,
            spread(near_product),
            r0 * HEAD_DIM**-0.5,
            rows_q,
            None,
        )
        far1_product = grad_f * far1_ref[pl.ds(at, ROWS), :]
        add_up(0, near_product)
        add_up(8, far1_product)
        add_up(16, grad_f * far2_ref[pl.ds(at, ROWS), :])
        spread_far = spread(far1_product)
        along = jnp.where(lanes, spread_far[:, :WIN], spread_far[:, WIN:])
        shifted = jnp.where(far_two, grad_pair - spread_far, 0.0).astype(BF16)
        plain = jnp.where(far_two, grad_pair, 0.0).astype(BF16)
        pair_weight = jnp.where(far_two, mm(lift_q, lift_heads, NT), 0.0).astype(BF16)
        pair_bend = jnp.where(far_two, mm(bend_q, bend_heads, NT), 0.0).astype(BF16)
        before = states_ref[0, pl.ds(pl.multiple_of(step * PAIR, PAIR), PAIR), :]
        scaled_along = (along * (-1.0 / HEAD_DIM)).astype(BF16)
        state_lift = mm(jnp.concatenate([grad, scaled_along], axis=1), before[:, : 2 * PAIR], NT)
        state_bend = mm(grad, before[:, 2 * PAIR :], NT)
        d_query = (
            d_query
            + (mm(shifted, lift_heads) + jnp.where(carried, state_lift, 0.0))
            * (r1 * jnp.minimum(lift_qf, 1.0))
            + (mm(plain, bend_heads) + jnp.where(carried, state_bend, 0.0))
            * (r2 * (1.0 - bend_qf * bend_qf))
        )
        out_ref[0, pl.ds(at, ROWS), :] = d_query.astype(BF16)
        rows_a = lift_qf * r1
        rows_t = bend_qf * r2
        d_lift = fold(mm(shifted, rows_a.astype(BF16), TN))
        d_bend = fold(mm(plain, rows_t.astype(BF16), TN))
        d_value = fold(
            mm(
                jnp.concatenate([weights, pair_weight, pair_bend], axis=0),
                jnp.concatenate([grad_f * r0, grad_f * r1, grad_f * r2], axis=0).astype(BF16),
                TN,
            )
        )
        after = adjoint[...]
        parts = key_side(after.astype(BF16), lift_k[:ROWS], bend_k[:ROWS], value[:ROWS])
        closing = scalars[step]
        live = iota((ROWS, PAIR), 0) + first >= jnp.maximum(closing, floor)
        pad = jnp.zeros((TAIL, PAIR), F32)
        d_lift = d_lift + jnp.concatenate([jnp.where(live, parts[0], 0.0), pad], axis=0)
        d_bend = d_bend + jnp.concatenate([jnp.where(live, parts[1], 0.0), pad], axis=0)
        d_value = d_value + jnp.concatenate([jnp.where(live, parts[2], 0.0), pad], axis=0)
        d_key = d_key + d_lift * jnp.minimum(lift_kf, 1.0) + d_bend * (1.0 - bend_kf * bend_kf)
        out_ref[1, pl.ds(at, ROWS), :] = jnp.concatenate(
            [d_key[TAIL:ROWS], d_key[ROWS:] + key_carry[...]], axis=0
        ).astype(BF16)
        out_ref[2, pl.ds(at, ROWS), :] = jnp.concatenate(
            [d_value[TAIL:ROWS], d_value[ROWS:] + value_carry[...]], axis=0
        ).astype(BF16)
        key_carry[...] = d_key[:TAIL]
        value_carry[...] = d_value[:TAIL]
        from_lift = mm(
            jnp.where(carried, rows_a, 0.0).astype(BF16),
            jnp.concatenate([grad, along.astype(BF16)], axis=1),
            TN,
        )
        from_bend = mm(jnp.where(carried, rows_t, 0.0).astype(BF16), grad, TN)
        keep = (closing < floor).astype(F32)
        adjoint[...] = keep * after + block_only(jnp.concatenate([from_lift, from_bend], axis=1))
        return carry

    lax.fori_loop(0, steps, body, 0)


def resume(kernel, done, scalars, qkv_ref, message_ref, start_ref, blend_ref, *refs):
    kernel(scalars, qkv_ref, message_ref, start_ref, blend_ref, *refs[done:])


def pair_specs(rows, first=0):
    return {
        "qkv": pl.BlockSpec((3, rows, PAIR), lambda p, s: (0, 0, p + first)),
        "message": pl.BlockSpec((1, HEAD_DIM + TAIL, 3 * PAIR), lambda p, s: (p + first, 0, 0)),
        "start": pl.BlockSpec((rows, PAIR), lambda p, s: (0, 0)),
        "blend": pl.BlockSpec((3, PAIR), lambda p, s: (0, p + first)),
        "column": pl.BlockSpec((rows, PAIR), lambda p, s: (0, p + first)),
        "states": pl.BlockSpec((1, rows // ROWS * PAIR, 3 * PAIR), lambda p, s: (p + first, 0, 0)),
        "sums": pl.BlockSpec((24, PAIR), lambda p, s: (0, p)),
        "query": pl.BlockSpec((1, rows, PAIR), lambda p, s: (0, 0, p)),
        "head_rows": pl.BlockSpec((ROWS, PAIR), lambda p, s: (0, p)),
    }


def call(kernel, ins, outs, out_shapes, scratch, grid, name, flops, moved, aliases={}):
    return pl.pallas_call(
        kernel,
        out_shape=out_shapes,
        grid_spec=pltpu.PrefetchScalarGridSpec(
            num_scalar_prefetch=1,
            grid=(grid,),
            in_specs=ins,
            out_specs=outs,
            scratch_shapes=scratch,
        ),
        input_output_aliases=aliases,
        compiler_params=pltpu.CompilerParams(
            dimension_semantics=("arbitrary",), vmem_limit_bytes=56 * 1024 * 1024
        ),
        cost_estimate=pl.CostEstimate(flops=flops, bytes_accessed=moved, transcendentals=0),
        name=name,
    )


def norm_parts(source):
    centered = source - jnp.mean(source, axis=-1, keepdims=True)
    spread_of = jnp.mean(centered * centered, axis=-1, keepdims=True)
    scale = lax.rsqrt(spread_of + EPS)
    return centered * scale, scale


def norm_back(d_out, gain, normal, scale):
    e = d_out * gain
    inner = jnp.mean(e, axis=-1, keepdims=True)
    along = jnp.mean(e * normal, axis=-1, keepdims=True)
    return scale * (e - inner - normal * along), jnp.sum(d_out * normal, axis=0)


def bits(size):
    return [1 << b for b in range(int(math.log2(size)))]


def phases():
    dp = bits(lax.axis_size("dp"))
    core, rest = dp[:1], dp[1:]
    mid = len(rest) // 2
    far = [("dp", m) for m in rest[mid:]]
    near = [("dp", m) for m in rest[:mid]] + [("head", m) for m in bits(lax.axis_size("head"))]
    groups = []
    for run in (far, near, [("dp", m) for m in core]):
        groups += [run[i : i + 2] for i in range(0, len(run), 2)]
    return groups


def relative_bits():
    return [pair for group in phases() for pair in group]


def all_flips():
    order = relative_bits()
    flips = []
    for index in range(1 << len(order)):
        chosen = [pair for place, pair in enumerate(order) if index >> place & 1]
        flips.append(tuple(sum(m for a, m in chosen if a == axis) for axis in ("dp", "head")))
    return flips


def peer(array, group, combo):
    n_dp, n_head = lax.axis_size("dp"), lax.axis_size("head")
    chosen = [pair for place, pair in enumerate(group) if combo >> place & 1]
    flip_dp = sum(m for axis, m in chosen if axis == "dp")
    flip_head = sum(m for axis, m in chosen if axis == "head")
    pairs = [
        (d * n_head + h, (d ^ flip_dp) * n_head + (h ^ flip_head))
        for d in range(n_dp)
        for h in range(n_head)
    ]
    return lax.ppermute(array, ("dp", "head"), pairs)


def widen(block, group, axis, after=None):
    others = [peer(block, group, combo) for combo in range(1, 1 << len(group))]
    if after is not None:
        others, after = lax.optimization_barrier((others, after))
    whole = jnp.concatenate([block] + others, axis=axis)
    return whole if after is None else (whole, after)


def narrow(keep, gives, group):
    total = keep.astype(F32)
    for combo, give in enumerate(gives, 1):
        total = total + peer(give.astype(BF16), group, combo).astype(F32)
    return total


def narrow_axis(total, group, axis):
    parts = jnp.split(total, 1 << len(group), axis=axis)
    return narrow(parts[0], parts[1:], group)


def sum_everywhere(array):
    for group in reversed(phases()):
        array = array + sum(peer(array, group, combo) for combo in range(1, 1 << len(group)))
    return array


def pass_along(local, keep, shift):
    size = lax.axis_size("head")
    pairs = [(i, i + shift) for i in range(size) if 0 <= i + shift < size]
    arrived = lax.ppermute(local, "head", pairs)
    for _ in range(size - 2):
        rows = iota(local.shape, 1) < HEAD_DIM
        total = local.astype(F32) + jnp.where(rows, keep * arrived.astype(F32), 0.0)
        arrived = lax.ppermute(total.astype(BF16), "head", pairs)
    return arrived


def per_device(
    tokens,
    ln1_gain,
    qkv_weight,
    out_weight,
    blend,
    ln2_gain,
    in_weight,
    down_weight,
    cotangent,
    lengths,
):
    rows, width = tokens.shape
    n_dp, n_head = lax.axis_size("dp"), lax.axis_size("head")
    pairs = width // PAIR
    steps = rows // ROWS
    groups = phases()
    flips = all_flips()

    shards = jnp.concatenate([qkv_weight, out_weight.T[None]], axis=0)[None]
    feed = jnp.stack([in_weight, down_weight])
    for group in groups[:-1]:
        shards = widen(shards, group, 0)
    others = peer(shards, groups[-1], 1)
    feed, others = lax.optimization_barrier((feed, others))

    item_lengths = lengths[0]
    slots = item_lengths.shape[0]
    ends = jnp.sum(
        jnp.where(iota((slots, slots), 1) <= iota((slots, slots), 0), item_lengths[None, :], 0),
        axis=1,
    )
    offset = lax.axis_index("head") * rows
    local = jnp.arange(rows, dtype=jnp.int32)
    place = local + offset
    total = ends[slots - 1]
    item_start = jnp.max(
        jnp.where(ends[None, :] <= place[:, None], ends[None, :], 0), axis=1
    )
    start = jnp.where(place < total, item_start - offset, local)
    carried_rows = jnp.sum((start < 0).astype(jnp.int32))
    scalars = jnp.concatenate(
        [
            start.reshape(steps, ROWS)[:, ROWS - TAIL - 1],
            carried_rows[None],
            start[rows - 1 :],
            (total - offset)[None],
            lax.axis_index("dp").astype(jnp.int32)[None],
            lax.axis_index("head").astype(jnp.int32)[None],
        ]
    )
    start_wide = jnp.broadcast_to(start[:, None], (rows, PAIR))
    keep_all = (start[rows - 1] < 0).astype(F32)
    blend_wide = jnp.repeat(blend, HEAD_DIM, axis=1)

    spec = pair_specs(rows)
    wide = jax.ShapeDtypeStruct((rows, width), F32)
    states_shape = jax.ShapeDtypeStruct((pairs, steps * PAIR, 3 * PAIR), BF16)
    message_shape = jax.ShapeDtypeStruct((pairs, HEAD_DIM + TAIL, 3 * PAIR), BF16)
    big = rows * width
    part = rows // 3

    def whole_spec(shape):
        return pl.BlockSpec(shape, lambda p, s: (0,) * len(shape))

    qkv, normed_one, qkv_all, out_all, closing = call(
        functools.partial(project_kernel, flips=flips),
        [
            pl.BlockSpec((part, width), lambda p, s: (p, 0)),
            whole_spec((1, width)),
            whole_spec(shards.shape),
            whole_spec(shards.shape),
        ],
        [
            pl.BlockSpec((3, part, width), lambda p, s: (0, p, 0)),
            pl.BlockSpec((part, width), lambda p, s: (p, 0)),
            whole_spec((3, width, width)),
            whole_spec((width, width)),
            whole_spec(message_shape.shape),
        ],
        [
            jax.ShapeDtypeStruct((3, rows, width), BF16),
            jax.ShapeDtypeStruct((rows, width), BF16),
            jax.ShapeDtypeStruct((3, width, width), BF16),
            jax.ShapeDtypeStruct((width, width), BF16),
            message_shape,
        ],
        [
            pltpu.VMEM((pairs, PAIR, 3 * PAIR), F32),
            pltpu.VMEM((n_head, 4, n_dp, width // n_dp, width // n_head), BF16),
        ],
        3,
        "project",
        6 * big * width,
        12 * big,
    )(scalars, tokens, ln1_gain[None], shards, others)
    feed = widen(feed, groups[0], 1)
    feed, closing = lax.optimization_barrier((feed, closing))
    message = pass_along(closing, keep_all, 1)

    key_scratch = pltpu.VMEM((rows + TAIL, PAIR), BF16)
    state_scratch = pltpu.VMEM((PAIR, 3 * PAIR), F32)
    tail_scratch = pltpu.VMEM((TAIL, PAIR), F32)
    results = ()
    count = pairs // 2
    for first in (0, count):
        spec = pair_specs(rows, first)
        results = call(
            functools.partial(resume, forward_kernel, len(results)),
            [spec["qkv"], spec["message"], spec["start"], spec["blend"]]
            + [pl.BlockSpec(memory_space=pl.ANY)] * len(results),
            [spec["column"]] * 6 + [spec["states"]],
            [jax.ShapeDtypeStruct((rows, width), BF16)] + [wide] * 5 + [states_shape],
            [key_scratch, key_scratch, state_scratch],
            count,
            "forward",
            4000 * big,
            20 * big,
            {5 + i: i for i in range(len(results))},
        )(scalars, qkv, message, start_wide, blend_wide, *results)
        if not first:
            feed, results = widen(feed, groups[1], 1, results)
            feed, message = lax.optimization_barrier((feed, message))
    for group in groups[2:]:
        feed = widen(feed, group, 1)
    in_all, down_all = feed[0], feed[1]
    mixed, near, far1, far2, inv_l, inv_d, states = results

    spec = pair_specs(rows)
    residual = tokens.astype(F32)
    hidden = residual + lax.dot_general(mixed, out_all, NT, preferred_element_type=F32)
    normal_two, scale_two = norm_parts(hidden)
    normed_two = (normal_two * ln2_gain).astype(BF16)
    inner = lax.dot_general(normed_two, in_all, NT, preferred_element_type=F32)
    c0 = math.sqrt(2.0 / math.pi)
    bent = jnp.tanh(c0 * (inner + 0.044715 * (inner * inner * inner)))
    active = (0.5 * inner * (1.0 + bent)).astype(BF16)
    layer_out = (hidden + jnp.dot(active, down_all, preferred_element_type=F32)).astype(BF16)
    d_active = lax.dot_general(cotangent, down_all, NT, preferred_element_type=F32)
    down_grad = lax.dot_general(active, cotangent, TN, preferred_element_type=F32)
    slope = 0.5 * (1.0 + bent) + 0.5 * inner * (1.0 - bent * bent) * c0 * (
        1.0 + 3.0 * 0.044715 * inner * inner
    )
    d_inner = (d_active * slope).astype(BF16)
    in_grad = lax.dot_general(d_inner, normed_two, TN, preferred_element_type=F32)
    d_normed_two = jnp.dot(d_inner, in_all, preferred_element_type=F32)
    d_hidden_part, gain_two_part = norm_back(d_normed_two, ln2_gain, normal_two, scale_two)
    d_hidden = cotangent.astype(F32) + d_hidden_part
    d_branch = d_hidden.astype(BF16)
    d_mixed = jnp.dot(d_branch, out_all, preferred_element_type=F32).astype(BF16)
    out_grad = lax.dot_general(d_branch, mixed, TN, preferred_element_type=F32)

    front_keys = qkv[1:, :ROWS]
    back = call(
        prologue_kernel,
        [
            spec["query"],
            pl.BlockSpec((2, ROWS, PAIR), lambda p, s: (0, 0, p)),
            spec["message"],
            spec["start"],
            spec["blend"],
            spec["column"],
            spec["head_rows"],
            spec["column"],
            spec["head_rows"],
            spec["column"],
        ],
        spec["message"],
        message_shape,
        [state_scratch],
        pairs,
        "prologue",
        500 * big,
        20 * big,
    )(scalars, qkv, front_keys, message, start_wide, blend_wide, d_mixed, near, far1, inv_l, inv_d)
    back_in = pass_along(back, keep_all, -1)

    half = in_grad.shape[0] // 2
    keep = jnp.stack([in_grad[:half], down_grad[:half]])
    give = jnp.stack([in_grad[half:], down_grad[half:]]).astype(BF16)
    feed_share = narrow(keep, [give], groups[-1])
    left = list(reversed(groups[:-1]))

    d_qkv = jnp.zeros((3, 8, PAIR), BF16)
    sums = []
    first = 0
    for count in (pairs // 4, pairs // 2, pairs // 4):
        spec = pair_specs(rows, first)
        more = {13: 0} if first else {}
        d_qkv, part_sums = call(
            backward_kernel,
            [spec["qkv"], spec["message"], spec["start"], spec["blend"]]
            + [spec["column"]] * 6
            + [spec["states"], spec["message"], pl.BlockSpec(memory_space=pl.ANY)],
            [spec["qkv"], spec["sums"]],
            [
                jax.ShapeDtypeStruct((3, rows, width), BF16),
                jax.ShapeDtypeStruct((24, count * PAIR), F32),
            ],
            [key_scratch, key_scratch, state_scratch, tail_scratch, tail_scratch],
            count,
            "backward",
            16000 * big * count // pairs,
            40 * big * count // pairs,
            more,
        )(
            scalars,
            qkv,
            message,
            start_wide,
            blend_wide,
            d_mixed,
            near,
            far1,
            far2,
            inv_l,
            inv_d,
            states,
            back_in,
            d_qkv,
        )
        sums.append(part_sums)
        first += count
        if left and first < pairs:
            feed_share, back_in = lax.optimization_barrier((feed_share, back_in))
            feed_share = narrow_axis(feed_share, left.pop(0), 1)
    for group in left:
        feed_share = narrow_axis(feed_share, group, 1)
    feed_share, d_qkv = lax.optimization_barrier((feed_share, d_qkv))
    sums = jnp.concatenate(sums, axis=1)
    blend_part = jnp.sum(sums.reshape(3, 8, blend.shape[1], HEAD_DIM), axis=(1, 3))

    shard_shape = (n_dp * n_head // 2, 4, width // n_dp, width // n_head)
    shard_spec = pl.BlockSpec((shard_shape[0], 1) + shard_shape[2:], lambda p, s: (0, p, 0, 0))
    keep, give = call(
        functools.partial(weight_grad_kernel, flips=flips),
        [
            whole_spec((rows, width)),
            pl.BlockSpec((1, rows, width), lambda p, s: (jnp.minimum(p, 2), 0, 0)),
            whole_spec((width, width)),
        ],
        [shard_spec, shard_spec],
        [jax.ShapeDtypeStruct(shard_shape, F32), jax.ShapeDtypeStruct(shard_shape, BF16)],
        [pltpu.VMEM((n_head, n_dp, width // n_dp, width // n_head), F32)],
        4,
        "weight_grad",
        6 * big * width,
        8 * big,
    )(scalars, normed_one, d_qkv, out_grad)
    share = narrow(keep, [give], groups[-1])
    d_qkv, give = lax.optimization_barrier((d_qkv, give))
    for group in reversed(groups[:-1]):
        share = narrow_axis(share, group, 0)
    d_normed_one = jnp.einsum("cte,cde->td", d_qkv, qkv_all, preferred_element_type=F32)
    normal_one, scale_one = norm_parts(residual)
    d_residual_part, gain_one_part = norm_back(d_normed_one, ln1_gain, normal_one, scale_one)
    input_grad = d_hidden + d_residual_part
    gathered = jnp.concatenate([gain_one_part, gain_two_part, blend_part.reshape(-1)])
    total_sums = sum_everywhere(gathered[None])[0]
    gain_one, gain_two = total_sums[:width], total_sums[width : 2 * width]
    blend_sum = total_sums[2 * width :].reshape(blend.shape)
    qkv_share, out_share = share[0, :3], share[0, 3].T
    in_share, down_share = feed_share[0], feed_share[1]
    return (
        layer_out,
        input_grad,
        gain_one,
        qkv_share,
        out_share,
        blend_sum,
        gain_two,
        in_share,
        down_share,
    )


def solution(mesh):
    return jax.shard_map(
        per_device,
        mesh=mesh,
        in_specs=(
            P(("dp", "head"), None),
            P(),
            P(None, "dp", "head"),
            P("head", "dp"),
            P(),
            P(),
            P(("dp", "head"), None),
            P(("dp", "head"), None),
            P(("dp", "head"), None),
            P("dp", None),
        ),
        out_specs=(
            P(("dp", "head"), None),
            P(("dp", "head"), None),
            P(),
            P(None, "dp", "head"),
            P("head", "dp"),
            P(),
            P(),
            P(("dp", "head"), None),
            P(("dp", "head"), None),
        ),
        check_vma=False,
    )
```

```python
import functools
import math

import jax
import jax.numpy as jnp
from jax import lax
from jax.experimental import pallas as pl
from jax.experimental.pallas import tpu as pltpu
from jax.sharding import PartitionSpec as P

HEAD_DIM = 64
BAND = 30
ROWS = 96
TAIL = 32
WIN = ROWS + TAIL
PAIR = 2 * HEAD_DIM
EPS = 1e-05
NEG = -1e30
CARRIED, LAST, VALID, ROW_AT, COLUMN_AT = range(-5, 0)
F32 = jnp.float32
BF16 = jnp.bfloat16
NT = (((1,), (1,)), ((), ()))
TN = (((0,), (0,)), ((), ()))
NN = (((1,), (0,)), ((), ()))


def mm(left, right, dims=NN):
    return lax.dot_general(left, right, dims, preferred_element_type=F32)


def iota(shape, axis):
    return lax.broadcasted_iota(jnp.int32, shape, axis)


def lift(values):
    return jnp.where(values > 0, values + 1.0, jnp.exp(jnp.minimum(values, 0.0)))


def head_lanes(dtype):
    first = (iota((1, PAIR), 1) < HEAD_DIM).astype(F32)
    return first.astype(dtype), (1.0 - first).astype(dtype)


def split_heads(block):
    first, second = head_lanes(block.dtype)
    return jnp.concatenate([block * first, block * second], axis=0)


def same_head():
    return (iota((PAIR, PAIR), 0) < HEAD_DIM) == (iota((PAIR, PAIR), 1) < HEAD_DIM)


def block_only(wide):
    keep = same_head()
    parts = [
        jnp.where(keep, wide[:, p * PAIR : (p + 1) * PAIR], 0.0)
        for p in range(wide.shape[1] // PAIR)
    ]
    return jnp.concatenate(parts, axis=1)


def fold(tall):
    half = tall.shape[0] // 2
    lanes = iota((half, PAIR), 1) < HEAD_DIM
    return jnp.where(lanes, tall[:half], tall[half:])


def two(half):
    return jnp.concatenate([half, half], axis=1)


def masks(step, start):
    row = iota((ROWS, WIN), 0) + step * ROWS
    first = step * ROWS - TAIL
    key = iota((ROWS, WIN), 1) + first
    floor = jnp.maximum(first, 0)
    causal = key <= row
    near = causal & (key >= jnp.maximum(start, row - (BAND - 1)))
    far = causal & (key >= jnp.maximum(start, floor))
    return near, far, start < floor, row, floor, first


def near_weights(query, key_heads, near):
    scores = mm(query, key_heads, NT) * (HEAD_DIM**-0.5)
    parts = []
    for h in range(2):
        part = jnp.where(near, scores[:, h * WIN : (h + 1) * WIN], NEG)
        parts.append(jnp.exp(part - jnp.max(part, axis=1, keepdims=True)))
    return jnp.concatenate(parts, axis=1)


def spread(product):
    high = product.astype(BF16)
    low = (product - high.astype(F32)).astype(BF16)
    table = (
        ((iota((2 * PAIR, 2 * WIN), 0) % PAIR) < HEAD_DIM) == (iota((2 * PAIR, 2 * WIN), 1) < WIN)
    ).astype(F32)
    return mm(jnp.concatenate([high, low], axis=1), table.astype(BF16))


def load_keys(qkv_ref, message_ref, keys, values):
    rows = qkv_ref.shape[1]
    keys[pl.ds(0, TAIL), :] = message_ref[0, pl.ds(HEAD_DIM, TAIL), :PAIR]
    keys[pl.ds(TAIL, rows), :] = qkv_ref[1]
    values[pl.ds(0, TAIL), :] = message_ref[0, pl.ds(HEAD_DIM, TAIL), PAIR : 2 * PAIR]
    values[pl.ds(TAIL, rows), :] = qkv_ref[2]


def fold_state(wide):
    kept = block_only(wide)
    return (kept[:HEAD_DIM] + kept[HEAD_DIM:]).astype(BF16)


def unfold_state(message):
    half = message[:HEAD_DIM].astype(F32)
    return block_only(jnp.concatenate([half, half], axis=0))


def project_kernel(
    scalars,
    tokens_ref,
    gain_ref,
    own_ref,
    other_ref,
    qkv_ref,
    normed_ref,
    weight_ref,
    out_weight_ref,
    message_ref,
    state,
    placed,
    *,
    flips,
):
    step = pl.program_id(0)
    rows, width = tokens_ref.shape
    pairs = width // PAIR
    half, _, tall, wide = own_ref.shape
    last = jnp.maximum(scalars[scalars.shape[0] + LAST], 0)

    @pl.when(step == 0)
    def _():
        for index, (flip_row, flip_column) in enumerate(flips):
            row = scalars[scalars.shape[0] + ROW_AT] ^ flip_row
            column = scalars[scalars.shape[0] + COLUMN_AT] ^ flip_column
            piece = own_ref[index] if index < half else other_ref[index - half]
            for c in range(4):
                placed[column, c, row] = piece[c]
        for h in range(width // wide):
            at = pl.ds(h * wide, wide)
            weight_ref[:, :, at] = placed[h, :3].reshape(3, width, wide)
            out_weight_ref[:, at] = placed[h, 3].reshape(width, wide)
        state[...] = jnp.zeros(state.shape, F32)

    normed = (norm_parts(tokens_ref[...].astype(F32))[0] * gain_ref[...]).astype(BF16)
    normed_ref[...] = normed
    for c in range(3):
        qkv_ref[c] = mm(normed, weight_ref[c]).astype(BF16)
    live = iota((rows, PAIR), 0) + step * rows >= last
    ones = jnp.ones((rows, PAIR), BF16)
    for p in range(pairs):
        at = pl.ds(p * PAIR, PAIR)
        key = qkv_ref[1, :, at].astype(F32)
        value = qkv_ref[2, :, at]
        lifted = jnp.where(live, lift(key), 0.0).astype(BF16)
        bent = jnp.where(live, jnp.tanh(key), 0.0).astype(BF16)
        state[p, :, : 2 * PAIR] += mm(lifted, jnp.concatenate([value, ones], axis=1), TN)
        state[p, :, 2 * PAIR :] += mm(bent, value, TN)

    @pl.when(step == pl.num_programs(0) - 1)
    def _():
        for p in range(pairs):
            at = pl.ds(p * PAIR, PAIR)
            message_ref[p, pl.ds(0, HEAD_DIM), :] = fold_state(state[p])
            message_ref[p, pl.ds(HEAD_DIM, TAIL), :] = jnp.concatenate(
                [
                    qkv_ref[1, pl.ds(rows - TAIL, TAIL), at],
                    qkv_ref[2, pl.ds(rows - TAIL, TAIL), at],
                    jnp.zeros((TAIL, PAIR), BF16),
                ],
                axis=1,
            )


def weight_grad_kernel(
    scalars,
    normed_ref,
    d_qkv_ref,
    out_grad_ref,
    weight_ref,
    keep_ref,
    give_ref,
    gain_ref,
    whole,
    *,
    flips,
):
    c = pl.program_id(0)
    half, _, tall, wide = keep_ref.shape

    def place(total):
        for h in range(total.shape[1] // wide):
            part = total[:, h * wide : (h + 1) * wide]
            whole[h] = part.reshape(whole.shape[1:])

    @pl.when(c == 0)
    def _():
        gain_ref[...] = jnp.zeros(gain_ref.shape, F32)

    @pl.when(c < 3)
    def _():
        total = mm(normed_ref[...], d_qkv_ref[0], TN)
        place(total)
        product = total * weight_ref[0].astype(F32)
        high = product.astype(BF16)
        low = (product - high.astype(F32)).astype(BF16)
        ones = jnp.ones((8, product.shape[1]), BF16)
        gain_ref[...] += mm(ones, high, NT) + mm(ones, low, NT)

    @pl.when(c == 3)
    def _():
        place(out_grad_ref[...])

    for index, (flip_row, flip_column) in enumerate(flips):
        row = scalars[scalars.shape[0] + ROW_AT] ^ flip_row
        column = scalars[scalars.shape[0] + COLUMN_AT] ^ flip_column
        if index < half:
            keep_ref[index, 0] = whole[column, row]
        else:
            give_ref[index - half, 0] = whole[column, row].astype(BF16)


def forward_kernel(
    scalars,
    qkv_ref,
    message_ref,
    start_ref,
    blend_ref,
    att_ref,
    near_ref,
    far1_ref,
    far2_ref,
    invl_ref,
    invd_ref,
    states_ref,
    keys,
    values,
    state,
):
    rows = qkv_ref.shape[1]
    load_keys(qkv_ref, message_ref, keys, values)
    state[...] = unfold_state(message_ref[0])
    count_valid = scalars[scalars.shape[0] + VALID]
    b0, b1, b2 = (blend_ref[pl.ds(f, 1), :] for f in range(3))

    def body(step, carry):
        at = pl.multiple_of(step * ROWS, 32)
        query = qkv_ref[0, pl.ds(at, ROWS), :]
        key = keys[pl.ds(at, WIN), :]
        value = values[pl.ds(at, WIN), :]
        start = start_ref[pl.ds(at, ROWS), :]
        near_mask, far_mask, carried, row, floor, first = masks(step, start)
        query_f = query.astype(F32)
        key_f = key.astype(F32)
        lift_q = lift(query_f).astype(BF16)
        bend_q = jnp.tanh(query_f).astype(BF16)
        lift_k = lift(key_f)
        bend_k = jnp.tanh(key_f)
        ones = jnp.ones((WIN, PAIR), BF16)
        value_heads = jnp.concatenate([split_heads(value), split_heads(ones)], axis=1)
        weights = near_weights(query, split_heads(key), near_mask).astype(BF16)
        near_out = mm(weights, value_heads)
        inv_l = 1.0 / near_out[:, PAIR:]
        near = near_out[:, :PAIR] * inv_l
        before = state[...]
        before_low = before.astype(BF16)
        states_ref[0, pl.ds(pl.multiple_of(step * PAIR, PAIR), PAIR), :] = before_low
        far_two = two(far_mask)
        pair_weight = jnp.where(far_two, mm(lift_q, split_heads(lift_k.astype(BF16)), NT), 0.0)
        elu_out = mm(pair_weight.astype(BF16), value_heads)
        elu_state = mm(lift_q, before_low[:, : 2 * PAIR])
        numerator = elu_out[:, :PAIR] + jnp.where(carried, elu_state[:, :PAIR], 0.0)
        inv_d = 1.0 / (elu_out[:, PAIR:] + jnp.where(carried, elu_state[:, PAIR:], 0.0))
        far1 = numerator * inv_d
        pair_bend = jnp.where(far_two, mm(bend_q, split_heads(bend_k.astype(BF16)), NT), 0.0)
        tanh_out = mm(pair_bend.astype(BF16), value_heads[:, :PAIR]) + jnp.where(
            carried, mm(bend_q, before_low[:, 2 * PAIR :]), 0.0
        )
        far2 = tanh_out / (row - start + 1).astype(F32)
        mixed = jnp.where(row < count_valid, b0 * near + b1 * far1 + b2 * far2, 0.0)
        att_ref[pl.ds(at, ROWS), :] = mixed.astype(BF16)
        near_ref[pl.ds(at, ROWS), :] = near
        far1_ref[pl.ds(at, ROWS), :] = far1
        far2_ref[pl.ds(at, ROWS), :] = far2
        invl_ref[pl.ds(at, ROWS), :] = inv_l
        invd_ref[pl.ds(at, ROWS), :] = inv_d
        closing = scalars[step]
        live = iota((ROWS, PAIR), 0) + first >= jnp.maximum(closing, floor)
        lifted = jnp.where(live, lift_k[:ROWS], 0.0).astype(BF16)
        bent = jnp.where(live, bend_k[:ROWS], 0.0).astype(BF16)
        with_ones = jnp.concatenate([value[:ROWS], ones[:ROWS]], axis=1)
        added = jnp.concatenate([mm(lifted, with_ones, TN), mm(bent, value[:ROWS], TN)], axis=1)
        keep = (closing < floor).astype(F32)
        state[...] = keep * before + block_only(added)
        return carry

    lax.fori_loop(0, rows // ROWS, body, 0, unroll=2)


def near_back(query, key_heads, grad_pair, near_mask, spread_near, scale_q, rows_q, rows_g):
    weights = near_weights(query, key_heads, near_mask)
    shifted = (weights * (grad_pair - spread_near)).astype(BF16)
    d_query = mm(shifted, key_heads) * scale_q
    d_key = fold(mm(shifted, rows_q, TN))
    return weights.astype(BF16), d_query, d_key


def prologue_kernel(
    scalars,
    query_ref,
    key_ref,
    message_ref,
    start_ref,
    blend_ref,
    grad_ref,
    near_ref,
    far1_ref,
    invl_ref,
    invd_ref,
    back_ref,
    adjoint,
):
    rows = query_ref.shape[1]
    step_rows = rows // 3
    count_valid = scalars[scalars.shape[0] + VALID]
    b0, b1, b2 = (blend_ref[pl.ds(f, 1), :] for f in range(3))
    adjoint[...] = jnp.zeros(adjoint.shape, F32)

    tails = message_ref[0, pl.ds(HEAD_DIM, TAIL), :]
    key = jnp.concatenate([tails[:, :PAIR], key_ref[0]], axis=0)
    value = jnp.concatenate([tails[:, PAIR : 2 * PAIR], key_ref[1]], axis=0)
    start = start_ref[pl.ds(0, ROWS), :]
    near_mask, _, _, row, _, _ = masks(0, start)
    query = query_ref[0, pl.ds(0, ROWS), :]
    grad_f = jnp.where(row < count_valid, grad_ref[pl.ds(0, ROWS), :].astype(F32), 0.0)
    grad = grad_f.astype(BF16)
    scale = b0 * invl_ref[...]
    rows_q = (query.astype(F32) * (scale * HEAD_DIM**-0.5)).astype(BF16)
    rows_g = (grad_f * scale).astype(BF16)
    weights, _, d_key = near_back(
        query,
        split_heads(key),
        mm(grad, split_heads(value), NT),
        near_mask,
        spread(grad_f * near_ref[...]),
        scale * HEAD_DIM**-0.5,
        rows_q,
        rows_g,
    )
    back_ref[0, pl.ds(HEAD_DIM, TAIL), :] = jnp.concatenate(
        [d_key[:TAIL], fold(mm(weights, rows_g, TN))[:TAIL], jnp.zeros((TAIL, PAIR), F32)], axis=1
    ).astype(BF16)
    heads = same_head().astype(F32).astype(BF16)
    heads = jnp.concatenate([heads, heads], axis=0)

    for step in range(3):
        at = step * step_rows

        @pl.when(scalars[scalars.shape[0] + CARRIED] > at)
        def _():
            here = pl.ds(at, step_rows)
            row = iota((step_rows, PAIR), 0) + at
            start = start_ref[here, :]
            grad_f = jnp.where(row < count_valid, grad_ref[here, :].astype(F32), 0.0)
            grad = grad_f.astype(BF16)
            product = grad_f * far1_ref[here, :]
            high = product.astype(BF16)
            low = (product - high.astype(F32)).astype(BF16)
            along = mm(jnp.concatenate([high, low], axis=1), heads).astype(BF16)
            query_f = query_ref[0, here, :].astype(F32)
            live = start < 0
            scaled = jnp.where(live, lift(query_f) * (b1 * invd_ref[here, :]), 0.0)
            bent = jnp.where(
                live, jnp.tanh(query_f) * (b2 / (row - start + 1).astype(F32)), 0.0
            )
            adjoint[:, : 2 * PAIR] += mm(
                scaled.astype(BF16), jnp.concatenate([grad, along], axis=1), TN
            )
            adjoint[:, 2 * PAIR :] += mm(bent.astype(BF16), grad, TN)

    back_ref[0, pl.ds(0, HEAD_DIM), :] = fold_state(adjoint[...])


def key_side(adjoint_low, lift_k, bend_k, value):
    ones = jnp.full(value.shape, -1.0 / HEAD_DIM, BF16)
    d_lift = mm(jnp.concatenate([value, ones], axis=1), adjoint_low[:, : 2 * PAIR], NT)
    d_bend = mm(value, adjoint_low[:, 2 * PAIR :], NT)
    both = jnp.concatenate([adjoint_low[:, :PAIR], adjoint_low[:, 2 * PAIR :]], axis=0)
    d_value = mm(jnp.concatenate([lift_k, bend_k], axis=1), both)
    return d_lift, d_bend, d_value


def backward_kernel(
    scalars,
    qkv_ref,
    message_ref,
    start_ref,
    blend_ref,
    grad_ref,
    near_ref,
    far1_ref,
    far2_ref,
    invl_ref,
    invd_ref,
    states_ref,
    back_ref,
    done_ref,
    out_ref,
    sums_ref,
    keys,
    values,
    adjoint,
    key_carry,
    value_carry,
):
    rows = qkv_ref.shape[1]
    steps = rows // ROWS
    load_keys(qkv_ref, message_ref, keys, values)
    count_valid = scalars[scalars.shape[0] + VALID]
    last = scalars[scalars.shape[0] + LAST]
    b0, b1, b2 = (blend_ref[pl.ds(f, 1), :] for f in range(3))
    lanes = iota((ROWS, PAIR), 1) < HEAD_DIM

    arrived = unfold_state(back_ref[0])
    tail_grads = back_ref[0, pl.ds(HEAD_DIM, TAIL), :].astype(F32)
    end_key = keys[pl.ds(rows, TAIL), :].astype(F32)
    end_lift, end_bend = lift(end_key), jnp.tanh(end_key)
    end_parts = key_side(
        arrived.astype(BF16), end_lift.astype(BF16), end_bend.astype(BF16), values[pl.ds(rows, TAIL), :]
    )
    live = iota((TAIL, PAIR), 0) + (rows - TAIL) >= last
    key_carry[...] = tail_grads[:, :PAIR] + jnp.where(
        live,
        end_parts[0] * jnp.minimum(end_lift, 1.0) + end_parts[1] * (1.0 - end_bend * end_bend),
        0.0,
    )
    value_carry[...] = tail_grads[:, PAIR : 2 * PAIR] + jnp.where(live, end_parts[2], 0.0)
    adjoint[...] = jnp.where(last < rows - TAIL, 1.0, 0.0) * arrived
    sums_ref[...] = jnp.zeros(sums_ref.shape, F32)

    def add_up(place, product):
        sums_ref[pl.ds(place, 8), :] += jnp.sum(product.reshape(ROWS // 8, 8, PAIR), axis=0)

    def body(back, carry):
        step = steps - 1 - back
        at = pl.multiple_of(step * ROWS, 32)
        query = qkv_ref[0, pl.ds(at, ROWS), :]
        key = keys[pl.ds(at, WIN), :]
        value = values[pl.ds(at, WIN), :]
        start = start_ref[pl.ds(at, ROWS), :]
        near_mask, far_mask, carried, row, floor, first = masks(step, start)
        far_two = two(far_mask)
        grad_f = jnp.where(row < count_valid, grad_ref[pl.ds(at, ROWS), :].astype(F32), 0.0)
        grad = grad_f.astype(BF16)
        query_f = query.astype(F32)
        key_f = key.astype(F32)
        lift_qf, bend_qf = lift(query_f), jnp.tanh(query_f)
        lift_kf, bend_kf = lift(key_f), jnp.tanh(key_f)
        lift_q, bend_q = lift_qf.astype(BF16), bend_qf.astype(BF16)
        lift_k, bend_k = lift_kf.astype(BF16), bend_kf.astype(BF16)
        lift_heads, bend_heads = split_heads(lift_k), split_heads(bend_k)
        r0 = b0 * invl_ref[pl.ds(at, ROWS), :]
        r1 = b1 * invd_ref[pl.ds(at, ROWS), :]
        r2 = b2 / (row - start + 1).astype(F32)
        grad_pair = mm(grad, split_heads(value), NT)
        rows_q = (query_f * (r0 * HEAD_DIM**-0.5)).astype(BF16)
        near_product = grad_f * near_ref[pl.ds(at, ROWS), :]
        weights, d_query, d_key = near_back(
            query,
            split_heads(key),
            grad_pair,
            near_mask,
            spread(near_product),
            r0 * HEAD_DIM**-0.5,
            rows_q,
            None,
        )
        far1_product = grad_f * far1_ref[pl.ds(at, ROWS), :]
        add_up(0, near_product)
        add_up(8, far1_product)
        add_up(16, grad_f * far2_ref[pl.ds(at, ROWS), :])
        spread_far = spread(far1_product)
        along = jnp.where(lanes, spread_far[:, :WIN], spread_far[:, WIN:])
        shifted = jnp.where(far_two, grad_pair - spread_far, 0.0).astype(BF16)
        plain = jnp.where(far_two, grad_pair, 0.0).astype(BF16)
        pair_weight = jnp.where(far_two, mm(lift_q, lift_heads, NT), 0.0).astype(BF16)
        pair_bend = jnp.where(far_two, mm(bend_q, bend_heads, NT), 0.0).astype(BF16)
        before = states_ref[0, pl.ds(pl.multiple_of(step * PAIR, PAIR), PAIR), :]
        scaled_along = (along * (-1.0 / HEAD_DIM)).astype(BF16)
        state_lift = mm(jnp.concatenate([grad, scaled_along], axis=1), before[:, : 2 * PAIR], NT)
        state_bend = mm(grad, before[:, 2 * PAIR :], NT)
        d_query = (
            d_query
            + (mm(shifted, lift_heads) + jnp.where(carried, state_lift, 0.0))
            * (r1 * jnp.minimum(lift_qf, 1.0))
            + (mm(plain, bend_heads) + jnp.where(carried, state_bend, 0.0))
            * (r2 * (1.0 - bend_qf * bend_qf))
        )
        out_ref[0, pl.ds(at, ROWS), :] = d_query.astype(BF16)
        rows_a = lift_qf * r1
        rows_t = bend_qf * r2
        d_lift = fold(mm(shifted, rows_a.astype(BF16), TN))
        d_bend = fold(mm(plain, rows_t.astype(BF16), TN))
        d_value = fold(
            mm(
                jnp.concatenate([weights, pair_weight, pair_bend], axis=0),
                jnp.concatenate([grad_f * r0, grad_f * r1, grad_f * r2], axis=0).astype(BF16),
                TN,
            )
        )
        after = adjoint[...]
        parts = key_side(after.astype(BF16), lift_k[:ROWS], bend_k[:ROWS], value[:ROWS])
        closing = scalars[step]
        live = iota((ROWS, PAIR), 0) + first >= jnp.maximum(closing, floor)
        pad = jnp.zeros((TAIL, PAIR), F32)
        d_lift = d_lift + jnp.concatenate([jnp.where(live, parts[0], 0.0), pad], axis=0)
        d_bend = d_bend + jnp.concatenate([jnp.where(live, parts[1], 0.0), pad], axis=0)
        d_value = d_value + jnp.concatenate([jnp.where(live, parts[2], 0.0), pad], axis=0)
        d_key = d_key + d_lift * jnp.minimum(lift_kf, 1.0) + d_bend * (1.0 - bend_kf * bend_kf)
        out_ref[1, pl.ds(at, ROWS), :] = jnp.concatenate(
            [d_key[TAIL:ROWS], d_key[ROWS:] + key_carry[...]], axis=0
        ).astype(BF16)
        out_ref[2, pl.ds(at, ROWS), :] = jnp.concatenate(
            [d_value[TAIL:ROWS], d_value[ROWS:] + value_carry[...]], axis=0
        ).astype(BF16)
        key_carry[...] = d_key[:TAIL]
        value_carry[...] = d_value[:TAIL]
        from_lift = mm(
            jnp.where(carried, rows_a, 0.0).astype(BF16),
            jnp.concatenate([grad, along.astype(BF16)], axis=1),
            TN,
        )
        from_bend = mm(jnp.where(carried, rows_t, 0.0).astype(BF16), grad, TN)
        keep = (closing < floor).astype(F32)
        adjoint[...] = keep * after + block_only(jnp.concatenate([from_lift, from_bend], axis=1))
        return carry

    lax.fori_loop(0, steps, body, 0)


def feed_kernel(
    scalars,
    mixed_ref,
    tokens_ref,
    cotangent_ref,
    out_weight_ref,
    gain_ref,
    own_ref,
    other_ref,
    layer_ref,
    d_hidden_ref,
    d_branch_ref,
    d_mixed_ref,
    normed_ref,
    active_ref,
    d_inner_ref,
    sums_ref,
):
    c0 = math.sqrt(2.0 / math.pi)
    hidden = tokens_ref[...].astype(F32) + mm(mixed_ref[...], out_weight_ref[...], NT)
    normal, scale = norm_parts(hidden)
    normed = (normal * gain_ref[...]).astype(BF16)
    normed_ref[...] = normed
    cotangent = cotangent_ref[...]
    half, width = own_ref.shape[1:]
    chunk = min(512, half)
    layer = hidden
    d_normed = jnp.zeros(hidden.shape, F32)
    for place, ref in enumerate((own_ref, other_ref)):
        for first in range(0, half, chunk):
            into = ref[0, pl.ds(first, chunk), :]
            down = ref[1, pl.ds(first, chunk), :]
            inner = mm(normed, into, NT)
            d_active = mm(cotangent, down, NT)
            square = inner * inner
            bent = jnp.tanh(inner * (c0 + (c0 * 0.044715) * square))
            gate = 0.5 + 0.5 * bent
            active = (inner * gate).astype(BF16)
            slope = gate + inner * (0.5 - 0.5 * bent * bent) * (
                c0 + (3.0 * 0.044715 * c0) * square
            )
            d_inner = (d_active * slope).astype(BF16)
            at = pl.ds(place * half + first, chunk)
            active_ref[:, at] = active
            d_inner_ref[:, at] = d_inner
            layer = layer + mm(active, down)
            d_normed = d_normed + mm(d_inner, into)
    layer_ref[...] = layer.astype(BF16)
    d_part, gain_rows = norm_back(d_normed, gain_ref[...], normal, scale)
    d_hidden = cotangent.astype(F32) + d_part
    d_hidden_ref[...] = d_hidden
    d_branch = d_hidden.astype(BF16)
    d_branch_ref[...] = d_branch
    d_mixed_ref[...] = mm(d_branch, out_weight_ref[...]).astype(BF16)

    @pl.when(pl.program_id(0) == 0)
    def _():
        sums_ref[...] = jnp.zeros(sums_ref.shape, F32)

    sums_ref[...] += gain_rows


def feed_grad_kernel(
    scalars,
    normed_ref,
    cotangent_ref,
    active_ref,
    d_inner_ref,
    mixed_ref,
    d_branch_ref,
    keep_ref,
    give_ref,
    out_grad_ref,
):
    step = pl.program_id(0)
    steps = pl.num_programs(0)

    @pl.when(step == 0)
    def _():
        out_grad_ref[...] = mm(d_branch_ref[...], mixed_ref[...], TN)

    @pl.when(step < steps // 2)
    def _():
        keep_ref[0] = mm(d_inner_ref[...], normed_ref[...], TN)
        keep_ref[1] = mm(active_ref[...], cotangent_ref[...], TN)

    @pl.when(step >= steps // 2)
    def _():
        give_ref[0] = mm(d_inner_ref[...], normed_ref[...], TN).astype(BF16)
        give_ref[1] = mm(active_ref[...], cotangent_ref[...], TN).astype(BF16)


def input_kernel(
    scalars, d_qkv_ref, weight_ref, tokens_ref, d_hidden_ref, gain_ref, input_grad_ref
):
    d_normed = mm(d_qkv_ref[0], weight_ref[0], NT)
    for c in range(1, 3):
        d_normed = d_normed + mm(d_qkv_ref[c], weight_ref[c], NT)
    normal, scale = norm_parts(tokens_ref[...].astype(F32))
    d_part, _ = norm_back(d_normed, gain_ref[...], normal, scale)
    input_grad_ref[...] = d_hidden_ref[...] + d_part


def resume(kernel, done, scalars, qkv_ref, message_ref, start_ref, blend_ref, *refs):
    kernel(scalars, qkv_ref, message_ref, start_ref, blend_ref, *refs[done:])


def pair_specs(rows, first=0):
    return {
        "qkv": pl.BlockSpec((3, rows, PAIR), lambda p, s: (0, 0, p + first)),
        "message": pl.BlockSpec((1, HEAD_DIM + TAIL, 3 * PAIR), lambda p, s: (p + first, 0, 0)),
        "start": pl.BlockSpec((rows, PAIR), lambda p, s: (0, 0)),
        "blend": pl.BlockSpec((3, PAIR), lambda p, s: (0, p + first)),
        "column": pl.BlockSpec((rows, PAIR), lambda p, s: (0, p + first)),
        "states": pl.BlockSpec((1, rows // ROWS * PAIR, 3 * PAIR), lambda p, s: (p + first, 0, 0)),
        "sums": pl.BlockSpec((24, PAIR), lambda p, s: (0, p)),
        "query": pl.BlockSpec((1, rows, PAIR), lambda p, s: (0, 0, p)),
        "head_rows": pl.BlockSpec((ROWS, PAIR), lambda p, s: (0, p)),
    }


def call(kernel, ins, outs, out_shapes, scratch, grid, name, flops, moved, aliases={}):
    return pl.pallas_call(
        kernel,
        out_shape=out_shapes,
        grid_spec=pltpu.PrefetchScalarGridSpec(
            num_scalar_prefetch=1,
            grid=(grid,),
            in_specs=ins,
            out_specs=outs,
            scratch_shapes=scratch,
        ),
        input_output_aliases=aliases,
        compiler_params=pltpu.CompilerParams(
            dimension_semantics=("arbitrary",), vmem_limit_bytes=56 * 1024 * 1024
        ),
        cost_estimate=pl.CostEstimate(flops=flops, bytes_accessed=moved, transcendentals=0),
        name=name,
    )


def norm_parts(source):
    centered = source - jnp.mean(source, axis=-1, keepdims=True)
    spread_of = jnp.mean(centered * centered, axis=-1, keepdims=True)
    scale = lax.rsqrt(spread_of + EPS)
    return centered * scale, scale


def norm_back(d_out, gain, normal, scale):
    e = d_out * gain
    inner = jnp.mean(e, axis=-1, keepdims=True)
    along = jnp.mean(e * normal, axis=-1, keepdims=True)
    rows = jnp.sum((d_out * normal).reshape(-1, 8, d_out.shape[1]), axis=0)
    return scale * (e - inner - normal * along), rows


def bits(size):
    return [1 << b for b in range(int(math.log2(size)))]


def phases():
    dp = bits(lax.axis_size("dp"))
    core, rest = dp[:1], dp[1:]
    mid = len(rest) // 2
    far = [("dp", m) for m in rest[mid:]]
    near = [("dp", m) for m in rest[:mid]] + [("head", m) for m in bits(lax.axis_size("head"))]
    groups = []
    for run in (far, near, [("dp", m) for m in core]):
        groups += [run[i : i + 2] for i in range(0, len(run), 2)]
    return groups


def relative_bits():
    return [pair for group in phases() for pair in group]


def all_flips():
    order = relative_bits()
    flips = []
    for index in range(1 << len(order)):
        chosen = [pair for place, pair in enumerate(order) if index >> place & 1]
        flips.append(tuple(sum(m for a, m in chosen if a == axis) for axis in ("dp", "head")))
    return flips


def peer(array, group, combo):
    n_dp, n_head = lax.axis_size("dp"), lax.axis_size("head")
    chosen = [pair for place, pair in enumerate(group) if combo >> place & 1]
    flip_dp = sum(m for axis, m in chosen if axis == "dp")
    flip_head = sum(m for axis, m in chosen if axis == "head")
    pairs = [
        (d * n_head + h, (d ^ flip_dp) * n_head + (h ^ flip_head))
        for d in range(n_dp)
        for h in range(n_head)
    ]
    return lax.ppermute(array, ("dp", "head"), pairs)


def widen(block, group, axis, after=None):
    others = [peer(block, group, combo) for combo in range(1, 1 << len(group))]
    if after is not None:
        others, after = lax.optimization_barrier((others, after))
    whole = jnp.concatenate([block] + others, axis=axis)
    return whole if after is None else (whole, after)


def narrow(keep, gives, group):
    total = keep.astype(F32)
    for combo, give in enumerate(gives, 1):
        total = total + peer(give.astype(BF16), group, combo).astype(F32)
    return total


def narrow_axis(total, group, axis):
    parts = jnp.split(total, 1 << len(group), axis=axis)
    return narrow(parts[0], parts[1:], group)


def add_peers(array, group):
    return array + sum(peer(array, group, combo) for combo in range(1, 1 << len(group)))


def pass_along(local, keep, shift):
    size = lax.axis_size("head")
    pairs = [(i, i + shift) for i in range(size) if 0 <= i + shift < size]
    arrived = lax.ppermute(local, "head", pairs)
    for _ in range(size - 2):
        rows = iota(local.shape, 1) < HEAD_DIM
        total = local.astype(F32) + jnp.where(rows, keep * arrived.astype(F32), 0.0)
        arrived = lax.ppermute(total.astype(BF16), "head", pairs)
    return arrived


def per_device(
    tokens,
    ln1_gain,
    qkv_weight,
    out_weight,
    blend,
    ln2_gain,
    in_weight,
    down_weight,
    cotangent,
    lengths,
):
    rows, width = tokens.shape
    n_dp, n_head = lax.axis_size("dp"), lax.axis_size("head")
    pairs = width // PAIR
    steps = rows // ROWS
    groups = phases()
    flips = all_flips()

    shards = jnp.concatenate([qkv_weight, out_weight.T[None]], axis=0)[None]
    feed = jnp.stack([in_weight, down_weight])
    for group in groups[:-1]:
        shards = widen(shards, group, 0)
    others = peer(shards, groups[-1], 1)
    feed, others = lax.optimization_barrier((feed, others))

    item_lengths = lengths[0]
    slots = item_lengths.shape[0]
    ends = jnp.sum(
        jnp.where(iota((slots, slots), 1) <= iota((slots, slots), 0), item_lengths[None, :], 0),
        axis=1,
    )
    offset = lax.axis_index("head") * rows
    local = jnp.arange(rows, dtype=jnp.int32)
    place = local + offset
    total = ends[slots - 1]
    item_start = jnp.max(
        jnp.where(ends[None, :] <= place[:, None], ends[None, :], 0), axis=1
    )
    start = jnp.where(place < total, item_start - offset, local)
    carried_rows = jnp.sum((start < 0).astype(jnp.int32))
    scalars = jnp.concatenate(
        [
            start.reshape(steps, ROWS)[:, ROWS - TAIL - 1],
            carried_rows[None],
            start[rows - 1 :],
            (total - offset)[None],
            lax.axis_index("dp").astype(jnp.int32)[None],
            lax.axis_index("head").astype(jnp.int32)[None],
        ]
    )
    start_wide = jnp.broadcast_to(start[:, None], (rows, PAIR))
    keep_all = (start[rows - 1] < 0).astype(F32)
    blend_wide = jnp.repeat(blend, HEAD_DIM, axis=1)

    spec = pair_specs(rows)
    wide = jax.ShapeDtypeStruct((rows, width), F32)
    states_shape = jax.ShapeDtypeStruct((pairs, steps * PAIR, 3 * PAIR), BF16)
    message_shape = jax.ShapeDtypeStruct((pairs, HEAD_DIM + TAIL, 3 * PAIR), BF16)
    big = rows * width
    part = rows // 3

    def whole_spec(shape):
        return pl.BlockSpec(shape, lambda p, s: (0,) * len(shape))

    qkv, normed_one, qkv_all, out_all, closing = call(
        functools.partial(project_kernel, flips=flips),
        [
            pl.BlockSpec((part, width), lambda p, s: (p, 0)),
            whole_spec((1, width)),
            whole_spec(shards.shape),
            whole_spec(shards.shape),
        ],
        [
            pl.BlockSpec((3, part, width), lambda p, s: (0, p, 0)),
            pl.BlockSpec((part, width), lambda p, s: (p, 0)),
            whole_spec((3, width, width)),
            whole_spec((width, width)),
            whole_spec(message_shape.shape),
        ],
        [
            jax.ShapeDtypeStruct((3, rows, width), BF16),
            jax.ShapeDtypeStruct((rows, width), BF16),
            jax.ShapeDtypeStruct((3, width, width), BF16),
            jax.ShapeDtypeStruct((width, width), BF16),
            message_shape,
        ],
        [
            pltpu.VMEM((pairs, PAIR, 3 * PAIR), F32),
            pltpu.VMEM((n_head, 4, n_dp, width // n_dp, width // n_head), BF16),
        ],
        3,
        "project",
        6 * big * width,
        12 * big,
    )(scalars, tokens, ln1_gain[None], shards, others)
    feed = widen(feed, groups[0], 1)
    feed, closing = lax.optimization_barrier((feed, closing))
    message = pass_along(closing, keep_all, 1)

    key_scratch = pltpu.VMEM((rows + TAIL, PAIR), BF16)
    state_scratch = pltpu.VMEM((PAIR, 3 * PAIR), F32)
    tail_scratch = pltpu.VMEM((TAIL, PAIR), F32)
    results = ()
    count = pairs // 2
    for first in (0, count):
        spec = pair_specs(rows, first)
        results = call(
            functools.partial(resume, forward_kernel, len(results)),
            [spec["qkv"], spec["message"], spec["start"], spec["blend"]]
            + [pl.BlockSpec(memory_space=pl.ANY)] * len(results),
            [spec["column"]] * 6 + [spec["states"]],
            [jax.ShapeDtypeStruct((rows, width), BF16)] + [wide] * 5 + [states_shape],
            [key_scratch, key_scratch, state_scratch],
            count,
            "forward",
            4000 * big,
            20 * big,
            {5 + i: i for i in range(len(results))},
        )(scalars, qkv, message, start_wide, blend_wide, *results)
        if not first:
            feed, results = widen(feed, groups[1], 1, results)
            feed, message = lax.optimization_barrier((feed, message))
    for group in groups[2:-1]:
        feed = widen(feed, group, 1)
    feed_other = peer(feed, groups[-1], 1)
    mixed, near, far1, far2, inv_l, inv_d, states = results

    spec = pair_specs(rows)
    low = jax.ShapeDtypeStruct((rows, width), BF16)
    row_spec = pl.BlockSpec((part, width), lambda p, s: (p, 0))
    hidden_units = 2 * feed.shape[1]
    unit_spec = pl.BlockSpec((part, hidden_units), lambda p, s: (p, 0))
    unit_shape = jax.ShapeDtypeStruct((rows, hidden_units), BF16)
    sums_shape = jax.ShapeDtypeStruct((8, width), F32)
    layer_out, d_hidden, d_branch, d_mixed, normed_two, active, d_inner, gain_two_rows = call(
        feed_kernel,
        [row_spec] * 3
        + [
            whole_spec((width, width)),
            whole_spec((1, width)),
            whole_spec(feed.shape),
            whole_spec(feed.shape),
        ],
        [row_spec] * 5 + [unit_spec] * 2 + [whole_spec((8, width))],
        [low, wide, low, low, low, unit_shape, unit_shape, sums_shape],
        [],
        3,
        "feed",
        8 * big * hidden_units,
        32 * big,
    )(scalars, mixed, tokens, cotangent, out_all, ln2_gain[None], feed, feed_other)

    front_keys = qkv[1:, :ROWS]
    back = call(
        prologue_kernel,
        [
            spec["query"],
            pl.BlockSpec((2, ROWS, PAIR), lambda p, s: (0, 0, p)),
            spec["message"],
            spec["start"],
            spec["blend"],
            spec["column"],
            spec["head_rows"],
            spec["column"],
            spec["head_rows"],
            spec["column"],
        ],
        spec["message"],
        message_shape,
        [state_scratch],
        pairs,
        "prologue",
        500 * big,
        20 * big,
    )(scalars, qkv, front_keys, message, start_wide, blend_wide, d_mixed, near, far1, inv_l, inv_d)
    d_inner, _ = lax.optimization_barrier((d_inner, back))
    back_in = pass_along(back, keep_all, -1)

    unit = hidden_units // 4
    columns = pl.BlockSpec((rows, unit), lambda p, s: (0, p))
    half_shape = (2, 2 * unit, width)
    keep, give, out_grad = call(
        feed_grad_kernel,
        [whole_spec((rows, width))] * 2 + [columns] * 2 + [whole_spec((rows, width))] * 2,
        [
            pl.BlockSpec((2, unit, width), lambda p, s: (0, jnp.minimum(p, 1), 0)),
            pl.BlockSpec((2, unit, width), lambda p, s: (0, jnp.maximum(p - 2, 0), 0)),
            whole_spec((width, width)),
        ],
        [
            jax.ShapeDtypeStruct(half_shape, F32),
            jax.ShapeDtypeStruct(half_shape, BF16),
            jax.ShapeDtypeStruct((width, width), F32),
        ],
        [],
        4,
        "feed_grad",
        4 * big * hidden_units,
        24 * big,
    )(scalars, normed_two, cotangent, active, d_inner, mixed, d_branch)
    feed_share = narrow(keep, [give], groups[-1])
    left = list(reversed(groups[:-1]))

    d_qkv = jnp.zeros((3, 8, PAIR), BF16)
    sums = []
    first = 0
    for count in (pairs // 4, pairs // 2, pairs // 4):
        spec = pair_specs(rows, first)
        more = {13: 0} if first else {}
        d_qkv, part_sums = call(
            backward_kernel,
            [spec["qkv"], spec["message"], spec["start"], spec["blend"]]
            + [spec["column"]] * 6
            + [spec["states"], spec["message"], pl.BlockSpec(memory_space=pl.ANY)],
            [spec["qkv"], spec["sums"]],
            [
                jax.ShapeDtypeStruct((3, rows, width), BF16),
                jax.ShapeDtypeStruct((24, count * PAIR), F32),
            ],
            [key_scratch, key_scratch, state_scratch, tail_scratch, tail_scratch],
            count,
            "backward",
            16000 * big * count // pairs,
            40 * big * count // pairs,
            more,
        )(
            scalars,
            qkv,
            message,
            start_wide,
            blend_wide,
            d_mixed,
            near,
            far1,
            far2,
            inv_l,
            inv_d,
            states,
            back_in,
            d_qkv,
        )
        sums.append(part_sums)
        first += count
        if left and first < pairs:
            _, back_in = lax.optimization_barrier((feed_share, back_in))
            feed_share = narrow_axis(feed_share, left.pop(0), 1)
    for group in left:
        feed_share = narrow_axis(feed_share, group, 1)
    feed_share, d_qkv = lax.optimization_barrier((feed_share, d_qkv))
    sums = jnp.concatenate(sums, axis=1)
    blend_part = jnp.sum(sums.reshape(3, 8, blend.shape[1], HEAD_DIM), axis=(1, 3))

    shard_shape = (n_dp * n_head // 2, 4, width // n_dp, width // n_head)
    shard_spec = pl.BlockSpec((shard_shape[0], 1) + shard_shape[2:], lambda p, s: (0, p, 0, 0))
    keep, give, gain_one_rows = call(
        functools.partial(weight_grad_kernel, flips=flips),
        [
            whole_spec((rows, width)),
            pl.BlockSpec((1, rows, width), lambda p, s: (jnp.minimum(p, 2), 0, 0)),
            whole_spec((width, width)),
            pl.BlockSpec((1, width, width), lambda p, s: (jnp.minimum(p, 2), 0, 0)),
        ],
        [shard_spec, shard_spec, whole_spec((8, width))],
        [
            jax.ShapeDtypeStruct(shard_shape, F32),
            jax.ShapeDtypeStruct(shard_shape, BF16),
            sums_shape,
        ],
        [pltpu.VMEM((n_head, n_dp, width // n_dp, width // n_head), F32)],
        4,
        "weight_grad",
        6 * big * width,
        8 * big,
    )(scalars, normed_one, d_qkv, out_grad, qkv_all)
    parts = [gain_one_rows[0] / ln1_gain, jnp.sum(gain_two_rows, axis=0), blend_part.reshape(-1)]
    total_sums = jnp.concatenate(parts)[None]
    share = narrow(keep, [give], groups[-1])
    total_sums = add_peers(total_sums, groups[-1])
    for group in reversed(groups[:-1]):
        _, total_sums = lax.optimization_barrier((share, total_sums))
        share = narrow_axis(share, group, 0)
        total_sums = add_peers(total_sums, group)
    d_qkv, give = lax.optimization_barrier((d_qkv, give))
    input_grad = call(
        input_kernel,
        [
            pl.BlockSpec((3, part, width), lambda p, s: (0, p, 0)),
            whole_spec((3, width, width)),
            row_spec,
            row_spec,
            whole_spec((1, width)),
        ],
        row_spec,
        wide,
        [],
        3,
        "input",
        6 * big * width,
        24 * big,
    )(scalars, d_qkv, qkv_all, tokens, d_hidden, ln1_gain[None])
    total_sums = total_sums[0]
    gain_one, gain_two = total_sums[:width], total_sums[width : 2 * width]
    blend_sum = total_sums[2 * width :].reshape(blend.shape)
    qkv_share, out_share = share[0, :3], share[0, 3].T
    in_share, down_share = feed_share[0], feed_share[1]
    return (
        layer_out,
        input_grad,
        gain_one,
        qkv_share,
        out_share,
        blend_sum,
        gain_two,
        in_share,
        down_share,
    )


def solution(mesh):
    return jax.shard_map(
        per_device,
        mesh=mesh,
        in_specs=(
            P(("dp", "head"), None),
            P(),
            P(None, "dp", "head"),
            P("head", "dp"),
            P(),
            P(),
            P(("dp", "head"), None),
            P(("dp", "head"), None),
            P(("dp", "head"), None),
            P("dp", None),
        ),
        out_specs=(
            P(("dp", "head"), None),
            P(("dp", "head"), None),
            P(),
            P(None, "dp", "head"),
            P("head", "dp"),
            P(),
            P(),
            P(("dp", "head"), None),
            P(("dp", "head"), None),
        ),
        check_vma=False,
    )
```

```python
import functools
import math

import jax
import jax.numpy as jnp
from jax import lax
from jax.experimental import pallas as pl
from jax.experimental.pallas import tpu as pltpu
from jax.sharding import PartitionSpec as P

HEAD_DIM = 64
BAND = 30
ROWS = 96
TAIL = 32
WIN = ROWS + TAIL
PAIR = 2 * HEAD_DIM
EPS = 1e-05
NEG = -1e30
CARRIED, LAST, VALID, ROW_AT, COLUMN_AT = range(-5, 0)
F32 = jnp.float32
BF16 = jnp.bfloat16
NT = (((1,), (1,)), ((), ()))
TN = (((0,), (0,)), ((), ()))
NN = (((1,), (0,)), ((), ()))


def mm(left, right, dims=NN):
    return lax.dot_general(left, right, dims, preferred_element_type=F32)


def iota(shape, axis):
    return lax.broadcasted_iota(jnp.int32, shape, axis)


def lift(values):
    return jnp.where(values > 0, values + 1.0, jnp.exp(jnp.minimum(values, 0.0)))


def head_lanes(dtype):
    first = (iota((1, PAIR), 1) < HEAD_DIM).astype(F32)
    return first.astype(dtype), (1.0 - first).astype(dtype)


def split_heads(block):
    first, second = head_lanes(block.dtype)
    return jnp.concatenate([block * first, block * second], axis=0)


def same_head():
    return (iota((PAIR, PAIR), 0) < HEAD_DIM) == (iota((PAIR, PAIR), 1) < HEAD_DIM)


def block_only(wide):
    keep = same_head()
    parts = [
        jnp.where(keep, wide[:, p * PAIR : (p + 1) * PAIR], 0.0)
        for p in range(wide.shape[1] // PAIR)
    ]
    return jnp.concatenate(parts, axis=1)


def fold(tall):
    half = tall.shape[0] // 2
    lanes = iota((half, PAIR), 1) < HEAD_DIM
    return jnp.where(lanes, tall[:half], tall[half:])


def two(half):
    return jnp.concatenate([half, half], axis=1)


def masks(step, start):
    row = iota((ROWS, WIN), 0) + step * ROWS
    first = step * ROWS - TAIL
    key = iota((ROWS, WIN), 1) + first
    floor = jnp.maximum(first, 0)
    causal = key <= row
    near = causal & (key >= jnp.maximum(start, row - (BAND - 1)))
    far = causal & (key >= jnp.maximum(start, floor))
    return near, far, start < floor, row, floor, first


def near_weights(query, key_heads, near):
    scores = mm(query, key_heads, NT) * (HEAD_DIM**-0.5)
    parts = []
    for h in range(2):
        part = jnp.where(near, scores[:, h * WIN : (h + 1) * WIN], NEG)
        parts.append(jnp.exp(part - jnp.max(part, axis=1, keepdims=True)))
    return jnp.concatenate(parts, axis=1)


def spread(product):
    high = product.astype(BF16)
    low = (product - high.astype(F32)).astype(BF16)
    table = (
        ((iota((2 * PAIR, 2 * WIN), 0) % PAIR) < HEAD_DIM) == (iota((2 * PAIR, 2 * WIN), 1) < WIN)
    ).astype(F32)
    return mm(jnp.concatenate([high, low], axis=1), table.astype(BF16))


def load_keys(qkv_ref, message_ref, keys, values):
    rows = qkv_ref.shape[1]
    keys[pl.ds(0, TAIL), :] = message_ref[0, pl.ds(HEAD_DIM, TAIL), :PAIR]
    keys[pl.ds(TAIL, rows), :] = qkv_ref[1]
    values[pl.ds(0, TAIL), :] = message_ref[0, pl.ds(HEAD_DIM, TAIL), PAIR : 2 * PAIR]
    values[pl.ds(TAIL, rows), :] = qkv_ref[2]


def fold_state(wide):
    kept = block_only(wide)
    return (kept[:HEAD_DIM] + kept[HEAD_DIM:]).astype(BF16)


def unfold_state(message):
    half = message[:HEAD_DIM].astype(F32)
    return block_only(jnp.concatenate([half, half], axis=0))


def project_kernel(
    scalars,
    tokens_ref,
    gain_ref,
    own_ref,
    other_ref,
    qkv_ref,
    normed_ref,
    weight_ref,
    out_weight_ref,
    message_ref,
    state,
    placed,
    *,
    flips,
):
    step = pl.program_id(0)
    rows, width = tokens_ref.shape
    pairs = width // PAIR
    half, _, tall, wide = own_ref.shape
    last = jnp.maximum(scalars[scalars.shape[0] + LAST], 0)

    @pl.when(step == 0)
    def _():
        for index, (flip_row, flip_column) in enumerate(flips):
            row = scalars[scalars.shape[0] + ROW_AT] ^ flip_row
            column = scalars[scalars.shape[0] + COLUMN_AT] ^ flip_column
            piece = own_ref[index] if index < half else other_ref[index - half]
            for c in range(4):
                placed[column, c, row] = piece[c]
        for h in range(width // wide):
            at = pl.ds(h * wide, wide)
            weight_ref[:, :, at] = placed[h, :3].reshape(3, width, wide)
            out_weight_ref[:, at] = placed[h, 3].reshape(width, wide)
        state[...] = jnp.zeros(state.shape, F32)

    normed = (norm_parts(tokens_ref[...].astype(F32))[0] * gain_ref[...]).astype(BF16)
    normed_ref[...] = normed
    for c in range(3):
        qkv_ref[c] = mm(normed, weight_ref[c]).astype(BF16)
    live = iota((rows, PAIR), 0) + step * rows >= last
    ones = jnp.ones((rows, PAIR), BF16)
    for p in range(pairs):
        at = pl.ds(p * PAIR, PAIR)
        key = qkv_ref[1, :, at].astype(F32)
        value = qkv_ref[2, :, at]
        lifted = jnp.where(live, lift(key), 0.0).astype(BF16)
        bent = jnp.where(live, jnp.tanh(key), 0.0).astype(BF16)
        state[p, :, : 2 * PAIR] += mm(lifted, jnp.concatenate([value, ones], axis=1), TN)
        state[p, :, 2 * PAIR :] += mm(bent, value, TN)

    @pl.when(step == pl.num_programs(0) - 1)
    def _():
        for p in range(pairs):
            at = pl.ds(p * PAIR, PAIR)
            message_ref[p, pl.ds(0, HEAD_DIM), :] = fold_state(state[p])
            message_ref[p, pl.ds(HEAD_DIM, TAIL), :] = jnp.concatenate(
                [
                    qkv_ref[1, pl.ds(rows - TAIL, TAIL), at],
                    qkv_ref[2, pl.ds(rows - TAIL, TAIL), at],
                    jnp.zeros((TAIL, PAIR), BF16),
                ],
                axis=1,
            )


def weight_grad_kernel(
    scalars,
    normed_ref,
    d_qkv_ref,
    out_grad_ref,
    weight_ref,
    keep_ref,
    give_ref,
    gain_ref,
    whole,
    *,
    flips,
):
    c = pl.program_id(0)
    half, _, tall, wide = keep_ref.shape

    def place(total):
        for h in range(total.shape[1] // wide):
            part = total[:, h * wide : (h + 1) * wide]
            whole[h] = part.reshape(whole.shape[1:])

    @pl.when(c == 0)
    def _():
        gain_ref[...] = jnp.zeros(gain_ref.shape, F32)

    @pl.when(c < 3)
    def _():
        total = mm(normed_ref[...], d_qkv_ref[0], TN)
        place(total)
        product = total * weight_ref[0].astype(F32)
        high = product.astype(BF16)
        low = (product - high.astype(F32)).astype(BF16)
        ones = jnp.ones((8, product.shape[1]), BF16)
        gain_ref[...] += mm(ones, high, NT) + mm(ones, low, NT)

    @pl.when(c == 3)
    def _():
        place(out_grad_ref[...])

    for index, (flip_row, flip_column) in enumerate(flips):
        row = scalars[scalars.shape[0] + ROW_AT] ^ flip_row
        column = scalars[scalars.shape[0] + COLUMN_AT] ^ flip_column
        if index < half:
            keep_ref[index, 0] = whole[column, row]
        else:
            give_ref[index - half, 0] = whole[column, row].astype(BF16)


def forward_kernel(
    scalars,
    qkv_ref,
    message_ref,
    start_ref,
    blend_ref,
    att_ref,
    near_ref,
    far1_ref,
    far2_ref,
    invl_ref,
    invd_ref,
    states_ref,
    keys,
    values,
    state,
):
    rows = qkv_ref.shape[1]
    load_keys(qkv_ref, message_ref, keys, values)
    state[...] = unfold_state(message_ref[0])
    count_valid = scalars[scalars.shape[0] + VALID]
    b0, b1, b2 = (blend_ref[pl.ds(f, 1), :] for f in range(3))

    def body(step, carry):
        at = pl.multiple_of(step * ROWS, 32)
        query = qkv_ref[0, pl.ds(at, ROWS), :]
        key = keys[pl.ds(at, WIN), :]
        value = values[pl.ds(at, WIN), :]
        start = start_ref[pl.ds(at, ROWS), :]
        near_mask, far_mask, carried, row, floor, first = masks(step, start)
        query_f = query.astype(F32)
        key_f = key.astype(F32)
        lift_q = lift(query_f).astype(BF16)
        bend_q = jnp.tanh(query_f).astype(BF16)
        lift_k = lift(key_f)
        bend_k = jnp.tanh(key_f)
        ones = jnp.ones((WIN, PAIR), BF16)
        value_heads = jnp.concatenate([split_heads(value), split_heads(ones)], axis=1)
        weights = near_weights(query, split_heads(key), near_mask).astype(BF16)
        near_out = mm(weights, value_heads)
        inv_l = 1.0 / near_out[:, PAIR:]
        near = near_out[:, :PAIR] * inv_l
        before = state[...]
        before_low = before.astype(BF16)
        states_ref[0, pl.ds(pl.multiple_of(step * PAIR, PAIR), PAIR), :] = before_low
        far_two = two(far_mask)
        pair_weight = jnp.where(far_two, mm(lift_q, split_heads(lift_k.astype(BF16)), NT), 0.0)
        elu_out = mm(pair_weight.astype(BF16), value_heads)
        elu_state = mm(lift_q, before_low[:, : 2 * PAIR])
        numerator = elu_out[:, :PAIR] + jnp.where(carried, elu_state[:, :PAIR], 0.0)
        inv_d = 1.0 / (elu_out[:, PAIR:] + jnp.where(carried, elu_state[:, PAIR:], 0.0))
        far1 = numerator * inv_d
        pair_bend = jnp.where(far_two, mm(bend_q, split_heads(bend_k.astype(BF16)), NT), 0.0)
        tanh_out = mm(pair_bend.astype(BF16), value_heads[:, :PAIR]) + jnp.where(
            carried, mm(bend_q, before_low[:, 2 * PAIR :]), 0.0
        )
        far2 = tanh_out / (row - start + 1).astype(F32)
        mixed = jnp.where(row < count_valid, b0 * near + b1 * far1 + b2 * far2, 0.0)
        att_ref[pl.ds(at, ROWS), :] = mixed.astype(BF16)
        near_ref[pl.ds(at, ROWS), :] = near
        far1_ref[pl.ds(at, ROWS), :] = far1
        far2_ref[pl.ds(at, ROWS), :] = far2
        invl_ref[pl.ds(at, ROWS), :] = inv_l
        invd_ref[pl.ds(at, ROWS), :] = inv_d
        closing = scalars[step]
        live = iota((ROWS, PAIR), 0) + first >= jnp.maximum(closing, floor)
        lifted = jnp.where(live, lift_k[:ROWS], 0.0).astype(BF16)
        bent = jnp.where(live, bend_k[:ROWS], 0.0).astype(BF16)
        with_ones = jnp.concatenate([value[:ROWS], ones[:ROWS]], axis=1)
        added = jnp.concatenate([mm(lifted, with_ones, TN), mm(bent, value[:ROWS], TN)], axis=1)
        keep = (closing < floor).astype(F32)
        state[...] = keep * before + block_only(added)
        return carry

    lax.fori_loop(0, rows // ROWS, body, 0, unroll=4)


def near_back(query, key_heads, grad_pair, near_mask, spread_near, scale_q, rows_q, rows_g):
    weights = near_weights(query, key_heads, near_mask)
    shifted = (weights * (grad_pair - spread_near)).astype(BF16)
    d_query = mm(shifted, key_heads) * scale_q
    d_key = fold(mm(shifted, rows_q, TN))
    return weights.astype(BF16), d_query, d_key


def prologue_kernel(
    scalars,
    query_ref,
    key_ref,
    value_ref,
    message_ref,
    start_ref,
    blend_ref,
    grad_ref,
    near_ref,
    far1_ref,
    invl_ref,
    invd_ref,
    back_ref,
    adjoint,
):
    rows = query_ref.shape[1]
    step_rows = rows // 3
    count_valid = scalars[scalars.shape[0] + VALID]
    b0, b1, b2 = (blend_ref[pl.ds(f, 1), :] for f in range(3))
    adjoint[...] = jnp.zeros(adjoint.shape, F32)

    tails = message_ref[0, pl.ds(HEAD_DIM, TAIL), :]
    key = jnp.concatenate([tails[:, :PAIR], key_ref[0]], axis=0)
    value = jnp.concatenate([tails[:, PAIR : 2 * PAIR], value_ref[0]], axis=0)
    start = start_ref[pl.ds(0, ROWS), :]
    near_mask, _, _, row, _, _ = masks(0, start)
    query = query_ref[0, pl.ds(0, ROWS), :]
    grad_f = jnp.where(row < count_valid, grad_ref[pl.ds(0, ROWS), :].astype(F32), 0.0)
    grad = grad_f.astype(BF16)
    scale = b0 * invl_ref[...]
    rows_q = (query.astype(F32) * (scale * HEAD_DIM**-0.5)).astype(BF16)
    rows_g = (grad_f * scale).astype(BF16)
    weights, _, d_key = near_back(
        query,
        split_heads(key),
        mm(grad, split_heads(value), NT),
        near_mask,
        spread(grad_f * near_ref[...]),
        scale * HEAD_DIM**-0.5,
        rows_q,
        rows_g,
    )
    back_ref[0, pl.ds(HEAD_DIM, TAIL), :] = jnp.concatenate(
        [d_key[:TAIL], fold(mm(weights, rows_g, TN))[:TAIL], jnp.zeros((TAIL, PAIR), F32)], axis=1
    ).astype(BF16)
    heads = same_head().astype(F32).astype(BF16)
    heads = jnp.concatenate([heads, heads], axis=0)

    for step in range(3):
        at = step * step_rows

        @pl.when(scalars[scalars.shape[0] + CARRIED] > at)
        def _():
            here = pl.ds(at, step_rows)
            row = iota((step_rows, PAIR), 0) + at
            start = start_ref[here, :]
            grad_f = jnp.where(row < count_valid, grad_ref[here, :].astype(F32), 0.0)
            grad = grad_f.astype(BF16)
            product = grad_f * far1_ref[here, :]
            high = product.astype(BF16)
            low = (product - high.astype(F32)).astype(BF16)
            along = mm(jnp.concatenate([high, low], axis=1), heads).astype(BF16)
            query_f = query_ref[0, here, :].astype(F32)
            live = start < 0
            scaled = jnp.where(live, lift(query_f) * (b1 * invd_ref[here, :]), 0.0)
            bent = jnp.where(
                live, jnp.tanh(query_f) * (b2 / (row - start + 1).astype(F32)), 0.0
            )
            adjoint[:, : 2 * PAIR] += mm(
                scaled.astype(BF16), jnp.concatenate([grad, along], axis=1), TN
            )
            adjoint[:, 2 * PAIR :] += mm(bent.astype(BF16), grad, TN)

    back_ref[0, pl.ds(0, HEAD_DIM), :] = fold_state(adjoint[...])


def key_side(adjoint_low, lift_k, bend_k, value):
    ones = jnp.full(value.shape, -1.0 / HEAD_DIM, BF16)
    d_lift = mm(jnp.concatenate([value, ones], axis=1), adjoint_low[:, : 2 * PAIR], NT)
    d_bend = mm(value, adjoint_low[:, 2 * PAIR :], NT)
    both = jnp.concatenate([adjoint_low[:, :PAIR], adjoint_low[:, 2 * PAIR :]], axis=0)
    d_value = mm(jnp.concatenate([lift_k, bend_k], axis=1), both)
    return d_lift, d_bend, d_value


def backward_kernel(
    scalars,
    qkv_ref,
    message_ref,
    start_ref,
    blend_ref,
    grad_ref,
    near_ref,
    far1_ref,
    far2_ref,
    invl_ref,
    invd_ref,
    states_ref,
    back_ref,
    done_ref,
    out_ref,
    sums_ref,
    keys,
    values,
    adjoint,
    key_carry,
    value_carry,
):
    rows = qkv_ref.shape[1]
    steps = rows // ROWS
    load_keys(qkv_ref, message_ref, keys, values)
    count_valid = scalars[scalars.shape[0] + VALID]
    last = scalars[scalars.shape[0] + LAST]
    b0, b1, b2 = (blend_ref[pl.ds(f, 1), :] for f in range(3))
    lanes = iota((ROWS, PAIR), 1) < HEAD_DIM

    arrived = unfold_state(back_ref[0])
    tail_grads = back_ref[0, pl.ds(HEAD_DIM, TAIL), :].astype(F32)
    end_key = keys[pl.ds(rows, TAIL), :].astype(F32)
    end_lift, end_bend = lift(end_key), jnp.tanh(end_key)
    end_parts = key_side(
        arrived.astype(BF16), end_lift.astype(BF16), end_bend.astype(BF16), values[pl.ds(rows, TAIL), :]
    )
    live = iota((TAIL, PAIR), 0) + (rows - TAIL) >= last
    key_carry[...] = tail_grads[:, :PAIR] + jnp.where(
        live,
        end_parts[0] * jnp.minimum(end_lift, 1.0) + end_parts[1] * (1.0 - end_bend * end_bend),
        0.0,
    )
    value_carry[...] = tail_grads[:, PAIR : 2 * PAIR] + jnp.where(live, end_parts[2], 0.0)
    adjoint[...] = jnp.where(last < rows - TAIL, 1.0, 0.0) * arrived
    sums_ref[...] = jnp.zeros(sums_ref.shape, F32)

    def add_up(place, product):
        sums_ref[pl.ds(place, 8), :] += jnp.sum(product.reshape(ROWS // 8, 8, PAIR), axis=0)

    def body(back, carry):
        step = steps - 1 - back
        at = pl.multiple_of(step * ROWS, 32)
        query = qkv_ref[0, pl.ds(at, ROWS), :]
        key = keys[pl.ds(at, WIN), :]
        value = values[pl.ds(at, WIN), :]
        start = start_ref[pl.ds(at, ROWS), :]
        near_mask, far_mask, carried, row, floor, first = masks(step, start)
        far_two = two(far_mask)
        grad_f = jnp.where(row < count_valid, grad_ref[pl.ds(at, ROWS), :].astype(F32), 0.0)
        grad = grad_f.astype(BF16)
        query_f = query.astype(F32)
        key_f = key.astype(F32)
        lift_qf, bend_qf = lift(query_f), jnp.tanh(query_f)
        lift_kf, bend_kf = lift(key_f), jnp.tanh(key_f)
        lift_q, bend_q = lift_qf.astype(BF16), bend_qf.astype(BF16)
        lift_k, bend_k = lift_kf.astype(BF16), bend_kf.astype(BF16)
        lift_heads, bend_heads = split_heads(lift_k), split_heads(bend_k)
        r0 = b0 * invl_ref[pl.ds(at, ROWS), :]
        r1 = b1 * invd_ref[pl.ds(at, ROWS), :]
        r2 = b2 / (row - start + 1).astype(F32)
        grad_pair = mm(grad, split_heads(value), NT)
        rows_q = (query_f * (r0 * HEAD_DIM**-0.5)).astype(BF16)
        near_product = grad_f * near_ref[pl.ds(at, ROWS), :]
        weights, d_query, d_key = near_back(
            query,
            split_heads(key),
            grad_pair,
            near_mask,
            spread(near_product),
            r0 * HEAD_DIM**-0.5,
            rows_q,
            None,
        )
        far1_product = grad_f * far1_ref[pl.ds(at, ROWS), :]
        add_up(0, near_product)
        add_up(8, far1_product)
        add_up(16, grad_f * far2_ref[pl.ds(at, ROWS), :])
        spread_far = spread(far1_product)
        along = jnp.where(lanes, spread_far[:, :WIN], spread_far[:, WIN:])
        shifted = jnp.where(far_two, grad_pair - spread_far, 0.0).astype(BF16)
        plain = jnp.where(far_two, grad_pair, 0.0).astype(BF16)
        pair_weight = jnp.where(far_two, mm(lift_q, lift_heads, NT), 0.0).astype(BF16)
        pair_bend = jnp.where(far_two, mm(bend_q, bend_heads, NT), 0.0).astype(BF16)
        before = states_ref[0, pl.ds(pl.multiple_of(step * PAIR, PAIR), PAIR), :]
        scaled_along = (along * (-1.0 / HEAD_DIM)).astype(BF16)
        state_lift = mm(jnp.concatenate([grad, scaled_along], axis=1), before[:, : 2 * PAIR], NT)
        state_bend = mm(grad, before[:, 2 * PAIR :], NT)
        d_query = (
            d_query
            + (mm(shifted, lift_heads) + jnp.where(carried, state_lift, 0.0))
            * (r1 * jnp.minimum(lift_qf, 1.0))
            + (mm(plain, bend_heads) + jnp.where(carried, state_bend, 0.0))
            * (r2 * (1.0 - bend_qf * bend_qf))
        )
        out_ref[0, pl.ds(at, ROWS), :] = d_query.astype(BF16)
        rows_a = lift_qf * r1
        rows_t = bend_qf * r2
        d_lift = fold(mm(shifted, rows_a.astype(BF16), TN))
        d_bend = fold(mm(plain, rows_t.astype(BF16), TN))
        d_value = fold(
            mm(
                jnp.concatenate([weights, pair_weight, pair_bend], axis=0),
                jnp.concatenate([grad_f * r0, grad_f * r1, grad_f * r2], axis=0).astype(BF16),
                TN,
            )
        )
        after = adjoint[...]
        parts = key_side(after.astype(BF16), lift_k[:ROWS], bend_k[:ROWS], value[:ROWS])
        closing = scalars[step]
        live = iota((ROWS, PAIR), 0) + first >= jnp.maximum(closing, floor)
        pad = jnp.zeros((TAIL, PAIR), F32)
        d_lift = d_lift + jnp.concatenate([jnp.where(live, parts[0], 0.0), pad], axis=0)
        d_bend = d_bend + jnp.concatenate([jnp.where(live, parts[1], 0.0), pad], axis=0)
        d_value = d_value + jnp.concatenate([jnp.where(live, parts[2], 0.0), pad], axis=0)
        d_key = d_key + d_lift * jnp.minimum(lift_kf, 1.0) + d_bend * (1.0 - bend_kf * bend_kf)
        out_ref[1, pl.ds(at, ROWS), :] = jnp.concatenate(
            [d_key[TAIL:ROWS], d_key[ROWS:] + key_carry[...]], axis=0
        ).astype(BF16)
        out_ref[2, pl.ds(at, ROWS), :] = jnp.concatenate(
            [d_value[TAIL:ROWS], d_value[ROWS:] + value_carry[...]], axis=0
        ).astype(BF16)
        key_carry[...] = d_key[:TAIL]
        value_carry[...] = d_value[:TAIL]
        from_lift = mm(
            jnp.where(carried, rows_a, 0.0).astype(BF16),
            jnp.concatenate([grad, along.astype(BF16)], axis=1),
            TN,
        )
        from_bend = mm(jnp.where(carried, rows_t, 0.0).astype(BF16), grad, TN)
        keep = (closing < floor).astype(F32)
        adjoint[...] = keep * after + block_only(jnp.concatenate([from_lift, from_bend], axis=1))
        return carry

    lax.fori_loop(0, steps, body, 0, unroll=4)


def feed_kernel(
    scalars,
    mixed_ref,
    tokens_ref,
    cotangent_ref,
    out_weight_ref,
    gain_ref,
    own_ref,
    other_ref,
    layer_ref,
    d_hidden_ref,
    d_branch_ref,
    d_mixed_ref,
    normed_ref,
    active_ref,
    d_inner_ref,
    sums_ref,
):
    c0 = math.sqrt(2.0 / math.pi)
    hidden = tokens_ref[...].astype(F32) + mm(mixed_ref[...], out_weight_ref[...], NT)
    normal, scale = norm_parts(hidden)
    normed = (normal * gain_ref[...]).astype(BF16)
    normed_ref[...] = normed
    cotangent = cotangent_ref[...]
    half, width = own_ref.shape[1:]
    chunk = min(512, half)
    layer = hidden
    d_normed = jnp.zeros(hidden.shape, F32)
    for place, ref in enumerate((own_ref, other_ref)):
        for first in range(0, half, chunk):
            into = ref[0, pl.ds(first, chunk), :]
            down = ref[1, pl.ds(first, chunk), :]
            inner = mm(normed, into, NT)
            d_active = mm(cotangent, down, NT)
            square = inner * inner
            bent = jnp.tanh(inner * (c0 + (c0 * 0.044715) * square))
            gate = 0.5 + 0.5 * bent
            active = (inner * gate).astype(BF16)
            slope = gate + inner * (0.5 - 0.5 * bent * bent) * (
                c0 + (3.0 * 0.044715 * c0) * square
            )
            d_inner = (d_active * slope).astype(BF16)
            at = pl.ds(place * half + first, chunk)
            active_ref[:, at] = active
            d_inner_ref[:, at] = d_inner
            layer = layer + mm(active, down)
            d_normed = d_normed + mm(d_inner, into)
    layer_ref[...] = layer.astype(BF16)
    d_part, gain_rows = norm_back(d_normed, gain_ref[...], normal, scale)
    d_hidden = cotangent.astype(F32) + d_part
    d_hidden_ref[...] = d_hidden
    d_branch = d_hidden.astype(BF16)
    d_branch_ref[...] = d_branch
    d_mixed_ref[...] = mm(d_branch, out_weight_ref[...]).astype(BF16)

    @pl.when(pl.program_id(0) == 0)
    def _():
        sums_ref[...] = jnp.zeros(sums_ref.shape, F32)

    sums_ref[...] += gain_rows


def feed_grad_kernel(
    scalars, normed_ref, cotangent_ref, active_ref, d_inner_ref, *refs
):
    refs[-1][0] = mm(d_inner_ref[...], normed_ref[...], TN).astype(refs[-1].dtype)
    refs[-1][1] = mm(active_ref[...], cotangent_ref[...], TN).astype(refs[-1].dtype)
    if len(refs) > 1:
        mixed_ref, d_branch_ref, out_grad_ref, _ = refs

        @pl.when(pl.program_id(0) == 0)
        def _():
            out_grad_ref[...] = mm(d_branch_ref[...], mixed_ref[...], TN)


def input_kernel(
    scalars, d_qkv_ref, weight_ref, tokens_ref, d_hidden_ref, gain_ref, input_grad_ref
):
    d_normed = mm(d_qkv_ref[0], weight_ref[0], NT)
    for c in range(1, 3):
        d_normed = d_normed + mm(d_qkv_ref[c], weight_ref[c], NT)
    normal, scale = norm_parts(tokens_ref[...].astype(F32))
    d_part, _ = norm_back(d_normed, gain_ref[...], normal, scale)
    input_grad_ref[...] = d_hidden_ref[...] + d_part


def resume(kernel, done, scalars, qkv_ref, message_ref, start_ref, blend_ref, *refs):
    kernel(scalars, qkv_ref, message_ref, start_ref, blend_ref, *refs[done:])


def pair_specs(rows, first=0):
    return {
        "qkv": pl.BlockSpec((3, rows, PAIR), lambda p, s: (0, 0, p + first)),
        "message": pl.BlockSpec((1, HEAD_DIM + TAIL, 3 * PAIR), lambda p, s: (p + first, 0, 0)),
        "start": pl.BlockSpec((rows, PAIR), lambda p, s: (0, 0)),
        "blend": pl.BlockSpec((3, PAIR), lambda p, s: (0, p + first)),
        "column": pl.BlockSpec((rows, PAIR), lambda p, s: (0, p + first)),
        "states": pl.BlockSpec((1, rows // ROWS * PAIR, 3 * PAIR), lambda p, s: (p + first, 0, 0)),
        "sums": pl.BlockSpec((24, PAIR), lambda p, s: (0, p)),
        "query": pl.BlockSpec((1, rows, PAIR), lambda p, s: (0, 0, p)),
        "head_rows": pl.BlockSpec((ROWS, PAIR), lambda p, s: (0, p)),
    }


def call(kernel, ins, outs, out_shapes, scratch, grid, name, flops, moved, aliases={}):
    return pl.pallas_call(
        kernel,
        out_shape=out_shapes,
        grid_spec=pltpu.PrefetchScalarGridSpec(
            num_scalar_prefetch=1,
            grid=(grid,),
            in_specs=ins,
            out_specs=outs,
            scratch_shapes=scratch,
        ),
        input_output_aliases=aliases,
        compiler_params=pltpu.CompilerParams(
            dimension_semantics=("arbitrary",), vmem_limit_bytes=56 * 1024 * 1024
        ),
        cost_estimate=pl.CostEstimate(flops=flops, bytes_accessed=moved, transcendentals=0),
        name=name,
    )


def norm_parts(source):
    centered = source - jnp.mean(source, axis=-1, keepdims=True)
    spread_of = jnp.mean(centered * centered, axis=-1, keepdims=True)
    scale = lax.rsqrt(spread_of + EPS)
    return centered * scale, scale


def norm_back(d_out, gain, normal, scale):
    e = d_out * gain
    inner = jnp.mean(e, axis=-1, keepdims=True)
    along = jnp.mean(e * normal, axis=-1, keepdims=True)
    rows = jnp.sum((d_out * normal).reshape(-1, 8, d_out.shape[1]), axis=0)
    return scale * (e - inner - normal * along), rows


def bits(size):
    return [1 << b for b in range(int(math.log2(size)))]


def phases():
    dp = bits(lax.axis_size("dp"))
    core, rest = dp[:1], dp[1:]
    mid = len(rest) // 2
    far = [("dp", m) for m in rest[mid:]]
    near = [("dp", m) for m in rest[:mid]] + [("head", m) for m in bits(lax.axis_size("head"))]
    groups = []
    for run in (far, near, [("dp", m) for m in core]):
        groups += [run[i : i + 2] for i in range(0, len(run), 2)]
    return groups


def relative_bits():
    return [pair for group in phases() for pair in group]


def all_flips():
    order = relative_bits()
    flips = []
    for index in range(1 << len(order)):
        chosen = [pair for place, pair in enumerate(order) if index >> place & 1]
        flips.append(tuple(sum(m for a, m in chosen if a == axis) for axis in ("dp", "head")))
    return flips


def peer(array, group, combo):
    n_dp, n_head = lax.axis_size("dp"), lax.axis_size("head")
    chosen = [pair for place, pair in enumerate(group) if combo >> place & 1]
    flip_dp = sum(m for axis, m in chosen if axis == "dp")
    flip_head = sum(m for axis, m in chosen if axis == "head")
    pairs = [
        (d * n_head + h, (d ^ flip_dp) * n_head + (h ^ flip_head))
        for d in range(n_dp)
        for h in range(n_head)
    ]
    return lax.ppermute(array, ("dp", "head"), pairs)


def widen(block, group, axis, after=None):
    others = [peer(block, group, combo) for combo in range(1, 1 << len(group))]
    if after is not None:
        others, after = lax.optimization_barrier((others, after))
    whole = jnp.concatenate([block] + others, axis=axis)
    return whole if after is None else (whole, after)


def narrow(keep, gives, group, after=None):
    arrived = [peer(give.astype(BF16), group, combo) for combo, give in enumerate(gives, 1)]
    if after is not None:
        arrived, _ = lax.optimization_barrier((arrived, after))
    return keep.astype(F32) + sum(part.astype(F32) for part in arrived)


def narrow_axis(total, group, axis, after=None):
    parts = jnp.split(total, 1 << len(group), axis=axis)
    return narrow(parts[0], parts[1:], group, after)


def pass_along(local, keep, shift):
    size = lax.axis_size("head")
    pairs = [(i, i + shift) for i in range(size) if 0 <= i + shift < size]
    arrived = lax.ppermute(local, "head", pairs)
    for _ in range(size - 2):
        rows = iota(local.shape, 1) < HEAD_DIM
        total = local.astype(F32) + jnp.where(rows, keep * arrived.astype(F32), 0.0)
        arrived = lax.ppermute(total.astype(BF16), "head", pairs)
    return arrived


def per_device(
    tokens,
    ln1_gain,
    qkv_weight,
    out_weight,
    blend,
    ln2_gain,
    in_weight,
    down_weight,
    cotangent,
    lengths,
):
    rows, width = tokens.shape
    n_dp, n_head = lax.axis_size("dp"), lax.axis_size("head")
    pairs = width // PAIR
    steps = rows // ROWS
    groups = phases()
    flips = all_flips()

    shards = jnp.concatenate([qkv_weight, out_weight.T[None]], axis=0)[None]
    feed = jnp.stack([in_weight, down_weight])
    shards = widen(shards, groups[0], 0)
    feed, _ = lax.optimization_barrier((feed, shards))
    feed = widen(feed, groups[0][:1], 1)
    for group in groups[1:-1]:
        shards = widen(shards, group, 0)
    shards, feed = lax.optimization_barrier((shards, feed))
    others = peer(shards, groups[-1], 1)

    item_lengths = lengths[0]
    slots = item_lengths.shape[0]
    ends = jnp.sum(
        jnp.where(iota((slots, slots), 1) <= iota((slots, slots), 0), item_lengths[None, :], 0),
        axis=1,
    )
    offset = lax.axis_index("head") * rows
    local = jnp.arange(rows, dtype=jnp.int32)
    place = local + offset
    total = ends[slots - 1]
    item_start = jnp.max(
        jnp.where(ends[None, :] <= place[:, None], ends[None, :], 0), axis=1
    )
    start = jnp.where(place < total, item_start - offset, local)
    carried_rows = jnp.sum((start < 0).astype(jnp.int32))
    scalars = jnp.concatenate(
        [
            start.reshape(steps, ROWS)[:, ROWS - TAIL - 1],
            carried_rows[None],
            start[rows - 1 :],
            (total - offset)[None],
            lax.axis_index("dp").astype(jnp.int32)[None],
            lax.axis_index("head").astype(jnp.int32)[None],
        ]
    )
    start_wide = jnp.broadcast_to(start[:, None], (rows, PAIR))
    keep_all = (start[rows - 1] < 0).astype(F32)
    blend_wide = jnp.repeat(blend, HEAD_DIM, axis=1)

    spec = pair_specs(rows)
    wide = jax.ShapeDtypeStruct((rows, width), F32)
    states_shape = jax.ShapeDtypeStruct((pairs, steps * PAIR, 3 * PAIR), BF16)
    message_shape = jax.ShapeDtypeStruct((pairs, HEAD_DIM + TAIL, 3 * PAIR), BF16)
    big = rows * width
    part = rows // 3

    def whole_spec(shape):
        return pl.BlockSpec(shape, lambda p, s: (0,) * len(shape))

    qkv, normed_one, qkv_all, out_all, closing = call(
        functools.partial(project_kernel, flips=flips),
        [
            pl.BlockSpec((part, width), lambda p, s: (p, 0)),
            whole_spec((1, width)),
            whole_spec(shards.shape),
            whole_spec(shards.shape),
        ],
        [
            pl.BlockSpec((3, part, width), lambda p, s: (0, p, 0)),
            pl.BlockSpec((part, width), lambda p, s: (p, 0)),
            whole_spec((3, width, width)),
            whole_spec((width, width)),
            whole_spec(message_shape.shape),
        ],
        [
            jax.ShapeDtypeStruct((3, rows, width), BF16),
            jax.ShapeDtypeStruct((rows, width), BF16),
            jax.ShapeDtypeStruct((3, width, width), BF16),
            jax.ShapeDtypeStruct((width, width), BF16),
            message_shape,
        ],
        [
            pltpu.VMEM((pairs, PAIR, 3 * PAIR), F32),
            pltpu.VMEM((n_head, 4, n_dp, width // n_dp, width // n_head), BF16),
        ],
        3,
        "project",
        6 * big * width,
        12 * big,
    )(scalars, tokens, ln1_gain[None], shards, others)
    for pair in groups[0][1:]:
        feed, _ = widen(feed, [pair], 1, closing)
    message = pass_along(closing, keep_all, 1)

    key_scratch = pltpu.VMEM((rows + TAIL, PAIR), BF16)
    state_scratch = pltpu.VMEM((PAIR, 3 * PAIR), F32)
    tail_scratch = pltpu.VMEM((TAIL, PAIR), F32)
    results = ()
    count = pairs // 2
    for first in (0, count):
        spec = pair_specs(rows, first)
        results = call(
            functools.partial(resume, forward_kernel, len(results)),
            [spec["qkv"], spec["message"], spec["start"], spec["blend"]]
            + [pl.BlockSpec(memory_space=pl.ANY)] * len(results),
            [spec["column"]] * 6 + [spec["states"]],
            [jax.ShapeDtypeStruct((rows, width), BF16)] + [wide] * 5 + [states_shape],
            [key_scratch, key_scratch, state_scratch],
            count,
            "forward",
            4000 * big,
            20 * big,
            {5 + i: i for i in range(len(results))},
        )(scalars, qkv, message, start_wide, blend_wide, *results)
        if not first:
            feed, results = widen(feed, groups[1], 1, results)
            feed, message = lax.optimization_barrier((feed, message))
    for group in groups[2:-1]:
        feed = widen(feed, group, 1)
    feed_other = peer(feed, groups[-1], 1)
    mixed, near, far1, far2, inv_l, inv_d, states = results

    spec = pair_specs(rows)
    low = jax.ShapeDtypeStruct((rows, width), BF16)
    row_spec = pl.BlockSpec((part, width), lambda p, s: (p, 0))
    hidden_units = 2 * feed.shape[1]
    unit_spec = pl.BlockSpec((part, hidden_units), lambda p, s: (p, 0))
    unit_shape = jax.ShapeDtypeStruct((rows, hidden_units), BF16)
    sums_shape = jax.ShapeDtypeStruct((8, width), F32)
    layer_out, d_hidden, d_branch, d_mixed, normed_two, active, d_inner, gain_two_rows = call(
        feed_kernel,
        [row_spec] * 3
        + [
            whole_spec((width, width)),
            whole_spec((1, width)),
            whole_spec(feed.shape),
            whole_spec(feed.shape),
        ],
        [row_spec] * 5 + [unit_spec] * 2 + [whole_spec((8, width))],
        [low, wide, low, low, low, unit_shape, unit_shape, sums_shape],
        [],
        3,
        "feed",
        8 * big * hidden_units,
        32 * big,
    )(scalars, mixed, tokens, cotangent, out_all, ln2_gain[None], feed, feed_other)

    back = call(
        prologue_kernel,
        [
            spec["query"],
            pl.BlockSpec((1, ROWS, PAIR), lambda p, s: (1, 0, p)),
            pl.BlockSpec((1, ROWS, PAIR), lambda p, s: (2, 0, p)),
            spec["message"],
            spec["start"],
            spec["blend"],
            spec["column"],
            spec["head_rows"],
            spec["column"],
            spec["head_rows"],
            spec["column"],
        ],
        spec["message"],
        message_shape,
        [state_scratch],
        pairs,
        "prologue",
        500 * big,
        20 * big,
    )(scalars, qkv, qkv, qkv, message, start_wide, blend_wide, d_mixed, near, far1, inv_l, inv_d)
    d_inner, _ = lax.optimization_barrier((d_inner, back))
    back_in = pass_along(back, keep_all, -1)

    unit = hidden_units // 4
    half_shape = (2, 2 * unit, width)
    whole_rows = whole_spec((rows, width))

    def feed_grad(place, kind, d_inner, more_ins, more_in_specs, more_outs, more_out_specs):
        columns = pl.BlockSpec((rows, unit), lambda p, s: (0, p + 2 * place))
        return call(
            feed_grad_kernel,
            [whole_rows] * 2 + [columns] * 2 + more_in_specs,
            more_out_specs + [pl.BlockSpec((2, unit, width), lambda p, s: (0, p, 0))],
            more_outs + [jax.ShapeDtypeStruct(half_shape, kind)],
            [],
            2,
            "feed_grad",
            2 * big * hidden_units,
            12 * big,
        )(scalars, normed_two, cotangent, active, d_inner, *more_ins)

    out_grad, keep = feed_grad(
        0,
        F32,
        d_inner,
        [mixed, d_branch],
        [whole_rows] * 2,
        [jax.ShapeDtypeStruct((width, width), F32)],
        [whole_spec((width, width))],
    )
    d_inner, back_in, out_grad = lax.optimization_barrier((d_inner, back_in, out_grad))
    (give,) = feed_grad(1, BF16, d_inner, [], [], [], [])
    feed_share = narrow(keep, [give], groups[-1])
    left = list(reversed(groups[:-1]))

    d_qkv = jnp.zeros((3, 8, PAIR), BF16)
    sums = []
    first = 0
    for count in (pairs // 4, pairs // 2, pairs // 4):
        spec = pair_specs(rows, first)
        more = {13: 0} if first else {}
        d_qkv, part_sums = call(
            backward_kernel,
            [spec["qkv"], spec["message"], spec["start"], spec["blend"]]
            + [spec["column"]] * 6
            + [spec["states"], spec["message"], pl.BlockSpec(memory_space=pl.ANY)],
            [spec["qkv"], spec["sums"]],
            [
                jax.ShapeDtypeStruct((3, rows, width), BF16),
                jax.ShapeDtypeStruct((24, count * PAIR), F32),
            ],
            [key_scratch, key_scratch, state_scratch, tail_scratch, tail_scratch],
            count,
            "backward",
            16000 * big * count // pairs,
            40 * big * count // pairs,
            more,
        )(
            scalars,
            qkv,
            message,
            start_wide,
            blend_wide,
            d_mixed,
            near,
            far1,
            far2,
            inv_l,
            inv_d,
            states,
            back_in,
            d_qkv,
        )
        sums.append(part_sums)
        first += count
        if left and first < pairs:
            _, back_in = lax.optimization_barrier((feed_share, back_in))
            feed_share = narrow_axis(feed_share, left.pop(0), 1)
    for group in left:
        feed_share = narrow_axis(feed_share, group, 1)
    feed_share, d_qkv = lax.optimization_barrier((feed_share, d_qkv))
    sums = jnp.concatenate(sums, axis=1)
    blend_part = jnp.sum(sums.reshape(3, 8, blend.shape[1], HEAD_DIM), axis=(1, 3))

    shard_shape = (n_dp * n_head // 2, 4, width // n_dp, width // n_head)
    shard_spec = pl.BlockSpec((shard_shape[0], 1) + shard_shape[2:], lambda p, s: (0, p, 0, 0))
    keep, give, gain_one_rows = call(
        functools.partial(weight_grad_kernel, flips=flips),
        [
            whole_spec((rows, width)),
            pl.BlockSpec((1, rows, width), lambda p, s: (jnp.minimum(p, 2), 0, 0)),
            whole_spec((width, width)),
            pl.BlockSpec((1, width, width), lambda p, s: (jnp.minimum(p, 2), 0, 0)),
        ],
        [shard_spec, shard_spec, whole_spec((8, width))],
        [
            jax.ShapeDtypeStruct(shard_shape, F32),
            jax.ShapeDtypeStruct(shard_shape, BF16),
            sums_shape,
        ],
        [pltpu.VMEM((n_head, n_dp, width // n_dp, width // n_head), F32)],
        4,
        "weight_grad",
        6 * big * width,
        8 * big,
    )(scalars, normed_one, d_qkv, out_grad, qkv_all)
    parts = [gain_one_rows[0] / ln1_gain, jnp.sum(gain_two_rows, axis=0), blend_part.reshape(-1)]
    total_sums = jnp.concatenate(parts)[None]
    share = narrow(keep, [give], groups[-1])
    hops = list(reversed(relative_bits()))
    total_sums = total_sums + peer(total_sums, [hops[0]], 1)
    total_sums, d_qkv, _ = lax.optimization_barrier((total_sums, d_qkv, share))
    total_sums = total_sums + peer(total_sums, [hops[1]], 1)
    input_grad = call(
        input_kernel,
        [
            pl.BlockSpec((3, part, width), lambda p, s: (0, p, 0)),
            whole_spec((3, width, width)),
            row_spec,
            row_spec,
            whole_spec((1, width)),
        ],
        row_spec,
        wide,
        [],
        3,
        "input",
        6 * big * width,
        24 * big,
    )(scalars, d_qkv, qkv_all, tokens, d_hidden, ln1_gain[None])
    share = narrow_axis(share, groups[-2], 0, input_grad)
    total_sums, _ = lax.optimization_barrier((total_sums, input_grad))
    total_sums = total_sums + peer(total_sums, [hops[2]], 1)
    for group in reversed(groups[:-2]):
        parts = jnp.split(share, 1 << len(group), axis=0)
        gives = [part.astype(BF16) for part in parts[1:]]
        total_sums, _ = lax.optimization_barrier((total_sums, gives))
        share = narrow(parts[0], gives, group)
    for pair in hops[3:]:
        total_sums = total_sums + peer(total_sums, [pair], 1)
    total_sums = total_sums[0]
    gain_one, gain_two = total_sums[:width], total_sums[width : 2 * width]
    blend_sum = total_sums[2 * width :].reshape(blend.shape)
    qkv_share, out_share = share[0, :3], share[0, 3].T
    in_share, down_share = feed_share[0], feed_share[1]
    return (
        layer_out,
        input_grad,
        gain_one,
        qkv_share,
        out_share,
        blend_sum,
        gain_two,
        in_share,
        down_share,
    )


def solution(mesh):
    return jax.shard_map(
        per_device,
        mesh=mesh,
        in_specs=(
            P(("dp", "head"), None),
            P(),
            P(None, "dp", "head"),
            P("head", "dp"),
            P(),
            P(),
            P(("dp", "head"), None),
            P(("dp", "head"), None),
            P(("dp", "head"), None),
            P("dp", None),
        ),
        out_specs=(
            P(("dp", "head"), None),
            P(("dp", "head"), None),
            P(),
            P(None, "dp", "head"),
            P("head", "dp"),
            P(),
            P(),
            P(("dp", "head"), None),
            P(("dp", "head"), None),
        ),
        check_vma=False,
    )
```

```python
import functools
import math

import jax
import jax.numpy as jnp
from jax import lax
from jax.experimental import pallas as pl
from jax.experimental.pallas import tpu as pltpu
from jax.sharding import PartitionSpec as P

HEAD_DIM = 64
BAND = 30
ROWS = 96
TAIL = 32
WIN = ROWS + TAIL
PAIR = 2 * HEAD_DIM
EPS = 1e-05
NEG = -1e30
CARRIED, LAST, VALID, ROW_AT, COLUMN_AT = range(-5, 0)
F32 = jnp.float32
BF16 = jnp.bfloat16
NT = (((1,), (1,)), ((), ()))
TN = (((0,), (0,)), ((), ()))
NN = (((1,), (0,)), ((), ()))


def mm(left, right, dims=NN):
    return lax.dot_general(left, right, dims, preferred_element_type=F32)


def iota(shape, axis):
    return lax.broadcasted_iota(jnp.int32, shape, axis)


def lift(values):
    return jnp.where(values > 0, values + 1.0, jnp.exp(jnp.minimum(values, 0.0)))


def head_lanes(dtype):
    first = (iota((1, PAIR), 1) < HEAD_DIM).astype(F32)
    return first.astype(dtype), (1.0 - first).astype(dtype)


def split_heads(block):
    first, second = head_lanes(block.dtype)
    return jnp.concatenate([block * first, block * second], axis=0)


def same_head():
    return (iota((PAIR, PAIR), 0) < HEAD_DIM) == (iota((PAIR, PAIR), 1) < HEAD_DIM)


def block_only(wide):
    keep = same_head()
    parts = [
        jnp.where(keep, wide[:, p * PAIR : (p + 1) * PAIR], 0.0)
        for p in range(wide.shape[1] // PAIR)
    ]
    return jnp.concatenate(parts, axis=1)


def fold(tall):
    half = tall.shape[0] // 2
    lanes = iota((half, PAIR), 1) < HEAD_DIM
    return jnp.where(lanes, tall[:half], tall[half:])


def two(half):
    return jnp.concatenate([half, half], axis=1)


def masks(step, start):
    row = iota((ROWS, WIN), 0) + step * ROWS
    first = step * ROWS - TAIL
    key = iota((ROWS, WIN), 1) + first
    floor = jnp.maximum(first, 0)
    causal = key <= row
    near = causal & (key >= jnp.maximum(start, row - (BAND - 1)))
    far = causal & (key >= jnp.maximum(start, floor))
    return near, far, start < floor, row, floor, first


def near_scores(query, key_heads):
    return mm(query * jnp.asarray(HEAD_DIM**-0.5, BF16), key_heads, NT)


def near_weights(scores, near):
    parts = []
    for h in range(2):
        part = jnp.where(near, scores[:, h * WIN : (h + 1) * WIN], NEG)
        parts.append(jnp.exp(part - jnp.max(part, axis=1, keepdims=True)))
    return jnp.concatenate(parts, axis=1)


def spread(product):
    first = iota(product.shape, 1) < HEAD_DIM
    sums = [
        jnp.sum(jnp.where(keep, product, 0.0), axis=1, keepdims=True) for keep in (first, ~first)
    ]
    return jnp.concatenate([jnp.broadcast_to(part, (ROWS, WIN)) for part in sums], axis=1)


def load_keys(qkv_ref, message_ref, keys, values):
    rows = qkv_ref.shape[1]
    keys[pl.ds(0, TAIL), :] = message_ref[0, pl.ds(HEAD_DIM, TAIL), :PAIR]
    keys[pl.ds(TAIL, rows), :] = qkv_ref[1]
    values[pl.ds(0, TAIL), :] = message_ref[0, pl.ds(HEAD_DIM, TAIL), PAIR : 2 * PAIR]
    values[pl.ds(TAIL, rows), :] = qkv_ref[2]


def fold_state(wide):
    kept = block_only(wide)
    return (kept[:HEAD_DIM] + kept[HEAD_DIM:]).astype(BF16)


def unfold_state(message):
    half = message[:HEAD_DIM].astype(F32)
    return block_only(jnp.concatenate([half, half], axis=0))


def project_kernel(
    scalars,
    tokens_ref,
    gain_ref,
    own_ref,
    other_ref,
    qkv_ref,
    normed_ref,
    weight_ref,
    out_weight_ref,
    message_ref,
    state,
    placed,
    *,
    flips,
):
    step = pl.program_id(0)
    rows, width = tokens_ref.shape
    pairs = width // PAIR
    half, _, tall, wide = own_ref.shape
    last = jnp.maximum(scalars[scalars.shape[0] + LAST], 0)

    @pl.when(step == 0)
    def _():
        for index, (flip_row, flip_column) in enumerate(flips):
            row = scalars[scalars.shape[0] + ROW_AT] ^ flip_row
            column = scalars[scalars.shape[0] + COLUMN_AT] ^ flip_column
            piece = own_ref[index] if index < half else other_ref[index - half]
            for c in range(4):
                placed[column, c, row] = piece[c]
        for h in range(width // wide):
            at = pl.ds(h * wide, wide)
            weight_ref[:, :, at] = placed[h, :3].reshape(3, width, wide)
            out_weight_ref[:, at] = placed[h, 3].reshape(width, wide)
        state[...] = jnp.zeros(state.shape, F32)

    normed = (norm_parts(tokens_ref[...].astype(F32))[0] * gain_ref[...]).astype(BF16)
    normed_ref[...] = normed
    for c in range(3):
        qkv_ref[c] = mm(normed, weight_ref[c]).astype(BF16)
    live = iota((rows, PAIR), 0) + step * rows >= last
    ones = jnp.ones((rows, PAIR), BF16)
    for p in range(pairs):
        at = pl.ds(p * PAIR, PAIR)
        key = qkv_ref[1, :, at].astype(F32)
        value = qkv_ref[2, :, at]
        lifted = jnp.where(live, lift(key), 0.0).astype(BF16)
        bent = jnp.where(live, jnp.tanh(key), 0.0).astype(BF16)
        state[p, :, : 2 * PAIR] += mm(lifted, jnp.concatenate([value, ones], axis=1), TN)
        state[p, :, 2 * PAIR :] += mm(bent, value, TN)

    @pl.when(step == pl.num_programs(0) - 1)
    def _():
        for p in range(pairs):
            at = pl.ds(p * PAIR, PAIR)
            message_ref[p, pl.ds(0, HEAD_DIM), :] = fold_state(state[p])
            message_ref[p, pl.ds(HEAD_DIM, TAIL), :] = jnp.concatenate(
                [
                    qkv_ref[1, pl.ds(rows - TAIL, TAIL), at],
                    qkv_ref[2, pl.ds(rows - TAIL, TAIL), at],
                    jnp.zeros((TAIL, PAIR), BF16),
                ],
                axis=1,
            )


def weight_grad_kernel(
    scalars,
    normed_ref,
    d_qkv_ref,
    out_grad_ref,
    weight_ref,
    keep_ref,
    give_ref,
    gain_ref,
    whole,
    *,
    flips,
):
    c = pl.program_id(0)
    half, _, tall, wide = keep_ref.shape

    def place(total):
        for h in range(total.shape[1] // wide):
            part = total[:, h * wide : (h + 1) * wide]
            whole[h] = part.reshape(whole.shape[1:])

    @pl.when(c == 0)
    def _():
        gain_ref[...] = jnp.zeros(gain_ref.shape, F32)

    @pl.when(c < 3)
    def _():
        total = mm(normed_ref[...], d_qkv_ref[0], TN)
        place(total)
        product = total * weight_ref[0].astype(F32)
        high = product.astype(BF16)
        low = (product - high.astype(F32)).astype(BF16)
        ones = jnp.ones((8, product.shape[1]), BF16)
        gain_ref[...] += mm(ones, high, NT) + mm(ones, low, NT)

    @pl.when(c == 3)
    def _():
        place(out_grad_ref[...])

    for index, (flip_row, flip_column) in enumerate(flips):
        row = scalars[scalars.shape[0] + ROW_AT] ^ flip_row
        column = scalars[scalars.shape[0] + COLUMN_AT] ^ flip_column
        if index < half:
            keep_ref[index, 0] = whole[column, row]
        else:
            give_ref[index - half, 0] = whole[column, row].astype(BF16)


def forward_kernel(
    scalars,
    qkv_ref,
    message_ref,
    start_ref,
    blend_ref,
    att_ref,
    near_ref,
    far1_ref,
    far2_ref,
    invl_ref,
    invd_ref,
    states_ref,
    keys,
    values,
    state,
):
    rows = qkv_ref.shape[1]
    load_keys(qkv_ref, message_ref, keys, values)
    state[...] = unfold_state(message_ref[0])
    count_valid = scalars[scalars.shape[0] + VALID]
    b0, b1, b2 = (blend_ref[pl.ds(f, 1), :] for f in range(3))

    def body(step, carry):
        at = pl.multiple_of(step * ROWS, 32)
        query = qkv_ref[0, pl.ds(at, ROWS), :]
        key = keys[pl.ds(at, WIN), :]
        value = values[pl.ds(at, WIN), :]
        start = start_ref[pl.ds(at, ROWS), :]
        near_mask, far_mask, carried, row, floor, first = masks(step, start)
        query_f = query.astype(F32)
        key_f = key.astype(F32)
        lift_q = lift(query_f).astype(BF16)
        bend_q = jnp.tanh(query_f).astype(BF16)
        lift_k = lift(key_f)
        bend_k = jnp.tanh(key_f)
        ones = jnp.ones((WIN, PAIR), BF16)
        value_heads = jnp.concatenate([split_heads(value), split_heads(ones)], axis=1)
        before = state[...]
        before_low = before.astype(BF16)
        scores = near_scores(query, split_heads(key))
        pair_weight = mm(lift_q, split_heads(lift_k.astype(BF16)), NT)
        pair_bend = mm(bend_q, split_heads(bend_k.astype(BF16)), NT)
        elu_state = mm(lift_q, before_low[:, : 2 * PAIR])
        tanh_state = mm(bend_q, before_low[:, 2 * PAIR :])
        states_ref[0, pl.ds(pl.multiple_of(step * PAIR, PAIR), PAIR), :] = before_low
        closing = scalars[step]
        live = iota((ROWS, PAIR), 0) + first >= jnp.maximum(closing, floor)
        lifted = jnp.where(live, lift_k[:ROWS], 0.0).astype(BF16)
        bent = jnp.where(live, bend_k[:ROWS], 0.0).astype(BF16)
        with_ones = jnp.concatenate([value[:ROWS], ones[:ROWS]], axis=1)
        added = jnp.concatenate([mm(lifted, with_ones, TN), mm(bent, value[:ROWS], TN)], axis=1)
        keep = (closing < floor).astype(F32)
        state[...] = keep * before + block_only(added)
        far_two = two(far_mask)
        pair_weight = jnp.where(far_two, pair_weight, 0.0).astype(BF16)
        pair_bend = jnp.where(far_two, pair_bend, 0.0).astype(BF16)
        elu_out = mm(pair_weight, value_heads)
        tanh_out = mm(pair_bend, value_heads[:, :PAIR]) + jnp.where(carried, tanh_state, 0.0)
        weights = near_weights(scores, near_mask).astype(BF16)
        near_out = mm(weights, value_heads)
        numerator = elu_out[:, :PAIR] + jnp.where(carried, elu_state[:, :PAIR], 0.0)
        inv_d = 1.0 / (elu_out[:, PAIR:] + jnp.where(carried, elu_state[:, PAIR:], 0.0))
        far1 = numerator * inv_d
        inv_l = 1.0 / near_out[:, PAIR:]
        near = near_out[:, :PAIR] * inv_l
        far2 = tanh_out / (row - start + 1).astype(F32)
        mixed = jnp.where(row < count_valid, b0 * near + b1 * far1 + b2 * far2, 0.0)
        att_ref[pl.ds(at, ROWS), :] = mixed.astype(BF16)
        near_ref[pl.ds(at, ROWS), :] = near
        far1_ref[pl.ds(at, ROWS), :] = far1
        far2_ref[pl.ds(at, ROWS), :] = far2
        invl_ref[pl.ds(at, ROWS), :] = inv_l
        invd_ref[pl.ds(at, ROWS), :] = inv_d
        return carry

    lax.fori_loop(0, rows // ROWS, body, 0, unroll=4)


def near_back(scores, grad_pair, near_mask, spread_near):
    weights = near_weights(scores, near_mask)
    return weights.astype(BF16), (weights * (grad_pair - spread_near)).astype(BF16)


def prologue_kernel(
    scalars,
    query_ref,
    key_ref,
    value_ref,
    message_ref,
    start_ref,
    blend_ref,
    grad_ref,
    near_ref,
    far1_ref,
    invl_ref,
    invd_ref,
    back_ref,
    adjoint,
):
    rows = query_ref.shape[1]
    step_rows = rows // 3
    count_valid = scalars[scalars.shape[0] + VALID]
    b0, b1, b2 = (blend_ref[pl.ds(f, 1), :] for f in range(3))
    adjoint[...] = jnp.zeros(adjoint.shape, F32)

    tails = message_ref[0, pl.ds(HEAD_DIM, TAIL), :]
    key = jnp.concatenate([tails[:, :PAIR], key_ref[0]], axis=0)
    value = jnp.concatenate([tails[:, PAIR : 2 * PAIR], value_ref[0]], axis=0)
    start = start_ref[pl.ds(0, ROWS), :]
    near_mask, _, _, row, _, _ = masks(0, start)
    query = query_ref[0, pl.ds(0, ROWS), :]
    grad_f = jnp.where(row < count_valid, grad_ref[pl.ds(0, ROWS), :].astype(F32), 0.0)
    grad = grad_f.astype(BF16)
    scale = b0 * invl_ref[...]
    rows_q = (query.astype(F32) * (scale * HEAD_DIM**-0.5)).astype(BF16)
    rows_g = (grad_f * scale).astype(BF16)
    weights, shifted = near_back(
        near_scores(query, split_heads(key)),
        mm(grad, split_heads(value), NT),
        near_mask,
        spread(grad_f * near_ref[...]),
    )
    d_key = fold(mm(shifted, rows_q, TN))
    back_ref[0, pl.ds(HEAD_DIM, TAIL), :] = jnp.concatenate(
        [d_key[:TAIL], fold(mm(weights, rows_g, TN))[:TAIL], jnp.zeros((TAIL, PAIR), F32)], axis=1
    ).astype(BF16)
    heads = same_head().astype(F32).astype(BF16)
    heads = jnp.concatenate([heads, heads], axis=0)

    for step in range(3):
        at = step * step_rows

        @pl.when(scalars[scalars.shape[0] + CARRIED] > at)
        def _():
            here = pl.ds(at, step_rows)
            row = iota((step_rows, PAIR), 0) + at
            start = start_ref[here, :]
            grad_f = jnp.where(row < count_valid, grad_ref[here, :].astype(F32), 0.0)
            grad = grad_f.astype(BF16)
            product = grad_f * far1_ref[here, :]
            high = product.astype(BF16)
            low = (product - high.astype(F32)).astype(BF16)
            along = mm(jnp.concatenate([high, low], axis=1), heads).astype(BF16)
            query_f = query_ref[0, here, :].astype(F32)
            live = start < 0
            scaled = jnp.where(live, lift(query_f) * (b1 * invd_ref[here, :]), 0.0)
            bent = jnp.where(
                live, jnp.tanh(query_f) * (b2 / (row - start + 1).astype(F32)), 0.0
            )
            adjoint[:, : 2 * PAIR] += mm(
                scaled.astype(BF16), jnp.concatenate([grad, along], axis=1), TN
            )
            adjoint[:, 2 * PAIR :] += mm(bent.astype(BF16), grad, TN)

    back_ref[0, pl.ds(0, HEAD_DIM), :] = fold_state(adjoint[...])


def key_side(adjoint_low, lift_k, bend_k, value):
    ones = jnp.full(value.shape, -1.0 / HEAD_DIM, BF16)
    d_lift = mm(jnp.concatenate([value, ones], axis=1), adjoint_low[:, : 2 * PAIR], NT)
    d_bend = mm(value, adjoint_low[:, 2 * PAIR :], NT)
    both = jnp.concatenate([adjoint_low[:, :PAIR], adjoint_low[:, 2 * PAIR :]], axis=0)
    d_value = mm(jnp.concatenate([lift_k, bend_k], axis=1), both)
    return d_lift, d_bend, d_value


def backward_kernel(
    scalars,
    qkv_ref,
    message_ref,
    start_ref,
    blend_ref,
    grad_ref,
    near_ref,
    far1_ref,
    far2_ref,
    invl_ref,
    invd_ref,
    states_ref,
    back_ref,
    done_ref,
    out_ref,
    sums_ref,
    keys,
    values,
    adjoint,
    key_carry,
    value_carry,
):
    rows = qkv_ref.shape[1]
    steps = rows // ROWS
    load_keys(qkv_ref, message_ref, keys, values)
    count_valid = scalars[scalars.shape[0] + VALID]
    last = scalars[scalars.shape[0] + LAST]
    b0, b1, b2 = (blend_ref[pl.ds(f, 1), :] for f in range(3))
    lanes = iota((ROWS, PAIR), 1) < HEAD_DIM

    arrived = unfold_state(back_ref[0])
    tail_grads = back_ref[0, pl.ds(HEAD_DIM, TAIL), :].astype(F32)
    end_key = keys[pl.ds(rows, TAIL), :].astype(F32)
    end_lift, end_bend = lift(end_key), jnp.tanh(end_key)
    end_parts = key_side(
        arrived.astype(BF16), end_lift.astype(BF16), end_bend.astype(BF16), values[pl.ds(rows, TAIL), :]
    )
    live = iota((TAIL, PAIR), 0) + (rows - TAIL) >= last
    key_carry[...] = tail_grads[:, :PAIR] + jnp.where(
        live,
        end_parts[0] * jnp.minimum(end_lift, 1.0) + end_parts[1] * (1.0 - end_bend * end_bend),
        0.0,
    )
    value_carry[...] = tail_grads[:, PAIR : 2 * PAIR] + jnp.where(live, end_parts[2], 0.0)
    adjoint[...] = jnp.where(last < rows - TAIL, 1.0, 0.0) * arrived
    sums_ref[...] = jnp.zeros(sums_ref.shape, F32)

    def add_up(place, product):
        sums_ref[pl.ds(place, 8), :] += jnp.sum(product.reshape(ROWS // 8, 8, PAIR), axis=0)

    def body(back, carry):
        step = steps - 1 - back
        at = pl.multiple_of(step * ROWS, 32)
        query = qkv_ref[0, pl.ds(at, ROWS), :]
        key = keys[pl.ds(at, WIN), :]
        value = values[pl.ds(at, WIN), :]
        start = start_ref[pl.ds(at, ROWS), :]
        near_mask, far_mask, carried, row, floor, first = masks(step, start)
        far_two = two(far_mask)
        grad_f = jnp.where(row < count_valid, grad_ref[pl.ds(at, ROWS), :].astype(F32), 0.0)
        grad = grad_f.astype(BF16)
        query_f = query.astype(F32)
        key_f = key.astype(F32)
        lift_qf, bend_qf = lift(query_f), jnp.tanh(query_f)
        lift_kf, bend_kf = lift(key_f), jnp.tanh(key_f)
        lift_q, bend_q = lift_qf.astype(BF16), bend_qf.astype(BF16)
        lift_k, bend_k = lift_kf.astype(BF16), bend_kf.astype(BF16)
        lift_heads, bend_heads = split_heads(lift_k), split_heads(bend_k)
        r0 = b0 * invl_ref[pl.ds(at, ROWS), :]
        r1 = b1 * invd_ref[pl.ds(at, ROWS), :]
        r2 = b2 / (row - start + 1).astype(F32)
        key_heads = split_heads(key)
        before = states_ref[0, pl.ds(pl.multiple_of(step * PAIR, PAIR), PAIR), :]
        near_product = grad_f * near_ref[pl.ds(at, ROWS), :]
        far1_product = grad_f * far1_ref[pl.ds(at, ROWS), :]
        grad_pair = mm(grad, split_heads(value), NT)
        scores = near_scores(query, key_heads)
        pair_weight = mm(lift_q, lift_heads, NT)
        pair_bend = mm(bend_q, bend_heads, NT)
        state_bend = mm(grad, before[:, 2 * PAIR :], NT)
        spread_far = spread(far1_product)
        spread_near = spread(near_product)
        along = jnp.where(lanes, spread_far[:, :WIN], spread_far[:, WIN:])
        scaled_along = (along * (-1.0 / HEAD_DIM)).astype(BF16)
        state_lift = mm(jnp.concatenate([grad, scaled_along], axis=1), before[:, : 2 * PAIR], NT)
        after = adjoint[...]
        parts = key_side(after.astype(BF16), lift_k[:ROWS], bend_k[:ROWS], value[:ROWS])
        rows_q = (query_f * (r0 * HEAD_DIM**-0.5)).astype(BF16)
        rows_a = lift_qf * r1
        rows_t = bend_qf * r2
        from_lift = mm(
            jnp.where(carried, rows_a, 0.0).astype(BF16),
            jnp.concatenate([grad, along.astype(BF16)], axis=1),
            TN,
        )
        from_bend = mm(jnp.where(carried, rows_t, 0.0).astype(BF16), grad, TN)
        closing = scalars[step]
        keep = (closing < floor).astype(F32)
        adjoint[...] = keep * after + block_only(jnp.concatenate([from_lift, from_bend], axis=1))
        add_up(0, near_product)
        add_up(8, far1_product)
        add_up(16, grad_f * far2_ref[pl.ds(at, ROWS), :])
        shifted = jnp.where(far_two, grad_pair - spread_far, 0.0).astype(BF16)
        plain = jnp.where(far_two, grad_pair, 0.0).astype(BF16)
        pair_weight = jnp.where(far_two, pair_weight, 0.0).astype(BF16)
        pair_bend = jnp.where(far_two, pair_bend, 0.0).astype(BF16)
        weights, shifted_near = near_back(scores, grad_pair, near_mask, spread_near)
        d_query = mm(shifted_near, key_heads) * (r0 * HEAD_DIM**-0.5)
        d_query = (
            d_query
            + (mm(shifted, lift_heads) + jnp.where(carried, state_lift, 0.0))
            * (r1 * jnp.minimum(lift_qf, 1.0))
            + (mm(plain, bend_heads) + jnp.where(carried, state_bend, 0.0))
            * (r2 * (1.0 - bend_qf * bend_qf))
        )
        out_ref[0, pl.ds(at, ROWS), :] = d_query.astype(BF16)
        d_key = fold(mm(shifted_near, rows_q, TN))
        d_lift = fold(mm(shifted, rows_a.astype(BF16), TN))
        d_bend = fold(mm(plain, rows_t.astype(BF16), TN))
        d_value = fold(
            mm(
                jnp.concatenate([weights, pair_weight, pair_bend], axis=0),
                jnp.concatenate([grad_f * r0, grad_f * r1, grad_f * r2], axis=0).astype(BF16),
                TN,
            )
        )
        live = iota((ROWS, PAIR), 0) + first >= jnp.maximum(closing, floor)
        pad = jnp.zeros((TAIL, PAIR), F32)
        d_lift = d_lift + jnp.concatenate([jnp.where(live, parts[0], 0.0), pad], axis=0)
        d_bend = d_bend + jnp.concatenate([jnp.where(live, parts[1], 0.0), pad], axis=0)
        d_value = d_value + jnp.concatenate([jnp.where(live, parts[2], 0.0), pad], axis=0)
        d_key = d_key + d_lift * jnp.minimum(lift_kf, 1.0) + d_bend * (1.0 - bend_kf * bend_kf)
        out_ref[1, pl.ds(at, ROWS), :] = jnp.concatenate(
            [d_key[TAIL:ROWS], d_key[ROWS:] + key_carry[...]], axis=0
        ).astype(BF16)
        out_ref[2, pl.ds(at, ROWS), :] = jnp.concatenate(
            [d_value[TAIL:ROWS], d_value[ROWS:] + value_carry[...]], axis=0
        ).astype(BF16)
        key_carry[...] = d_key[:TAIL]
        value_carry[...] = d_value[:TAIL]
        return carry

    lax.fori_loop(0, steps, body, 0, unroll=4)


def feed_kernel(
    scalars,
    mixed_ref,
    tokens_ref,
    cotangent_ref,
    out_weight_ref,
    gain_ref,
    own_ref,
    other_ref,
    layer_ref,
    d_hidden_ref,
    d_branch_ref,
    d_mixed_ref,
    normed_ref,
    active_ref,
    d_inner_ref,
    sums_ref,
):
    c0 = math.sqrt(2.0 / math.pi)
    hidden = tokens_ref[...].astype(F32) + mm(mixed_ref[...], out_weight_ref[...], NT)
    normal, scale = norm_parts(hidden)
    normed = (normal * gain_ref[...]).astype(BF16)
    normed_ref[...] = normed
    cotangent = cotangent_ref[...]
    half, width = own_ref.shape[1:]
    chunk = min(512, half)
    layer = hidden
    d_normed = jnp.zeros(hidden.shape, F32)
    for place, ref in enumerate((own_ref, other_ref)):
        for first in range(0, half, chunk):
            into = ref[0, pl.ds(first, chunk), :]
            down = ref[1, pl.ds(first, chunk), :]
            inner = mm(normed, into, NT)
            d_active = mm(cotangent, down, NT)
            square = inner * inner
            bent = jnp.tanh(inner * (c0 + (c0 * 0.044715) * square))
            gate = 0.5 + 0.5 * bent
            active = (inner * gate).astype(BF16)
            slope = gate + inner * (0.5 - 0.5 * bent * bent) * (
                c0 + (3.0 * 0.044715 * c0) * square
            )
            d_inner = (d_active * slope).astype(BF16)
            at = pl.ds(place * half + first, chunk)
            active_ref[:, at] = active
            d_inner_ref[:, at] = d_inner
            layer = layer + mm(active, down)
            d_normed = d_normed + mm(d_inner, into)
    layer_ref[...] = layer.astype(BF16)
    d_part, gain_rows = norm_back(d_normed, gain_ref[...], normal, scale)
    d_hidden = cotangent.astype(F32) + d_part
    d_hidden_ref[...] = d_hidden
    d_branch = d_hidden.astype(BF16)
    d_branch_ref[...] = d_branch
    d_mixed_ref[...] = mm(d_branch, out_weight_ref[...]).astype(BF16)

    @pl.when(pl.program_id(0) == 0)
    def _():
        sums_ref[...] = jnp.zeros(sums_ref.shape, F32)

    sums_ref[...] += gain_rows


def feed_grad_kernel(
    scalars, normed_ref, cotangent_ref, active_ref, d_inner_ref, *refs
):
    refs[-1][0] = mm(d_inner_ref[...], normed_ref[...], TN).astype(refs[-1].dtype)
    refs[-1][1] = mm(active_ref[...], cotangent_ref[...], TN).astype(refs[-1].dtype)
    if len(refs) > 1:
        mixed_ref, d_branch_ref, out_grad_ref, _ = refs

        @pl.when(pl.program_id(0) == 0)
        def _():
            out_grad_ref[...] = mm(d_branch_ref[...], mixed_ref[...], TN)


def input_kernel(
    scalars, d_qkv_ref, weight_ref, tokens_ref, d_hidden_ref, gain_ref, input_grad_ref
):
    d_normed = mm(d_qkv_ref[0], weight_ref[0], NT)
    for c in range(1, 3):
        d_normed = d_normed + mm(d_qkv_ref[c], weight_ref[c], NT)
    normal, scale = norm_parts(tokens_ref[...].astype(F32))
    d_part, _ = norm_back(d_normed, gain_ref[...], normal, scale)
    input_grad_ref[...] = d_hidden_ref[...] + d_part


def resume(kernel, done, scalars, qkv_ref, message_ref, start_ref, blend_ref, *refs):
    kernel(scalars, qkv_ref, message_ref, start_ref, blend_ref, *refs[done:])


def pair_specs(rows, first=0):
    return {
        "qkv": pl.BlockSpec((3, rows, PAIR), lambda p, s: (0, 0, p + first)),
        "message": pl.BlockSpec((1, HEAD_DIM + TAIL, 3 * PAIR), lambda p, s: (p + first, 0, 0)),
        "start": pl.BlockSpec((rows, PAIR), lambda p, s: (0, 0)),
        "blend": pl.BlockSpec((3, PAIR), lambda p, s: (0, p + first)),
        "column": pl.BlockSpec((rows, PAIR), lambda p, s: (0, p + first)),
        "states": pl.BlockSpec((1, rows // ROWS * PAIR, 3 * PAIR), lambda p, s: (p + first, 0, 0)),
        "sums": pl.BlockSpec((24, PAIR), lambda p, s: (0, p)),
        "query": pl.BlockSpec((1, rows, PAIR), lambda p, s: (0, 0, p)),
        "head_rows": pl.BlockSpec((ROWS, PAIR), lambda p, s: (0, p)),
    }


def call(kernel, ins, outs, out_shapes, scratch, grid, name, flops, moved, aliases={}):
    return pl.pallas_call(
        kernel,
        out_shape=out_shapes,
        grid_spec=pltpu.PrefetchScalarGridSpec(
            num_scalar_prefetch=1,
            grid=(grid,),
            in_specs=ins,
            out_specs=outs,
            scratch_shapes=scratch,
        ),
        input_output_aliases=aliases,
        compiler_params=pltpu.CompilerParams(
            dimension_semantics=("arbitrary",), vmem_limit_bytes=56 * 1024 * 1024
        ),
        cost_estimate=pl.CostEstimate(flops=flops, bytes_accessed=moved, transcendentals=0),
        name=name,
    )


def norm_parts(source):
    centered = source - jnp.mean(source, axis=-1, keepdims=True)
    spread_of = jnp.mean(centered * centered, axis=-1, keepdims=True)
    scale = lax.rsqrt(spread_of + EPS)
    return centered * scale, scale


def norm_back(d_out, gain, normal, scale):
    e = d_out * gain
    inner = jnp.mean(e, axis=-1, keepdims=True)
    along = jnp.mean(e * normal, axis=-1, keepdims=True)
    rows = jnp.sum((d_out * normal).reshape(-1, 8, d_out.shape[1]), axis=0)
    return scale * (e - inner - normal * along), rows


def bits(size):
    return [1 << b for b in range(int(math.log2(size)))]


def phases():
    dp = bits(lax.axis_size("dp"))
    core, rest = dp[:1], dp[1:]
    mid = len(rest) // 2
    far = [("dp", m) for m in rest[mid:]]
    near = [("dp", m) for m in rest[:mid]] + [("head", m) for m in bits(lax.axis_size("head"))]
    groups = []
    for run in (far, near, [("dp", m) for m in core]):
        groups += [run[i : i + 2] for i in range(0, len(run), 2)]
    return groups


def relative_bits():
    return [pair for group in phases() for pair in group]


def all_flips():
    order = relative_bits()
    flips = []
    for index in range(1 << len(order)):
        chosen = [pair for place, pair in enumerate(order) if index >> place & 1]
        flips.append(tuple(sum(m for a, m in chosen if a == axis) for axis in ("dp", "head")))
    return flips


def peer(array, group, combo):
    n_dp, n_head = lax.axis_size("dp"), lax.axis_size("head")
    chosen = [pair for place, pair in enumerate(group) if combo >> place & 1]
    flip_dp = sum(m for axis, m in chosen if axis == "dp")
    flip_head = sum(m for axis, m in chosen if axis == "head")
    pairs = [
        (d * n_head + h, (d ^ flip_dp) * n_head + (h ^ flip_head))
        for d in range(n_dp)
        for h in range(n_head)
    ]
    return lax.ppermute(array, ("dp", "head"), pairs)


def widen(block, group, axis, after=None):
    others = [peer(block, group, combo) for combo in range(1, 1 << len(group))]
    if after is not None:
        others, after = lax.optimization_barrier((others, after))
    whole = jnp.concatenate([block] + others, axis=axis)
    return whole if after is None else (whole, after)


def narrow(keep, gives, group, after=None):
    arrived = [peer(give.astype(BF16), group, combo) for combo, give in enumerate(gives, 1)]
    if after is not None:
        arrived, _ = lax.optimization_barrier((arrived, after))
    return keep.astype(F32) + sum(part.astype(F32) for part in arrived)


def narrow_axis(total, group, axis, after=None):
    parts = jnp.split(total, 1 << len(group), axis=axis)
    return narrow(parts[0], parts[1:], group, after)


def pass_along(local, keep, shift):
    size = lax.axis_size("head")
    pairs = [(i, i + shift) for i in range(size) if 0 <= i + shift < size]
    arrived = lax.ppermute(local, "head", pairs)
    for _ in range(size - 2):
        rows = iota(local.shape, 1) < HEAD_DIM
        total = local.astype(F32) + jnp.where(rows, keep * arrived.astype(F32), 0.0)
        arrived = lax.ppermute(total.astype(BF16), "head", pairs)
    return arrived


def per_device(
    tokens,
    ln1_gain,
    qkv_weight,
    out_weight,
    blend,
    ln2_gain,
    in_weight,
    down_weight,
    cotangent,
    lengths,
):
    rows, width = tokens.shape
    n_dp, n_head = lax.axis_size("dp"), lax.axis_size("head")
    pairs = width // PAIR
    steps = rows // ROWS
    groups = phases()
    flips = all_flips()

    shards = jnp.concatenate([qkv_weight, out_weight.T[None]], axis=0)[None]
    feed = jnp.stack([in_weight, down_weight])
    shards = widen(shards, groups[0], 0)
    feed, _ = lax.optimization_barrier((feed, shards))
    feed = widen(feed, groups[0][:1], 1)
    for group in groups[1:-1]:
        shards = widen(shards, group, 0)
    shards, feed = lax.optimization_barrier((shards, feed))
    others = peer(shards, groups[-1], 1)

    item_lengths = lengths[0]
    slots = item_lengths.shape[0]
    ends = jnp.sum(
        jnp.where(iota((slots, slots), 1) <= iota((slots, slots), 0), item_lengths[None, :], 0),
        axis=1,
    )
    offset = lax.axis_index("head") * rows
    local = jnp.arange(rows, dtype=jnp.int32)
    place = local + offset
    total = ends[slots - 1]
    item_start = jnp.max(
        jnp.where(ends[None, :] <= place[:, None], ends[None, :], 0), axis=1
    )
    start = jnp.where(place < total, item_start - offset, local)
    carried_rows = jnp.sum((start < 0).astype(jnp.int32))
    scalars = jnp.concatenate(
        [
            start.reshape(steps, ROWS)[:, ROWS - TAIL - 1],
            carried_rows[None],
            start[rows - 1 :],
            (total - offset)[None],
            lax.axis_index("dp").astype(jnp.int32)[None],
            lax.axis_index("head").astype(jnp.int32)[None],
        ]
    )
    start_wide = jnp.broadcast_to(start[:, None], (rows, PAIR))
    keep_all = (start[rows - 1] < 0).astype(F32)
    blend_wide = jnp.repeat(blend, HEAD_DIM, axis=1)

    spec = pair_specs(rows)
    wide = jax.ShapeDtypeStruct((rows, width), F32)
    states_shape = jax.ShapeDtypeStruct((pairs, steps * PAIR, 3 * PAIR), BF16)
    message_shape = jax.ShapeDtypeStruct((pairs, HEAD_DIM + TAIL, 3 * PAIR), BF16)
    big = rows * width
    part = rows // 3

    def whole_spec(shape):
        return pl.BlockSpec(shape, lambda p, s: (0,) * len(shape))

    qkv, normed_one, qkv_all, out_all, closing = call(
        functools.partial(project_kernel, flips=flips),
        [
            pl.BlockSpec((part, width), lambda p, s: (p, 0)),
            whole_spec((1, width)),
            whole_spec(shards.shape),
            whole_spec(shards.shape),
        ],
        [
            pl.BlockSpec((3, part, width), lambda p, s: (0, p, 0)),
            pl.BlockSpec((part, width), lambda p, s: (p, 0)),
            whole_spec((3, width, width)),
            whole_spec((width, width)),
            whole_spec(message_shape.shape),
        ],
        [
            jax.ShapeDtypeStruct((3, rows, width), BF16),
            jax.ShapeDtypeStruct((rows, width), BF16),
            jax.ShapeDtypeStruct((3, width, width), BF16),
            jax.ShapeDtypeStruct((width, width), BF16),
            message_shape,
        ],
        [
            pltpu.VMEM((pairs, PAIR, 3 * PAIR), F32),
            pltpu.VMEM((n_head, 4, n_dp, width // n_dp, width // n_head), BF16),
        ],
        3,
        "project",
        6 * big * width,
        12 * big,
    )(scalars, tokens, ln1_gain[None], shards, others)
    for pair in groups[0][1:]:
        feed, _ = widen(feed, [pair], 1, closing)
    message = pass_along(closing, keep_all, 1)

    key_scratch = pltpu.VMEM((rows + TAIL, PAIR), BF16)
    state_scratch = pltpu.VMEM((PAIR, 3 * PAIR), F32)
    tail_scratch = pltpu.VMEM((TAIL, PAIR), F32)
    results = ()
    count = pairs // 2
    for first in (0, count):
        spec = pair_specs(rows, first)
        results = call(
            functools.partial(resume, forward_kernel, len(results)),
            [spec["qkv"], spec["message"], spec["start"], spec["blend"]]
            + [pl.BlockSpec(memory_space=pl.ANY)] * len(results),
            [spec["column"]] * 6 + [spec["states"]],
            [jax.ShapeDtypeStruct((rows, width), BF16)] + [wide] * 5 + [states_shape],
            [key_scratch, key_scratch, state_scratch],
            count,
            "forward",
            4000 * big,
            20 * big,
            {5 + i: i for i in range(len(results))},
        )(scalars, qkv, message, start_wide, blend_wide, *results)
        if not first:
            feed, results = widen(feed, groups[1], 1, results)
            feed, message = lax.optimization_barrier((feed, message))
    for group in groups[2:-1]:
        feed = widen(feed, group, 1)
    feed_other = peer(feed, groups[-1], 1)
    mixed, near, far1, far2, inv_l, inv_d, states = results

    spec = pair_specs(rows)
    low = jax.ShapeDtypeStruct((rows, width), BF16)
    row_spec = pl.BlockSpec((part, width), lambda p, s: (p, 0))
    hidden_units = 2 * feed.shape[1]
    unit_spec = pl.BlockSpec((part, hidden_units), lambda p, s: (p, 0))
    unit_shape = jax.ShapeDtypeStruct((rows, hidden_units), BF16)
    sums_shape = jax.ShapeDtypeStruct((8, width), F32)
    layer_out, d_hidden, d_branch, d_mixed, normed_two, active, d_inner, gain_two_rows = call(
        feed_kernel,
        [row_spec] * 3
        + [
            whole_spec((width, width)),
            whole_spec((1, width)),
            whole_spec(feed.shape),
            whole_spec(feed.shape),
        ],
        [row_spec] * 5 + [unit_spec] * 2 + [whole_spec((8, width))],
        [low, wide, low, low, low, unit_shape, unit_shape, sums_shape],
        [],
        3,
        "feed",
        8 * big * hidden_units,
        32 * big,
    )(scalars, mixed, tokens, cotangent, out_all, ln2_gain[None], feed, feed_other)

    back = call(
        prologue_kernel,
        [
            spec["query"],
            pl.BlockSpec((1, ROWS, PAIR), lambda p, s: (1, 0, p)),
            pl.BlockSpec((1, ROWS, PAIR), lambda p, s: (2, 0, p)),
            spec["message"],
            spec["start"],
            spec["blend"],
            spec["column"],
            spec["head_rows"],
            spec["column"],
            spec["head_rows"],
            spec["column"],
        ],
        spec["message"],
        message_shape,
        [state_scratch],
        pairs,
        "prologue",
        500 * big,
        20 * big,
    )(scalars, qkv, qkv, qkv, message, start_wide, blend_wide, d_mixed, near, far1, inv_l, inv_d)
    d_inner, _ = lax.optimization_barrier((d_inner, back))
    back_in = pass_along(back, keep_all, -1)

    unit = hidden_units // 4
    half_shape = (2, 2 * unit, width)
    whole_rows = whole_spec((rows, width))

    def feed_grad(place, kind, d_inner, more_ins, more_in_specs, more_outs, more_out_specs):
        columns = pl.BlockSpec((rows, unit), lambda p, s: (0, p + 2 * place))
        return call(
            feed_grad_kernel,
            [whole_rows] * 2 + [columns] * 2 + more_in_specs,
            more_out_specs + [pl.BlockSpec((2, unit, width), lambda p, s: (0, p, 0))],
            more_outs + [jax.ShapeDtypeStruct(half_shape, kind)],
            [],
            2,
            "feed_grad",
            2 * big * hidden_units,
            12 * big,
        )(scalars, normed_two, cotangent, active, d_inner, *more_ins)

    out_grad, keep = feed_grad(
        0,
        F32,
        d_inner,
        [mixed, d_branch],
        [whole_rows] * 2,
        [jax.ShapeDtypeStruct((width, width), F32)],
        [whole_spec((width, width))],
    )
    d_inner, back_in, out_grad = lax.optimization_barrier((d_inner, back_in, out_grad))
    (give,) = feed_grad(1, BF16, d_inner, [], [], [], [])
    feed_share = narrow(keep, [give], groups[-1])
    left = list(reversed(groups[:-1]))

    d_qkv = jnp.zeros((3, 8, PAIR), BF16)
    sums = []
    first = 0
    for count in (pairs // 4, pairs // 2, pairs // 4):
        spec = pair_specs(rows, first)
        more = {13: 0} if first else {}
        d_qkv, part_sums = call(
            backward_kernel,
            [spec["qkv"], spec["message"], spec["start"], spec["blend"]]
            + [spec["column"]] * 6
            + [spec["states"], spec["message"], pl.BlockSpec(memory_space=pl.ANY)],
            [spec["qkv"], spec["sums"]],
            [
                jax.ShapeDtypeStruct((3, rows, width), BF16),
                jax.ShapeDtypeStruct((24, count * PAIR), F32),
            ],
            [key_scratch, key_scratch, state_scratch, tail_scratch, tail_scratch],
            count,
            "backward",
            16000 * big * count // pairs,
            40 * big * count // pairs,
            more,
        )(
            scalars,
            qkv,
            message,
            start_wide,
            blend_wide,
            d_mixed,
            near,
            far1,
            far2,
            inv_l,
            inv_d,
            states,
            back_in,
            d_qkv,
        )
        sums.append(part_sums)
        first += count
        if left and first < pairs:
            _, back_in = lax.optimization_barrier((feed_share, back_in))
            feed_share = narrow_axis(feed_share, left.pop(0), 1)
    for group in left:
        feed_share = narrow_axis(feed_share, group, 1)
    feed_share, d_qkv = lax.optimization_barrier((feed_share, d_qkv))
    sums = jnp.concatenate(sums, axis=1)
    blend_part = jnp.sum(sums.reshape(3, 8, blend.shape[1], HEAD_DIM), axis=(1, 3))

    shard_shape = (n_dp * n_head // 2, 4, width // n_dp, width // n_head)
    shard_spec = pl.BlockSpec((shard_shape[0], 1) + shard_shape[2:], lambda p, s: (0, p, 0, 0))
    keep, give, gain_one_rows = call(
        functools.partial(weight_grad_kernel, flips=flips),
        [
            whole_spec((rows, width)),
            pl.BlockSpec((1, rows, width), lambda p, s: (jnp.minimum(p, 2), 0, 0)),
            whole_spec((width, width)),
            pl.BlockSpec((1, width, width), lambda p, s: (jnp.minimum(p, 2), 0, 0)),
        ],
        [shard_spec, shard_spec, whole_spec((8, width))],
        [
            jax.ShapeDtypeStruct(shard_shape, F32),
            jax.ShapeDtypeStruct(shard_shape, BF16),
            sums_shape,
        ],
        [pltpu.VMEM((n_head, n_dp, width // n_dp, width // n_head), F32)],
        4,
        "weight_grad",
        6 * big * width,
        8 * big,
    )(scalars, normed_one, d_qkv, out_grad, qkv_all)
    parts = [gain_one_rows[0] / ln1_gain, jnp.sum(gain_two_rows, axis=0), blend_part.reshape(-1)]
    total_sums = jnp.concatenate(parts)[None]
    share = narrow(keep, [give], groups[-1])
    hops = list(reversed(relative_bits()))
    total_sums = total_sums + peer(total_sums, [hops[0]], 1)
    total_sums, d_qkv, _ = lax.optimization_barrier((total_sums, d_qkv, share))
    total_sums = total_sums + peer(total_sums, [hops[1]], 1)
    input_grad = call(
        input_kernel,
        [
            pl.BlockSpec((3, part, width), lambda p, s: (0, p, 0)),
            whole_spec((3, width, width)),
            row_spec,
            row_spec,
            whole_spec((1, width)),
        ],
        row_spec,
        wide,
        [],
        3,
        "input",
        6 * big * width,
        24 * big,
    )(scalars, d_qkv, qkv_all, tokens, d_hidden, ln1_gain[None])
    share = narrow_axis(share, groups[-2], 0, input_grad)
    total_sums, _ = lax.optimization_barrier((total_sums, input_grad))
    total_sums = total_sums + peer(total_sums, [hops[2]], 1)
    for group in reversed(groups[:-2]):
        parts = jnp.split(share, 1 << len(group), axis=0)
        gives = [part.astype(BF16) for part in parts[1:]]
        total_sums, _ = lax.optimization_barrier((total_sums, gives))
        share = narrow(parts[0], gives, group)
    for pair in hops[3:]:
        total_sums = total_sums + peer(total_sums, [pair], 1)
    total_sums = total_sums[0]
    gain_one, gain_two = total_sums[:width], total_sums[width : 2 * width]
    blend_sum = total_sums[2 * width :].reshape(blend.shape)
    qkv_share, out_share = share[0, :3], share[0, 3].T
    in_share, down_share = feed_share[0], feed_share[1]
    return (
        layer_out,
        input_grad,
        gain_one,
        qkv_share,
        out_share,
        blend_sum,
        gain_two,
        in_share,
        down_share,
    )


def solution(mesh):
    return jax.shard_map(
        per_device,
        mesh=mesh,
        in_specs=(
            P(("dp", "head"), None),
            P(),
            P(None, "dp", "head"),
            P("head", "dp"),
            P(),
            P(),
            P(("dp", "head"), None),
            P(("dp", "head"), None),
            P(("dp", "head"), None),
            P("dp", None),
        ),
        out_specs=(
            P(("dp", "head"), None),
            P(("dp", "head"), None),
            P(),
            P(None, "dp", "head"),
            P("head", "dp"),
            P(),
            P(),
            P(("dp", "head"), None),
            P(("dp", "head"), None),
        ),
        check_vma=False,
    )
```

```python
import functools
import math

import jax
import jax.numpy as jnp
from jax import lax
from jax.experimental import pallas as pl
from jax.experimental.pallas import tpu as pltpu
from jax.sharding import PartitionSpec as P

HEAD_DIM = 64
BAND = 30
ROWS = 96
TAIL = 32
WIN = ROWS + TAIL
PAIR = 2 * HEAD_DIM
EPS = 1e-05
NEG = -1e30
CARRIED, LAST, VALID, ROW_AT, COLUMN_AT = range(-5, 0)
F32 = jnp.float32
BF16 = jnp.bfloat16
NT = (((1,), (1,)), ((), ()))
TN = (((0,), (0,)), ((), ()))
NN = (((1,), (0,)), ((), ()))


def mm(left, right, dims=NN):
    return lax.dot_general(left, right, dims, preferred_element_type=F32)


def iota(shape, axis):
    return lax.broadcasted_iota(jnp.int32, shape, axis)


def lift(values):
    return jnp.where(values > 0, values + 1.0, jnp.exp(jnp.minimum(values, 0.0)))


def head_lanes(dtype):
    first = (iota((1, PAIR), 1) < HEAD_DIM).astype(F32)
    return first.astype(dtype), (1.0 - first).astype(dtype)


def split_heads(block):
    first, second = head_lanes(block.dtype)
    return jnp.concatenate([block * first, block * second], axis=0)


def same_head():
    return (iota((PAIR, PAIR), 0) < HEAD_DIM) == (iota((PAIR, PAIR), 1) < HEAD_DIM)


def block_only(wide):
    keep = same_head()
    parts = [
        jnp.where(keep, wide[:, p * PAIR : (p + 1) * PAIR], 0.0)
        for p in range(wide.shape[1] // PAIR)
    ]
    return jnp.concatenate(parts, axis=1)


def fold(tall):
    half = tall.shape[0] // 2
    lanes = iota((half, PAIR), 1) < HEAD_DIM
    return jnp.where(lanes, tall[:half], tall[half:])


def two(half):
    return jnp.concatenate([half, half], axis=1)


def masks(step, start):
    row = iota((ROWS, WIN), 0) + step * ROWS
    first = step * ROWS - TAIL
    key = iota((ROWS, WIN), 1) + first
    floor = jnp.maximum(first, 0)
    causal = key <= row
    near = causal & (key >= jnp.maximum(start, row - (BAND - 1)))
    far = causal & (key >= jnp.maximum(start, floor))
    return near, far, start < floor, row, floor, first


def near_scores(query, key_heads):
    return mm(query * jnp.asarray(HEAD_DIM**-0.5, BF16), key_heads, NT)


def near_weights(scores, near):
    parts = []
    for h in range(2):
        part = jnp.where(near, scores[:, h * WIN : (h + 1) * WIN], NEG)
        parts.append(jnp.exp(part - jnp.max(part, axis=1, keepdims=True)))
    return jnp.concatenate(parts, axis=1)


def spread(product):
    first = iota(product.shape, 1) < HEAD_DIM
    sums = [
        jnp.sum(jnp.where(keep, product, 0.0), axis=1, keepdims=True) for keep in (first, ~first)
    ]
    return jnp.concatenate([jnp.broadcast_to(part, (ROWS, WIN)) for part in sums], axis=1)


def load_keys(qkv_ref, message_ref, keys, values):
    rows = qkv_ref.shape[1]
    keys[pl.ds(0, TAIL), :] = message_ref[0, pl.ds(HEAD_DIM, TAIL), :PAIR]
    keys[pl.ds(TAIL, rows), :] = qkv_ref[1]
    values[pl.ds(0, TAIL), :] = message_ref[0, pl.ds(HEAD_DIM, TAIL), PAIR : 2 * PAIR]
    values[pl.ds(TAIL, rows), :] = qkv_ref[2]


def fold_state(wide):
    kept = block_only(wide)
    return (kept[:HEAD_DIM] + kept[HEAD_DIM:]).astype(BF16)


def unfold_state(message):
    half = message[:HEAD_DIM].astype(F32)
    return block_only(jnp.concatenate([half, half], axis=0))


def project_kernel(
    scalars,
    tokens_ref,
    gain_ref,
    own_ref,
    other_ref,
    qkv_ref,
    normed_ref,
    weight_ref,
    out_weight_ref,
    message_ref,
    state,
    placed,
    *,
    flips,
):
    step = pl.program_id(0)
    rows, width = tokens_ref.shape
    pairs = width // PAIR
    half, _, tall, wide = own_ref.shape
    last = jnp.maximum(scalars[scalars.shape[0] + LAST], 0)

    @pl.when(step == 0)
    def _():
        for index, (flip_row, flip_column) in enumerate(flips):
            row = scalars[scalars.shape[0] + ROW_AT] ^ flip_row
            column = scalars[scalars.shape[0] + COLUMN_AT] ^ flip_column
            piece = own_ref[index] if index < half else other_ref[index - half]
            for c in range(4):
                placed[column, c, row] = piece[c]
        for h in range(width // wide):
            at = pl.ds(h * wide, wide)
            weight_ref[:, :, at] = placed[h, :3].reshape(3, width, wide)
            out_weight_ref[:, at] = placed[h, 3].reshape(width, wide)
        state[...] = jnp.zeros(state.shape, F32)

    normed = (norm_parts(tokens_ref[...].astype(F32))[0] * gain_ref[...]).astype(BF16)
    normed_ref[...] = normed
    for c in (1, 2, 0):
        qkv_ref[c] = mm(normed, weight_ref[c]).astype(BF16)
    live = iota((rows, PAIR), 0) + step * rows >= last
    ones = jnp.ones((rows, PAIR), BF16)
    for p in range(pairs):
        at = pl.ds(p * PAIR, PAIR)
        key = qkv_ref[1, :, at].astype(F32)
        value = qkv_ref[2, :, at]
        lifted = jnp.where(live, lift(key), 0.0).astype(BF16)
        bent = jnp.where(live, jnp.tanh(key), 0.0).astype(BF16)
        state[p, :, : 2 * PAIR] += mm(lifted, jnp.concatenate([value, ones], axis=1), TN)
        state[p, :, 2 * PAIR :] += mm(bent, value, TN)

    @pl.when(step == pl.num_programs(0) - 1)
    def _():
        for p in range(pairs):
            at = pl.ds(p * PAIR, PAIR)
            message_ref[p, pl.ds(0, HEAD_DIM), :] = fold_state(state[p])
            message_ref[p, pl.ds(HEAD_DIM, TAIL), :] = jnp.concatenate(
                [
                    qkv_ref[1, pl.ds(rows - TAIL, TAIL), at],
                    qkv_ref[2, pl.ds(rows - TAIL, TAIL), at],
                    jnp.zeros((TAIL, PAIR), BF16),
                ],
                axis=1,
            )


def weight_grad_kernel(
    scalars,
    normed_ref,
    d_qkv_ref,
    out_grad_ref,
    weight_ref,
    keep_ref,
    give_ref,
    gain_ref,
    whole,
    *,
    flips,
):
    c = pl.program_id(0)
    half, _, tall, wide = keep_ref.shape

    def place(total):
        for h in range(total.shape[1] // wide):
            part = total[:, h * wide : (h + 1) * wide]
            whole[h] = part.reshape(whole.shape[1:])

    @pl.when(c == 0)
    def _():
        gain_ref[...] = jnp.zeros(gain_ref.shape, F32)

    @pl.when(c < 3)
    def _():
        total = mm(normed_ref[...], d_qkv_ref[0], TN)
        place(total)
        product = total * weight_ref[0].astype(F32)
        high = product.astype(BF16)
        low = (product - high.astype(F32)).astype(BF16)
        ones = jnp.ones((8, product.shape[1]), BF16)
        gain_ref[...] += mm(ones, high, NT) + mm(ones, low, NT)

    @pl.when(c == 3)
    def _():
        place(out_grad_ref[...])

    for index, (flip_row, flip_column) in enumerate(flips):
        row = scalars[scalars.shape[0] + ROW_AT] ^ flip_row
        column = scalars[scalars.shape[0] + COLUMN_AT] ^ flip_column
        if index < half:
            keep_ref[index, 0] = whole[column, row]
        else:
            give_ref[index - half, 0] = whole[column, row].astype(BF16)


def forward_kernel(
    scalars,
    qkv_ref,
    message_ref,
    start_ref,
    blend_ref,
    att_ref,
    near_ref,
    far1_ref,
    far2_ref,
    invl_ref,
    invd_ref,
    states_ref,
    keys,
    values,
    state,
):
    rows = qkv_ref.shape[1]
    load_keys(qkv_ref, message_ref, keys, values)
    state[...] = unfold_state(message_ref[0])
    count_valid = scalars[scalars.shape[0] + VALID]
    b0, b1, b2 = (blend_ref[pl.ds(f, 1), :] for f in range(3))

    def begin(step):
        at = pl.multiple_of(step * ROWS, 32)
        query = qkv_ref[0, pl.ds(at, ROWS), :]
        key = keys[pl.ds(at, WIN), :]
        value = values[pl.ds(at, WIN), :]
        start = start_ref[pl.ds(at, ROWS), :]
        near_mask, far_mask, carried, row, floor, first = masks(step, start)
        query_f = query.astype(F32)
        key_f = key.astype(F32)
        lift_q = lift(query_f).astype(BF16)
        bend_q = jnp.tanh(query_f).astype(BF16)
        lift_k = lift(key_f)
        bend_k = jnp.tanh(key_f)
        ones = jnp.ones((WIN, PAIR), BF16)
        value_heads = jnp.concatenate([split_heads(value), split_heads(ones)], axis=1)
        before = state[...]
        before_low = before.astype(BF16)
        scores = near_scores(query, split_heads(key))
        pair_weight = mm(lift_q, split_heads(lift_k.astype(BF16)), NT)
        pair_bend = mm(bend_q, split_heads(bend_k.astype(BF16)), NT)
        elu_state = mm(lift_q, before_low[:, : 2 * PAIR])
        tanh_state = mm(bend_q, before_low[:, 2 * PAIR :])
        states_ref[0, pl.ds(pl.multiple_of(step * PAIR, PAIR), PAIR), :] = before_low
        closing = scalars[step]
        live = iota((ROWS, PAIR), 0) + first >= jnp.maximum(closing, floor)
        lifted = jnp.where(live, lift_k[:ROWS], 0.0).astype(BF16)
        bent = jnp.where(live, bend_k[:ROWS], 0.0).astype(BF16)
        with_ones = jnp.concatenate([value[:ROWS], ones[:ROWS]], axis=1)
        added = jnp.concatenate([mm(lifted, with_ones, TN), mm(bent, value[:ROWS], TN)], axis=1)
        keep = (closing < floor).astype(F32)
        state[...] = keep * before + block_only(added)
        def finish():
            far_two = two(far_mask)
            low_weight = jnp.where(far_two, pair_weight, 0.0).astype(BF16)
            low_bend = jnp.where(far_two, pair_bend, 0.0).astype(BF16)
            elu_out = mm(low_weight, value_heads)
            tanh_out = mm(low_bend, value_heads[:, :PAIR]) + jnp.where(carried, tanh_state, 0.0)
            weights = near_weights(scores, near_mask).astype(BF16)
            near_out = mm(weights, value_heads)
            numerator = elu_out[:, :PAIR] + jnp.where(carried, elu_state[:, :PAIR], 0.0)
            inv_d = 1.0 / (elu_out[:, PAIR:] + jnp.where(carried, elu_state[:, PAIR:], 0.0))
            far1 = numerator * inv_d
            inv_l = 1.0 / near_out[:, PAIR:]
            near = near_out[:, :PAIR] * inv_l
            far2 = tanh_out / (row - start + 1).astype(F32)
            mixed = jnp.where(row < count_valid, b0 * near + b1 * far1 + b2 * far2, 0.0)
            att_ref[pl.ds(at, ROWS), :] = mixed.astype(BF16)
            near_ref[pl.ds(at, ROWS), :] = near
            far1_ref[pl.ds(at, ROWS), :] = far1
            far2_ref[pl.ds(at, ROWS), :] = far2
            invl_ref[pl.ds(at, ROWS), :] = inv_l
            invd_ref[pl.ds(at, ROWS), :] = inv_d

        return finish

    def body(both, carry):
        finishes = [begin(both * 2 + half) for half in range(2)]
        for finish in finishes:
            finish()
        return carry

    lax.fori_loop(0, rows // ROWS // 2, body, 0, unroll=2)


def near_back(scores, grad_pair, near_mask, spread_near):
    weights = near_weights(scores, near_mask)
    return weights.astype(BF16), (weights * (grad_pair - spread_near)).astype(BF16)


def prologue_kernel(
    scalars,
    query_ref,
    key_ref,
    value_ref,
    message_ref,
    start_ref,
    blend_ref,
    grad_ref,
    near_ref,
    far1_ref,
    invl_ref,
    invd_ref,
    back_ref,
    adjoint,
):
    rows = query_ref.shape[1]
    step_rows = rows // 3
    count_valid = scalars[scalars.shape[0] + VALID]
    b0, b1, b2 = (blend_ref[pl.ds(f, 1), :] for f in range(3))
    adjoint[...] = jnp.zeros(adjoint.shape, F32)

    tails = message_ref[0, pl.ds(HEAD_DIM, TAIL), :]
    key = jnp.concatenate([tails[:, :PAIR], key_ref[0]], axis=0)
    value = jnp.concatenate([tails[:, PAIR : 2 * PAIR], value_ref[0]], axis=0)
    start = start_ref[pl.ds(0, ROWS), :]
    near_mask, _, _, row, _, _ = masks(0, start)
    query = query_ref[0, pl.ds(0, ROWS), :]
    grad_f = jnp.where(row < count_valid, grad_ref[pl.ds(0, ROWS), :].astype(F32), 0.0)
    grad = grad_f.astype(BF16)
    scale = b0 * invl_ref[...]
    rows_q = (query.astype(F32) * (scale * HEAD_DIM**-0.5)).astype(BF16)
    rows_g = (grad_f * scale).astype(BF16)
    weights, shifted = near_back(
        near_scores(query, split_heads(key)),
        mm(grad, split_heads(value), NT),
        near_mask,
        spread(grad_f * near_ref[...]),
    )
    d_key = fold(mm(shifted, rows_q, TN))
    back_ref[0, pl.ds(HEAD_DIM, TAIL), :] = jnp.concatenate(
        [d_key[:TAIL], fold(mm(weights, rows_g, TN))[:TAIL], jnp.zeros((TAIL, PAIR), F32)], axis=1
    ).astype(BF16)
    heads = same_head().astype(F32).astype(BF16)
    heads = jnp.concatenate([heads, heads], axis=0)

    for step in range(3):
        at = step * step_rows

        @pl.when(scalars[scalars.shape[0] + CARRIED] > at)
        def _():
            here = pl.ds(at, step_rows)
            row = iota((step_rows, PAIR), 0) + at
            start = start_ref[here, :]
            grad_f = jnp.where(row < count_valid, grad_ref[here, :].astype(F32), 0.0)
            grad = grad_f.astype(BF16)
            product = grad_f * far1_ref[here, :]
            high = product.astype(BF16)
            low = (product - high.astype(F32)).astype(BF16)
            along = mm(jnp.concatenate([high, low], axis=1), heads).astype(BF16)
            query_f = query_ref[0, here, :].astype(F32)
            live = start < 0
            scaled = jnp.where(live, lift(query_f) * (b1 * invd_ref[here, :]), 0.0)
            bent = jnp.where(
                live, jnp.tanh(query_f) * (b2 / (row - start + 1).astype(F32)), 0.0
            )
            adjoint[:, : 2 * PAIR] += mm(
                scaled.astype(BF16), jnp.concatenate([grad, along], axis=1), TN
            )
            adjoint[:, 2 * PAIR :] += mm(bent.astype(BF16), grad, TN)

    back_ref[0, pl.ds(0, HEAD_DIM), :] = fold_state(adjoint[...])


def key_side(adjoint_low, lift_k, bend_k, value):
    ones = jnp.full(value.shape, -1.0 / HEAD_DIM, BF16)
    d_lift = mm(jnp.concatenate([value, ones], axis=1), adjoint_low[:, : 2 * PAIR], NT)
    d_bend = mm(value, adjoint_low[:, 2 * PAIR :], NT)
    both = jnp.concatenate([adjoint_low[:, :PAIR], adjoint_low[:, 2 * PAIR :]], axis=0)
    d_value = mm(jnp.concatenate([lift_k, bend_k], axis=1), both)
    return d_lift, d_bend, d_value


def backward_kernel(
    scalars,
    qkv_ref,
    message_ref,
    start_ref,
    blend_ref,
    grad_ref,
    near_ref,
    far1_ref,
    far2_ref,
    invl_ref,
    invd_ref,
    states_ref,
    back_ref,
    done_ref,
    out_ref,
    sums_ref,
    keys,
    values,
    adjoint,
    key_carry,
    value_carry,
):
    rows = qkv_ref.shape[1]
    steps = rows // ROWS
    load_keys(qkv_ref, message_ref, keys, values)
    count_valid = scalars[scalars.shape[0] + VALID]
    last = scalars[scalars.shape[0] + LAST]
    b0, b1, b2 = (blend_ref[pl.ds(f, 1), :] for f in range(3))
    lanes = iota((ROWS, PAIR), 1) < HEAD_DIM

    arrived = unfold_state(back_ref[0])
    tail_grads = back_ref[0, pl.ds(HEAD_DIM, TAIL), :].astype(F32)
    end_key = keys[pl.ds(rows, TAIL), :].astype(F32)
    end_lift, end_bend = lift(end_key), jnp.tanh(end_key)
    end_parts = key_side(
        arrived.astype(BF16), end_lift.astype(BF16), end_bend.astype(BF16), values[pl.ds(rows, TAIL), :]
    )
    live = iota((TAIL, PAIR), 0) + (rows - TAIL) >= last
    key_carry[...] = tail_grads[:, :PAIR] + jnp.where(
        live,
        end_parts[0] * jnp.minimum(end_lift, 1.0) + end_parts[1] * (1.0 - end_bend * end_bend),
        0.0,
    )
    value_carry[...] = tail_grads[:, PAIR : 2 * PAIR] + jnp.where(live, end_parts[2], 0.0)
    adjoint[...] = jnp.where(last < rows - TAIL, 1.0, 0.0) * arrived
    sums_ref[...] = jnp.zeros(sums_ref.shape, F32)

    def add_up(place, product):
        sums_ref[pl.ds(place, 8), :] += jnp.sum(product.reshape(ROWS // 8, 8, PAIR), axis=0)

    def begin(back):
        step = steps - 1 - back
        at = pl.multiple_of(step * ROWS, 32)
        query = qkv_ref[0, pl.ds(at, ROWS), :]
        key = keys[pl.ds(at, WIN), :]
        value = values[pl.ds(at, WIN), :]
        start = start_ref[pl.ds(at, ROWS), :]
        near_mask, far_mask, carried, row, floor, first = masks(step, start)
        far_two = two(far_mask)
        grad_f = jnp.where(row < count_valid, grad_ref[pl.ds(at, ROWS), :].astype(F32), 0.0)
        grad = grad_f.astype(BF16)
        query_f = query.astype(F32)
        key_f = key.astype(F32)
        lift_qf, bend_qf = lift(query_f), jnp.tanh(query_f)
        lift_kf, bend_kf = lift(key_f), jnp.tanh(key_f)
        lift_q, bend_q = lift_qf.astype(BF16), bend_qf.astype(BF16)
        lift_k, bend_k = lift_kf.astype(BF16), bend_kf.astype(BF16)
        lift_heads, bend_heads = split_heads(lift_k), split_heads(bend_k)
        r0 = b0 * invl_ref[pl.ds(at, ROWS), :]
        r1 = b1 * invd_ref[pl.ds(at, ROWS), :]
        r2 = b2 / (row - start + 1).astype(F32)
        key_heads = split_heads(key)
        before = states_ref[0, pl.ds(pl.multiple_of(step * PAIR, PAIR), PAIR), :]
        near_product = grad_f * near_ref[pl.ds(at, ROWS), :]
        far1_product = grad_f * far1_ref[pl.ds(at, ROWS), :]
        grad_pair = mm(grad, split_heads(value), NT)
        scores = near_scores(query, key_heads)
        pair_weight = mm(lift_q, lift_heads, NT)
        pair_bend = mm(bend_q, bend_heads, NT)
        state_bend = mm(grad, before[:, 2 * PAIR :], NT)
        spread_far = spread(far1_product)
        spread_near = spread(near_product)
        along = jnp.where(lanes, spread_far[:, :WIN], spread_far[:, WIN:])
        scaled_along = (along * (-1.0 / HEAD_DIM)).astype(BF16)
        state_lift = mm(jnp.concatenate([grad, scaled_along], axis=1), before[:, : 2 * PAIR], NT)
        after = adjoint[...]
        parts = key_side(after.astype(BF16), lift_k[:ROWS], bend_k[:ROWS], value[:ROWS])
        rows_q = (query_f * (r0 * HEAD_DIM**-0.5)).astype(BF16)
        rows_a = lift_qf * r1
        rows_t = bend_qf * r2
        from_lift = mm(
            jnp.where(carried, rows_a, 0.0).astype(BF16),
            jnp.concatenate([grad, along.astype(BF16)], axis=1),
            TN,
        )
        from_bend = mm(jnp.where(carried, rows_t, 0.0).astype(BF16), grad, TN)
        closing = scalars[step]
        keep = (closing < floor).astype(F32)
        adjoint[...] = keep * after + block_only(jnp.concatenate([from_lift, from_bend], axis=1))
        add_up(0, near_product)
        add_up(8, far1_product)
        add_up(16, grad_f * far2_ref[pl.ds(at, ROWS), :])
        def finish():
            shifted = jnp.where(far_two, grad_pair - spread_far, 0.0).astype(BF16)
            plain = jnp.where(far_two, grad_pair, 0.0).astype(BF16)
            low_weight = jnp.where(far_two, pair_weight, 0.0).astype(BF16)
            low_bend = jnp.where(far_two, pair_bend, 0.0).astype(BF16)
            weights, shifted_near = near_back(scores, grad_pair, near_mask, spread_near)
            d_query = mm(shifted_near, key_heads) * (r0 * HEAD_DIM**-0.5)
            d_query = (
                d_query
                + (mm(shifted, lift_heads) + jnp.where(carried, state_lift, 0.0))
                * (r1 * jnp.minimum(lift_qf, 1.0))
                + (mm(plain, bend_heads) + jnp.where(carried, state_bend, 0.0))
                * (r2 * (1.0 - bend_qf * bend_qf))
            )
            out_ref[0, pl.ds(at, ROWS), :] = d_query.astype(BF16)
            d_key = fold(mm(shifted_near, rows_q, TN))
            d_lift = fold(mm(shifted, rows_a.astype(BF16), TN))
            d_bend = fold(mm(plain, rows_t.astype(BF16), TN))
            d_value = fold(
                mm(
                    jnp.concatenate([weights, low_weight, low_bend], axis=0),
                    jnp.concatenate([grad_f * r0, grad_f * r1, grad_f * r2], axis=0).astype(BF16),
                    TN,
                )
            )
            live = iota((ROWS, PAIR), 0) + first >= jnp.maximum(closing, floor)
            pad = jnp.zeros((TAIL, PAIR), F32)
            d_lift = d_lift + jnp.concatenate([jnp.where(live, parts[0], 0.0), pad], axis=0)
            d_bend = d_bend + jnp.concatenate([jnp.where(live, parts[1], 0.0), pad], axis=0)
            d_value = d_value + jnp.concatenate([jnp.where(live, parts[2], 0.0), pad], axis=0)
            d_key = d_key + d_lift * jnp.minimum(lift_kf, 1.0) + d_bend * (1.0 - bend_kf * bend_kf)
            out_ref[1, pl.ds(at, ROWS), :] = jnp.concatenate(
                [d_key[TAIL:ROWS], d_key[ROWS:] + key_carry[...]], axis=0
            ).astype(BF16)
            out_ref[2, pl.ds(at, ROWS), :] = jnp.concatenate(
                [d_value[TAIL:ROWS], d_value[ROWS:] + value_carry[...]], axis=0
            ).astype(BF16)
            key_carry[...] = d_key[:TAIL]
            value_carry[...] = d_value[:TAIL]

        return finish

    def body(both, carry):
        finishes = [begin(both * 2 + half) for half in range(2)]
        for finish in finishes:
            finish()
        return carry

    lax.fori_loop(0, steps // 2, body, 0, unroll=2)


def feed_kernel(
    scalars,
    mixed_ref,
    tokens_ref,
    cotangent_ref,
    out_weight_ref,
    gain_ref,
    own_ref,
    other_ref,
    layer_ref,
    d_hidden_ref,
    d_branch_ref,
    d_mixed_ref,
    normed_ref,
    active_ref,
    d_inner_ref,
    sums_ref,
):
    c0 = math.sqrt(2.0 / math.pi)
    hidden = tokens_ref[...].astype(F32) + mm(mixed_ref[...], out_weight_ref[...], NT)
    normal, scale = norm_parts(hidden)
    normed = (normal * gain_ref[...]).astype(BF16)
    normed_ref[...] = normed
    cotangent = cotangent_ref[...]
    half, width = own_ref.shape[1:]
    chunk = min(512, half)
    layer = hidden
    d_normed = jnp.zeros(hidden.shape, F32)
    slots = [(ref, first) for ref in (own_ref, other_ref) for first in range(0, half, chunk)]

    def opening(slot):
        ref, first = slot
        into = ref[0, pl.ds(first, chunk), :]
        down = ref[1, pl.ds(first, chunk), :]
        return into, down, mm(normed, into, NT), mm(cotangent, down, NT)

    ready = opening(slots[0])
    for place in range(len(slots)):
        into, down, inner, d_active = ready
        if place + 1 < len(slots):
            ready = opening(slots[place + 1])
        square = inner * inner
        bent = jnp.tanh(inner * (c0 + (c0 * 0.044715) * square))
        gate = 0.5 + 0.5 * bent
        active = (inner * gate).astype(BF16)
        slope = gate + inner * (0.5 - 0.5 * bent * bent) * (c0 + (3.0 * 0.044715 * c0) * square)
        d_inner = (d_active * slope).astype(BF16)
        at = pl.ds(place * chunk, chunk)
        active_ref[:, at] = active
        d_inner_ref[:, at] = d_inner
        layer = layer + mm(active, down)
        d_normed = d_normed + mm(d_inner, into)
    layer_ref[...] = layer.astype(BF16)
    d_part, gain_rows = norm_back(d_normed, gain_ref[...], normal, scale)
    d_hidden = cotangent.astype(F32) + d_part
    d_hidden_ref[...] = d_hidden
    d_branch = d_hidden.astype(BF16)
    d_branch_ref[...] = d_branch
    d_mixed_ref[...] = mm(d_branch, out_weight_ref[...]).astype(BF16)

    @pl.when(pl.program_id(0) == 0)
    def _():
        sums_ref[...] = jnp.zeros(sums_ref.shape, F32)

    sums_ref[...] += gain_rows


def feed_grad_kernel(
    scalars, normed_ref, cotangent_ref, active_ref, d_inner_ref, *refs
):
    refs[-1][0] = mm(d_inner_ref[...], normed_ref[...], TN).astype(refs[-1].dtype)
    refs[-1][1] = mm(active_ref[...], cotangent_ref[...], TN).astype(refs[-1].dtype)
    if len(refs) > 1:
        mixed_ref, d_branch_ref, out_grad_ref, _ = refs

        @pl.when(pl.program_id(0) == 0)
        def _():
            out_grad_ref[...] = mm(d_branch_ref[...], mixed_ref[...], TN)


def input_kernel(
    scalars, d_qkv_ref, weight_ref, tokens_ref, d_hidden_ref, gain_ref, input_grad_ref
):
    d_normed = mm(d_qkv_ref[0], weight_ref[0], NT)
    for c in range(1, 3):
        d_normed = d_normed + mm(d_qkv_ref[c], weight_ref[c], NT)
    normal, scale = norm_parts(tokens_ref[...].astype(F32))
    d_part, _ = norm_back(d_normed, gain_ref[...], normal, scale)
    input_grad_ref[...] = d_hidden_ref[...] + d_part


def resume(kernel, done, scalars, qkv_ref, message_ref, start_ref, blend_ref, *refs):
    kernel(scalars, qkv_ref, message_ref, start_ref, blend_ref, *refs[done:])


def pair_specs(rows, first=0):
    return {
        "qkv": pl.BlockSpec((3, rows, PAIR), lambda p, s: (0, 0, p + first)),
        "message": pl.BlockSpec((1, HEAD_DIM + TAIL, 3 * PAIR), lambda p, s: (p + first, 0, 0)),
        "start": pl.BlockSpec((rows, PAIR), lambda p, s: (0, 0)),
        "blend": pl.BlockSpec((3, PAIR), lambda p, s: (0, p + first)),
        "column": pl.BlockSpec((rows, PAIR), lambda p, s: (0, p + first)),
        "states": pl.BlockSpec((1, rows // ROWS * PAIR, 3 * PAIR), lambda p, s: (p + first, 0, 0)),
        "sums": pl.BlockSpec((24, PAIR), lambda p, s: (0, p)),
        "query": pl.BlockSpec((1, rows, PAIR), lambda p, s: (0, 0, p)),
        "head_rows": pl.BlockSpec((ROWS, PAIR), lambda p, s: (0, p)),
    }


def call(kernel, ins, outs, out_shapes, scratch, grid, name, flops, moved, aliases={}):
    return pl.pallas_call(
        kernel,
        out_shape=out_shapes,
        grid_spec=pltpu.PrefetchScalarGridSpec(
            num_scalar_prefetch=1,
            grid=(grid,),
            in_specs=ins,
            out_specs=outs,
            scratch_shapes=scratch,
        ),
        input_output_aliases=aliases,
        compiler_params=pltpu.CompilerParams(
            dimension_semantics=("arbitrary",), vmem_limit_bytes=56 * 1024 * 1024
        ),
        cost_estimate=pl.CostEstimate(flops=flops, bytes_accessed=moved, transcendentals=0),
        name=name,
    )


def norm_parts(source):
    centered = source - jnp.mean(source, axis=-1, keepdims=True)
    spread_of = jnp.mean(centered * centered, axis=-1, keepdims=True)
    scale = lax.rsqrt(spread_of + EPS)
    return centered * scale, scale


def norm_back(d_out, gain, normal, scale):
    e = d_out * gain
    inner = jnp.mean(e, axis=-1, keepdims=True)
    along = jnp.mean(e * normal, axis=-1, keepdims=True)
    rows = jnp.sum((d_out * normal).reshape(-1, 8, d_out.shape[1]), axis=0)
    return scale * (e - inner - normal * along), rows


def bits(size):
    return [1 << b for b in range(int(math.log2(size)))]


def phases():
    dp = bits(lax.axis_size("dp"))
    core, rest = dp[:1], dp[1:]
    mid = len(rest) // 2
    far = [("dp", m) for m in rest[mid:]]
    near = [("dp", m) for m in rest[:mid]] + [("head", m) for m in bits(lax.axis_size("head"))]
    groups = []
    for run in (far, near, [("dp", m) for m in core]):
        groups += [run[i : i + 2] for i in range(0, len(run), 2)]
    return groups


def relative_bits():
    return [pair for group in phases() for pair in group]


def all_flips():
    order = relative_bits()
    flips = []
    for index in range(1 << len(order)):
        chosen = [pair for place, pair in enumerate(order) if index >> place & 1]
        flips.append(tuple(sum(m for a, m in chosen if a == axis) for axis in ("dp", "head")))
    return flips


def peer(array, group, combo):
    n_dp, n_head = lax.axis_size("dp"), lax.axis_size("head")
    chosen = [pair for place, pair in enumerate(group) if combo >> place & 1]
    flip_dp = sum(m for axis, m in chosen if axis == "dp")
    flip_head = sum(m for axis, m in chosen if axis == "head")
    pairs = [
        (d * n_head + h, (d ^ flip_dp) * n_head + (h ^ flip_head))
        for d in range(n_dp)
        for h in range(n_head)
    ]
    return lax.ppermute(array, ("dp", "head"), pairs)


def widen(block, group, axis, after=None):
    others = [peer(block, group, combo) for combo in range(1, 1 << len(group))]
    if after is not None:
        others, after = lax.optimization_barrier((others, after))
    whole = jnp.concatenate([block] + others, axis=axis)
    return whole if after is None else (whole, after)


def narrow(keep, gives, group, after=None):
    arrived = [peer(give.astype(BF16), group, combo) for combo, give in enumerate(gives, 1)]
    if after is not None:
        arrived, _ = lax.optimization_barrier((arrived, after))
    return keep.astype(F32) + sum(part.astype(F32) for part in arrived)


def narrow_axis(total, group, axis, after=None):
    parts = jnp.split(total, 1 << len(group), axis=axis)
    return narrow(parts[0], parts[1:], group, after)


def pass_along(local, keep, shift):
    size = lax.axis_size("head")
    pairs = [(i, i + shift) for i in range(size) if 0 <= i + shift < size]
    arrived = lax.ppermute(local, "head", pairs)
    for _ in range(size - 2):
        rows = iota(local.shape, 1) < HEAD_DIM
        total = local.astype(F32) + jnp.where(rows, keep * arrived.astype(F32), 0.0)
        arrived = lax.ppermute(total.astype(BF16), "head", pairs)
    return arrived


def per_device(
    tokens,
    ln1_gain,
    qkv_weight,
    out_weight,
    blend,
    ln2_gain,
    in_weight,
    down_weight,
    cotangent,
    lengths,
):
    rows, width = tokens.shape
    n_dp, n_head = lax.axis_size("dp"), lax.axis_size("head")
    pairs = width // PAIR
    steps = rows // ROWS
    groups = phases()
    flips = all_flips()

    shards = jnp.concatenate([qkv_weight, out_weight.T[None]], axis=0)[None]
    feed = jnp.stack([in_weight, down_weight])
    shards = widen(shards, groups[0], 0)
    feed, _ = lax.optimization_barrier((feed, shards))
    feed = widen(feed, groups[0][:1], 1)
    for group in groups[1:-1]:
        shards = widen(shards, group, 0)
    shards, feed = lax.optimization_barrier((shards, feed))
    others = peer(shards, groups[-1], 1)

    item_lengths = lengths[0]
    slots = item_lengths.shape[0]
    ends = jnp.sum(
        jnp.where(iota((slots, slots), 1) <= iota((slots, slots), 0), item_lengths[None, :], 0),
        axis=1,
    )
    offset = lax.axis_index("head") * rows
    local = jnp.arange(rows, dtype=jnp.int32)
    place = local + offset
    total = ends[slots - 1]
    item_start = jnp.max(
        jnp.where(ends[None, :] <= place[:, None], ends[None, :], 0), axis=1
    )
    start = jnp.where(place < total, item_start - offset, local)
    carried_rows = jnp.sum((start < 0).astype(jnp.int32))
    scalars = jnp.concatenate(
        [
            start.reshape(steps, ROWS)[:, ROWS - TAIL - 1],
            carried_rows[None],
            start[rows - 1 :],
            (total - offset)[None],
            lax.axis_index("dp").astype(jnp.int32)[None],
            lax.axis_index("head").astype(jnp.int32)[None],
        ]
    )
    start_wide = jnp.broadcast_to(start[:, None], (rows, PAIR))
    keep_all = (start[rows - 1] < 0).astype(F32)
    blend_wide = jnp.repeat(blend, HEAD_DIM, axis=1)

    spec = pair_specs(rows)
    wide = jax.ShapeDtypeStruct((rows, width), F32)
    states_shape = jax.ShapeDtypeStruct((pairs, steps * PAIR, 3 * PAIR), BF16)
    message_shape = jax.ShapeDtypeStruct((pairs, HEAD_DIM + TAIL, 3 * PAIR), BF16)
    big = rows * width
    part = rows // 3

    def whole_spec(shape):
        return pl.BlockSpec(shape, lambda p, s: (0,) * len(shape))

    qkv, normed_one, qkv_all, out_all, closing = call(
        functools.partial(project_kernel, flips=flips),
        [
            pl.BlockSpec((part, width), lambda p, s: (p, 0)),
            whole_spec((1, width)),
            whole_spec(shards.shape),
            whole_spec(shards.shape),
        ],
        [
            pl.BlockSpec((3, part, width), lambda p, s: (0, p, 0)),
            pl.BlockSpec((part, width), lambda p, s: (p, 0)),
            whole_spec((3, width, width)),
            whole_spec((width, width)),
            whole_spec(message_shape.shape),
        ],
        [
            jax.ShapeDtypeStruct((3, rows, width), BF16),
            jax.ShapeDtypeStruct((rows, width), BF16),
            jax.ShapeDtypeStruct((3, width, width), BF16),
            jax.ShapeDtypeStruct((width, width), BF16),
            message_shape,
        ],
        [
            pltpu.VMEM((pairs, PAIR, 3 * PAIR), F32),
            pltpu.VMEM((n_head, 4, n_dp, width // n_dp, width // n_head), BF16),
        ],
        3,
        "project",
        6 * big * width,
        12 * big,
    )(scalars, tokens, ln1_gain[None], shards, others)
    for pair in groups[0][1:]:
        feed, _ = widen(feed, [pair], 1, closing)
    message = pass_along(closing, keep_all, 1)

    key_scratch = pltpu.VMEM((rows + TAIL, PAIR), BF16)
    state_scratch = pltpu.VMEM((PAIR, 3 * PAIR), F32)
    tail_scratch = pltpu.VMEM((TAIL, PAIR), F32)
    results = ()
    most = pairs - pairs // 4
    for first, count in ((0, most), (most, pairs - most)):
        spec = pair_specs(rows, first)
        results = call(
            functools.partial(resume, forward_kernel, len(results)),
            [spec["qkv"], spec["message"], spec["start"], spec["blend"]]
            + [pl.BlockSpec(memory_space=pl.ANY)] * len(results),
            [spec["column"]] * 6 + [spec["states"]],
            [jax.ShapeDtypeStruct((rows, width), BF16)] + [wide] * 5 + [states_shape],
            [key_scratch, key_scratch, state_scratch],
            count,
            "forward",
            8000 * big * count // pairs,
            40 * big * count // pairs,
            {5 + i: i for i in range(len(results))},
        )(scalars, qkv, message, start_wide, blend_wide, *results)
        if not first:
            feed, results = widen(feed, groups[1], 1, results)
            feed, message = lax.optimization_barrier((feed, message))
    for group in groups[2:-1]:
        feed = widen(feed, group, 1)
    feed_other = peer(feed, groups[-1], 1)
    mixed, near, far1, far2, inv_l, inv_d, states = results

    spec = pair_specs(rows)
    low = jax.ShapeDtypeStruct((rows, width), BF16)
    row_spec = pl.BlockSpec((part, width), lambda p, s: (p, 0))
    hidden_units = 2 * feed.shape[1]
    unit_spec = pl.BlockSpec((part, hidden_units), lambda p, s: (p, 0))
    unit_shape = jax.ShapeDtypeStruct((rows, hidden_units), BF16)
    sums_shape = jax.ShapeDtypeStruct((8, width), F32)
    layer_out, d_hidden, d_branch, d_mixed, normed_two, active, d_inner, gain_two_rows = call(
        feed_kernel,
        [row_spec] * 3
        + [
            whole_spec((width, width)),
            whole_spec((1, width)),
            whole_spec(feed.shape),
            whole_spec(feed.shape),
        ],
        [row_spec] * 5 + [unit_spec] * 2 + [whole_spec((8, width))],
        [low, wide, low, low, low, unit_shape, unit_shape, sums_shape],
        [],
        3,
        "feed",
        8 * big * hidden_units,
        32 * big,
    )(scalars, mixed, tokens, cotangent, out_all, ln2_gain[None], feed, feed_other)

    back = call(
        prologue_kernel,
        [
            spec["query"],
            pl.BlockSpec((1, ROWS, PAIR), lambda p, s: (1, 0, p)),
            pl.BlockSpec((1, ROWS, PAIR), lambda p, s: (2, 0, p)),
            spec["message"],
            spec["start"],
            spec["blend"],
            spec["column"],
            spec["head_rows"],
            spec["column"],
            spec["head_rows"],
            spec["column"],
        ],
        spec["message"],
        message_shape,
        [state_scratch],
        pairs,
        "prologue",
        500 * big,
        20 * big,
    )(scalars, qkv, qkv, qkv, message, start_wide, blend_wide, d_mixed, near, far1, inv_l, inv_d)
    d_inner, _ = lax.optimization_barrier((d_inner, back))
    back_in = pass_along(back, keep_all, -1)

    unit = hidden_units // 4
    half_shape = (2, 2 * unit, width)
    whole_rows = whole_spec((rows, width))

    def feed_grad(place, kind, d_inner, more_ins, more_in_specs, more_outs, more_out_specs):
        columns = pl.BlockSpec((rows, unit), lambda p, s: (0, p + 2 * place))
        return call(
            feed_grad_kernel,
            [whole_rows] * 2 + [columns] * 2 + more_in_specs,
            more_out_specs + [pl.BlockSpec((2, unit, width), lambda p, s: (0, p, 0))],
            more_outs + [jax.ShapeDtypeStruct(half_shape, kind)],
            [],
            2,
            "feed_grad",
            2 * big * hidden_units,
            12 * big,
        )(scalars, normed_two, cotangent, active, d_inner, *more_ins)

    out_grad, keep = feed_grad(
        0,
        F32,
        d_inner,
        [mixed, d_branch],
        [whole_rows] * 2,
        [jax.ShapeDtypeStruct((width, width), F32)],
        [whole_spec((width, width))],
    )
    d_inner, back_in, out_grad = lax.optimization_barrier((d_inner, back_in, out_grad))
    (give,) = feed_grad(1, BF16, d_inner, [], [], [], [])
    feed_share = narrow(keep, [give], groups[-1])
    left = list(reversed(groups[:-1]))

    d_qkv = jnp.zeros((3, 8, PAIR), BF16)
    sums = []
    first = 0
    for count in (pairs // 4, pairs // 2, pairs // 4):
        spec = pair_specs(rows, first)
        more = {13: 0} if first else {}
        d_qkv, part_sums = call(
            backward_kernel,
            [spec["qkv"], spec["message"], spec["start"], spec["blend"]]
            + [spec["column"]] * 6
            + [spec["states"], spec["message"], pl.BlockSpec(memory_space=pl.ANY)],
            [spec["qkv"], spec["sums"]],
            [
                jax.ShapeDtypeStruct((3, rows, width), BF16),
                jax.ShapeDtypeStruct((24, count * PAIR), F32),
            ],
            [key_scratch, key_scratch, state_scratch, tail_scratch, tail_scratch],
            count,
            "backward",
            16000 * big * count // pairs,
            40 * big * count // pairs,
            more,
        )(
            scalars,
            qkv,
            message,
            start_wide,
            blend_wide,
            d_mixed,
            near,
            far1,
            far2,
            inv_l,
            inv_d,
            states,
            back_in,
            d_qkv,
        )
        sums.append(part_sums)
        first += count
        if left and first < pairs:
            _, back_in = lax.optimization_barrier((feed_share, back_in))
            feed_share = narrow_axis(feed_share, left.pop(0), 1)
    for group in left:
        feed_share = narrow_axis(feed_share, group, 1)
    feed_share, d_qkv = lax.optimization_barrier((feed_share, d_qkv))
    sums = jnp.concatenate(sums, axis=1)
    blend_part = jnp.sum(sums.reshape(3, 8, blend.shape[1], HEAD_DIM), axis=(1, 3))

    shard_shape = (n_dp * n_head // 2, 4, width // n_dp, width // n_head)
    shard_spec = pl.BlockSpec((shard_shape[0], 1) + shard_shape[2:], lambda p, s: (0, p, 0, 0))
    keep, give, gain_one_rows = call(
        functools.partial(weight_grad_kernel, flips=flips),
        [
            whole_spec((rows, width)),
            pl.BlockSpec((1, rows, width), lambda p, s: (jnp.minimum(p, 2), 0, 0)),
            whole_spec((width, width)),
            pl.BlockSpec((1, width, width), lambda p, s: (jnp.minimum(p, 2), 0, 0)),
        ],
        [shard_spec, shard_spec, whole_spec((8, width))],
        [
            jax.ShapeDtypeStruct(shard_shape, F32),
            jax.ShapeDtypeStruct(shard_shape, BF16),
            sums_shape,
        ],
        [pltpu.VMEM((n_head, n_dp, width // n_dp, width // n_head), F32)],
        4,
        "weight_grad",
        6 * big * width,
        8 * big,
    )(scalars, normed_one, d_qkv, out_grad, qkv_all)
    parts = [gain_one_rows[0] / ln1_gain, jnp.sum(gain_two_rows, axis=0), blend_part.reshape(-1)]
    total_sums = jnp.concatenate(parts)[None]
    share = narrow(keep, [give], groups[-1])
    hops = list(reversed(relative_bits()))
    total_sums = total_sums + peer(total_sums, [hops[0]], 1)
    total_sums, d_qkv, _ = lax.optimization_barrier((total_sums, d_qkv, share))
    total_sums = total_sums + peer(total_sums, [hops[1]], 1)
    fine = rows // 6
    fine_spec = pl.BlockSpec((fine, width), lambda p, s: (p, 0))
    input_grad = call(
        input_kernel,
        [
            pl.BlockSpec((3, fine, width), lambda p, s: (0, p, 0)),
            whole_spec((3, width, width)),
            fine_spec,
            fine_spec,
            whole_spec((1, width)),
        ],
        fine_spec,
        wide,
        [],
        6,
        "input",
        6 * big * width,
        24 * big,
    )(scalars, d_qkv, qkv_all, tokens, d_hidden, ln1_gain[None])
    share = narrow_axis(share, groups[-2], 0, input_grad)
    total_sums, _ = lax.optimization_barrier((total_sums, input_grad))
    total_sums = total_sums + peer(total_sums, [hops[2]], 1)
    for group in reversed(groups[:-2]):
        parts = jnp.split(share, 1 << len(group), axis=0)
        gives = [part.astype(BF16) for part in parts[1:]]
        total_sums, _ = lax.optimization_barrier((total_sums, gives))
        share = narrow(parts[0], gives, group)
    for pair in hops[3:]:
        total_sums = total_sums + peer(total_sums, [pair], 1)
    total_sums = total_sums[0]
    gain_one, gain_two = total_sums[:width], total_sums[width : 2 * width]
    blend_sum = total_sums[2 * width :].reshape(blend.shape)
    qkv_share, out_share = share[0, :3], share[0, 3].T
    in_share, down_share = feed_share[0], feed_share[1]
    return (
        layer_out,
        input_grad,
        gain_one,
        qkv_share,
        out_share,
        blend_sum,
        gain_two,
        in_share,
        down_share,
    )


def solution(mesh):
    return jax.shard_map(
        per_device,
        mesh=mesh,
        in_specs=(
            P(("dp", "head"), None),
            P(),
            P(None, "dp", "head"),
            P("head", "dp"),
            P(),
            P(),
            P(("dp", "head"), None),
            P(("dp", "head"), None),
            P(("dp", "head"), None),
            P("dp", None),
        ),
        out_specs=(
            P(("dp", "head"), None),
            P(("dp", "head"), None),
            P(),
            P(None, "dp", "head"),
            P("head", "dp"),
            P(),
            P(),
            P(("dp", "head"), None),
            P(("dp", "head"), None),
        ),
        check_vma=False,
    )
```

```python
import functools
import math

import jax
import jax.numpy as jnp
from jax import lax
from jax.experimental import pallas as pl
from jax.experimental.pallas import tpu as pltpu
from jax.sharding import PartitionSpec as P

HEAD_DIM = 64
BAND = 30
ROWS = 96
TAIL = 32
WIN = ROWS + TAIL
PAIR = 2 * HEAD_DIM
EPS = 1e-05
NEG = -1e30
CARRIED, LAST, VALID, ROW_AT, COLUMN_AT = range(-5, 0)
F32 = jnp.float32
BF16 = jnp.bfloat16
NT = (((1,), (1,)), ((), ()))
TN = (((0,), (0,)), ((), ()))
NN = (((1,), (0,)), ((), ()))


def mm(left, right, dims=NN):
    return lax.dot_general(left, right, dims, preferred_element_type=F32)


def iota(shape, axis):
    return lax.broadcasted_iota(jnp.int32, shape, axis)


def lift(values):
    return jnp.where(values > 0, values + 1.0, jnp.exp(jnp.minimum(values, 0.0)))


def head_lanes(dtype):
    first = (iota((1, PAIR), 1) < HEAD_DIM).astype(F32)
    return first.astype(dtype), (1.0 - first).astype(dtype)


def split_heads(block):
    first, second = head_lanes(block.dtype)
    return jnp.concatenate([block * first, block * second], axis=0)


def same_head():
    return (iota((PAIR, PAIR), 0) < HEAD_DIM) == (iota((PAIR, PAIR), 1) < HEAD_DIM)


def block_only(wide):
    keep = same_head()
    parts = [
        jnp.where(keep, wide[:, p * PAIR : (p + 1) * PAIR], 0.0)
        for p in range(wide.shape[1] // PAIR)
    ]
    return jnp.concatenate(parts, axis=1)


def fold(tall):
    half = tall.shape[0] // 2
    lanes = iota((half, PAIR), 1) < HEAD_DIM
    return jnp.where(lanes, tall[:half], tall[half:])


def two(half):
    return jnp.concatenate([half, half], axis=1)


def masks(row, start, first):
    key = iota(row.shape, 1) + first
    floor = jnp.maximum(first, 0)
    causal = key <= row
    near = causal & (key >= jnp.maximum(start, row - (BAND - 1)))
    far = causal & (key >= jnp.maximum(start, floor))
    count = 1.0 / (row - start + 1).astype(F32)
    return jnp.where(near, 0.0, NEG), far.astype(F32), jnp.where(start < floor, -count, count)


def near_scores(query, key_heads):
    return mm(query * jnp.asarray(HEAD_DIM**-0.5, BF16), key_heads, NT)


def near_weights(scores, bias):
    parts = []
    for h in range(2):
        part = scores[:, h * WIN : (h + 1) * WIN] + bias
        parts.append(jnp.exp(part - jnp.max(part, axis=1, keepdims=True)))
    return jnp.concatenate(parts, axis=1)


def spread(product):
    first = iota(product.shape, 1) < HEAD_DIM
    sums = [
        jnp.sum(jnp.where(keep, product, 0.0), axis=1, keepdims=True) for keep in (first, ~first)
    ]
    return jnp.concatenate([jnp.broadcast_to(part, (ROWS, WIN)) for part in sums], axis=1)


def load_keys(qkv_ref, message_ref, keys, values):
    rows = qkv_ref.shape[1]
    keys[pl.ds(0, TAIL), :] = message_ref[0, pl.ds(HEAD_DIM, TAIL), :PAIR]
    keys[pl.ds(TAIL, rows), :] = qkv_ref[1]
    values[pl.ds(0, TAIL), :] = message_ref[0, pl.ds(HEAD_DIM, TAIL), PAIR : 2 * PAIR]
    values[pl.ds(TAIL, rows), :] = qkv_ref[2]


def fold_state(wide):
    kept = block_only(wide)
    return (kept[:HEAD_DIM] + kept[HEAD_DIM:]).astype(BF16)


def unfold_state(message):
    half = message[:HEAD_DIM].astype(F32)
    return block_only(jnp.concatenate([half, half], axis=0))


def project_kernel(
    scalars,
    tokens_ref,
    gain_ref,
    own_ref,
    other_ref,
    qkv_ref,
    normed_ref,
    weight_ref,
    out_weight_ref,
    message_ref,
    state,
    placed,
    *,
    flips,
):
    step = pl.program_id(0)
    rows, width = tokens_ref.shape
    pairs = width // PAIR
    half, _, tall, wide = own_ref.shape
    last = jnp.maximum(scalars[scalars.shape[0] + LAST], 0)

    @pl.when(step == 0)
    def _():
        for index, (flip_row, flip_column) in enumerate(flips):
            row = scalars[scalars.shape[0] + ROW_AT] ^ flip_row
            column = scalars[scalars.shape[0] + COLUMN_AT] ^ flip_column
            piece = own_ref[index] if index < half else other_ref[index - half]
            for c in range(4):
                placed[column, c, row] = piece[c]
        for h in range(width // wide):
            at = pl.ds(h * wide, wide)
            weight_ref[:, :, at] = placed[h, :3].reshape(3, width, wide)
            out_weight_ref[:, at] = placed[h, 3].reshape(width, wide)
        state[...] = jnp.zeros(state.shape, F32)

    normed = (norm_parts(tokens_ref[...].astype(F32))[0] * gain_ref[...]).astype(BF16)
    normed_ref[...] = normed
    for c in (1, 2, 0):
        qkv_ref[c] = mm(normed, weight_ref[c]).astype(BF16)
    live = iota((rows, PAIR), 0) + step * rows >= last
    ones = jnp.ones((rows, PAIR), BF16)
    for p in range(pairs):
        at = pl.ds(p * PAIR, PAIR)
        key = qkv_ref[1, :, at].astype(F32)
        value = qkv_ref[2, :, at]
        lifted = jnp.where(live, lift(key), 0.0).astype(BF16)
        bent = jnp.where(live, jnp.tanh(key), 0.0).astype(BF16)
        state[p, :, : 2 * PAIR] += mm(lifted, jnp.concatenate([value, ones], axis=1), TN)
        state[p, :, 2 * PAIR :] += mm(bent, value, TN)

    @pl.when(step == pl.num_programs(0) - 1)
    def _():
        for p in range(pairs):
            at = pl.ds(p * PAIR, PAIR)
            message_ref[p, pl.ds(0, HEAD_DIM), :] = fold_state(state[p])
            message_ref[p, pl.ds(HEAD_DIM, TAIL), :] = jnp.concatenate(
                [
                    qkv_ref[1, pl.ds(rows - TAIL, TAIL), at],
                    qkv_ref[2, pl.ds(rows - TAIL, TAIL), at],
                    jnp.zeros((TAIL, PAIR), BF16),
                ],
                axis=1,
            )


def weight_grad_kernel(
    scalars,
    normed_ref,
    d_qkv_ref,
    out_grad_ref,
    weight_ref,
    keep_ref,
    give_ref,
    gain_ref,
    whole,
    *,
    flips,
):
    c = pl.program_id(0)
    half, _, tall, wide = keep_ref.shape

    def place(total):
        for h in range(total.shape[1] // wide):
            part = total[:, h * wide : (h + 1) * wide]
            whole[h] = part.reshape(whole.shape[1:])

    @pl.when(c == 0)
    def _():
        gain_ref[...] = jnp.zeros(gain_ref.shape, F32)

    @pl.when(c < 3)
    def _():
        total = mm(normed_ref[...], d_qkv_ref[0], TN)
        place(total)
        product = total * weight_ref[0].astype(F32)
        high = product.astype(BF16)
        low = (product - high.astype(F32)).astype(BF16)
        ones = jnp.ones((8, product.shape[1]), BF16)
        gain_ref[...] += mm(ones, high, NT) + mm(ones, low, NT)

    @pl.when(c == 3)
    def _():
        place(out_grad_ref[...])

    for index, (flip_row, flip_column) in enumerate(flips):
        row = scalars[scalars.shape[0] + ROW_AT] ^ flip_row
        column = scalars[scalars.shape[0] + COLUMN_AT] ^ flip_column
        if index < half:
            keep_ref[index, 0] = whole[column, row]
        else:
            give_ref[index - half, 0] = whole[column, row].astype(BF16)


def forward_kernel(
    scalars,
    qkv_ref,
    message_ref,
    bias_ref,
    far_ref,
    tally_ref,
    blend_ref,
    att_ref,
    near_ref,
    far1_ref,
    far2_ref,
    invl_ref,
    invd_ref,
    states_ref,
    keys,
    values,
    state,
):
    rows = qkv_ref.shape[1]
    load_keys(qkv_ref, message_ref, keys, values)
    state[...] = unfold_state(message_ref[0])
    count_valid = scalars[scalars.shape[0] + VALID]
    b0, b1, b2 = (blend_ref[pl.ds(f, 1), :] for f in range(3))

    def begin(step):
        at = pl.multiple_of(step * ROWS, 32)
        query = qkv_ref[0, pl.ds(at, ROWS), :]
        key = keys[pl.ds(at, WIN), :]
        value = values[pl.ds(at, WIN), :]
        first = step * ROWS - TAIL
        floor = jnp.maximum(first, 0)
        tally = tally_ref[pl.ds(at, ROWS), :]
        carried = tally < 0.0
        far_two = two(far_ref[pl.ds(at, ROWS), :].astype(F32))
        query_f = query.astype(F32)
        key_f = key.astype(F32)
        lift_qf, bend_qf = lift(query_f), jnp.tanh(query_f)
        lift_q, bend_q = lift_qf.astype(BF16), bend_qf.astype(BF16)
        lift_k = lift(key_f)
        bend_k = jnp.tanh(key_f)
        ones = jnp.ones((WIN, PAIR), BF16)
        value_heads = jnp.concatenate([split_heads(value), split_heads(ones)], axis=1)
        before = state[...]
        before_low = before.astype(BF16)
        scores = near_scores(query, split_heads(key))
        pair_weight = mm(lift_q, split_heads(lift_k.astype(BF16)), NT)
        pair_bend = mm(bend_q, split_heads(bend_k.astype(BF16)), NT)
        elu_state = mm(
            jnp.where(carried, lift_qf, 0.0).astype(BF16), before_low[:, : 2 * PAIR]
        )
        tanh_state = mm(jnp.where(carried, bend_qf, 0.0).astype(BF16), before_low[:, 2 * PAIR :])
        states_ref[0, pl.ds(pl.multiple_of(step * PAIR, PAIR), PAIR), :] = before_low
        closing = scalars[step]
        live = iota((ROWS, PAIR), 0) + first >= jnp.maximum(closing, floor)
        lifted = jnp.where(live, lift_k[:ROWS], 0.0).astype(BF16)
        bent = jnp.where(live, bend_k[:ROWS], 0.0).astype(BF16)
        with_ones = jnp.concatenate([value[:ROWS], ones[:ROWS]], axis=1)
        added = jnp.concatenate([mm(lifted, with_ones, TN), mm(bent, value[:ROWS], TN)], axis=1)
        keep = (closing < floor).astype(F32)
        state[...] = keep * before + block_only(added)
        def finish():
            low_weight = (pair_weight * far_two).astype(BF16)
            low_bend = (pair_bend * far_two).astype(BF16)
            elu_out = mm(low_weight, value_heads)
            tanh_out = mm(low_bend, value_heads[:, :PAIR]) + tanh_state
            weights = near_weights(scores, bias_ref[pl.ds(at, ROWS), :].astype(F32)).astype(BF16)
            near_out = mm(weights, value_heads)
            numerator = elu_out[:, :PAIR] + elu_state[:, :PAIR]
            inv_d = 1.0 / (elu_out[:, PAIR:] + elu_state[:, PAIR:])
            far1 = numerator * inv_d
            inv_l = 1.0 / near_out[:, PAIR:]
            near = near_out[:, :PAIR] * inv_l
            far2 = tanh_out * jnp.abs(tally)
            row = iota((ROWS, PAIR), 0) + at
            mixed = jnp.where(row < count_valid, b0 * near + b1 * far1 + b2 * far2, 0.0)
            att_ref[pl.ds(at, ROWS), :] = mixed.astype(BF16)
            near_ref[pl.ds(at, ROWS), :] = near
            far1_ref[pl.ds(at, ROWS), :] = far1
            far2_ref[pl.ds(at, ROWS), :] = far2
            invl_ref[pl.ds(at, ROWS), :] = inv_l
            invd_ref[pl.ds(at, ROWS), :] = inv_d

        return finish

    def body(both, carry):
        finishes = [begin(both * 2 + half) for half in range(2)]
        for finish in finishes:
            finish()
        return carry

    lax.fori_loop(0, rows // ROWS // 2, body, 0, unroll=2)


def near_back(scores, grad_pair, bias, spread_near):
    weights = near_weights(scores, bias)
    return weights.astype(BF16), (weights * (grad_pair - spread_near)).astype(BF16)


def prologue_kernel(
    scalars,
    query_ref,
    key_ref,
    value_ref,
    message_ref,
    start_ref,
    blend_ref,
    grad_ref,
    near_ref,
    far1_ref,
    invl_ref,
    invd_ref,
    back_ref,
    adjoint,
):
    rows = query_ref.shape[1]
    step_rows = rows // 3
    b0, b1, b2 = (blend_ref[pl.ds(f, 1), :] for f in range(3))
    adjoint[...] = jnp.zeros(adjoint.shape, F32)

    tails = message_ref[0, pl.ds(HEAD_DIM, TAIL), :]
    key = jnp.concatenate([tails[:, :PAIR], key_ref[0]], axis=0)
    value = jnp.concatenate([tails[:, PAIR : 2 * PAIR], value_ref[0]], axis=0)
    start = start_ref[pl.ds(0, ROWS), :]
    row = iota((ROWS, WIN), 0)
    bias, _, _ = masks(row, start, -TAIL)
    query = query_ref[0, pl.ds(0, ROWS), :]
    grad = grad_ref[pl.ds(0, ROWS), :]
    grad_f = grad.astype(F32)
    scale = b0 * invl_ref[...]
    rows_q = (query.astype(F32) * (scale * HEAD_DIM**-0.5)).astype(BF16)
    rows_g = (grad_f * scale).astype(BF16)
    weights, shifted = near_back(
        near_scores(query, split_heads(key)),
        mm(grad, split_heads(value), NT),
        bias,
        spread(grad_f * near_ref[...]),
    )
    d_key = fold(mm(shifted, rows_q, TN))
    back_ref[0, pl.ds(HEAD_DIM, TAIL), :] = jnp.concatenate(
        [d_key[:TAIL], fold(mm(weights, rows_g, TN))[:TAIL], jnp.zeros((TAIL, PAIR), F32)], axis=1
    ).astype(BF16)
    heads = same_head().astype(F32).astype(BF16)
    heads = jnp.concatenate([heads, heads], axis=0)

    for step in range(3):
        at = step * step_rows

        @pl.when(scalars[scalars.shape[0] + CARRIED] > at)
        def _():
            here = pl.ds(at, step_rows)
            row = iota((step_rows, PAIR), 0) + at
            start = start_ref[here, :]
            grad = grad_ref[here, :]
            grad_f = grad.astype(F32)
            product = grad_f * far1_ref[here, :]
            high = product.astype(BF16)
            low = (product - high.astype(F32)).astype(BF16)
            along = mm(jnp.concatenate([high, low], axis=1), heads).astype(BF16)
            query_f = query_ref[0, here, :].astype(F32)
            live = start < 0
            scaled = jnp.where(live, lift(query_f) * (b1 * invd_ref[here, :]), 0.0)
            bent = jnp.where(
                live, jnp.tanh(query_f) * (b2 / (row - start + 1).astype(F32)), 0.0
            )
            adjoint[:, : 2 * PAIR] += mm(
                scaled.astype(BF16), jnp.concatenate([grad, along], axis=1), TN
            )
            adjoint[:, 2 * PAIR :] += mm(bent.astype(BF16), grad, TN)

    back_ref[0, pl.ds(0, HEAD_DIM), :] = fold_state(adjoint[...])


def key_side(adjoint_low, lift_k, bend_k, value):
    ones = jnp.full(value.shape, -1.0 / HEAD_DIM, BF16)
    d_lift = mm(jnp.concatenate([value, ones], axis=1), adjoint_low[:, : 2 * PAIR], NT)
    d_bend = mm(value, adjoint_low[:, 2 * PAIR :], NT)
    both = jnp.concatenate([adjoint_low[:, :PAIR], adjoint_low[:, 2 * PAIR :]], axis=0)
    d_value = mm(jnp.concatenate([lift_k, bend_k], axis=1), both)
    return d_lift, d_bend, d_value


def backward_kernel(
    scalars,
    qkv_ref,
    message_ref,
    bias_ref,
    far_ref,
    tally_ref,
    blend_ref,
    grad_ref,
    near_ref,
    far1_ref,
    far2_ref,
    invl_ref,
    invd_ref,
    states_ref,
    back_ref,
    done_ref,
    out_ref,
    sums_ref,
    keys,
    values,
    adjoint,
    key_carry,
    value_carry,
):
    rows = qkv_ref.shape[1]
    steps = rows // ROWS
    load_keys(qkv_ref, message_ref, keys, values)
    last = scalars[scalars.shape[0] + LAST]
    b0, b1, b2 = (blend_ref[pl.ds(f, 1), :] for f in range(3))
    lanes = iota((ROWS, PAIR), 1) < HEAD_DIM

    arrived = unfold_state(back_ref[0])
    tail_grads = back_ref[0, pl.ds(HEAD_DIM, TAIL), :].astype(F32)
    end_key = keys[pl.ds(rows, TAIL), :].astype(F32)
    end_lift, end_bend = lift(end_key), jnp.tanh(end_key)
    end_parts = key_side(
        arrived.astype(BF16), end_lift.astype(BF16), end_bend.astype(BF16), values[pl.ds(rows, TAIL), :]
    )
    live = iota((TAIL, PAIR), 0) + (rows - TAIL) >= last
    key_carry[...] = tail_grads[:, :PAIR] + jnp.where(
        live,
        end_parts[0] * jnp.minimum(end_lift, 1.0) + end_parts[1] * (1.0 - end_bend * end_bend),
        0.0,
    )
    value_carry[...] = tail_grads[:, PAIR : 2 * PAIR] + jnp.where(live, end_parts[2], 0.0)
    adjoint[...] = jnp.where(last < rows - TAIL, 1.0, 0.0) * arrived
    sums_ref[...] = jnp.zeros(sums_ref.shape, F32)

    def add_up(place, product):
        sums_ref[pl.ds(place, 8), :] += jnp.sum(product.reshape(ROWS // 8, 8, PAIR), axis=0)

    def begin(back):
        step = steps - 1 - back
        at = pl.multiple_of(step * ROWS, 32)
        query = qkv_ref[0, pl.ds(at, ROWS), :]
        key = keys[pl.ds(at, WIN), :]
        value = values[pl.ds(at, WIN), :]
        first = step * ROWS - TAIL
        floor = jnp.maximum(first, 0)
        tally = tally_ref[pl.ds(at, ROWS), :]
        carried = tally < 0.0
        far_two = two(far_ref[pl.ds(at, ROWS), :].astype(F32))
        grad = grad_ref[pl.ds(at, ROWS), :]
        grad_f = grad.astype(F32)
        query_f = query.astype(F32)
        key_f = key.astype(F32)
        lift_qf, bend_qf = lift(query_f), jnp.tanh(query_f)
        lift_kf, bend_kf = lift(key_f), jnp.tanh(key_f)
        lift_q, bend_q = lift_qf.astype(BF16), bend_qf.astype(BF16)
        lift_k, bend_k = lift_kf.astype(BF16), bend_kf.astype(BF16)
        lift_heads, bend_heads = split_heads(lift_k), split_heads(bend_k)
        r0 = b0 * invl_ref[pl.ds(at, ROWS), :]
        r1 = b1 * invd_ref[pl.ds(at, ROWS), :]
        r2 = b2 * jnp.abs(tally)
        key_heads = split_heads(key)
        before = states_ref[0, pl.ds(pl.multiple_of(step * PAIR, PAIR), PAIR), :]
        near_product = grad_f * near_ref[pl.ds(at, ROWS), :]
        far1_product = grad_f * far1_ref[pl.ds(at, ROWS), :]
        grad_pair = mm(grad, split_heads(value), NT)
        scores = near_scores(query, key_heads)
        pair_weight = mm(lift_q, lift_heads, NT)
        pair_bend = mm(bend_q, bend_heads, NT)
        state_bend = mm(grad, before[:, 2 * PAIR :], NT)
        spread_far = spread(far1_product)
        spread_near = spread(near_product)
        along = jnp.where(lanes, spread_far[:, :WIN], spread_far[:, WIN:])
        scaled_along = (along * (-1.0 / HEAD_DIM)).astype(BF16)
        state_lift = mm(jnp.concatenate([grad, scaled_along], axis=1), before[:, : 2 * PAIR], NT)
        after = adjoint[...]
        parts = key_side(after.astype(BF16), lift_k[:ROWS], bend_k[:ROWS], value[:ROWS])
        rows_q = (query_f * (r0 * HEAD_DIM**-0.5)).astype(BF16)
        rows_a = lift_qf * r1
        rows_t = bend_qf * r2
        from_lift = mm(
            jnp.where(carried, rows_a, 0.0).astype(BF16),
            jnp.concatenate([grad, along.astype(BF16)], axis=1),
            TN,
        )
        from_bend = mm(jnp.where(carried, rows_t, 0.0).astype(BF16), grad, TN)
        closing = scalars[step]
        keep = (closing < floor).astype(F32)
        adjoint[...] = keep * after + block_only(jnp.concatenate([from_lift, from_bend], axis=1))
        add_up(0, near_product)
        add_up(8, far1_product)
        add_up(16, grad_f * far2_ref[pl.ds(at, ROWS), :])
        def finish():
            shifted = ((grad_pair - spread_far) * far_two).astype(BF16)
            plain = (grad_pair * far_two).astype(BF16)
            low_weight = (pair_weight * far_two).astype(BF16)
            low_bend = (pair_bend * far_two).astype(BF16)
            weights, shifted_near = near_back(
                scores, grad_pair, bias_ref[pl.ds(at, ROWS), :].astype(F32), spread_near
            )
            d_query = mm(shifted_near, key_heads) * (r0 * HEAD_DIM**-0.5)
            d_query = (
                d_query
                + (mm(shifted, lift_heads) + jnp.where(carried, state_lift, 0.0))
                * (r1 * jnp.minimum(lift_qf, 1.0))
                + (mm(plain, bend_heads) + jnp.where(carried, state_bend, 0.0))
                * (r2 * (1.0 - bend_qf * bend_qf))
            )
            out_ref[0, pl.ds(at, ROWS), :] = d_query.astype(BF16)
            d_key = fold(mm(shifted_near, rows_q, TN))
            d_lift = fold(mm(shifted, rows_a.astype(BF16), TN))
            d_bend = fold(mm(plain, rows_t.astype(BF16), TN))
            d_value = fold(
                mm(
                    jnp.concatenate([weights, low_weight, low_bend], axis=0),
                    jnp.concatenate([grad_f * r0, grad_f * r1, grad_f * r2], axis=0).astype(BF16),
                    TN,
                )
            )
            live = iota((ROWS, PAIR), 0) + first >= jnp.maximum(closing, floor)
            pad = jnp.zeros((TAIL, PAIR), F32)
            d_lift = d_lift + jnp.concatenate([jnp.where(live, parts[0], 0.0), pad], axis=0)
            d_bend = d_bend + jnp.concatenate([jnp.where(live, parts[1], 0.0), pad], axis=0)
            d_value = d_value + jnp.concatenate([jnp.where(live, parts[2], 0.0), pad], axis=0)
            d_key = d_key + d_lift * jnp.minimum(lift_kf, 1.0) + d_bend * (1.0 - bend_kf * bend_kf)
            out_ref[1, pl.ds(at, ROWS), :] = jnp.concatenate(
                [d_key[TAIL:ROWS], d_key[ROWS:] + key_carry[...]], axis=0
            ).astype(BF16)
            out_ref[2, pl.ds(at, ROWS), :] = jnp.concatenate(
                [d_value[TAIL:ROWS], d_value[ROWS:] + value_carry[...]], axis=0
            ).astype(BF16)
            key_carry[...] = d_key[:TAIL]
            value_carry[...] = d_value[:TAIL]

        return finish

    def body(both, carry):
        finishes = [begin(both * 2 + half) for half in range(2)]
        for finish in finishes:
            finish()
        return carry

    lax.fori_loop(0, steps // 2, body, 0, unroll=2)


def feed_kernel(
    scalars,
    mixed_ref,
    tokens_ref,
    cotangent_ref,
    out_weight_ref,
    gain_ref,
    own_ref,
    other_ref,
    layer_ref,
    d_hidden_ref,
    d_branch_ref,
    d_mixed_ref,
    normed_ref,
    active_ref,
    d_inner_ref,
    sums_ref,
):
    c0 = math.sqrt(2.0 / math.pi)
    hidden = tokens_ref[...].astype(F32) + mm(mixed_ref[...], out_weight_ref[...], NT)
    normal, scale = norm_parts(hidden)
    normed = (normal * gain_ref[...]).astype(BF16)
    normed_ref[...] = normed
    cotangent = cotangent_ref[...]
    half, width = own_ref.shape[1:]
    chunk = min(512, half)
    layer = hidden
    d_normed = jnp.zeros(hidden.shape, F32)
    slots = [(ref, first) for ref in (own_ref, other_ref) for first in range(0, half, chunk)]

    def opening(slot):
        ref, first = slot
        into = ref[0, pl.ds(first, chunk), :]
        down = ref[1, pl.ds(first, chunk), :]
        return into, down, mm(normed, into, NT), mm(cotangent, down, NT)

    ready = opening(slots[0])
    for place in range(len(slots)):
        into, down, inner, d_active = ready
        if place + 1 < len(slots):
            ready = opening(slots[place + 1])
        square = inner * inner
        bent = jnp.tanh(inner * (c0 + (c0 * 0.044715) * square))
        gate = 0.5 + 0.5 * bent
        active = (inner * gate).astype(BF16)
        slope = gate + inner * (0.5 - 0.5 * bent * bent) * (c0 + (3.0 * 0.044715 * c0) * square)
        d_inner = (d_active * slope).astype(BF16)
        at = pl.ds(place * chunk, chunk)
        active_ref[:, at] = active
        d_inner_ref[:, at] = d_inner
        layer = layer + mm(active, down)
        d_normed = d_normed + mm(d_inner, into)
    layer_ref[...] = layer.astype(BF16)
    d_part, gain_rows = norm_back(d_normed, gain_ref[...], normal, scale)
    d_hidden = cotangent.astype(F32) + d_part
    d_hidden_ref[...] = d_hidden
    d_branch = d_hidden.astype(BF16)
    d_branch_ref[...] = d_branch
    row = iota(hidden.shape, 0) + pl.program_id(0) * hidden.shape[0]
    d_mixed = mm(d_branch, out_weight_ref[...])
    d_mixed_ref[...] = jnp.where(row < scalars[scalars.shape[0] + VALID], d_mixed, 0.0).astype(BF16)

    @pl.when(pl.program_id(0) == 0)
    def _():
        sums_ref[...] = jnp.zeros(sums_ref.shape, F32)

    sums_ref[...] += gain_rows


def feed_grad_kernel(
    scalars, normed_ref, cotangent_ref, active_ref, d_inner_ref, *refs
):
    refs[-1][0] = mm(d_inner_ref[...], normed_ref[...], TN).astype(refs[-1].dtype)
    refs[-1][1] = mm(active_ref[...], cotangent_ref[...], TN).astype(refs[-1].dtype)
    if len(refs) > 1:
        mixed_ref, d_branch_ref, out_grad_ref, _ = refs

        @pl.when(pl.program_id(0) == 0)
        def _():
            out_grad_ref[...] = mm(d_branch_ref[...], mixed_ref[...], TN)


def input_kernel(
    scalars, d_qkv_ref, weight_ref, tokens_ref, d_hidden_ref, gain_ref, input_grad_ref
):
    d_normed = mm(d_qkv_ref[0], weight_ref[0], NT)
    for c in range(1, 3):
        d_normed = d_normed + mm(d_qkv_ref[c], weight_ref[c], NT)
    normal, scale = norm_parts(tokens_ref[...].astype(F32))
    d_part, _ = norm_back(d_normed, gain_ref[...], normal, scale)
    input_grad_ref[...] = d_hidden_ref[...] + d_part


def resume(kernel, ins, done, *refs):
    kernel(*refs[:ins], *refs[ins + done :])


def pair_specs(rows, first=0):
    return {
        "qkv": pl.BlockSpec((3, rows, PAIR), lambda p, s: (0, 0, p + first)),
        "message": pl.BlockSpec((1, HEAD_DIM + TAIL, 3 * PAIR), lambda p, s: (p + first, 0, 0)),
        "start": pl.BlockSpec((rows, PAIR), lambda p, s: (0, 0)),
        "blend": pl.BlockSpec((3, PAIR), lambda p, s: (0, p + first)),
        "column": pl.BlockSpec((rows, PAIR), lambda p, s: (0, p + first)),
        "states": pl.BlockSpec((1, rows // ROWS * PAIR, 3 * PAIR), lambda p, s: (p + first, 0, 0)),
        "sums": pl.BlockSpec((24, PAIR), lambda p, s: (0, p)),
        "query": pl.BlockSpec((1, rows, PAIR), lambda p, s: (0, 0, p)),
        "head_rows": pl.BlockSpec((ROWS, PAIR), lambda p, s: (0, p)),
    }


def call(kernel, ins, outs, out_shapes, scratch, grid, name, flops, moved, aliases={}):
    return pl.pallas_call(
        kernel,
        out_shape=out_shapes,
        grid_spec=pltpu.PrefetchScalarGridSpec(
            num_scalar_prefetch=1,
            grid=(grid,),
            in_specs=ins,
            out_specs=outs,
            scratch_shapes=scratch,
        ),
        input_output_aliases=aliases,
        compiler_params=pltpu.CompilerParams(
            dimension_semantics=("arbitrary",), vmem_limit_bytes=56 * 1024 * 1024
        ),
        cost_estimate=pl.CostEstimate(flops=flops, bytes_accessed=moved, transcendentals=0),
        name=name,
    )


def norm_parts(source):
    centered = source - jnp.mean(source, axis=-1, keepdims=True)
    spread_of = jnp.mean(centered * centered, axis=-1, keepdims=True)
    scale = lax.rsqrt(spread_of + EPS)
    return centered * scale, scale


def norm_back(d_out, gain, normal, scale):
    e = d_out * gain
    inner = jnp.mean(e, axis=-1, keepdims=True)
    along = jnp.mean(e * normal, axis=-1, keepdims=True)
    rows = jnp.sum((d_out * normal).reshape(-1, 8, d_out.shape[1]), axis=0)
    return scale * (e - inner - normal * along), rows


def bits(size):
    return [1 << b for b in range(int(math.log2(size)))]


def phases():
    dp = bits(lax.axis_size("dp"))
    core, rest = dp[:1], dp[1:]
    mid = len(rest) // 2
    far = [("dp", m) for m in rest[mid:]]
    near = [("dp", m) for m in rest[:mid]] + [("head", m) for m in bits(lax.axis_size("head"))]
    groups = []
    for run in (far, near, [("dp", m) for m in core]):
        groups += [run[i : i + 2] for i in range(0, len(run), 2)]
    return groups


def relative_bits():
    return [pair for group in phases() for pair in group]


def all_flips():
    order = relative_bits()
    flips = []
    for index in range(1 << len(order)):
        chosen = [pair for place, pair in enumerate(order) if index >> place & 1]
        flips.append(tuple(sum(m for a, m in chosen if a == axis) for axis in ("dp", "head")))
    return flips


def peer(array, group, combo):
    n_dp, n_head = lax.axis_size("dp"), lax.axis_size("head")
    chosen = [pair for place, pair in enumerate(group) if combo >> place & 1]
    flip_dp = sum(m for axis, m in chosen if axis == "dp")
    flip_head = sum(m for axis, m in chosen if axis == "head")
    pairs = [
        (d * n_head + h, (d ^ flip_dp) * n_head + (h ^ flip_head))
        for d in range(n_dp)
        for h in range(n_head)
    ]
    return lax.ppermute(array, ("dp", "head"), pairs)


def widen(block, group, axis, after=None):
    others = [peer(block, group, combo) for combo in range(1, 1 << len(group))]
    if after is not None:
        others, after = lax.optimization_barrier((others, after))
    whole = jnp.concatenate([block] + others, axis=axis)
    return whole if after is None else (whole, after)


def narrow(keep, gives, group, after=None):
    arrived = [peer(give.astype(BF16), group, combo) for combo, give in enumerate(gives, 1)]
    if after is not None:
        arrived, _ = lax.optimization_barrier((arrived, after))
    return keep.astype(F32) + sum(part.astype(F32) for part in arrived)


def narrow_axis(total, group, axis, after=None):
    parts = jnp.split(total, 1 << len(group), axis=axis)
    return narrow(parts[0], parts[1:], group, after)


def pass_along(local, keep, shift):
    size = lax.axis_size("head")
    pairs = [(i, i + shift) for i in range(size) if 0 <= i + shift < size]
    arrived = lax.ppermute(local, "head", pairs)
    for _ in range(size - 2):
        rows = iota(local.shape, 1) < HEAD_DIM
        total = local.astype(F32) + jnp.where(rows, keep * arrived.astype(F32), 0.0)
        arrived = lax.ppermute(total.astype(BF16), "head", pairs)
    return arrived


def per_device(
    tokens,
    ln1_gain,
    qkv_weight,
    out_weight,
    blend,
    ln2_gain,
    in_weight,
    down_weight,
    cotangent,
    lengths,
):
    rows, width = tokens.shape
    n_dp, n_head = lax.axis_size("dp"), lax.axis_size("head")
    pairs = width // PAIR
    steps = rows // ROWS
    groups = phases()
    flips = all_flips()

    shards = jnp.concatenate([qkv_weight, out_weight.T[None]], axis=0)[None]
    feed = jnp.stack([in_weight, down_weight])
    shards = widen(shards, groups[0], 0)
    feed, _ = lax.optimization_barrier((feed, shards))
    feed = widen(feed, groups[0][:1], 1)
    for group in groups[1:-1]:
        shards = widen(shards, group, 0)
    shards, feed = lax.optimization_barrier((shards, feed))
    others = peer(shards, groups[-1], 1)

    item_lengths = lengths[0]
    slots = item_lengths.shape[0]
    ends = jnp.sum(
        jnp.where(iota((slots, slots), 1) <= iota((slots, slots), 0), item_lengths[None, :], 0),
        axis=1,
    )
    offset = lax.axis_index("head") * rows
    local = jnp.arange(rows, dtype=jnp.int32)
    place = local + offset
    total = ends[slots - 1]
    item_start = jnp.max(
        jnp.where(ends[None, :] <= place[:, None], ends[None, :], 0), axis=1
    )
    start = jnp.where(place < total, item_start - offset, local)
    carried_rows = jnp.sum((start < 0).astype(jnp.int32))
    scalars = jnp.concatenate(
        [
            start.reshape(steps, ROWS)[:, ROWS - TAIL - 1],
            carried_rows[None],
            start[rows - 1 :],
            (total - offset)[None],
            lax.axis_index("dp").astype(jnp.int32)[None],
            lax.axis_index("head").astype(jnp.int32)[None],
        ]
    )
    start_wide = jnp.broadcast_to(start[:, None], (rows, PAIR))
    row_wide = jnp.broadcast_to(local[:, None], (rows, PAIR))
    bias, far, tally = masks(row_wide, start_wide, row_wide // ROWS * ROWS - TAIL)
    tables = (bias.astype(BF16), far.astype(BF16), tally)
    keep_all = (start[rows - 1] < 0).astype(F32)
    blend_wide = jnp.repeat(blend, HEAD_DIM, axis=1)

    spec = pair_specs(rows)
    wide = jax.ShapeDtypeStruct((rows, width), F32)
    states_shape = jax.ShapeDtypeStruct((pairs, steps * PAIR, 3 * PAIR), BF16)
    message_shape = jax.ShapeDtypeStruct((pairs, HEAD_DIM + TAIL, 3 * PAIR), BF16)
    big = rows * width
    part = rows // 3

    def whole_spec(shape):
        return pl.BlockSpec(shape, lambda p, s: (0,) * len(shape))

    others, start_wide, tables = lax.optimization_barrier((others, start_wide, tables))
    qkv, normed_one, qkv_all, out_all, closing = call(
        functools.partial(project_kernel, flips=flips),
        [
            pl.BlockSpec((part, width), lambda p, s: (p, 0)),
            whole_spec((1, width)),
            whole_spec(shards.shape),
            whole_spec(shards.shape),
        ],
        [
            pl.BlockSpec((3, part, width), lambda p, s: (0, p, 0)),
            pl.BlockSpec((part, width), lambda p, s: (p, 0)),
            whole_spec((3, width, width)),
            whole_spec((width, width)),
            whole_spec(message_shape.shape),
        ],
        [
            jax.ShapeDtypeStruct((3, rows, width), BF16),
            jax.ShapeDtypeStruct((rows, width), BF16),
            jax.ShapeDtypeStruct((3, width, width), BF16),
            jax.ShapeDtypeStruct((width, width), BF16),
            message_shape,
        ],
        [
            pltpu.VMEM((pairs, PAIR, 3 * PAIR), F32),
            pltpu.VMEM((n_head, 4, n_dp, width // n_dp, width // n_head), BF16),
        ],
        3,
        "project",
        6 * big * width,
        12 * big,
    )(scalars, tokens, ln1_gain[None], shards, others)
    for pair in groups[0][1:]:
        feed, _ = widen(feed, [pair], 1, closing)
    message = pass_along(closing, keep_all, 1)

    key_scratch = pltpu.VMEM((rows + TAIL, PAIR), BF16)
    state_scratch = pltpu.VMEM((PAIR, 3 * PAIR), F32)
    tail_scratch = pltpu.VMEM((TAIL, PAIR), F32)
    results = ()
    most = pairs - pairs // 4
    for first, count in ((0, most), (most, pairs - most)):
        spec = pair_specs(rows, first)
        results = call(
            functools.partial(resume, forward_kernel, 7, len(results)),
            [spec["qkv"], spec["message"]]
            + [spec["start"]] * 3
            + [spec["blend"]]
            + [pl.BlockSpec(memory_space=pl.ANY)] * len(results),
            [spec["column"]] * 6 + [spec["states"]],
            [jax.ShapeDtypeStruct((rows, width), BF16)] + [wide] * 5 + [states_shape],
            [key_scratch, key_scratch, state_scratch],
            count,
            "forward",
            8000 * big * count // pairs,
            40 * big * count // pairs,
            {7 + i: i for i in range(len(results))},
        )(scalars, qkv, message, *tables, blend_wide, *results)
        if not first:
            feed, results = widen(feed, groups[1], 1, results)
            feed, message = lax.optimization_barrier((feed, message))
    for group in groups[2:-1]:
        feed = widen(feed, group, 1)
    feed_other = peer(feed, groups[-1], 1)
    mixed, near, far1, far2, inv_l, inv_d, states = results

    spec = pair_specs(rows)
    low = jax.ShapeDtypeStruct((rows, width), BF16)
    row_spec = pl.BlockSpec((part, width), lambda p, s: (p, 0))
    hidden_units = 2 * feed.shape[1]
    unit_spec = pl.BlockSpec((part, hidden_units), lambda p, s: (p, 0))
    unit_shape = jax.ShapeDtypeStruct((rows, hidden_units), BF16)
    sums_shape = jax.ShapeDtypeStruct((8, width), F32)
    layer_out, d_hidden, d_branch, d_mixed, normed_two, active, d_inner, gain_two_rows = call(
        feed_kernel,
        [row_spec] * 3
        + [
            whole_spec((width, width)),
            whole_spec((1, width)),
            whole_spec(feed.shape),
            whole_spec(feed.shape),
        ],
        [row_spec] * 5 + [unit_spec] * 2 + [whole_spec((8, width))],
        [low, wide, low, low, low, unit_shape, unit_shape, sums_shape],
        [],
        3,
        "feed",
        8 * big * hidden_units,
        32 * big,
    )(scalars, mixed, tokens, cotangent, out_all, ln2_gain[None], feed, feed_other)

    back = call(
        prologue_kernel,
        [
            spec["query"],
            pl.BlockSpec((1, ROWS, PAIR), lambda p, s: (1, 0, p)),
            pl.BlockSpec((1, ROWS, PAIR), lambda p, s: (2, 0, p)),
            spec["message"],
            spec["start"],
            spec["blend"],
            spec["column"],
            spec["head_rows"],
            spec["column"],
            spec["head_rows"],
            spec["column"],
        ],
        spec["message"],
        message_shape,
        [state_scratch],
        pairs,
        "prologue",
        500 * big,
        20 * big,
    )(scalars, qkv, qkv, qkv, message, start_wide, blend_wide, d_mixed, near, far1, inv_l, inv_d)
    d_inner, _ = lax.optimization_barrier((d_inner, back))
    back_in = pass_along(back, keep_all, -1)

    unit = hidden_units // 4
    half_shape = (2, 2 * unit, width)
    whole_rows = whole_spec((rows, width))

    def feed_grad(place, kind, d_inner, more_ins, more_in_specs, more_outs, more_out_specs):
        columns = pl.BlockSpec((rows, unit), lambda p, s: (0, p + 2 * place))
        return call(
            feed_grad_kernel,
            [whole_rows] * 2 + [columns] * 2 + more_in_specs,
            more_out_specs + [pl.BlockSpec((2, unit, width), lambda p, s: (0, p, 0))],
            more_outs + [jax.ShapeDtypeStruct(half_shape, kind)],
            [],
            2,
            "feed_grad",
            2 * big * hidden_units,
            12 * big,
        )(scalars, normed_two, cotangent, active, d_inner, *more_ins)

    (give,) = feed_grad(1, BF16, d_inner, [], [], [], [])
    d_inner, _ = lax.optimization_barrier((d_inner, give))
    out_grad, keep = feed_grad(
        0,
        F32,
        d_inner,
        [mixed, d_branch],
        [whole_rows] * 2,
        [jax.ShapeDtypeStruct((width, width), F32)],
        [whole_spec((width, width))],
    )
    feed_share = narrow(keep, [give], groups[-1])
    left = list(reversed(groups[:-1]))
    _, back_in = lax.optimization_barrier((feed_share, back_in))
    feed_share = narrow_axis(feed_share, left.pop(0), 1)

    d_qkv = jnp.zeros((3, 8, PAIR), BF16)
    sums = []
    first = 0
    for count in (most, pairs - most):
        spec = pair_specs(rows, first)
        more = {15: 0} if first else {}
        d_qkv, part_sums = call(
            backward_kernel,
            [spec["qkv"], spec["message"]]
            + [spec["start"]] * 3
            + [spec["blend"]]
            + [spec["column"]] * 6
            + [spec["states"], spec["message"], pl.BlockSpec(memory_space=pl.ANY)],
            [spec["qkv"], spec["sums"]],
            [
                jax.ShapeDtypeStruct((3, rows, width), BF16),
                jax.ShapeDtypeStruct((24, count * PAIR), F32),
            ],
            [key_scratch, key_scratch, state_scratch, tail_scratch, tail_scratch],
            count,
            "backward",
            16000 * big * count // pairs,
            40 * big * count // pairs,
            more,
        )(
            scalars,
            qkv,
            message,
            *tables,
            blend_wide,
            d_mixed,
            near,
            far1,
            far2,
            inv_l,
            inv_d,
            states,
            back_in,
            d_qkv,
        )
        sums.append(part_sums)
        first += count
        if left and first < pairs:
            _, back_in = lax.optimization_barrier((feed_share, back_in))
            feed_share = narrow_axis(feed_share, left.pop(0), 1)
    for group in left:
        feed_share = narrow_axis(feed_share, group, 1)
    feed_share, d_qkv = lax.optimization_barrier((feed_share, d_qkv))
    sums = jnp.concatenate(sums, axis=1)
    blend_part = jnp.sum(sums.reshape(3, 8, blend.shape[1], HEAD_DIM), axis=(1, 3))

    shard_shape = (n_dp * n_head // 2, 4, width // n_dp, width // n_head)
    shard_spec = pl.BlockSpec((shard_shape[0], 1) + shard_shape[2:], lambda p, s: (0, p, 0, 0))
    keep, give, gain_one_rows = call(
        functools.partial(weight_grad_kernel, flips=flips),
        [
            whole_spec((rows, width)),
            pl.BlockSpec((1, rows, width), lambda p, s: (jnp.minimum(p, 2), 0, 0)),
            whole_spec((width, width)),
            pl.BlockSpec((1, width, width), lambda p, s: (jnp.minimum(p, 2), 0, 0)),
        ],
        [shard_spec, shard_spec, whole_spec((8, width))],
        [
            jax.ShapeDtypeStruct(shard_shape, F32),
            jax.ShapeDtypeStruct(shard_shape, BF16),
            sums_shape,
        ],
        [pltpu.VMEM((n_head, n_dp, width // n_dp, width // n_head), F32)],
        4,
        "weight_grad",
        6 * big * width,
        8 * big,
    )(scalars, normed_one, d_qkv, out_grad, qkv_all)
    parts = [gain_one_rows[0] / ln1_gain, jnp.sum(gain_two_rows, axis=0), blend_part.reshape(-1)]
    total_sums = jnp.concatenate(parts)[None]
    share = narrow(keep, [give], groups[-1])
    hops = list(reversed(relative_bits()))
    total_sums = total_sums + peer(total_sums, [hops[0]], 1)
    total_sums, d_qkv, _ = lax.optimization_barrier((total_sums, d_qkv, share))
    total_sums = total_sums + peer(total_sums, [hops[1]], 1)
    input_grad = call(
        input_kernel,
        [
            pl.BlockSpec((3, part, width), lambda p, s: (0, p, 0)),
            whole_spec((3, width, width)),
            row_spec,
            row_spec,
            whole_spec((1, width)),
        ],
        row_spec,
        wide,
        [],
        3,
        "input",
        6 * big * width,
        24 * big,
    )(scalars, d_qkv, qkv_all, tokens, d_hidden, ln1_gain[None])
    share = narrow_axis(share, groups[-2], 0, input_grad)
    total_sums, _ = lax.optimization_barrier((total_sums, input_grad))
    total_sums = total_sums + peer(total_sums, [hops[2]], 1)
    for group in reversed(groups[:-2]):
        parts = jnp.split(share, 1 << len(group), axis=0)
        gives = [part.astype(BF16) for part in parts[1:]]
        total_sums, _ = lax.optimization_barrier((total_sums, gives))
        share = narrow(parts[0], gives, group)
    for pair in hops[3:]:
        total_sums = total_sums + peer(total_sums, [pair], 1)
    total_sums = total_sums[0]
    gain_one, gain_two = total_sums[:width], total_sums[width : 2 * width]
    blend_sum = total_sums[2 * width :].reshape(blend.shape)
    qkv_share, out_share = share[0, :3], share[0, 3].T
    in_share, down_share = feed_share[0], feed_share[1]
    return (
        layer_out,
        input_grad,
        gain_one,
        qkv_share,
        out_share,
        blend_sum,
        gain_two,
        in_share,
        down_share,
    )


def solution(mesh):
    return jax.shard_map(
        per_device,
        mesh=mesh,
        in_specs=(
            P(("dp", "head"), None),
            P(),
            P(None, "dp", "head"),
            P("head", "dp"),
            P(),
            P(),
            P(("dp", "head"), None),
            P(("dp", "head"), None),
            P(("dp", "head"), None),
            P("dp", None),
        ),
        out_specs=(
            P(("dp", "head"), None),
            P(("dp", "head"), None),
            P(),
            P(None, "dp", "head"),
            P("head", "dp"),
            P(),
            P(),
            P(("dp", "head"), None),
            P(("dp", "head"), None),
        ),
        check_vma=False,
    )
```

```python
import functools
import math

import jax
import jax.numpy as jnp
from jax import lax
from jax.experimental import pallas as pl
from jax.experimental.pallas import tpu as pltpu
from jax.sharding import PartitionSpec as P

HEAD_DIM = 64
BAND = 30
ROWS = 96
TAIL = 32
WIN = ROWS + TAIL
PAIR = 2 * HEAD_DIM
EPS = 1e-05
NEG = -1e30
CARRIED, LAST, VALID, ROW_AT, COLUMN_AT = range(-5, 0)
F32 = jnp.float32
BF16 = jnp.bfloat16
NT = (((1,), (1,)), ((), ()))
TN = (((0,), (0,)), ((), ()))
NN = (((1,), (0,)), ((), ()))


def mm(left, right, dims=NN):
    return lax.dot_general(left, right, dims, preferred_element_type=F32)


def iota(shape, axis):
    return lax.broadcasted_iota(jnp.int32, shape, axis)


def lift(values):
    return jnp.where(values > 0, values + 1.0, jnp.exp(jnp.minimum(values, 0.0)))


def head_lanes(dtype):
    first = (iota((1, PAIR), 1) < HEAD_DIM).astype(F32)
    return first.astype(dtype), (1.0 - first).astype(dtype)


def split_heads(block):
    first, second = head_lanes(block.dtype)
    return jnp.concatenate([block * first, block * second], axis=0)


def same_head():
    return (iota((PAIR, PAIR), 0) < HEAD_DIM) == (iota((PAIR, PAIR), 1) < HEAD_DIM)


def block_only(wide):
    keep = same_head()
    parts = [
        jnp.where(keep, wide[:, p * PAIR : (p + 1) * PAIR], 0.0)
        for p in range(wide.shape[1] // PAIR)
    ]
    return jnp.concatenate(parts, axis=1)


def fold(tall):
    half = tall.shape[0] // 2
    lanes = iota((half, PAIR), 1) < HEAD_DIM
    return jnp.where(lanes, tall[:half], tall[half:])


def two(half):
    return jnp.concatenate([half, half], axis=1)


def masks(row, start, first):
    key = iota(row.shape, 1) + first
    floor = jnp.maximum(first, 0)
    causal = key <= row
    near = causal & (key >= jnp.maximum(start, row - (BAND - 1)))
    far = causal & (key >= jnp.maximum(start, floor))
    count = 1.0 / (row - start + 1).astype(F32)
    return jnp.where(near, 0.0, NEG), far.astype(F32), jnp.where(start < floor, -count, count)


def near_scores(query, key_heads):
    return mm(query * jnp.asarray(HEAD_DIM**-0.5, BF16), key_heads, NT)


def near_weights(scores, bias):
    parts = []
    for h in range(2):
        part = scores[:, h * WIN : (h + 1) * WIN] + bias
        parts.append(jnp.exp(part - jnp.max(part, axis=1, keepdims=True)))
    return jnp.concatenate(parts, axis=1)


def spread(product):
    first = iota(product.shape, 1) < HEAD_DIM
    sums = [
        jnp.sum(jnp.where(keep, product, 0.0), axis=1, keepdims=True) for keep in (first, ~first)
    ]
    return jnp.concatenate([jnp.broadcast_to(part, (ROWS, WIN)) for part in sums], axis=1)


def load_keys(qkv_ref, message_ref, keys, values):
    rows = qkv_ref.shape[1]
    keys[pl.ds(0, TAIL), :] = message_ref[0, pl.ds(HEAD_DIM, TAIL), :PAIR]
    keys[pl.ds(TAIL, rows), :] = qkv_ref[1]
    values[pl.ds(0, TAIL), :] = message_ref[0, pl.ds(HEAD_DIM, TAIL), PAIR : 2 * PAIR]
    values[pl.ds(TAIL, rows), :] = qkv_ref[2]


def fold_state(wide):
    kept = block_only(wide)
    return (kept[:HEAD_DIM] + kept[HEAD_DIM:]).astype(BF16)


def unfold_state(message):
    half = message[:HEAD_DIM].astype(F32)
    return block_only(jnp.concatenate([half, half], axis=0))


def project_kernel(
    scalars,
    tokens_ref,
    gain_ref,
    own_ref,
    other_ref,
    qkv_ref,
    normed_ref,
    weight_ref,
    out_weight_ref,
    message_ref,
    state,
    placed,
    *,
    flips,
):
    step = pl.program_id(0)
    rows, width = tokens_ref.shape
    pairs = width // PAIR
    half, _, tall, wide = own_ref.shape
    last = jnp.maximum(scalars[scalars.shape[0] + LAST], 0)

    @pl.when(step == 0)
    def _():
        for index, (flip_row, flip_column) in enumerate(flips):
            row = scalars[scalars.shape[0] + ROW_AT] ^ flip_row
            column = scalars[scalars.shape[0] + COLUMN_AT] ^ flip_column
            piece = own_ref[index] if index < half else other_ref[index - half]
            for c in range(4):
                placed[column, c, row] = piece[c]
        for h in range(width // wide):
            at = pl.ds(h * wide, wide)
            weight_ref[:, :, at] = placed[h, :3].reshape(3, width, wide)
            out_weight_ref[:, at] = placed[h, 3].reshape(width, wide)
        state[...] = jnp.zeros(state.shape, F32)

    normed = (norm_parts(tokens_ref[...].astype(F32))[0] * gain_ref[...]).astype(BF16)
    normed_ref[...] = normed
    for c in (1, 2, 0):
        qkv_ref[c] = mm(normed, weight_ref[c]).astype(BF16)
    live = iota((rows, PAIR), 0) + step * rows >= last
    ones = jnp.ones((rows, PAIR), BF16)
    for p in range(pairs):
        at = pl.ds(p * PAIR, PAIR)
        key = qkv_ref[1, :, at].astype(F32)
        value = qkv_ref[2, :, at]
        lifted = jnp.where(live, lift(key), 0.0).astype(BF16)
        bent = jnp.where(live, jnp.tanh(key), 0.0).astype(BF16)
        state[p, :, : 2 * PAIR] += mm(lifted, jnp.concatenate([value, ones], axis=1), TN)
        state[p, :, 2 * PAIR :] += mm(bent, value, TN)

    @pl.when(step == pl.num_programs(0) - 1)
    def _():
        for p in range(pairs):
            at = pl.ds(p * PAIR, PAIR)
            message_ref[p, pl.ds(0, HEAD_DIM), :] = fold_state(state[p])
            message_ref[p, pl.ds(HEAD_DIM, TAIL), :] = jnp.concatenate(
                [
                    qkv_ref[1, pl.ds(rows - TAIL, TAIL), at],
                    qkv_ref[2, pl.ds(rows - TAIL, TAIL), at],
                    jnp.zeros((TAIL, PAIR), BF16),
                ],
                axis=1,
            )


def weight_grad_kernel(
    scalars,
    normed_ref,
    d_qkv_ref,
    out_grad_ref,
    weight_ref,
    keep_ref,
    give_ref,
    gain_ref,
    whole,
    *,
    flips,
):
    c = pl.program_id(0)
    half, _, tall, wide = keep_ref.shape

    def place(total):
        for h in range(total.shape[1] // wide):
            part = total[:, h * wide : (h + 1) * wide]
            whole[h] = part.reshape(whole.shape[1:])

    @pl.when(c == 0)
    def _():
        gain_ref[...] = jnp.zeros(gain_ref.shape, F32)

    @pl.when(c < 3)
    def _():
        total = mm(normed_ref[...], d_qkv_ref[0], TN)
        place(total)
        product = total * weight_ref[0].astype(F32)
        high = product.astype(BF16)
        low = (product - high.astype(F32)).astype(BF16)
        ones = jnp.ones((8, product.shape[1]), BF16)
        gain_ref[...] += mm(ones, high, NT) + mm(ones, low, NT)

    @pl.when(c == 3)
    def _():
        place(out_grad_ref[...])

    for index, (flip_row, flip_column) in enumerate(flips):
        row = scalars[scalars.shape[0] + ROW_AT] ^ flip_row
        column = scalars[scalars.shape[0] + COLUMN_AT] ^ flip_column
        if index < half:
            keep_ref[index, 0] = whole[column, row]
        else:
            give_ref[index - half, 0] = whole[column, row].astype(BF16)


def forward_kernel(
    scalars,
    qkv_ref,
    message_ref,
    bias_ref,
    far_ref,
    tally_ref,
    blend_ref,
    att_ref,
    near_ref,
    far1_ref,
    far2_ref,
    invl_ref,
    invd_ref,
    states_ref,
    keys,
    values,
    state,
):
    rows = qkv_ref.shape[1]
    load_keys(qkv_ref, message_ref, keys, values)
    state[...] = unfold_state(message_ref[0])
    count_valid = scalars[scalars.shape[0] + VALID]
    b0, b1, b2 = (blend_ref[pl.ds(f, 1), :] for f in range(3))

    def begin(step):
        at = pl.multiple_of(step * ROWS, 32)
        query = qkv_ref[0, pl.ds(at, ROWS), :]
        key = keys[pl.ds(at, WIN), :]
        value = values[pl.ds(at, WIN), :]
        first = step * ROWS - TAIL
        floor = jnp.maximum(first, 0)
        tally = tally_ref[pl.ds(at, ROWS), :]
        carried = tally < 0.0
        far_two = two(far_ref[pl.ds(at, ROWS), :].astype(F32))
        query_f = query.astype(F32)
        key_f = key.astype(F32)
        lift_qf, bend_qf = lift(query_f), jnp.tanh(query_f)
        lift_q, bend_q = lift_qf.astype(BF16), bend_qf.astype(BF16)
        lift_k = lift(key_f)
        bend_k = jnp.tanh(key_f)
        ones = jnp.ones((WIN, PAIR), BF16)
        value_heads = jnp.concatenate([split_heads(value), split_heads(ones)], axis=1)
        before = state[...]
        before_low = before.astype(BF16)
        scores = near_scores(query, split_heads(key))
        pair_weight = mm(lift_q, split_heads(lift_k.astype(BF16)), NT)
        pair_bend = mm(bend_q, split_heads(bend_k.astype(BF16)), NT)
        elu_state = mm(
            jnp.where(carried, lift_qf, 0.0).astype(BF16), before_low[:, : 2 * PAIR]
        )
        tanh_state = mm(jnp.where(carried, bend_qf, 0.0).astype(BF16), before_low[:, 2 * PAIR :])
        states_ref[0, pl.ds(pl.multiple_of(step * PAIR, PAIR), PAIR), :] = before_low
        closing = scalars[step]
        live = iota((ROWS, PAIR), 0) + first >= jnp.maximum(closing, floor)
        lifted = jnp.where(live, lift_k[:ROWS], 0.0).astype(BF16)
        bent = jnp.where(live, bend_k[:ROWS], 0.0).astype(BF16)
        with_ones = jnp.concatenate([value[:ROWS], ones[:ROWS]], axis=1)
        added = jnp.concatenate([mm(lifted, with_ones, TN), mm(bent, value[:ROWS], TN)], axis=1)
        keep = (closing < floor).astype(F32)
        state[...] = keep * before + block_only(added)
        def finish():
            low_weight = (pair_weight * far_two).astype(BF16)
            low_bend = (pair_bend * far_two).astype(BF16)
            elu_out = mm(low_weight, value_heads)
            tanh_out = mm(low_bend, value_heads[:, :PAIR]) + tanh_state
            weights = near_weights(scores, bias_ref[pl.ds(at, ROWS), :].astype(F32)).astype(BF16)
            near_out = mm(weights, value_heads)
            numerator = elu_out[:, :PAIR] + elu_state[:, :PAIR]
            inv_d = 1.0 / (elu_out[:, PAIR:] + elu_state[:, PAIR:])
            far1 = numerator * inv_d
            inv_l = 1.0 / near_out[:, PAIR:]
            near = near_out[:, :PAIR] * inv_l
            far2 = tanh_out * jnp.abs(tally)
            row = iota((ROWS, PAIR), 0) + at
            mixed = jnp.where(row < count_valid, b0 * near + b1 * far1 + b2 * far2, 0.0)
            att_ref[pl.ds(at, ROWS), :] = mixed.astype(BF16)
            near_ref[pl.ds(at, ROWS), :] = near
            far1_ref[pl.ds(at, ROWS), :] = far1
            far2_ref[pl.ds(at, ROWS), :] = far2
            invl_ref[pl.ds(at, ROWS), :] = inv_l
            invd_ref[pl.ds(at, ROWS), :] = inv_d

        return finish

    def body(both, carry):
        finishes = [begin(both * 2 + half) for half in range(2)]
        for finish in finishes:
            finish()
        return carry

    lax.fori_loop(0, rows // ROWS // 2, body, 0, unroll=2)


def near_back(scores, grad_pair, bias, spread_near):
    weights = near_weights(scores, bias)
    return weights.astype(BF16), (weights * (grad_pair - spread_near)).astype(BF16)


def prologue_kernel(
    scalars,
    query_ref,
    key_ref,
    value_ref,
    message_ref,
    start_ref,
    blend_ref,
    grad_ref,
    near_ref,
    far1_ref,
    invl_ref,
    invd_ref,
    back_ref,
):
    rows = query_ref.shape[1]
    step_rows = rows // 3
    b0, b1, b2 = (blend_ref[pl.ds(f, 1), :] for f in range(3))

    tails = message_ref[0, pl.ds(HEAD_DIM, TAIL), :]
    key = jnp.concatenate([tails[:, :PAIR], key_ref[0]], axis=0)
    value = jnp.concatenate([tails[:, PAIR : 2 * PAIR], value_ref[0]], axis=0)
    start = start_ref[pl.ds(0, ROWS), :]
    row = iota((ROWS, WIN), 0)
    bias, _, _ = masks(row, start, -TAIL)
    query = query_ref[0, pl.ds(0, ROWS), :]
    grad = grad_ref[pl.ds(0, ROWS), :]
    grad_f = grad.astype(F32)
    scale = b0 * invl_ref[...]
    rows_q = (query.astype(F32) * (scale * HEAD_DIM**-0.5)).astype(BF16)
    rows_g = (grad_f * scale).astype(BF16)
    scores = near_scores(query, split_heads(key))
    grad_pair = mm(grad, split_heads(value), NT)
    spread_near = spread(grad_f * near_ref[...])
    heads = same_head().astype(F32).astype(BF16)
    heads = jnp.concatenate([heads, heads], axis=0)

    total = jnp.zeros((PAIR, 3 * PAIR), F32)
    for step in range(3):
        here = pl.ds(step * step_rows, step_rows)
        row = iota((step_rows, PAIR), 0) + step * step_rows
        start = start_ref[here, :]
        all_grad = grad_ref[here, :]
        product = all_grad.astype(F32) * far1_ref[here, :]
        high = product.astype(BF16)
        low = (product - high.astype(F32)).astype(BF16)
        along = mm(jnp.concatenate([high, low], axis=1), heads).astype(BF16)
        query_f = query_ref[0, here, :].astype(F32)
        live = start < 0
        scaled = jnp.where(live, lift(query_f) * (b1 * invd_ref[here, :]), 0.0)
        bent = jnp.where(live, jnp.tanh(query_f) * (b2 / (row - start + 1).astype(F32)), 0.0)
        from_lift = mm(scaled.astype(BF16), jnp.concatenate([all_grad, along], axis=1), TN)
        from_bend = mm(bent.astype(BF16), all_grad, TN)
        total = total + jnp.concatenate([from_lift, from_bend], axis=1)

    weights, shifted = near_back(scores, grad_pair, bias, spread_near)
    d_key = fold(mm(shifted, rows_q, TN))
    back_ref[0, pl.ds(HEAD_DIM, TAIL), :] = jnp.concatenate(
        [d_key[:TAIL], fold(mm(weights, rows_g, TN))[:TAIL], jnp.zeros((TAIL, PAIR), F32)], axis=1
    ).astype(BF16)
    back_ref[0, pl.ds(0, HEAD_DIM), :] = fold_state(total)


def key_side(adjoint_low, lift_k, bend_k, value):
    ones = jnp.full(value.shape, -1.0 / HEAD_DIM, BF16)
    d_lift = mm(jnp.concatenate([value, ones], axis=1), adjoint_low[:, : 2 * PAIR], NT)
    d_bend = mm(value, adjoint_low[:, 2 * PAIR :], NT)
    both = jnp.concatenate([adjoint_low[:, :PAIR], adjoint_low[:, 2 * PAIR :]], axis=0)
    d_value = mm(jnp.concatenate([lift_k, bend_k], axis=1), both)
    return d_lift, d_bend, d_value


def backward_kernel(
    scalars,
    qkv_ref,
    message_ref,
    bias_ref,
    far_ref,
    tally_ref,
    blend_ref,
    grad_ref,
    near_ref,
    far1_ref,
    far2_ref,
    invl_ref,
    invd_ref,
    states_ref,
    back_ref,
    done_ref,
    out_ref,
    sums_ref,
    keys,
    values,
    adjoint,
    key_carry,
    value_carry,
):
    rows = qkv_ref.shape[1]
    steps = rows // ROWS
    load_keys(qkv_ref, message_ref, keys, values)
    last = scalars[scalars.shape[0] + LAST]
    b0, b1, b2 = (blend_ref[pl.ds(f, 1), :] for f in range(3))
    lanes = iota((ROWS, PAIR), 1) < HEAD_DIM

    arrived = unfold_state(back_ref[0])
    tail_grads = back_ref[0, pl.ds(HEAD_DIM, TAIL), :].astype(F32)
    end_key = keys[pl.ds(rows, TAIL), :].astype(F32)
    end_lift, end_bend = lift(end_key), jnp.tanh(end_key)
    end_parts = key_side(
        arrived.astype(BF16), end_lift.astype(BF16), end_bend.astype(BF16), values[pl.ds(rows, TAIL), :]
    )
    live = iota((TAIL, PAIR), 0) + (rows - TAIL) >= last
    key_carry[...] = tail_grads[:, :PAIR] + jnp.where(
        live,
        end_parts[0] * jnp.minimum(end_lift, 1.0) + end_parts[1] * (1.0 - end_bend * end_bend),
        0.0,
    )
    value_carry[...] = tail_grads[:, PAIR : 2 * PAIR] + jnp.where(live, end_parts[2], 0.0)
    adjoint[...] = jnp.where(last < rows - TAIL, 1.0, 0.0) * arrived
    sums_ref[...] = jnp.zeros(sums_ref.shape, F32)

    def add_up(place, product):
        sums_ref[pl.ds(place, 8), :] += jnp.sum(product.reshape(ROWS // 8, 8, PAIR), axis=0)

    def begin(back):
        step = steps - 1 - back
        at = pl.multiple_of(step * ROWS, 32)
        query = qkv_ref[0, pl.ds(at, ROWS), :]
        key = keys[pl.ds(at, WIN), :]
        value = values[pl.ds(at, WIN), :]
        first = step * ROWS - TAIL
        floor = jnp.maximum(first, 0)
        tally = tally_ref[pl.ds(at, ROWS), :]
        carried = tally < 0.0
        far_two = two(far_ref[pl.ds(at, ROWS), :].astype(F32))
        grad = grad_ref[pl.ds(at, ROWS), :]
        grad_f = grad.astype(F32)
        query_f = query.astype(F32)
        key_f = key.astype(F32)
        lift_qf, bend_qf = lift(query_f), jnp.tanh(query_f)
        lift_kf, bend_kf = lift(key_f), jnp.tanh(key_f)
        lift_q, bend_q = lift_qf.astype(BF16), bend_qf.astype(BF16)
        lift_k, bend_k = lift_kf.astype(BF16), bend_kf.astype(BF16)
        lift_heads, bend_heads = split_heads(lift_k), split_heads(bend_k)
        r0 = b0 * invl_ref[pl.ds(at, ROWS), :]
        r1 = b1 * invd_ref[pl.ds(at, ROWS), :]
        r2 = b2 * jnp.abs(tally)
        key_heads = split_heads(key)
        before = states_ref[0, pl.ds(pl.multiple_of(step * PAIR, PAIR), PAIR), :]
        near_product = grad_f * near_ref[pl.ds(at, ROWS), :]
        far1_product = grad_f * far1_ref[pl.ds(at, ROWS), :]
        grad_pair = mm(grad, split_heads(value), NT)
        scores = near_scores(query, key_heads)
        pair_weight = mm(lift_q, lift_heads, NT)
        pair_bend = mm(bend_q, bend_heads, NT)
        state_bend = mm(grad, before[:, 2 * PAIR :], NT)
        spread_far = spread(far1_product)
        spread_near = spread(near_product)
        along = jnp.where(lanes, spread_far[:, :WIN], spread_far[:, WIN:])
        scaled_along = (along * (-1.0 / HEAD_DIM)).astype(BF16)
        state_lift = mm(jnp.concatenate([grad, scaled_along], axis=1), before[:, : 2 * PAIR], NT)
        after = adjoint[...]
        parts = key_side(after.astype(BF16), lift_k[:ROWS], bend_k[:ROWS], value[:ROWS])
        rows_q = (query_f * (r0 * HEAD_DIM**-0.5)).astype(BF16)
        rows_a = lift_qf * r1
        rows_t = bend_qf * r2
        from_lift = mm(
            jnp.where(carried, rows_a, 0.0).astype(BF16),
            jnp.concatenate([grad, along.astype(BF16)], axis=1),
            TN,
        )
        from_bend = mm(jnp.where(carried, rows_t, 0.0).astype(BF16), grad, TN)
        closing = scalars[step]
        keep = (closing < floor).astype(F32)
        adjoint[...] = keep * after + block_only(jnp.concatenate([from_lift, from_bend], axis=1))
        add_up(0, near_product)
        add_up(8, far1_product)
        add_up(16, grad_f * far2_ref[pl.ds(at, ROWS), :])
        def finish():
            shifted = ((grad_pair - spread_far) * far_two).astype(BF16)
            plain = (grad_pair * far_two).astype(BF16)
            low_weight = (pair_weight * far_two).astype(BF16)
            low_bend = (pair_bend * far_two).astype(BF16)
            weights, shifted_near = near_back(
                scores, grad_pair, bias_ref[pl.ds(at, ROWS), :].astype(F32), spread_near
            )
            d_query = mm(shifted_near, key_heads) * (r0 * HEAD_DIM**-0.5)
            d_query = (
                d_query
                + (mm(shifted, lift_heads) + jnp.where(carried, state_lift, 0.0))
                * (r1 * jnp.minimum(lift_qf, 1.0))
                + (mm(plain, bend_heads) + jnp.where(carried, state_bend, 0.0))
                * (r2 * (1.0 - bend_qf * bend_qf))
            )
            out_ref[0, pl.ds(at, ROWS), :] = d_query.astype(BF16)
            d_key = fold(mm(shifted_near, rows_q, TN))
            d_lift = fold(mm(shifted, rows_a.astype(BF16), TN))
            d_bend = fold(mm(plain, rows_t.astype(BF16), TN))
            d_value = fold(
                mm(
                    jnp.concatenate([weights, low_weight, low_bend], axis=0),
                    jnp.concatenate([grad_f * r0, grad_f * r1, grad_f * r2], axis=0).astype(BF16),
                    TN,
                )
            )
            live = iota((ROWS, PAIR), 0) + first >= jnp.maximum(closing, floor)
            pad = jnp.zeros((TAIL, PAIR), F32)
            d_lift = d_lift + jnp.concatenate([jnp.where(live, parts[0], 0.0), pad], axis=0)
            d_bend = d_bend + jnp.concatenate([jnp.where(live, parts[1], 0.0), pad], axis=0)
            d_value = d_value + jnp.concatenate([jnp.where(live, parts[2], 0.0), pad], axis=0)
            d_key = d_key + d_lift * jnp.minimum(lift_kf, 1.0) + d_bend * (1.0 - bend_kf * bend_kf)
            out_ref[1, pl.ds(at, ROWS), :] = jnp.concatenate(
                [d_key[TAIL:ROWS], d_key[ROWS:] + key_carry[...]], axis=0
            ).astype(BF16)
            out_ref[2, pl.ds(at, ROWS), :] = jnp.concatenate(
                [d_value[TAIL:ROWS], d_value[ROWS:] + value_carry[...]], axis=0
            ).astype(BF16)
            key_carry[...] = d_key[:TAIL]
            value_carry[...] = d_value[:TAIL]

        return finish

    def body(both, carry):
        finishes = [begin(both * 2 + half) for half in range(2)]
        for finish in finishes:
            finish()
        return carry

    lax.fori_loop(0, steps // 2, body, 0, unroll=2)


def feed_kernel(
    scalars,
    mixed_ref,
    tokens_ref,
    cotangent_ref,
    out_weight_ref,
    gain_ref,
    own_ref,
    other_ref,
    layer_ref,
    d_hidden_ref,
    d_branch_ref,
    d_mixed_ref,
    normed_ref,
    active_ref,
    d_inner_ref,
    sums_ref,
):
    c0 = math.sqrt(2.0 / math.pi)
    hidden = tokens_ref[...].astype(F32) + mm(mixed_ref[...], out_weight_ref[...], NT)
    normal, scale = norm_parts(hidden)
    normed = (normal * gain_ref[...]).astype(BF16)
    normed_ref[...] = normed
    cotangent = cotangent_ref[...]
    half, width = own_ref.shape[1:]
    chunk = min(512, half)
    layer = hidden
    d_normed = jnp.zeros(hidden.shape, F32)
    slots = [(ref, first) for ref in (own_ref, other_ref) for first in range(0, half, chunk)]

    def opening(slot):
        ref, first = slot
        into = ref[0, pl.ds(first, chunk), :]
        down = ref[1, pl.ds(first, chunk), :]
        return into, down, mm(normed, into, NT), mm(cotangent, down, NT)

    ready = opening(slots[0])
    for place in range(len(slots)):
        into, down, inner, d_active = ready
        if place + 1 < len(slots):
            ready = opening(slots[place + 1])
        square = inner * inner
        bent = jnp.tanh(inner * (c0 + (c0 * 0.044715) * square))
        gate = 0.5 + 0.5 * bent
        active = (inner * gate).astype(BF16)
        slope = gate + inner * (0.5 - 0.5 * bent * bent) * (c0 + (3.0 * 0.044715 * c0) * square)
        d_inner = (d_active * slope).astype(BF16)
        at = pl.ds(place * chunk, chunk)
        active_ref[:, at] = active
        d_inner_ref[:, at] = d_inner
        layer = layer + mm(active, down)
        d_normed = d_normed + mm(d_inner, into)
    layer_ref[...] = layer.astype(BF16)
    d_part, gain_rows = norm_back(d_normed, gain_ref[...], normal, scale)
    d_hidden = cotangent.astype(F32) + d_part
    d_hidden_ref[...] = d_hidden
    d_branch = d_hidden.astype(BF16)
    d_branch_ref[...] = d_branch
    row = iota(hidden.shape, 0) + pl.program_id(0) * hidden.shape[0]
    d_mixed = mm(d_branch, out_weight_ref[...])
    d_mixed_ref[...] = jnp.where(row < scalars[scalars.shape[0] + VALID], d_mixed, 0.0).astype(BF16)

    @pl.when(pl.program_id(0) == 0)
    def _():
        sums_ref[...] = jnp.zeros(sums_ref.shape, F32)

    sums_ref[...] += gain_rows


def feed_grad_kernel(
    scalars, normed_ref, cotangent_ref, active_ref, d_inner_ref, *refs
):
    refs[-1][0] = mm(d_inner_ref[...], normed_ref[...], TN).astype(refs[-1].dtype)
    refs[-1][1] = mm(active_ref[...], cotangent_ref[...], TN).astype(refs[-1].dtype)
    if len(refs) > 1:
        mixed_ref, d_branch_ref, out_grad_ref, _ = refs

        @pl.when(pl.program_id(0) == 0)
        def _():
            out_grad_ref[...] = mm(d_branch_ref[...], mixed_ref[...], TN)


def input_kernel(
    scalars, d_qkv_ref, weight_ref, tokens_ref, d_hidden_ref, gain_ref, input_grad_ref
):
    d_normed = mm(d_qkv_ref[0], weight_ref[0], NT)
    for c in range(1, 3):
        d_normed = d_normed + mm(d_qkv_ref[c], weight_ref[c], NT)
    normal, scale = norm_parts(tokens_ref[...].astype(F32))
    d_part, _ = norm_back(d_normed, gain_ref[...], normal, scale)
    input_grad_ref[...] = d_hidden_ref[...] + d_part


def resume(kernel, ins, done, *refs):
    kernel(*refs[:ins], *refs[ins + done :])


def pair_specs(rows, first=0):
    return {
        "qkv": pl.BlockSpec((3, rows, PAIR), lambda p, s: (0, 0, p + first)),
        "message": pl.BlockSpec((1, HEAD_DIM + TAIL, 3 * PAIR), lambda p, s: (p + first, 0, 0)),
        "start": pl.BlockSpec((rows, PAIR), lambda p, s: (0, 0)),
        "blend": pl.BlockSpec((3, PAIR), lambda p, s: (0, p + first)),
        "column": pl.BlockSpec((rows, PAIR), lambda p, s: (0, p + first)),
        "states": pl.BlockSpec((1, rows // ROWS * PAIR, 3 * PAIR), lambda p, s: (p + first, 0, 0)),
        "sums": pl.BlockSpec((24, PAIR), lambda p, s: (0, p)),
        "query": pl.BlockSpec((1, rows, PAIR), lambda p, s: (0, 0, p)),
        "head_rows": pl.BlockSpec((ROWS, PAIR), lambda p, s: (0, p)),
    }


def call(kernel, ins, outs, out_shapes, scratch, grid, name, flops, moved, aliases={}):
    return pl.pallas_call(
        kernel,
        out_shape=out_shapes,
        grid_spec=pltpu.PrefetchScalarGridSpec(
            num_scalar_prefetch=1,
            grid=(grid,),
            in_specs=ins,
            out_specs=outs,
            scratch_shapes=scratch,
        ),
        input_output_aliases=aliases,
        compiler_params=pltpu.CompilerParams(
            dimension_semantics=("arbitrary",), vmem_limit_bytes=56 * 1024 * 1024
        ),
        cost_estimate=pl.CostEstimate(flops=flops, bytes_accessed=moved, transcendentals=0),
        name=name,
    )


def norm_parts(source):
    centered = source - jnp.mean(source, axis=-1, keepdims=True)
    spread_of = jnp.mean(centered * centered, axis=-1, keepdims=True)
    scale = lax.rsqrt(spread_of + EPS)
    return centered * scale, scale


def norm_back(d_out, gain, normal, scale):
    e = d_out * gain
    inner = jnp.mean(e, axis=-1, keepdims=True)
    along = jnp.mean(e * normal, axis=-1, keepdims=True)
    rows = jnp.sum((d_out * normal).reshape(-1, 8, d_out.shape[1]), axis=0)
    return scale * (e - inner - normal * along), rows


def bits(size):
    return [1 << b for b in range(int(math.log2(size)))]


def phases():
    dp = bits(lax.axis_size("dp"))
    core, rest = dp[:1], dp[1:]
    mid = len(rest) // 2
    far = [("dp", m) for m in rest[mid:]]
    near = [("dp", m) for m in rest[:mid]] + [("head", m) for m in bits(lax.axis_size("head"))]
    groups = []
    for run in (far, near, [("dp", m) for m in core]):
        groups += [run[i : i + 2] for i in range(0, len(run), 2)]
    return groups


def relative_bits():
    return [pair for group in phases() for pair in group]


def all_flips():
    order = relative_bits()
    flips = []
    for index in range(1 << len(order)):
        chosen = [pair for place, pair in enumerate(order) if index >> place & 1]
        flips.append(tuple(sum(m for a, m in chosen if a == axis) for axis in ("dp", "head")))
    return flips


def peer(array, group, combo):
    n_dp, n_head = lax.axis_size("dp"), lax.axis_size("head")
    chosen = [pair for place, pair in enumerate(group) if combo >> place & 1]
    flip_dp = sum(m for axis, m in chosen if axis == "dp")
    flip_head = sum(m for axis, m in chosen if axis == "head")
    pairs = [
        (d * n_head + h, (d ^ flip_dp) * n_head + (h ^ flip_head))
        for d in range(n_dp)
        for h in range(n_head)
    ]
    return lax.ppermute(array, ("dp", "head"), pairs)


def widen(block, group, axis, after=None):
    others = [peer(block, group, combo) for combo in range(1, 1 << len(group))]
    if after is not None:
        others, after = lax.optimization_barrier((others, after))
    whole = jnp.concatenate([block] + others, axis=axis)
    return whole if after is None else (whole, after)


def narrow(keep, gives, group, after=None):
    arrived = [peer(give.astype(BF16), group, combo) for combo, give in enumerate(gives, 1)]
    if after is not None:
        arrived, _ = lax.optimization_barrier((arrived, after))
    return keep.astype(F32) + sum(part.astype(F32) for part in arrived)


def narrow_axis(total, group, axis, after=None):
    parts = jnp.split(total, 1 << len(group), axis=axis)
    return narrow(parts[0], parts[1:], group, after)


def pass_along(local, keep, shift):
    size = lax.axis_size("head")
    pairs = [(i, i + shift) for i in range(size) if 0 <= i + shift < size]
    arrived = lax.ppermute(local, "head", pairs)
    for _ in range(size - 2):
        rows = iota(local.shape, 1) < HEAD_DIM
        total = local.astype(F32) + jnp.where(rows, keep * arrived.astype(F32), 0.0)
        arrived = lax.ppermute(total.astype(BF16), "head", pairs)
    return arrived


def per_device(
    tokens,
    ln1_gain,
    qkv_weight,
    out_weight,
    blend,
    ln2_gain,
    in_weight,
    down_weight,
    cotangent,
    lengths,
):
    rows, width = tokens.shape
    n_dp, n_head = lax.axis_size("dp"), lax.axis_size("head")
    pairs = width // PAIR
    steps = rows // ROWS
    groups = phases()
    flips = all_flips()

    item_lengths = lengths[0]
    slots = item_lengths.shape[0]
    ends = jnp.sum(
        jnp.where(iota((slots, slots), 1) <= iota((slots, slots), 0), item_lengths[None, :], 0),
        axis=1,
    )
    offset = lax.axis_index("head") * rows
    local = jnp.arange(rows, dtype=jnp.int32)
    place = local + offset
    total = ends[slots - 1]
    item_start = jnp.max(
        jnp.where(ends[None, :] <= place[:, None], ends[None, :], 0), axis=1
    )
    start = jnp.where(place < total, item_start - offset, local)
    carried_rows = jnp.sum((start < 0).astype(jnp.int32))
    scalars = jnp.concatenate(
        [
            start.reshape(steps, ROWS)[:, ROWS - TAIL - 1],
            carried_rows[None],
            start[rows - 1 :],
            (total - offset)[None],
            lax.axis_index("dp").astype(jnp.int32)[None],
            lax.axis_index("head").astype(jnp.int32)[None],
        ]
    )
    shards = jnp.concatenate([qkv_weight, out_weight.T[None]], axis=0)[None]
    feed = jnp.stack([in_weight, down_weight])
    shards = widen(shards, groups[0], 0)
    feed, late, _ = lax.optimization_barrier((feed, start, shards))
    start_wide = jnp.broadcast_to(late[:, None], (rows, PAIR))
    row_wide = jnp.broadcast_to(local[:, None], (rows, PAIR))
    bias, far, tally = masks(row_wide, start_wide, row_wide // ROWS * ROWS - TAIL)
    tables = (bias.astype(BF16), far.astype(BF16), tally)
    feed = widen(feed, groups[0][:1], 1)
    for group in groups[1:-1]:
        shards = widen(shards, group, 0)
    shards, feed, start_wide, tables = lax.optimization_barrier((shards, feed, start_wide, tables))
    others = peer(shards, groups[-1], 1)

    keep_all = (start[rows - 1] < 0).astype(F32)
    blend_wide = jnp.repeat(blend, HEAD_DIM, axis=1)

    spec = pair_specs(rows)
    wide = jax.ShapeDtypeStruct((rows, width), F32)
    states_shape = jax.ShapeDtypeStruct((pairs, steps * PAIR, 3 * PAIR), BF16)
    message_shape = jax.ShapeDtypeStruct((pairs, HEAD_DIM + TAIL, 3 * PAIR), BF16)
    big = rows * width
    part = rows // 3

    def whole_spec(shape):
        return pl.BlockSpec(shape, lambda p, s: (0,) * len(shape))

    qkv, normed_one, qkv_all, out_all, closing = call(
        functools.partial(project_kernel, flips=flips),
        [
            pl.BlockSpec((part, width), lambda p, s: (p, 0)),
            whole_spec((1, width)),
            whole_spec(shards.shape),
            whole_spec(shards.shape),
        ],
        [
            pl.BlockSpec((3, part, width), lambda p, s: (0, p, 0)),
            pl.BlockSpec((part, width), lambda p, s: (p, 0)),
            whole_spec((3, width, width)),
            whole_spec((width, width)),
            whole_spec(message_shape.shape),
        ],
        [
            jax.ShapeDtypeStruct((3, rows, width), BF16),
            jax.ShapeDtypeStruct((rows, width), BF16),
            jax.ShapeDtypeStruct((3, width, width), BF16),
            jax.ShapeDtypeStruct((width, width), BF16),
            message_shape,
        ],
        [
            pltpu.VMEM((pairs, PAIR, 3 * PAIR), F32),
            pltpu.VMEM((n_head, 4, n_dp, width // n_dp, width // n_head), BF16),
        ],
        3,
        "project",
        6 * big * width,
        12 * big,
    )(scalars, tokens, ln1_gain[None], shards, others)
    for pair in groups[0][1:]:
        feed, _ = widen(feed, [pair], 1, closing)
    message = pass_along(closing, keep_all, 1)

    key_scratch = pltpu.VMEM((rows + TAIL, PAIR), BF16)
    state_scratch = pltpu.VMEM((PAIR, 3 * PAIR), F32)
    tail_scratch = pltpu.VMEM((TAIL, PAIR), F32)
    results = ()
    most = pairs - pairs // 4
    for first, count in ((0, most), (most, pairs - most)):
        spec = pair_specs(rows, first)
        results = call(
            functools.partial(resume, forward_kernel, 7, len(results)),
            [spec["qkv"], spec["message"]]
            + [spec["start"]] * 3
            + [spec["blend"]]
            + [pl.BlockSpec(memory_space=pl.ANY)] * len(results),
            [spec["column"]] * 6 + [spec["states"]],
            [jax.ShapeDtypeStruct((rows, width), BF16)] + [wide] * 5 + [states_shape],
            [key_scratch, key_scratch, state_scratch],
            count,
            "forward",
            8000 * big * count // pairs,
            40 * big * count // pairs,
            {7 + i: i for i in range(len(results))},
        )(scalars, qkv, message, *tables, blend_wide, *results)
        if not first:
            feed, results = widen(feed, groups[1], 1, results)
            feed, message = lax.optimization_barrier((feed, message))
    for group in groups[2:-1]:
        feed = widen(feed, group, 1)
    feed_other = peer(feed, groups[-1], 1)
    mixed, near, far1, far2, inv_l, inv_d, states = results

    spec = pair_specs(rows)
    low = jax.ShapeDtypeStruct((rows, width), BF16)
    row_spec = pl.BlockSpec((part, width), lambda p, s: (p, 0))
    hidden_units = 2 * feed.shape[1]
    unit_spec = pl.BlockSpec((part, hidden_units), lambda p, s: (p, 0))
    unit_shape = jax.ShapeDtypeStruct((rows, hidden_units), BF16)
    sums_shape = jax.ShapeDtypeStruct((8, width), F32)
    layer_out, d_hidden, d_branch, d_mixed, normed_two, active, d_inner, gain_two_rows = call(
        feed_kernel,
        [row_spec] * 3
        + [
            whole_spec((width, width)),
            whole_spec((1, width)),
            whole_spec(feed.shape),
            whole_spec(feed.shape),
        ],
        [row_spec] * 5 + [unit_spec] * 2 + [whole_spec((8, width))],
        [low, wide, low, low, low, unit_shape, unit_shape, sums_shape],
        [],
        3,
        "feed",
        8 * big * hidden_units,
        32 * big,
    )(scalars, mixed, tokens, cotangent, out_all, ln2_gain[None], feed, feed_other)

    back = call(
        prologue_kernel,
        [
            spec["query"],
            pl.BlockSpec((1, ROWS, PAIR), lambda p, s: (1, 0, p)),
            pl.BlockSpec((1, ROWS, PAIR), lambda p, s: (2, 0, p)),
            spec["message"],
            spec["start"],
            spec["blend"],
            spec["column"],
            spec["head_rows"],
            spec["column"],
            spec["head_rows"],
            spec["column"],
        ],
        spec["message"],
        message_shape,
        [],
        pairs,
        "prologue",
        500 * big,
        20 * big,
    )(scalars, qkv, qkv, qkv, message, start_wide, blend_wide, d_mixed, near, far1, inv_l, inv_d)
    d_inner, _ = lax.optimization_barrier((d_inner, back))
    back_in = pass_along(back, keep_all, -1)

    unit = hidden_units // 4
    half_shape = (2, 2 * unit, width)
    whole_rows = whole_spec((rows, width))

    def feed_grad(place, kind, d_inner, more_ins, more_in_specs, more_outs, more_out_specs):
        columns = pl.BlockSpec((rows, unit), lambda p, s: (0, p + 2 * place))
        return call(
            feed_grad_kernel,
            [whole_rows] * 2 + [columns] * 2 + more_in_specs,
            more_out_specs + [pl.BlockSpec((2, unit, width), lambda p, s: (0, p, 0))],
            more_outs + [jax.ShapeDtypeStruct(half_shape, kind)],
            [],
            2,
            "feed_grad",
            2 * big * hidden_units,
            12 * big,
        )(scalars, normed_two, cotangent, active, d_inner, *more_ins)

    (give,) = feed_grad(1, BF16, d_inner, [], [], [], [])
    d_inner, _ = lax.optimization_barrier((d_inner, give))
    out_grad, keep = feed_grad(
        0,
        F32,
        d_inner,
        [mixed, d_branch],
        [whole_rows] * 2,
        [jax.ShapeDtypeStruct((width, width), F32)],
        [whole_spec((width, width))],
    )
    feed_share = narrow(keep, [give], groups[-1])
    left = list(reversed(groups[:-1]))
    _, back_in = lax.optimization_barrier((feed_share, back_in))
    feed_share = narrow_axis(feed_share, left.pop(0), 1)

    d_qkv = jnp.zeros((3, 8, PAIR), BF16)
    sums = []
    first = 0
    for count in (most, pairs - most):
        spec = pair_specs(rows, first)
        more = {15: 0} if first else {}
        d_qkv, part_sums = call(
            backward_kernel,
            [spec["qkv"], spec["message"]]
            + [spec["start"]] * 3
            + [spec["blend"]]
            + [spec["column"]] * 6
            + [spec["states"], spec["message"], pl.BlockSpec(memory_space=pl.ANY)],
            [spec["qkv"], spec["sums"]],
            [
                jax.ShapeDtypeStruct((3, rows, width), BF16),
                jax.ShapeDtypeStruct((24, count * PAIR), F32),
            ],
            [key_scratch, key_scratch, state_scratch, tail_scratch, tail_scratch],
            count,
            "backward",
            16000 * big * count // pairs,
            40 * big * count // pairs,
            more,
        )(
            scalars,
            qkv,
            message,
            *tables,
            blend_wide,
            d_mixed,
            near,
            far1,
            far2,
            inv_l,
            inv_d,
            states,
            back_in,
            d_qkv,
        )
        sums.append(part_sums)
        first += count
        if left and first < pairs:
            _, back_in = lax.optimization_barrier((feed_share, back_in))
            feed_share = narrow_axis(feed_share, left.pop(0), 1)
    for group in left:
        feed_share = narrow_axis(feed_share, group, 1)
    feed_share, d_qkv = lax.optimization_barrier((feed_share, d_qkv))
    sums = jnp.concatenate(sums, axis=1)
    blend_part = jnp.sum(sums.reshape(3, 8, blend.shape[1], HEAD_DIM), axis=(1, 3))

    shard_shape = (n_dp * n_head // 2, 4, width // n_dp, width // n_head)
    shard_spec = pl.BlockSpec((shard_shape[0], 1) + shard_shape[2:], lambda p, s: (0, p, 0, 0))
    keep, give, gain_one_rows = call(
        functools.partial(weight_grad_kernel, flips=flips),
        [
            whole_spec((rows, width)),
            pl.BlockSpec((1, rows, width), lambda p, s: (jnp.minimum(p, 2), 0, 0)),
            whole_spec((width, width)),
            pl.BlockSpec((1, width, width), lambda p, s: (jnp.minimum(p, 2), 0, 0)),
        ],
        [shard_spec, shard_spec, whole_spec((8, width))],
        [
            jax.ShapeDtypeStruct(shard_shape, F32),
            jax.ShapeDtypeStruct(shard_shape, BF16),
            sums_shape,
        ],
        [pltpu.VMEM((n_head, n_dp, width // n_dp, width // n_head), F32)],
        4,
        "weight_grad",
        6 * big * width,
        8 * big,
    )(scalars, normed_one, d_qkv, out_grad, qkv_all)
    parts = [gain_one_rows[0] / ln1_gain, jnp.sum(gain_two_rows, axis=0), blend_part.reshape(-1)]
    total_sums = jnp.concatenate(parts)[None]
    share = narrow(keep, [give], groups[-1])
    hops = list(reversed(relative_bits()))
    total_sums = total_sums + peer(total_sums, [hops[0]], 1)
    total_sums, d_qkv, _ = lax.optimization_barrier((total_sums, d_qkv, share))
    total_sums = total_sums + peer(total_sums, [hops[1]], 1)
    input_grad = call(
        input_kernel,
        [
            pl.BlockSpec((3, part, width), lambda p, s: (0, p, 0)),
            whole_spec((3, width, width)),
            row_spec,
            row_spec,
            whole_spec((1, width)),
        ],
        row_spec,
        wide,
        [],
        3,
        "input",
        6 * big * width,
        24 * big,
    )(scalars, d_qkv, qkv_all, tokens, d_hidden, ln1_gain[None])
    share = narrow_axis(share, groups[-2], 0, input_grad)
    total_sums, _ = lax.optimization_barrier((total_sums, input_grad))
    total_sums = total_sums + peer(total_sums, [hops[2]], 1)
    for group in reversed(groups[:-2]):
        parts = jnp.split(share, 1 << len(group), axis=0)
        gives = [part.astype(BF16) for part in parts[1:]]
        total_sums, _ = lax.optimization_barrier((total_sums, gives))
        share = narrow(parts[0], gives, group)
    for pair in hops[3:]:
        total_sums = total_sums + peer(total_sums, [pair], 1)
    total_sums = total_sums[0]
    gain_one, gain_two = total_sums[:width], total_sums[width : 2 * width]
    blend_sum = total_sums[2 * width :].reshape(blend.shape)
    qkv_share, out_share = share[0, :3], share[0, 3].T
    in_share, down_share = feed_share[0], feed_share[1]
    return (
        layer_out,
        input_grad,
        gain_one,
        qkv_share,
        out_share,
        blend_sum,
        gain_two,
        in_share,
        down_share,
    )


def solution(mesh):
    return jax.shard_map(
        per_device,
        mesh=mesh,
        in_specs=(
            P(("dp", "head"), None),
            P(),
            P(None, "dp", "head"),
            P("head", "dp"),
            P(),
            P(),
            P(("dp", "head"), None),
            P(("dp", "head"), None),
            P(("dp", "head"), None),
            P("dp", None),
        ),
        out_specs=(
            P(("dp", "head"), None),
            P(("dp", "head"), None),
            P(),
            P(None, "dp", "head"),
            P("head", "dp"),
            P(),
            P(),
            P(("dp", "head"), None),
            P(("dp", "head"), None),
        ),
        check_vma=False,
    )
```

```python
import functools
import math

import jax
import jax.numpy as jnp
from jax import lax
from jax.experimental import pallas as pl
from jax.experimental.pallas import tpu as pltpu
from jax.sharding import PartitionSpec as P

HEAD_DIM = 64
BAND = 30
ROWS = 96
TAIL = 32
WIN = ROWS + TAIL
PAIR = 2 * HEAD_DIM
EPS = 1e-05
NEG = -1e30
CARRIED, LAST, VALID, ROW_AT, COLUMN_AT = range(-5, 0)
F32 = jnp.float32
BF16 = jnp.bfloat16
NT = (((1,), (1,)), ((), ()))
TN = (((0,), (0,)), ((), ()))
NN = (((1,), (0,)), ((), ()))


def mm(left, right, dims=NN):
    return lax.dot_general(left, right, dims, preferred_element_type=F32)


def iota(shape, axis):
    return lax.broadcasted_iota(jnp.int32, shape, axis)


def lift(values):
    return jnp.where(values > 0, values + 1.0, jnp.exp(jnp.minimum(values, 0.0)))


def head_lanes(dtype):
    first = (iota((1, PAIR), 1) < HEAD_DIM).astype(F32)
    return first.astype(dtype), (1.0 - first).astype(dtype)


def split_heads(block):
    first, second = head_lanes(block.dtype)
    return jnp.concatenate([block * first, block * second], axis=0)


def same_head():
    return (iota((PAIR, PAIR), 0) < HEAD_DIM) == (iota((PAIR, PAIR), 1) < HEAD_DIM)


def block_only(wide):
    keep = same_head()
    parts = [
        jnp.where(keep, wide[:, p * PAIR : (p + 1) * PAIR], 0.0)
        for p in range(wide.shape[1] // PAIR)
    ]
    return jnp.concatenate(parts, axis=1)


def fold(tall):
    half = tall.shape[0] // 2
    lanes = iota((half, PAIR), 1) < HEAD_DIM
    return jnp.where(lanes, tall[:half], tall[half:])


def two(half):
    return jnp.concatenate([half, half], axis=1)


def masks(row, start, first):
    key = iota(row.shape, 1) + first
    floor = jnp.maximum(first, 0)
    causal = key <= row
    near = causal & (key >= jnp.maximum(start, row - (BAND - 1)))
    far = causal & (key >= jnp.maximum(start, floor))
    count = 1.0 / (row - start + 1).astype(F32)
    return jnp.where(near, 0.0, NEG), far.astype(F32), jnp.where(start < floor, -count, count)


def near_scores(query, key_heads):
    return mm(query * jnp.asarray(HEAD_DIM**-0.5, BF16), key_heads, NT)


def near_weights(scores, bias):
    parts = []
    for h in range(2):
        part = scores[:, h * WIN : (h + 1) * WIN] + bias
        parts.append(jnp.exp(part - jnp.max(part, axis=1, keepdims=True)))
    return jnp.concatenate(parts, axis=1)


def spread(product):
    first = iota(product.shape, 1) < HEAD_DIM
    sums = [
        jnp.sum(jnp.where(keep, product, 0.0), axis=1, keepdims=True) for keep in (first, ~first)
    ]
    return jnp.concatenate([jnp.broadcast_to(part, (ROWS, WIN)) for part in sums], axis=1)


def load_keys(qkv_ref, message_ref, keys, values):
    rows = qkv_ref.shape[1]
    keys[pl.ds(0, TAIL), :] = message_ref[0, pl.ds(HEAD_DIM, TAIL), :PAIR]
    keys[pl.ds(TAIL, rows), :] = qkv_ref[1]
    values[pl.ds(0, TAIL), :] = message_ref[0, pl.ds(HEAD_DIM, TAIL), PAIR : 2 * PAIR]
    values[pl.ds(TAIL, rows), :] = qkv_ref[2]


def fold_state(wide):
    kept = block_only(wide)
    return (kept[:HEAD_DIM] + kept[HEAD_DIM:]).astype(BF16)


def unfold_state(message):
    half = message[:HEAD_DIM].astype(F32)
    return block_only(jnp.concatenate([half, half], axis=0))


def project_kernel(
    scalars,
    tokens_ref,
    gain_ref,
    own_ref,
    other_ref,
    qkv_ref,
    normed_ref,
    weight_ref,
    out_weight_ref,
    message_ref,
    state,
    placed,
    *,
    flips,
):
    step = pl.program_id(0)
    rows, width = tokens_ref.shape
    pairs = width // PAIR
    half, _, tall, wide = own_ref.shape
    last = jnp.maximum(scalars[scalars.shape[0] + LAST], 0)

    @pl.when(step == 0)
    def _():
        for index, (flip_row, flip_column) in enumerate(flips):
            row = scalars[scalars.shape[0] + ROW_AT] ^ flip_row
            column = scalars[scalars.shape[0] + COLUMN_AT] ^ flip_column
            piece = own_ref[index] if index < half else other_ref[index - half]
            for c in range(4):
                placed[column, c, row] = piece[c]
        for h in range(width // wide):
            at = pl.ds(h * wide, wide)
            weight_ref[:, :, at] = placed[h, :3].reshape(3, width, wide)
            out_weight_ref[:, at] = placed[h, 3].reshape(width, wide)
        state[...] = jnp.zeros(state.shape, F32)

    normed = (norm_parts(tokens_ref[...].astype(F32))[0] * gain_ref[...]).astype(BF16)
    normed_ref[...] = normed
    for c in (1, 2, 0):
        qkv_ref[c] = mm(normed, weight_ref[c]).astype(BF16)
    live = iota((rows, PAIR), 0) + step * rows >= last
    ones = jnp.ones((rows, PAIR), BF16)
    for p in range(pairs):
        at = pl.ds(p * PAIR, PAIR)
        key = qkv_ref[1, :, at].astype(F32)
        value = qkv_ref[2, :, at]
        lifted = jnp.where(live, lift(key), 0.0).astype(BF16)
        bent = jnp.where(live, jnp.tanh(key), 0.0).astype(BF16)
        state[p, :, : 2 * PAIR] += mm(lifted, jnp.concatenate([value, ones], axis=1), TN)
        state[p, :, 2 * PAIR :] += mm(bent, value, TN)

    @pl.when(step == pl.num_programs(0) - 1)
    def _():
        for p in range(pairs):
            at = pl.ds(p * PAIR, PAIR)
            message_ref[p, pl.ds(0, HEAD_DIM), :] = fold_state(state[p])
            message_ref[p, pl.ds(HEAD_DIM, TAIL), :] = jnp.concatenate(
                [
                    qkv_ref[1, pl.ds(rows - TAIL, TAIL), at],
                    qkv_ref[2, pl.ds(rows - TAIL, TAIL), at],
                    jnp.zeros((TAIL, PAIR), BF16),
                ],
                axis=1,
            )


def weight_grad_kernel(
    scalars,
    normed_ref,
    d_qkv_ref,
    out_grad_ref,
    weight_ref,
    keep_ref,
    give_ref,
    gain_ref,
    whole,
    *,
    flips,
):
    c = pl.program_id(0)
    half, _, tall, wide = keep_ref.shape

    def place(total):
        for h in range(total.shape[1] // wide):
            part = total[:, h * wide : (h + 1) * wide]
            whole[h] = part.reshape(whole.shape[1:])

    @pl.when(c == 0)
    def _():
        gain_ref[...] = jnp.zeros(gain_ref.shape, F32)

    @pl.when(c < 3)
    def _():
        total = mm(normed_ref[...], d_qkv_ref[0], TN)
        place(total)
        product = total * weight_ref[0].astype(F32)
        high = product.astype(BF16)
        low = (product - high.astype(F32)).astype(BF16)
        ones = jnp.ones((8, product.shape[1]), BF16)
        gain_ref[...] += mm(ones, high, NT) + mm(ones, low, NT)

    @pl.when(c == 3)
    def _():
        place(out_grad_ref[...])

    for index, (flip_row, flip_column) in enumerate(flips):
        row = scalars[scalars.shape[0] + ROW_AT] ^ flip_row
        column = scalars[scalars.shape[0] + COLUMN_AT] ^ flip_column
        if index < half:
            keep_ref[index, 0] = whole[column, row]
        else:
            give_ref[index - half, 0] = whole[column, row].astype(BF16)


def forward_kernel(
    scalars,
    qkv_ref,
    message_ref,
    bias_ref,
    far_ref,
    tally_ref,
    blend_ref,
    att_ref,
    near_ref,
    far1_ref,
    far2_ref,
    invl_ref,
    invd_ref,
    states_ref,
    keys,
    values,
    state,
):
    rows = qkv_ref.shape[1]
    load_keys(qkv_ref, message_ref, keys, values)
    state[...] = unfold_state(message_ref[0])
    count_valid = scalars[scalars.shape[0] + VALID]
    b0, b1, b2 = (blend_ref[pl.ds(f, 1), :] for f in range(3))

    def begin(step):
        at = pl.multiple_of(step * ROWS, 32)
        query = qkv_ref[0, pl.ds(at, ROWS), :]
        key = keys[pl.ds(at, WIN), :]
        value = values[pl.ds(at, WIN), :]
        first = step * ROWS - TAIL
        floor = jnp.maximum(first, 0)
        tally = tally_ref[pl.ds(at, ROWS), :]
        carried = tally < 0.0
        far_two = two(far_ref[pl.ds(at, ROWS), :].astype(F32))
        query_f = query.astype(F32)
        key_f = key.astype(F32)
        lift_qf, bend_qf = lift(query_f), jnp.tanh(query_f)
        lift_q, bend_q = lift_qf.astype(BF16), bend_qf.astype(BF16)
        lift_k = lift(key_f)
        bend_k = jnp.tanh(key_f)
        ones = jnp.ones((WIN, PAIR), BF16)
        value_heads = jnp.concatenate([split_heads(value), split_heads(ones)], axis=1)
        before = state[...]
        before_low = before.astype(BF16)
        scores = near_scores(query, split_heads(key))
        pair_weight = mm(lift_q, split_heads(lift_k.astype(BF16)), NT)
        pair_bend = mm(bend_q, split_heads(bend_k.astype(BF16)), NT)
        elu_state = mm(
            jnp.where(carried, lift_qf, 0.0).astype(BF16), before_low[:, : 2 * PAIR]
        )
        tanh_state = mm(jnp.where(carried, bend_qf, 0.0).astype(BF16), before_low[:, 2 * PAIR :])
        states_ref[0, pl.ds(pl.multiple_of(step * PAIR, PAIR), PAIR), :] = before_low
        closing = scalars[step]
        live = iota((ROWS, PAIR), 0) + first >= jnp.maximum(closing, floor)
        lifted = jnp.where(live, lift_k[:ROWS], 0.0).astype(BF16)
        bent = jnp.where(live, bend_k[:ROWS], 0.0).astype(BF16)
        with_ones = jnp.concatenate([value[:ROWS], ones[:ROWS]], axis=1)
        added = jnp.concatenate([mm(lifted, with_ones, TN), mm(bent, value[:ROWS], TN)], axis=1)
        keep = (closing < floor).astype(F32)
        state[...] = keep * before + block_only(added)
        def finish():
            low_weight = (pair_weight * far_two).astype(BF16)
            low_bend = (pair_bend * far_two).astype(BF16)
            elu_out = mm(low_weight, value_heads)
            tanh_out = mm(low_bend, value_heads[:, :PAIR]) + tanh_state
            weights = near_weights(scores, bias_ref[pl.ds(at, ROWS), :].astype(F32)).astype(BF16)
            near_out = mm(weights, value_heads)
            numerator = elu_out[:, :PAIR] + elu_state[:, :PAIR]
            inv_d = 1.0 / (elu_out[:, PAIR:] + elu_state[:, PAIR:])
            far1 = numerator * inv_d
            inv_l = 1.0 / near_out[:, PAIR:]
            near = near_out[:, :PAIR] * inv_l
            far2 = tanh_out * jnp.abs(tally)
            row = iota((ROWS, PAIR), 0) + at
            mixed = jnp.where(row < count_valid, b0 * near + b1 * far1 + b2 * far2, 0.0)
            att_ref[pl.ds(at, ROWS), :] = mixed.astype(BF16)
            near_ref[pl.ds(at, ROWS), :] = near
            far1_ref[pl.ds(at, ROWS), :] = far1
            far2_ref[pl.ds(at, ROWS), :] = far2
            invl_ref[pl.ds(at, ROWS), :] = inv_l
            invd_ref[pl.ds(at, ROWS), :] = inv_d

        return finish

    def body(both, carry):
        finishes = [begin(both * 2 + half) for half in range(2)]
        for finish in finishes:
            finish()
        return carry

    lax.fori_loop(0, rows // ROWS // 2, body, 0, unroll=4)


def near_back(scores, grad_pair, bias, spread_near):
    weights = near_weights(scores, bias)
    return weights.astype(BF16), (weights * (grad_pair - spread_near)).astype(BF16)


def prologue_kernel(
    scalars,
    query_ref,
    key_ref,
    value_ref,
    message_ref,
    start_ref,
    blend_ref,
    grad_ref,
    near_ref,
    far1_ref,
    invl_ref,
    invd_ref,
    back_ref,
):
    rows = query_ref.shape[1]
    step_rows = rows // 3
    b0, b1, b2 = (blend_ref[pl.ds(f, 1), :] for f in range(3))

    tails = message_ref[0, pl.ds(HEAD_DIM, TAIL), :]
    key = jnp.concatenate([tails[:, :PAIR], key_ref[0]], axis=0)
    value = jnp.concatenate([tails[:, PAIR : 2 * PAIR], value_ref[0]], axis=0)
    start = start_ref[pl.ds(0, ROWS), :]
    row = iota((ROWS, WIN), 0)
    bias, _, _ = masks(row, start, -TAIL)
    query = query_ref[0, pl.ds(0, ROWS), :]
    grad = grad_ref[pl.ds(0, ROWS), :]
    grad_f = grad.astype(F32)
    scale = b0 * invl_ref[...]
    rows_q = (query.astype(F32) * (scale * HEAD_DIM**-0.5)).astype(BF16)
    rows_g = (grad_f * scale).astype(BF16)
    scores = near_scores(query, split_heads(key))
    grad_pair = mm(grad, split_heads(value), NT)
    spread_near = spread(grad_f * near_ref[...])
    heads = same_head().astype(F32).astype(BF16)
    heads = jnp.concatenate([heads, heads], axis=0)

    total = jnp.zeros((PAIR, 3 * PAIR), F32)
    for step in range(3):
        here = pl.ds(step * step_rows, step_rows)
        row = iota((step_rows, PAIR), 0) + step * step_rows
        start = start_ref[here, :]
        all_grad = grad_ref[here, :]
        product = all_grad.astype(F32) * far1_ref[here, :]
        high = product.astype(BF16)
        low = (product - high.astype(F32)).astype(BF16)
        along = mm(jnp.concatenate([high, low], axis=1), heads).astype(BF16)
        query_f = query_ref[0, here, :].astype(F32)
        live = start < 0
        scaled = jnp.where(live, lift(query_f) * (b1 * invd_ref[here, :]), 0.0)
        bent = jnp.where(live, jnp.tanh(query_f) * (b2 / (row - start + 1).astype(F32)), 0.0)
        from_lift = mm(scaled.astype(BF16), jnp.concatenate([all_grad, along], axis=1), TN)
        from_bend = mm(bent.astype(BF16), all_grad, TN)
        total = total + jnp.concatenate([from_lift, from_bend], axis=1)

    weights, shifted = near_back(scores, grad_pair, bias, spread_near)
    d_key = fold(mm(shifted, rows_q, TN))
    back_ref[0, pl.ds(HEAD_DIM, TAIL), :] = jnp.concatenate(
        [d_key[:TAIL], fold(mm(weights, rows_g, TN))[:TAIL], jnp.zeros((TAIL, PAIR), F32)], axis=1
    ).astype(BF16)
    back_ref[0, pl.ds(0, HEAD_DIM), :] = fold_state(total)


def key_side(adjoint_low, lift_k, bend_k, value):
    ones = jnp.full(value.shape, -1.0 / HEAD_DIM, BF16)
    d_lift = mm(jnp.concatenate([value, ones], axis=1), adjoint_low[:, : 2 * PAIR], NT)
    d_bend = mm(value, adjoint_low[:, 2 * PAIR :], NT)
    both = jnp.concatenate([adjoint_low[:, :PAIR], adjoint_low[:, 2 * PAIR :]], axis=0)
    d_value = mm(jnp.concatenate([lift_k, bend_k], axis=1), both)
    return d_lift, d_bend, d_value


def backward_kernel(
    scalars,
    qkv_ref,
    message_ref,
    bias_ref,
    far_ref,
    tally_ref,
    blend_ref,
    grad_ref,
    near_ref,
    far1_ref,
    far2_ref,
    invl_ref,
    invd_ref,
    states_ref,
    back_ref,
    done_ref,
    out_ref,
    sums_ref,
    keys,
    values,
    adjoint,
    key_carry,
    value_carry,
):
    rows = qkv_ref.shape[1]
    steps = rows // ROWS
    load_keys(qkv_ref, message_ref, keys, values)
    last = scalars[scalars.shape[0] + LAST]
    b0, b1, b2 = (blend_ref[pl.ds(f, 1), :] for f in range(3))
    lanes = iota((ROWS, PAIR), 1) < HEAD_DIM

    arrived = unfold_state(back_ref[0])
    tail_grads = back_ref[0, pl.ds(HEAD_DIM, TAIL), :].astype(F32)
    end_key = keys[pl.ds(rows, TAIL), :].astype(F32)
    end_lift, end_bend = lift(end_key), jnp.tanh(end_key)
    end_parts = key_side(
        arrived.astype(BF16), end_lift.astype(BF16), end_bend.astype(BF16), values[pl.ds(rows, TAIL), :]
    )
    live = iota((TAIL, PAIR), 0) + (rows - TAIL) >= last
    key_carry[...] = tail_grads[:, :PAIR] + jnp.where(
        live,
        end_parts[0] * jnp.minimum(end_lift, 1.0) + end_parts[1] * (1.0 - end_bend * end_bend),
        0.0,
    )
    value_carry[...] = tail_grads[:, PAIR : 2 * PAIR] + jnp.where(live, end_parts[2], 0.0)
    adjoint[...] = jnp.where(last < rows - TAIL, 1.0, 0.0) * arrived
    sums_ref[...] = jnp.zeros(sums_ref.shape, F32)

    def add_up(place, product):
        sums_ref[pl.ds(place, 8), :] += jnp.sum(product.reshape(ROWS // 8, 8, PAIR), axis=0)

    def begin(back):
        step = steps - 1 - back
        at = pl.multiple_of(step * ROWS, 32)
        query = qkv_ref[0, pl.ds(at, ROWS), :]
        key = keys[pl.ds(at, WIN), :]
        value = values[pl.ds(at, WIN), :]
        first = step * ROWS - TAIL
        floor = jnp.maximum(first, 0)
        tally = tally_ref[pl.ds(at, ROWS), :]
        carried = tally < 0.0
        far_two = two(far_ref[pl.ds(at, ROWS), :].astype(F32))
        grad = grad_ref[pl.ds(at, ROWS), :]
        grad_f = grad.astype(F32)
        query_f = query.astype(F32)
        key_f = key.astype(F32)
        lift_qf, bend_qf = lift(query_f), jnp.tanh(query_f)
        lift_kf, bend_kf = lift(key_f), jnp.tanh(key_f)
        lift_q, bend_q = lift_qf.astype(BF16), bend_qf.astype(BF16)
        lift_k, bend_k = lift_kf.astype(BF16), bend_kf.astype(BF16)
        lift_heads, bend_heads = split_heads(lift_k), split_heads(bend_k)
        r0 = b0 * invl_ref[pl.ds(at, ROWS), :]
        r1 = b1 * invd_ref[pl.ds(at, ROWS), :]
        r2 = b2 * jnp.abs(tally)
        key_heads = split_heads(key)
        before = states_ref[0, pl.ds(pl.multiple_of(step * PAIR, PAIR), PAIR), :]
        near_product = grad_f * near_ref[pl.ds(at, ROWS), :]
        far1_product = grad_f * far1_ref[pl.ds(at, ROWS), :]
        grad_pair = mm(grad, split_heads(value), NT)
        scores = near_scores(query, key_heads)
        pair_weight = mm(lift_q, lift_heads, NT)
        pair_bend = mm(bend_q, bend_heads, NT)
        state_bend = mm(grad, before[:, 2 * PAIR :], NT)
        spread_far = spread(far1_product)
        spread_near = spread(near_product)
        along = jnp.where(lanes, spread_far[:, :WIN], spread_far[:, WIN:])
        scaled_along = (along * (-1.0 / HEAD_DIM)).astype(BF16)
        state_lift = mm(jnp.concatenate([grad, scaled_along], axis=1), before[:, : 2 * PAIR], NT)
        after = adjoint[...]
        parts = key_side(after.astype(BF16), lift_k[:ROWS], bend_k[:ROWS], value[:ROWS])
        rows_q = (query_f * (r0 * HEAD_DIM**-0.5)).astype(BF16)
        rows_a = lift_qf * r1
        rows_t = bend_qf * r2
        from_lift = mm(
            jnp.where(carried, rows_a, 0.0).astype(BF16),
            jnp.concatenate([grad, along.astype(BF16)], axis=1),
            TN,
        )
        from_bend = mm(jnp.where(carried, rows_t, 0.0).astype(BF16), grad, TN)
        closing = scalars[step]
        keep = (closing < floor).astype(F32)
        adjoint[...] = keep * after + block_only(jnp.concatenate([from_lift, from_bend], axis=1))
        add_up(0, near_product)
        add_up(8, far1_product)
        add_up(16, grad_f * far2_ref[pl.ds(at, ROWS), :])
        def finish():
            shifted = ((grad_pair - spread_far) * far_two).astype(BF16)
            plain = (grad_pair * far_two).astype(BF16)
            low_weight = (pair_weight * far_two).astype(BF16)
            low_bend = (pair_bend * far_two).astype(BF16)
            weights, shifted_near = near_back(
                scores, grad_pair, bias_ref[pl.ds(at, ROWS), :].astype(F32), spread_near
            )
            d_query = mm(shifted_near, key_heads) * (r0 * HEAD_DIM**-0.5)
            d_query = (
                d_query
                + (mm(shifted, lift_heads) + jnp.where(carried, state_lift, 0.0))
                * (r1 * jnp.minimum(lift_qf, 1.0))
                + (mm(plain, bend_heads) + jnp.where(carried, state_bend, 0.0))
                * (r2 * (1.0 - bend_qf * bend_qf))
            )
            out_ref[0, pl.ds(at, ROWS), :] = d_query.astype(BF16)
            d_key = fold(mm(shifted_near, rows_q, TN))
            d_lift = fold(mm(shifted, rows_a.astype(BF16), TN))
            d_bend = fold(mm(plain, rows_t.astype(BF16), TN))
            d_value = fold(
                mm(
                    jnp.concatenate([weights, low_weight, low_bend], axis=0),
                    jnp.concatenate([grad_f * r0, grad_f * r1, grad_f * r2], axis=0).astype(BF16),
                    TN,
                )
            )
            live = iota((ROWS, PAIR), 0) + first >= jnp.maximum(closing, floor)
            pad = jnp.zeros((TAIL, PAIR), F32)
            d_lift = d_lift + jnp.concatenate([jnp.where(live, parts[0], 0.0), pad], axis=0)
            d_bend = d_bend + jnp.concatenate([jnp.where(live, parts[1], 0.0), pad], axis=0)
            d_value = d_value + jnp.concatenate([jnp.where(live, parts[2], 0.0), pad], axis=0)
            d_key = d_key + d_lift * jnp.minimum(lift_kf, 1.0) + d_bend * (1.0 - bend_kf * bend_kf)
            out_ref[1, pl.ds(at, ROWS), :] = jnp.concatenate(
                [d_key[TAIL:ROWS], d_key[ROWS:] + key_carry[...]], axis=0
            ).astype(BF16)
            out_ref[2, pl.ds(at, ROWS), :] = jnp.concatenate(
                [d_value[TAIL:ROWS], d_value[ROWS:] + value_carry[...]], axis=0
            ).astype(BF16)
            key_carry[...] = d_key[:TAIL]
            value_carry[...] = d_value[:TAIL]

        return finish

    def body(both, carry):
        finishes = [begin(both * 2 + half) for half in range(2)]
        for finish in finishes:
            finish()
        return carry

    lax.fori_loop(0, steps // 2, body, 0, unroll=4)


def feed_kernel(
    scalars,
    mixed_ref,
    tokens_ref,
    cotangent_ref,
    out_weight_ref,
    gain_ref,
    own_ref,
    other_ref,
    layer_ref,
    d_hidden_ref,
    d_branch_ref,
    d_mixed_ref,
    normed_ref,
    active_ref,
    d_inner_ref,
    sums_ref,
):
    c0 = math.sqrt(2.0 / math.pi)
    hidden = tokens_ref[...].astype(F32) + mm(mixed_ref[...], out_weight_ref[...], NT)
    normal, scale = norm_parts(hidden)
    normed = (normal * gain_ref[...]).astype(BF16)
    normed_ref[...] = normed
    cotangent = cotangent_ref[...]
    half, width = own_ref.shape[1:]
    chunk = min(512, half)
    layer = hidden
    d_normed = jnp.zeros(hidden.shape, F32)
    slots = [(ref, first) for ref in (own_ref, other_ref) for first in range(0, half, chunk)]

    def opening(slot):
        ref, first = slot
        into = ref[0, pl.ds(first, chunk), :]
        down = ref[1, pl.ds(first, chunk), :]
        return into, down, mm(normed, into, NT), mm(cotangent, down, NT)

    ready = opening(slots[0])
    for place in range(len(slots)):
        into, down, inner, d_active = ready
        if place + 1 < len(slots):
            ready = opening(slots[place + 1])
        square = inner * inner
        bent = jnp.tanh(inner * (c0 + (c0 * 0.044715) * square))
        gate = 0.5 + 0.5 * bent
        active = (inner * gate).astype(BF16)
        slope = gate + inner * (0.5 - 0.5 * bent * bent) * (c0 + (3.0 * 0.044715 * c0) * square)
        d_inner = (d_active * slope).astype(BF16)
        at = pl.ds(place * chunk, chunk)
        active_ref[:, at] = active
        d_inner_ref[:, at] = d_inner
        layer = layer + mm(active, down)
        d_normed = d_normed + mm(d_inner, into)
    layer_ref[...] = layer.astype(BF16)
    d_part, gain_rows = norm_back(d_normed, gain_ref[...], normal, scale)
    d_hidden = cotangent.astype(F32) + d_part
    d_hidden_ref[...] = d_hidden
    d_branch = d_hidden.astype(BF16)
    d_branch_ref[...] = d_branch
    row = iota(hidden.shape, 0) + pl.program_id(0) * hidden.shape[0]
    d_mixed = mm(d_branch, out_weight_ref[...])
    d_mixed_ref[...] = jnp.where(row < scalars[scalars.shape[0] + VALID], d_mixed, 0.0).astype(BF16)

    @pl.when(pl.program_id(0) == 0)
    def _():
        sums_ref[...] = jnp.zeros(sums_ref.shape, F32)

    sums_ref[...] += gain_rows


def feed_grad_kernel(
    scalars, normed_ref, cotangent_ref, active_ref, d_inner_ref, *refs
):
    refs[-1][0] = mm(d_inner_ref[...], normed_ref[...], TN).astype(refs[-1].dtype)
    refs[-1][1] = mm(active_ref[...], cotangent_ref[...], TN).astype(refs[-1].dtype)
    if len(refs) > 1:
        mixed_ref, d_branch_ref, out_grad_ref, _ = refs

        @pl.when(pl.program_id(0) == 0)
        def _():
            out_grad_ref[...] = mm(d_branch_ref[...], mixed_ref[...], TN)


def input_kernel(
    scalars, d_qkv_ref, weight_ref, tokens_ref, d_hidden_ref, gain_ref, input_grad_ref
):
    d_normed = mm(d_qkv_ref[0], weight_ref[0], NT)
    for c in range(1, 3):
        d_normed = d_normed + mm(d_qkv_ref[c], weight_ref[c], NT)
    normal, scale = norm_parts(tokens_ref[...].astype(F32))
    d_part, _ = norm_back(d_normed, gain_ref[...], normal, scale)
    input_grad_ref[...] = d_hidden_ref[...] + d_part


def resume(kernel, ins, done, *refs):
    kernel(*refs[:ins], *refs[ins + done :])


def pair_specs(rows, first=0):
    return {
        "qkv": pl.BlockSpec((3, rows, PAIR), lambda p, s: (0, 0, p + first)),
        "message": pl.BlockSpec((1, HEAD_DIM + TAIL, 3 * PAIR), lambda p, s: (p + first, 0, 0)),
        "start": pl.BlockSpec((rows, PAIR), lambda p, s: (0, 0)),
        "blend": pl.BlockSpec((3, PAIR), lambda p, s: (0, p + first)),
        "column": pl.BlockSpec((rows, PAIR), lambda p, s: (0, p + first)),
        "states": pl.BlockSpec((1, rows // ROWS * PAIR, 3 * PAIR), lambda p, s: (p + first, 0, 0)),
        "sums": pl.BlockSpec((24, PAIR), lambda p, s: (0, p)),
        "query": pl.BlockSpec((1, rows, PAIR), lambda p, s: (0, 0, p)),
        "head_rows": pl.BlockSpec((ROWS, PAIR), lambda p, s: (0, p)),
    }


def call(kernel, ins, outs, out_shapes, scratch, grid, name, flops, moved, aliases={}):
    return pl.pallas_call(
        kernel,
        out_shape=out_shapes,
        grid_spec=pltpu.PrefetchScalarGridSpec(
            num_scalar_prefetch=1,
            grid=(grid,),
            in_specs=ins,
            out_specs=outs,
            scratch_shapes=scratch,
        ),
        input_output_aliases=aliases,
        compiler_params=pltpu.CompilerParams(
            dimension_semantics=("arbitrary",), vmem_limit_bytes=56 * 1024 * 1024
        ),
        cost_estimate=pl.CostEstimate(flops=flops, bytes_accessed=moved, transcendentals=0),
        name=name,
    )


def norm_parts(source):
    centered = source - jnp.mean(source, axis=-1, keepdims=True)
    spread_of = jnp.mean(centered * centered, axis=-1, keepdims=True)
    scale = lax.rsqrt(spread_of + EPS)
    return centered * scale, scale


def norm_back(d_out, gain, normal, scale):
    e = d_out * gain
    inner = jnp.mean(e, axis=-1, keepdims=True)
    along = jnp.mean(e * normal, axis=-1, keepdims=True)
    rows = jnp.sum((d_out * normal).reshape(-1, 8, d_out.shape[1]), axis=0)
    return scale * (e - inner - normal * along), rows


def bits(size):
    return [1 << b for b in range(int(math.log2(size)))]


def phases():
    dp = bits(lax.axis_size("dp"))
    core, rest = dp[:1], dp[1:]
    mid = len(rest) // 2
    far = [("dp", m) for m in rest[mid:]]
    near = [("dp", m) for m in rest[:mid]] + [("head", m) for m in bits(lax.axis_size("head"))]
    groups = []
    for run in (far, near, [("dp", m) for m in core]):
        groups += [run[i : i + 2] for i in range(0, len(run), 2)]
    return groups


def relative_bits():
    return [pair for group in phases() for pair in group]


def all_flips():
    order = relative_bits()
    flips = []
    for index in range(1 << len(order)):
        chosen = [pair for place, pair in enumerate(order) if index >> place & 1]
        flips.append(tuple(sum(m for a, m in chosen if a == axis) for axis in ("dp", "head")))
    return flips


def peer(array, group, combo):
    n_dp, n_head = lax.axis_size("dp"), lax.axis_size("head")
    chosen = [pair for place, pair in enumerate(group) if combo >> place & 1]
    flip_dp = sum(m for axis, m in chosen if axis == "dp")
    flip_head = sum(m for axis, m in chosen if axis == "head")
    pairs = [
        (d * n_head + h, (d ^ flip_dp) * n_head + (h ^ flip_head))
        for d in range(n_dp)
        for h in range(n_head)
    ]
    return lax.ppermute(array, ("dp", "head"), pairs)


def widen(block, group, axis, after=None):
    others = [peer(block, group, combo) for combo in range(1, 1 << len(group))]
    if after is not None:
        others, after = lax.optimization_barrier((others, after))
    whole = jnp.concatenate([block] + others, axis=axis)
    return whole if after is None else (whole, after)


def narrow(keep, gives, group, after=None):
    arrived = [peer(give.astype(BF16), group, combo) for combo, give in enumerate(gives, 1)]
    if after is not None:
        arrived, _ = lax.optimization_barrier((arrived, after))
    return keep.astype(F32) + sum(part.astype(F32) for part in arrived)


def narrow_axis(total, group, axis, after=None):
    parts = jnp.split(total, 1 << len(group), axis=axis)
    return narrow(parts[0], parts[1:], group, after)


def pass_along(local, keep, shift):
    size = lax.axis_size("head")
    pairs = [(i, i + shift) for i in range(size) if 0 <= i + shift < size]
    arrived = lax.ppermute(local, "head", pairs)
    for _ in range(size - 2):
        rows = iota(local.shape, 1) < HEAD_DIM
        total = local.astype(F32) + jnp.where(rows, keep * arrived.astype(F32), 0.0)
        arrived = lax.ppermute(total.astype(BF16), "head", pairs)
    return arrived


def per_device(
    tokens,
    ln1_gain,
    qkv_weight,
    out_weight,
    blend,
    ln2_gain,
    in_weight,
    down_weight,
    cotangent,
    lengths,
):
    rows, width = tokens.shape
    n_dp, n_head = lax.axis_size("dp"), lax.axis_size("head")
    pairs = width // PAIR
    steps = rows // ROWS
    groups = phases()
    flips = all_flips()

    item_lengths = lengths[0]
    slots = item_lengths.shape[0]
    ends = jnp.sum(
        jnp.where(iota((slots, slots), 1) <= iota((slots, slots), 0), item_lengths[None, :], 0),
        axis=1,
    )
    offset = lax.axis_index("head") * rows
    local = jnp.arange(rows, dtype=jnp.int32)
    place = local + offset
    total = ends[slots - 1]
    item_start = jnp.max(
        jnp.where(ends[None, :] <= place[:, None], ends[None, :], 0), axis=1
    )
    start = jnp.where(place < total, item_start - offset, local)
    carried_rows = jnp.sum((start < 0).astype(jnp.int32))
    scalars = jnp.concatenate(
        [
            start.reshape(steps, ROWS)[:, ROWS - TAIL - 1],
            carried_rows[None],
            start[rows - 1 :],
            (total - offset)[None],
            lax.axis_index("dp").astype(jnp.int32)[None],
            lax.axis_index("head").astype(jnp.int32)[None],
        ]
    )
    shards = jnp.concatenate([qkv_weight, out_weight.T[None]], axis=0)[None]
    feed = jnp.stack([in_weight, down_weight])
    shards = widen(shards, groups[0], 0)
    feed, late, _ = lax.optimization_barrier((feed, start, shards))
    start_wide = jnp.broadcast_to(late[:, None], (rows, PAIR))
    row_wide = jnp.broadcast_to(local[:, None], (rows, PAIR))
    bias, far, tally = masks(row_wide, start_wide, row_wide // ROWS * ROWS - TAIL)
    tables = (bias.astype(BF16), far.astype(BF16), tally)
    feed = widen(feed, groups[0][:1], 1)
    for group in groups[1:-1]:
        shards = widen(shards, group, 0)
    shards, feed, start_wide, tables = lax.optimization_barrier((shards, feed, start_wide, tables))
    others = peer(shards, groups[-1], 1)

    keep_all = (start[rows - 1] < 0).astype(F32)
    blend_wide = jnp.repeat(blend, HEAD_DIM, axis=1)

    spec = pair_specs(rows)
    wide = jax.ShapeDtypeStruct((rows, width), F32)
    states_shape = jax.ShapeDtypeStruct((pairs, steps * PAIR, 3 * PAIR), BF16)
    message_shape = jax.ShapeDtypeStruct((pairs, HEAD_DIM + TAIL, 3 * PAIR), BF16)
    big = rows * width
    part = rows // 3

    def whole_spec(shape):
        return pl.BlockSpec(shape, lambda p, s: (0,) * len(shape))

    qkv, normed_one, qkv_all, out_all, closing = call(
        functools.partial(project_kernel, flips=flips),
        [
            pl.BlockSpec((part, width), lambda p, s: (p, 0)),
            whole_spec((1, width)),
            whole_spec(shards.shape),
            whole_spec(shards.shape),
        ],
        [
            pl.BlockSpec((3, part, width), lambda p, s: (0, p, 0)),
            pl.BlockSpec((part, width), lambda p, s: (p, 0)),
            whole_spec((3, width, width)),
            whole_spec((width, width)),
            whole_spec(message_shape.shape),
        ],
        [
            jax.ShapeDtypeStruct((3, rows, width), BF16),
            jax.ShapeDtypeStruct((rows, width), BF16),
            jax.ShapeDtypeStruct((3, width, width), BF16),
            jax.ShapeDtypeStruct((width, width), BF16),
            message_shape,
        ],
        [
            pltpu.VMEM((pairs, PAIR, 3 * PAIR), F32),
            pltpu.VMEM((n_head, 4, n_dp, width // n_dp, width // n_head), BF16),
        ],
        3,
        "project",
        6 * big * width,
        12 * big,
    )(scalars, tokens, ln1_gain[None], shards, others)
    for pair in groups[0][1:]:
        feed, _ = widen(feed, [pair], 1, closing)
    message = pass_along(closing, keep_all, 1)

    key_scratch = pltpu.VMEM((rows + TAIL, PAIR), BF16)
    state_scratch = pltpu.VMEM((PAIR, 3 * PAIR), F32)
    tail_scratch = pltpu.VMEM((TAIL, PAIR), F32)
    results = ()
    most = pairs - pairs // 4
    for first, count in ((0, most), (most, pairs - most)):
        spec = pair_specs(rows, first)
        results = call(
            functools.partial(resume, forward_kernel, 7, len(results)),
            [spec["qkv"], spec["message"]]
            + [spec["start"]] * 3
            + [spec["blend"]]
            + [pl.BlockSpec(memory_space=pl.ANY)] * len(results),
            [spec["column"]] * 6 + [spec["states"]],
            [jax.ShapeDtypeStruct((rows, width), BF16)] + [wide] * 5 + [states_shape],
            [key_scratch, key_scratch, state_scratch],
            count,
            "forward",
            8000 * big * count // pairs,
            40 * big * count // pairs,
            {7 + i: i for i in range(len(results))},
        )(scalars, qkv, message, *tables, blend_wide, *results)
        if not first:
            feed, results = widen(feed, groups[1], 1, results)
            feed, message = lax.optimization_barrier((feed, message))
    for group in groups[2:-1]:
        feed = widen(feed, group, 1)
    feed_other = peer(feed, groups[-1], 1)
    mixed, near, far1, far2, inv_l, inv_d, states = results

    spec = pair_specs(rows)
    low = jax.ShapeDtypeStruct((rows, width), BF16)
    row_spec = pl.BlockSpec((part, width), lambda p, s: (p, 0))
    hidden_units = 2 * feed.shape[1]
    unit_spec = pl.BlockSpec((part, hidden_units), lambda p, s: (p, 0))
    unit_shape = jax.ShapeDtypeStruct((rows, hidden_units), BF16)
    sums_shape = jax.ShapeDtypeStruct((8, width), F32)
    layer_out, d_hidden, d_branch, d_mixed, normed_two, active, d_inner, gain_two_rows = call(
        feed_kernel,
        [row_spec] * 3
        + [
            whole_spec((width, width)),
            whole_spec((1, width)),
            whole_spec(feed.shape),
            whole_spec(feed.shape),
        ],
        [row_spec] * 5 + [unit_spec] * 2 + [whole_spec((8, width))],
        [low, wide, low, low, low, unit_shape, unit_shape, sums_shape],
        [],
        3,
        "feed",
        8 * big * hidden_units,
        32 * big,
    )(scalars, mixed, tokens, cotangent, out_all, ln2_gain[None], feed, feed_other)

    back = call(
        prologue_kernel,
        [
            spec["query"],
            pl.BlockSpec((1, ROWS, PAIR), lambda p, s: (1, 0, p)),
            pl.BlockSpec((1, ROWS, PAIR), lambda p, s: (2, 0, p)),
            spec["message"],
            spec["start"],
            spec["blend"],
            spec["column"],
            spec["head_rows"],
            spec["column"],
            spec["head_rows"],
            spec["column"],
        ],
        spec["message"],
        message_shape,
        [],
        pairs,
        "prologue",
        500 * big,
        20 * big,
    )(scalars, qkv, qkv, qkv, message, start_wide, blend_wide, d_mixed, near, far1, inv_l, inv_d)
    d_inner, _ = lax.optimization_barrier((d_inner, back))
    back_in = pass_along(back, keep_all, -1)

    unit = hidden_units // 4
    half_shape = (2, 2 * unit, width)
    whole_rows = whole_spec((rows, width))

    def feed_grad(place, kind, d_inner, more_ins, more_in_specs, more_outs, more_out_specs):
        columns = pl.BlockSpec((rows, unit), lambda p, s: (0, p + 2 * place))
        return call(
            feed_grad_kernel,
            [whole_rows] * 2 + [columns] * 2 + more_in_specs,
            more_out_specs + [pl.BlockSpec((2, unit, width), lambda p, s: (0, p, 0))],
            more_outs + [jax.ShapeDtypeStruct(half_shape, kind)],
            [],
            2,
            "feed_grad",
            2 * big * hidden_units,
            12 * big,
        )(scalars, normed_two, cotangent, active, d_inner, *more_ins)

    (give,) = feed_grad(1, BF16, d_inner, [], [], [], [])
    d_inner, _ = lax.optimization_barrier((d_inner, give))
    out_grad, keep = feed_grad(
        0,
        F32,
        d_inner,
        [mixed, d_branch],
        [whole_rows] * 2,
        [jax.ShapeDtypeStruct((width, width), F32)],
        [whole_spec((width, width))],
    )
    feed_share = narrow(keep, [give], groups[-1])
    left = list(reversed(groups[:-1]))
    _, back_in = lax.optimization_barrier((feed_share, back_in))
    feed_share = narrow_axis(feed_share, left.pop(0), 1)

    d_qkv = jnp.zeros((3, 8, PAIR), BF16)
    sums = []
    first = 0
    for count in (most, pairs - most):
        spec = pair_specs(rows, first)
        more = {15: 0} if first else {}
        d_qkv, part_sums = call(
            backward_kernel,
            [spec["qkv"], spec["message"]]
            + [spec["start"]] * 3
            + [spec["blend"]]
            + [spec["column"]] * 6
            + [spec["states"], spec["message"], pl.BlockSpec(memory_space=pl.ANY)],
            [spec["qkv"], spec["sums"]],
            [
                jax.ShapeDtypeStruct((3, rows, width), BF16),
                jax.ShapeDtypeStruct((24, count * PAIR), F32),
            ],
            [key_scratch, key_scratch, state_scratch, tail_scratch, tail_scratch],
            count,
            "backward",
            16000 * big * count // pairs,
            40 * big * count // pairs,
            more,
        )(
            scalars,
            qkv,
            message,
            *tables,
            blend_wide,
            d_mixed,
            near,
            far1,
            far2,
            inv_l,
            inv_d,
            states,
            back_in,
            d_qkv,
        )
        sums.append(part_sums)
        first += count
        if left and first < pairs:
            _, back_in = lax.optimization_barrier((feed_share, back_in))
            feed_share = narrow_axis(feed_share, left.pop(0), 1)
    for group in left:
        feed_share = narrow_axis(feed_share, group, 1)
    feed_share, d_qkv = lax.optimization_barrier((feed_share, d_qkv))
    sums = jnp.concatenate(sums, axis=1)
    blend_part = jnp.sum(sums.reshape(3, 8, blend.shape[1], HEAD_DIM), axis=(1, 3))

    shard_shape = (n_dp * n_head // 2, 4, width // n_dp, width // n_head)
    shard_spec = pl.BlockSpec((shard_shape[0], 1) + shard_shape[2:], lambda p, s: (0, p, 0, 0))
    keep, give, gain_one_rows = call(
        functools.partial(weight_grad_kernel, flips=flips),
        [
            whole_spec((rows, width)),
            pl.BlockSpec((1, rows, width), lambda p, s: (jnp.minimum(p, 2), 0, 0)),
            whole_spec((width, width)),
            pl.BlockSpec((1, width, width), lambda p, s: (jnp.minimum(p, 2), 0, 0)),
        ],
        [shard_spec, shard_spec, whole_spec((8, width))],
        [
            jax.ShapeDtypeStruct(shard_shape, F32),
            jax.ShapeDtypeStruct(shard_shape, BF16),
            sums_shape,
        ],
        [pltpu.VMEM((n_head, n_dp, width // n_dp, width // n_head), F32)],
        4,
        "weight_grad",
        6 * big * width,
        8 * big,
    )(scalars, normed_one, d_qkv, out_grad, qkv_all)
    parts = [gain_one_rows[0] / ln1_gain, jnp.sum(gain_two_rows, axis=0), blend_part.reshape(-1)]
    total_sums = jnp.concatenate(parts)[None]
    share = narrow(keep, [give], groups[-1])
    hops = list(reversed(relative_bits()))
    total_sums = total_sums + peer(total_sums, [hops[0]], 1)
    total_sums, d_qkv, _ = lax.optimization_barrier((total_sums, d_qkv, share))
    total_sums = total_sums + peer(total_sums, [hops[1]], 1)
    input_grad = call(
        input_kernel,
        [
            pl.BlockSpec((3, part, width), lambda p, s: (0, p, 0)),
            whole_spec((3, width, width)),
            row_spec,
            row_spec,
            whole_spec((1, width)),
        ],
        row_spec,
        wide,
        [],
        3,
        "input",
        6 * big * width,
        24 * big,
    )(scalars, d_qkv, qkv_all, tokens, d_hidden, ln1_gain[None])
    share = narrow_axis(share, groups[-2], 0, input_grad)
    total_sums, _ = lax.optimization_barrier((total_sums, input_grad))
    total_sums = total_sums + peer(total_sums, [hops[2]], 1)
    for group in reversed(groups[:-2]):
        parts = jnp.split(share, 1 << len(group), axis=0)
        arrived = [
            peer(part.astype(BF16), group, combo) for combo, part in enumerate(parts[1:], 1)
        ]
        total_sums, _ = lax.optimization_barrier((total_sums, arrived[0]))
        share = parts[0] + sum(part.astype(F32) for part in arrived)
    for pair in hops[3:]:
        total_sums = total_sums + peer(total_sums, [pair], 1)
    total_sums = total_sums[0]
    gain_one, gain_two = total_sums[:width], total_sums[width : 2 * width]
    blend_sum = total_sums[2 * width :].reshape(blend.shape)
    qkv_share, out_share = share[0, :3], share[0, 3].T
    in_share, down_share = feed_share[0], feed_share[1]
    return (
        layer_out,
        input_grad,
        gain_one,
        qkv_share,
        out_share,
        blend_sum,
        gain_two,
        in_share,
        down_share,
    )


def solution(mesh):
    return jax.shard_map(
        per_device,
        mesh=mesh,
        in_specs=(
            P(("dp", "head"), None),
            P(),
            P(None, "dp", "head"),
            P("head", "dp"),
            P(),
            P(),
            P(("dp", "head"), None),
            P(("dp", "head"), None),
            P(("dp", "head"), None),
            P("dp", None),
        ),
        out_specs=(
            P(("dp", "head"), None),
            P(("dp", "head"), None),
            P(),
            P(None, "dp", "head"),
            P("head", "dp"),
            P(),
            P(),
            P(("dp", "head"), None),
            P(("dp", "head"), None),
        ),
        check_vma=False,
    )
```

```python
import functools
import math

import jax
import jax.numpy as jnp
from jax import lax
from jax.experimental import pallas as pl
from jax.experimental.pallas import tpu as pltpu
from jax.sharding import PartitionSpec as P

HEAD_DIM = 64
BAND = 30
ROWS = 96
TAIL = 32
WIN = ROWS + TAIL
PAIR = 2 * HEAD_DIM
EPS = 1e-05
NEG = -1e30
CARRIED, LAST, VALID, ROW_AT, COLUMN_AT = range(-5, 0)
F32 = jnp.float32
BF16 = jnp.bfloat16
NT = (((1,), (1,)), ((), ()))
TN = (((0,), (0,)), ((), ()))
NN = (((1,), (0,)), ((), ()))


def mm(left, right, dims=NN):
    return lax.dot_general(left, right, dims, preferred_element_type=F32)


def iota(shape, axis):
    return lax.broadcasted_iota(jnp.int32, shape, axis)


def lift(values):
    return jnp.where(values > 0, values + 1.0, jnp.exp(jnp.minimum(values, 0.0)))


def head_lanes(dtype):
    first = (iota((1, PAIR), 1) < HEAD_DIM).astype(F32)
    return first.astype(dtype), (1.0 - first).astype(dtype)


def split_heads(block):
    first, second = head_lanes(block.dtype)
    return jnp.concatenate([block * first, block * second], axis=0)


def same_head():
    return (iota((PAIR, PAIR), 0) < HEAD_DIM) == (iota((PAIR, PAIR), 1) < HEAD_DIM)


def block_only(wide):
    keep = same_head()
    parts = [
        jnp.where(keep, wide[:, p * PAIR : (p + 1) * PAIR], 0.0)
        for p in range(wide.shape[1] // PAIR)
    ]
    return jnp.concatenate(parts, axis=1)


def fold(tall):
    half = tall.shape[0] // 2
    lanes = iota((half, PAIR), 1) < HEAD_DIM
    return jnp.where(lanes, tall[:half], tall[half:])


def two(half):
    return jnp.concatenate([half, half], axis=1)


def masks(row, start, first):
    key = iota(row.shape, 1) + first
    floor = jnp.maximum(first, 0)
    causal = key <= row
    near = causal & (key >= jnp.maximum(start, row - (BAND - 1)))
    far = causal & (key >= jnp.maximum(start, floor))
    count = 1.0 / (row - start + 1).astype(F32)
    return jnp.where(near, 0.0, NEG), far.astype(F32), jnp.where(start < floor, -count, count)


def near_scores(query, key_heads):
    return mm(query * jnp.asarray(HEAD_DIM**-0.5, BF16), key_heads, NT)


def near_weights(scores, bias):
    parts = []
    for h in range(2):
        part = scores[:, h * WIN : (h + 1) * WIN] + bias
        parts.append(jnp.exp(part - jnp.max(part, axis=1, keepdims=True)))
    return jnp.concatenate(parts, axis=1)


def spread(product):
    first = iota(product.shape, 1) < HEAD_DIM
    sums = [
        jnp.sum(jnp.where(keep, product, 0.0), axis=1, keepdims=True) for keep in (first, ~first)
    ]
    return jnp.concatenate([jnp.broadcast_to(part, (ROWS, WIN)) for part in sums], axis=1)


def load_keys(qkv_ref, message_ref, keys, values):
    rows = qkv_ref.shape[1]
    keys[pl.ds(0, TAIL), :] = message_ref[0, pl.ds(HEAD_DIM, TAIL), :PAIR]
    keys[pl.ds(TAIL, rows), :] = qkv_ref[1]
    values[pl.ds(0, TAIL), :] = message_ref[0, pl.ds(HEAD_DIM, TAIL), PAIR : 2 * PAIR]
    values[pl.ds(TAIL, rows), :] = qkv_ref[2]


def fold_state(wide):
    kept = block_only(wide)
    return (kept[:HEAD_DIM] + kept[HEAD_DIM:]).astype(BF16)


def unfold_state(message):
    half = message[:HEAD_DIM].astype(F32)
    return block_only(jnp.concatenate([half, half], axis=0))


def project_kernel(
    scalars,
    tokens_ref,
    gain_ref,
    own_ref,
    other_ref,
    qkv_ref,
    normed_ref,
    weight_ref,
    out_weight_ref,
    message_ref,
    state,
    placed,
    *,
    flips,
):
    step = pl.program_id(0)
    rows, width = tokens_ref.shape
    pairs = width // PAIR
    half, _, tall, wide = own_ref.shape
    last = jnp.maximum(scalars[scalars.shape[0] + LAST], 0)

    @pl.when(step == 0)
    def _():
        for index, (flip_row, flip_column) in enumerate(flips):
            row = scalars[scalars.shape[0] + ROW_AT] ^ flip_row
            column = scalars[scalars.shape[0] + COLUMN_AT] ^ flip_column
            piece = own_ref[index] if index < half else other_ref[index - half]
            for c in range(4):
                placed[column, c, row] = piece[c]
        for h in range(width // wide):
            at = pl.ds(h * wide, wide)
            weight_ref[:, :, at] = placed[h, :3].reshape(3, width, wide)
            out_weight_ref[:, at] = placed[h, 3].reshape(width, wide)
        state[...] = jnp.zeros(state.shape, F32)

    normed = (norm_parts(tokens_ref[...].astype(F32))[0] * gain_ref[...]).astype(BF16)
    normed_ref[...] = normed
    for c in (1, 2, 0):
        qkv_ref[c] = mm(normed, weight_ref[c]).astype(BF16)
    live = iota((rows, PAIR), 0) + step * rows >= last
    ones = jnp.ones((rows, PAIR), BF16)
    for p in range(pairs):
        at = pl.ds(p * PAIR, PAIR)
        key = qkv_ref[1, :, at].astype(F32)
        value = qkv_ref[2, :, at]
        lifted = jnp.where(live, lift(key), 0.0).astype(BF16)
        bent = jnp.where(live, jnp.tanh(key), 0.0).astype(BF16)
        state[p, :, : 2 * PAIR] += mm(lifted, jnp.concatenate([value, ones], axis=1), TN)
        state[p, :, 2 * PAIR :] += mm(bent, value, TN)

    @pl.when(step == pl.num_programs(0) - 1)
    def _():
        for p in range(pairs):
            at = pl.ds(p * PAIR, PAIR)
            message_ref[p, pl.ds(0, HEAD_DIM), :] = fold_state(state[p])
            message_ref[p, pl.ds(HEAD_DIM, TAIL), :] = jnp.concatenate(
                [
                    qkv_ref[1, pl.ds(rows - TAIL, TAIL), at],
                    qkv_ref[2, pl.ds(rows - TAIL, TAIL), at],
                    jnp.zeros((TAIL, PAIR), BF16),
                ],
                axis=1,
            )


def weight_grad_kernel(
    scalars,
    normed_ref,
    d_qkv_ref,
    out_grad_ref,
    weight_ref,
    keep_ref,
    give_ref,
    gain_ref,
    whole,
    *,
    flips,
):
    c = pl.program_id(0)
    half, _, tall, wide = keep_ref.shape

    def place(total):
        for h in range(total.shape[1] // wide):
            part = total[:, h * wide : (h + 1) * wide]
            whole[h] = part.reshape(whole.shape[1:])

    @pl.when(c == 0)
    def _():
        gain_ref[...] = jnp.zeros(gain_ref.shape, F32)

    @pl.when(c < 3)
    def _():
        total = mm(normed_ref[...], d_qkv_ref[0], TN)
        place(total)
        product = total * weight_ref[0].astype(F32)
        high = product.astype(BF16)
        low = (product - high.astype(F32)).astype(BF16)
        ones = jnp.ones((8, product.shape[1]), BF16)
        gain_ref[...] += mm(ones, high, NT) + mm(ones, low, NT)

    @pl.when(c == 3)
    def _():
        place(out_grad_ref[...])

    for index, (flip_row, flip_column) in enumerate(flips):
        row = scalars[scalars.shape[0] + ROW_AT] ^ flip_row
        column = scalars[scalars.shape[0] + COLUMN_AT] ^ flip_column
        if index < half:
            keep_ref[index, 0] = whole[column, row]
        else:
            give_ref[index - half, 0] = whole[column, row].astype(BF16)


def forward_kernel(
    scalars,
    qkv_ref,
    message_ref,
    bias_ref,
    far_ref,
    tally_ref,
    blend_ref,
    att_ref,
    near_ref,
    far1_ref,
    far2_ref,
    invl_ref,
    invd_ref,
    states_ref,
    keys,
    values,
    state,
):
    rows = qkv_ref.shape[1]
    load_keys(qkv_ref, message_ref, keys, values)
    state[...] = unfold_state(message_ref[0])
    count_valid = scalars[scalars.shape[0] + VALID]
    b0, b1, b2 = (blend_ref[pl.ds(f, 1), :] for f in range(3))

    def begin(step):
        at = pl.multiple_of(step * ROWS, 32)
        query = qkv_ref[0, pl.ds(at, ROWS), :]
        key = keys[pl.ds(at, WIN), :]
        value = values[pl.ds(at, WIN), :]
        first = step * ROWS - TAIL
        floor = jnp.maximum(first, 0)
        tally = tally_ref[pl.ds(at, ROWS), :]
        carried = tally < 0.0
        far_two = two(far_ref[pl.ds(at, ROWS), :].astype(F32))
        query_f = query.astype(F32)
        key_f = key.astype(F32)
        lift_qf, bend_qf = lift(query_f), jnp.tanh(query_f)
        lift_q, bend_q = lift_qf.astype(BF16), bend_qf.astype(BF16)
        lift_k = lift(key_f)
        bend_k = jnp.tanh(key_f)
        ones = jnp.ones((WIN, PAIR), BF16)
        value_heads = jnp.concatenate([split_heads(value), split_heads(ones)], axis=1)
        before = state[...]
        before_low = before.astype(BF16)
        scores = near_scores(query, split_heads(key))
        pair_weight = mm(lift_q, split_heads(lift_k.astype(BF16)), NT)
        pair_bend = mm(bend_q, split_heads(bend_k.astype(BF16)), NT)
        elu_state = mm(
            jnp.where(carried, lift_qf, 0.0).astype(BF16), before_low[:, : 2 * PAIR]
        )
        tanh_state = mm(jnp.where(carried, bend_qf, 0.0).astype(BF16), before_low[:, 2 * PAIR :])
        states_ref[0, pl.ds(pl.multiple_of(step * PAIR, PAIR), PAIR), :] = before_low
        closing = scalars[step]
        live = iota((ROWS, PAIR), 0) + first >= jnp.maximum(closing, floor)
        lifted = jnp.where(live, lift_k[:ROWS], 0.0).astype(BF16)
        bent = jnp.where(live, bend_k[:ROWS], 0.0).astype(BF16)
        with_ones = jnp.concatenate([value[:ROWS], ones[:ROWS]], axis=1)
        added = jnp.concatenate([mm(lifted, with_ones, TN), mm(bent, value[:ROWS], TN)], axis=1)
        keep = (closing < floor).astype(F32)
        state[...] = keep * before + block_only(added)
        def finish():
            low_weight = (pair_weight * far_two).astype(BF16)
            low_bend = (pair_bend * far_two).astype(BF16)
            elu_out = mm(low_weight, value_heads)
            tanh_out = mm(low_bend, value_heads[:, :PAIR]) + tanh_state
            weights = near_weights(scores, bias_ref[pl.ds(at, ROWS), :].astype(F32)).astype(BF16)
            near_out = mm(weights, value_heads)
            numerator = elu_out[:, :PAIR] + elu_state[:, :PAIR]
            inv_d = 1.0 / (elu_out[:, PAIR:] + elu_state[:, PAIR:])
            far1 = numerator * inv_d
            inv_l = 1.0 / near_out[:, PAIR:]
            near = near_out[:, :PAIR] * inv_l
            far2 = tanh_out * jnp.abs(tally)
            row = iota((ROWS, PAIR), 0) + at
            mixed = jnp.where(row < count_valid, b0 * near + b1 * far1 + b2 * far2, 0.0)
            att_ref[pl.ds(at, ROWS), :] = mixed.astype(BF16)
            near_ref[pl.ds(at, ROWS), :] = near
            far1_ref[pl.ds(at, ROWS), :] = far1
            far2_ref[pl.ds(at, ROWS), :] = far2
            invl_ref[pl.ds(at, ROWS), :] = inv_l
            invd_ref[pl.ds(at, ROWS), :] = inv_d

        return finish

    def body(both, carry):
        finishes = [begin(both * 2 + half) for half in range(2)]
        for finish in finishes:
            finish()
        return carry

    lax.fori_loop(0, rows // ROWS // 2, body, 0, unroll=4)


def near_back(scores, grad_pair, bias, spread_near):
    weights = near_weights(scores, bias)
    return weights.astype(BF16), (weights * (grad_pair - spread_near)).astype(BF16)


def prologue_kernel(
    scalars,
    query_ref,
    key_ref,
    value_ref,
    message_ref,
    start_ref,
    blend_ref,
    grad_ref,
    near_ref,
    far1_ref,
    invl_ref,
    invd_ref,
    back_ref,
):
    rows = query_ref.shape[1]
    step_rows = rows // 3
    b0, b1, b2 = (blend_ref[pl.ds(f, 1), :] for f in range(3))

    tails = message_ref[0, pl.ds(HEAD_DIM, TAIL), :]
    key = jnp.concatenate([tails[:, :PAIR], key_ref[0]], axis=0)
    value = jnp.concatenate([tails[:, PAIR : 2 * PAIR], value_ref[0]], axis=0)
    start = start_ref[pl.ds(0, ROWS), :]
    row = iota((ROWS, WIN), 0)
    bias, _, _ = masks(row, start, -TAIL)
    query = query_ref[0, pl.ds(0, ROWS), :]
    grad = grad_ref[pl.ds(0, ROWS), :]
    grad_f = grad.astype(F32)
    scale = b0 * invl_ref[...]
    rows_q = (query.astype(F32) * (scale * HEAD_DIM**-0.5)).astype(BF16)
    rows_g = (grad_f * scale).astype(BF16)
    scores = near_scores(query, split_heads(key))
    grad_pair = mm(grad, split_heads(value), NT)
    spread_near = spread(grad_f * near_ref[...])
    heads = same_head().astype(F32).astype(BF16)
    heads = jnp.concatenate([heads, heads], axis=0)

    total = jnp.zeros((PAIR, 3 * PAIR), F32)
    for step in range(3):
        here = pl.ds(step * step_rows, step_rows)
        row = iota((step_rows, PAIR), 0) + step * step_rows
        start = start_ref[here, :]
        all_grad = grad_ref[here, :]
        product = all_grad.astype(F32) * far1_ref[here, :]
        high = product.astype(BF16)
        low = (product - high.astype(F32)).astype(BF16)
        along = mm(jnp.concatenate([high, low], axis=1), heads).astype(BF16)
        query_f = query_ref[0, here, :].astype(F32)
        live = start < 0
        scaled = jnp.where(live, lift(query_f) * (b1 * invd_ref[here, :]), 0.0)
        bent = jnp.where(live, jnp.tanh(query_f) * (b2 / (row - start + 1).astype(F32)), 0.0)
        from_lift = mm(scaled.astype(BF16), jnp.concatenate([all_grad, along], axis=1), TN)
        from_bend = mm(bent.astype(BF16), all_grad, TN)
        total = total + jnp.concatenate([from_lift, from_bend], axis=1)

    weights, shifted = near_back(scores, grad_pair, bias, spread_near)
    d_key = fold(mm(shifted, rows_q, TN))
    back_ref[0, pl.ds(HEAD_DIM, TAIL), :] = jnp.concatenate(
        [d_key[:TAIL], fold(mm(weights, rows_g, TN))[:TAIL], jnp.zeros((TAIL, PAIR), F32)], axis=1
    ).astype(BF16)
    back_ref[0, pl.ds(0, HEAD_DIM), :] = fold_state(total)


def key_side(adjoint_low, lift_k, bend_k, value):
    ones = jnp.full(value.shape, -1.0 / HEAD_DIM, BF16)
    d_lift = mm(jnp.concatenate([value, ones], axis=1), adjoint_low[:, : 2 * PAIR], NT)
    d_bend = mm(value, adjoint_low[:, 2 * PAIR :], NT)
    both = jnp.concatenate([adjoint_low[:, :PAIR], adjoint_low[:, 2 * PAIR :]], axis=0)
    d_value = mm(jnp.concatenate([lift_k, bend_k], axis=1), both)
    return d_lift, d_bend, d_value


def backward_kernel(
    scalars,
    qkv_ref,
    message_ref,
    bias_ref,
    far_ref,
    tally_ref,
    blend_ref,
    grad_ref,
    near_ref,
    far1_ref,
    far2_ref,
    invl_ref,
    invd_ref,
    states_ref,
    back_ref,
    done_ref,
    out_ref,
    sums_ref,
    keys,
    values,
    adjoint,
    key_carry,
    value_carry,
):
    rows = qkv_ref.shape[1]
    steps = rows // ROWS
    load_keys(qkv_ref, message_ref, keys, values)
    last = scalars[scalars.shape[0] + LAST]
    b0, b1, b2 = (blend_ref[pl.ds(f, 1), :] for f in range(3))
    lanes = iota((ROWS, PAIR), 1) < HEAD_DIM

    arrived = unfold_state(back_ref[0])
    tail_grads = back_ref[0, pl.ds(HEAD_DIM, TAIL), :].astype(F32)
    end_key = keys[pl.ds(rows, TAIL), :].astype(F32)
    end_lift, end_bend = lift(end_key), jnp.tanh(end_key)
    end_parts = key_side(
        arrived.astype(BF16), end_lift.astype(BF16), end_bend.astype(BF16), values[pl.ds(rows, TAIL), :]
    )
    live = iota((TAIL, PAIR), 0) + (rows - TAIL) >= last
    key_carry[...] = tail_grads[:, :PAIR] + jnp.where(
        live,
        end_parts[0] * jnp.minimum(end_lift, 1.0) + end_parts[1] * (1.0 - end_bend * end_bend),
        0.0,
    )
    value_carry[...] = tail_grads[:, PAIR : 2 * PAIR] + jnp.where(live, end_parts[2], 0.0)
    adjoint[...] = jnp.where(last < rows - TAIL, 1.0, 0.0) * arrived
    sums_ref[...] = jnp.zeros(sums_ref.shape, F32)

    def add_up(place, product):
        sums_ref[pl.ds(place, 8), :] += jnp.sum(product.reshape(ROWS // 8, 8, PAIR), axis=0)

    def begin(back):
        step = steps - 1 - back
        at = pl.multiple_of(step * ROWS, 32)
        query = qkv_ref[0, pl.ds(at, ROWS), :]
        key = keys[pl.ds(at, WIN), :]
        value = values[pl.ds(at, WIN), :]
        first = step * ROWS - TAIL
        floor = jnp.maximum(first, 0)
        tally = tally_ref[pl.ds(at, ROWS), :]
        carried = tally < 0.0
        far_two = two(far_ref[pl.ds(at, ROWS), :].astype(F32))
        grad = grad_ref[pl.ds(at, ROWS), :]
        grad_f = grad.astype(F32)
        query_f = query.astype(F32)
        key_f = key.astype(F32)
        lift_qf, bend_qf = lift(query_f), jnp.tanh(query_f)
        lift_kf, bend_kf = lift(key_f), jnp.tanh(key_f)
        lift_q, bend_q = lift_qf.astype(BF16), bend_qf.astype(BF16)
        lift_k, bend_k = lift_kf.astype(BF16), bend_kf.astype(BF16)
        lift_heads, bend_heads = split_heads(lift_k), split_heads(bend_k)
        r0 = b0 * invl_ref[pl.ds(at, ROWS), :]
        r1 = b1 * invd_ref[pl.ds(at, ROWS), :]
        r2 = b2 * jnp.abs(tally)
        key_heads = split_heads(key)
        before = states_ref[0, pl.ds(pl.multiple_of(step * PAIR, PAIR), PAIR), :]
        near_product = grad_f * near_ref[pl.ds(at, ROWS), :]
        far1_product = grad_f * far1_ref[pl.ds(at, ROWS), :]
        grad_pair = mm(grad, split_heads(value), NT)
        scores = near_scores(query, key_heads)
        pair_weight = mm(lift_q, lift_heads, NT)
        pair_bend = mm(bend_q, bend_heads, NT)
        state_bend = mm(grad, before[:, 2 * PAIR :], NT)
        spread_far = spread(far1_product)
        spread_near = spread(near_product)
        along = jnp.where(lanes, spread_far[:, :WIN], spread_far[:, WIN:])
        scaled_along = (along * (-1.0 / HEAD_DIM)).astype(BF16)
        state_lift = mm(jnp.concatenate([grad, scaled_along], axis=1), before[:, : 2 * PAIR], NT)
        after = adjoint[...]
        parts = key_side(after.astype(BF16), lift_k[:ROWS], bend_k[:ROWS], value[:ROWS])
        rows_q = (query_f * (r0 * HEAD_DIM**-0.5)).astype(BF16)
        rows_a = lift_qf * r1
        rows_t = bend_qf * r2
        from_lift = mm(
            jnp.where(carried, rows_a, 0.0).astype(BF16),
            jnp.concatenate([grad, along.astype(BF16)], axis=1),
            TN,
        )
        from_bend = mm(jnp.where(carried, rows_t, 0.0).astype(BF16), grad, TN)
        closing = scalars[step]
        keep = (closing < floor).astype(F32)
        adjoint[...] = keep * after + block_only(jnp.concatenate([from_lift, from_bend], axis=1))
        add_up(0, near_product)
        add_up(8, far1_product)
        add_up(16, grad_f * far2_ref[pl.ds(at, ROWS), :])
        def finish():
            shifted = ((grad_pair - spread_far) * far_two).astype(BF16)
            plain = (grad_pair * far_two).astype(BF16)
            low_weight = (pair_weight * far_two).astype(BF16)
            low_bend = (pair_bend * far_two).astype(BF16)
            weights, shifted_near = near_back(
                scores, grad_pair, bias_ref[pl.ds(at, ROWS), :].astype(F32), spread_near
            )
            d_query = mm(shifted_near, key_heads) * (r0 * HEAD_DIM**-0.5)
            d_query = (
                d_query
                + (mm(shifted, lift_heads) + jnp.where(carried, state_lift, 0.0))
                * (r1 * jnp.minimum(lift_qf, 1.0))
                + (mm(plain, bend_heads) + jnp.where(carried, state_bend, 0.0))
                * (r2 * (1.0 - bend_qf * bend_qf))
            )
            out_ref[0, pl.ds(at, ROWS), :] = d_query.astype(BF16)
            d_key = fold(mm(shifted_near, rows_q, TN))
            d_lift = fold(mm(shifted, rows_a.astype(BF16), TN))
            d_bend = fold(mm(plain, rows_t.astype(BF16), TN))
            d_value = fold(
                mm(
                    jnp.concatenate([weights, low_weight, low_bend], axis=0),
                    jnp.concatenate([grad_f * r0, grad_f * r1, grad_f * r2], axis=0).astype(BF16),
                    TN,
                )
            )
            live = iota((ROWS, PAIR), 0) + first >= jnp.maximum(closing, floor)
            pad = jnp.zeros((TAIL, PAIR), F32)
            d_lift = d_lift + jnp.concatenate([jnp.where(live, parts[0], 0.0), pad], axis=0)
            d_bend = d_bend + jnp.concatenate([jnp.where(live, parts[1], 0.0), pad], axis=0)
            d_value = d_value + jnp.concatenate([jnp.where(live, parts[2], 0.0), pad], axis=0)
            d_key = d_key + d_lift * jnp.minimum(lift_kf, 1.0) + d_bend * (1.0 - bend_kf * bend_kf)
            out_ref[1, pl.ds(at, ROWS), :] = jnp.concatenate(
                [d_key[TAIL:ROWS], d_key[ROWS:] + key_carry[...]], axis=0
            ).astype(BF16)
            out_ref[2, pl.ds(at, ROWS), :] = jnp.concatenate(
                [d_value[TAIL:ROWS], d_value[ROWS:] + value_carry[...]], axis=0
            ).astype(BF16)
            key_carry[...] = d_key[:TAIL]
            value_carry[...] = d_value[:TAIL]

        return finish

    def body(both, carry):
        finishes = [begin(both * 2 + half) for half in range(2)]
        for finish in finishes:
            finish()
        return carry

    lax.fori_loop(0, steps // 2, body, 0, unroll=4)


def feed_kernel(
    scalars,
    mixed_ref,
    tokens_ref,
    cotangent_ref,
    out_weight_ref,
    gain_ref,
    own_ref,
    other_ref,
    layer_ref,
    d_hidden_ref,
    d_branch_ref,
    d_mixed_ref,
    normed_ref,
    active_ref,
    d_inner_ref,
    sums_ref,
):
    c0 = math.sqrt(2.0 / math.pi)
    hidden = tokens_ref[...].astype(F32) + mm(mixed_ref[...], out_weight_ref[...], NT)
    normal, scale = norm_parts(hidden)
    normed = (normal * gain_ref[...]).astype(BF16)
    normed_ref[...] = normed
    cotangent = cotangent_ref[...]
    half, width = own_ref.shape[1:]
    chunk = min(512, half)
    layer = hidden
    d_normed = jnp.zeros(hidden.shape, F32)
    slots = [(ref, first) for ref in (own_ref, other_ref) for first in range(0, half, chunk)]

    def opening(slot):
        ref, first = slot
        into = ref[0, pl.ds(first, chunk), :]
        down = ref[1, pl.ds(first, chunk), :]
        return into, down, mm(normed, into, NT), mm(cotangent, down, NT)

    ready = opening(slots[0])
    for place in range(len(slots)):
        into, down, inner, d_active = ready
        if place + 1 < len(slots):
            ready = opening(slots[place + 1])
        square = inner * inner
        bent = jnp.tanh(inner * (c0 + (c0 * 0.044715) * square))
        gate = 0.5 + 0.5 * bent
        active = (inner * gate).astype(BF16)
        slope = gate + inner * (0.5 - 0.5 * bent * bent) * (c0 + (3.0 * 0.044715 * c0) * square)
        d_inner = (d_active * slope).astype(BF16)
        at = pl.ds(place * chunk, chunk)
        active_ref[:, at] = active
        d_inner_ref[:, at] = d_inner
        layer = layer + mm(active, down)
        d_normed = d_normed + mm(d_inner, into)
    layer_ref[...] = layer.astype(BF16)
    d_part, gain_rows = norm_back(d_normed, gain_ref[...], normal, scale)
    d_hidden = cotangent.astype(F32) + d_part
    d_hidden_ref[...] = d_hidden
    d_branch = d_hidden.astype(BF16)
    d_branch_ref[...] = d_branch
    row = iota(hidden.shape, 0) + pl.program_id(0) * hidden.shape[0]
    d_mixed = mm(d_branch, out_weight_ref[...])
    d_mixed_ref[...] = jnp.where(row < scalars[scalars.shape[0] + VALID], d_mixed, 0.0).astype(BF16)

    @pl.when(pl.program_id(0) == 0)
    def _():
        sums_ref[...] = jnp.zeros(sums_ref.shape, F32)

    sums_ref[...] += gain_rows


def feed_grad_kernel(
    scalars, normed_ref, cotangent_ref, active_ref, d_inner_ref, *refs
):
    refs[-1][0] = mm(d_inner_ref[...], normed_ref[...], TN).astype(refs[-1].dtype)
    refs[-1][1] = mm(active_ref[...], cotangent_ref[...], TN).astype(refs[-1].dtype)
    if len(refs) > 1:
        mixed_ref, d_branch_ref, out_grad_ref, _ = refs

        @pl.when(pl.program_id(0) == 0)
        def _():
            out_grad_ref[...] = mm(d_branch_ref[...], mixed_ref[...], TN)


def input_kernel(
    scalars, d_qkv_ref, weight_ref, tokens_ref, d_hidden_ref, gain_ref, input_grad_ref
):
    d_normed = mm(d_qkv_ref[0], weight_ref[0], NT)
    for c in range(1, 3):
        d_normed = d_normed + mm(d_qkv_ref[c], weight_ref[c], NT)
    normal, scale = norm_parts(tokens_ref[...].astype(F32))
    d_part, _ = norm_back(d_normed, gain_ref[...], normal, scale)
    input_grad_ref[...] = d_hidden_ref[...] + d_part


def resume(kernel, ins, done, *refs):
    kernel(*refs[:ins], *refs[ins + done :])


def pair_specs(rows, first=0):
    return {
        "qkv": pl.BlockSpec((3, rows, PAIR), lambda p, s: (0, 0, p + first)),
        "message": pl.BlockSpec((1, HEAD_DIM + TAIL, 3 * PAIR), lambda p, s: (p + first, 0, 0)),
        "start": pl.BlockSpec((rows, PAIR), lambda p, s: (0, 0)),
        "blend": pl.BlockSpec((3, PAIR), lambda p, s: (0, p + first)),
        "column": pl.BlockSpec((rows, PAIR), lambda p, s: (0, p + first)),
        "states": pl.BlockSpec((1, rows // ROWS * PAIR, 3 * PAIR), lambda p, s: (p + first, 0, 0)),
        "sums": pl.BlockSpec((24, PAIR), lambda p, s: (0, p)),
        "query": pl.BlockSpec((1, rows, PAIR), lambda p, s: (0, 0, p)),
        "head_rows": pl.BlockSpec((ROWS, PAIR), lambda p, s: (0, p)),
    }


def call(kernel, ins, outs, out_shapes, scratch, grid, name, flops, moved, aliases={}):
    return pl.pallas_call(
        kernel,
        out_shape=out_shapes,
        grid_spec=pltpu.PrefetchScalarGridSpec(
            num_scalar_prefetch=1,
            grid=(grid,),
            in_specs=ins,
            out_specs=outs,
            scratch_shapes=scratch,
        ),
        input_output_aliases=aliases,
        compiler_params=pltpu.CompilerParams(
            dimension_semantics=("arbitrary",), vmem_limit_bytes=56 * 1024 * 1024
        ),
        cost_estimate=pl.CostEstimate(flops=flops, bytes_accessed=moved, transcendentals=0),
        name=name,
    )


def norm_parts(source):
    centered = source - jnp.mean(source, axis=-1, keepdims=True)
    spread_of = jnp.mean(centered * centered, axis=-1, keepdims=True)
    scale = lax.rsqrt(spread_of + EPS)
    return centered * scale, scale


def norm_back(d_out, gain, normal, scale):
    e = d_out * gain
    inner = jnp.mean(e, axis=-1, keepdims=True)
    along = jnp.mean(e * normal, axis=-1, keepdims=True)
    rows = jnp.sum((d_out * normal).reshape(-1, 8, d_out.shape[1]), axis=0)
    return scale * (e - inner - normal * along), rows


def bits(size):
    return [1 << b for b in range(int(math.log2(size)))]


def phases():
    dp = bits(lax.axis_size("dp"))
    core, rest = dp[:1], dp[1:]
    mid = len(rest) // 2
    far = [("dp", m) for m in rest[mid:]]
    near = [("dp", m) for m in rest[:mid]] + [("head", m) for m in bits(lax.axis_size("head"))]
    groups = []
    for run in (far, near, [("dp", m) for m in core]):
        groups += [run[i : i + 2] for i in range(0, len(run), 2)]
    return groups


def relative_bits():
    return [pair for group in phases() for pair in group]


def all_flips():
    order = relative_bits()
    flips = []
    for index in range(1 << len(order)):
        chosen = [pair for place, pair in enumerate(order) if index >> place & 1]
        flips.append(tuple(sum(m for a, m in chosen if a == axis) for axis in ("dp", "head")))
    return flips


def peer(array, group, combo):
    n_dp, n_head = lax.axis_size("dp"), lax.axis_size("head")
    chosen = [pair for place, pair in enumerate(group) if combo >> place & 1]
    flip_dp = sum(m for axis, m in chosen if axis == "dp")
    flip_head = sum(m for axis, m in chosen if axis == "head")
    pairs = [
        (d * n_head + h, (d ^ flip_dp) * n_head + (h ^ flip_head))
        for d in range(n_dp)
        for h in range(n_head)
    ]
    return lax.ppermute(array, ("dp", "head"), pairs)


def widen(block, group, axis, after=None):
    others = [peer(block, group, combo) for combo in range(1, 1 << len(group))]
    if after is not None:
        others, after = lax.optimization_barrier((others, after))
    whole = jnp.concatenate([block] + others, axis=axis)
    return whole if after is None else (whole, after)


def narrow(keep, gives, group, after=None):
    arrived = [peer(give.astype(BF16), group, combo) for combo, give in enumerate(gives, 1)]
    if after is not None:
        arrived, _ = lax.optimization_barrier((arrived, after))
    return keep.astype(F32) + sum(part.astype(F32) for part in arrived)


def narrow_axis(total, group, axis, after=None):
    parts = jnp.split(total, 1 << len(group), axis=axis)
    return narrow(parts[0], parts[1:], group, after)


def pass_along(local, keep, shift):
    size = lax.axis_size("head")
    pairs = [(i, i + shift) for i in range(size) if 0 <= i + shift < size]
    arrived = lax.ppermute(local, "head", pairs)
    for _ in range(size - 2):
        rows = iota(local.shape, 1) < HEAD_DIM
        total = local.astype(F32) + jnp.where(rows, keep * arrived.astype(F32), 0.0)
        arrived = lax.ppermute(total.astype(BF16), "head", pairs)
    return arrived


def per_device(
    tokens,
    ln1_gain,
    qkv_weight,
    out_weight,
    blend,
    ln2_gain,
    in_weight,
    down_weight,
    cotangent,
    lengths,
):
    rows, width = tokens.shape
    n_dp, n_head = lax.axis_size("dp"), lax.axis_size("head")
    pairs = width // PAIR
    steps = rows // ROWS
    groups = phases()
    flips = all_flips()

    item_lengths = lengths[0]
    slots = item_lengths.shape[0]
    ends = jnp.sum(
        jnp.where(iota((slots, slots), 1) <= iota((slots, slots), 0), item_lengths[None, :], 0),
        axis=1,
    )
    offset = lax.axis_index("head") * rows
    local = jnp.arange(rows, dtype=jnp.int32)
    place = local + offset
    total = ends[slots - 1]
    item_start = jnp.max(
        jnp.where(ends[None, :] <= place[:, None], ends[None, :], 0), axis=1
    )
    start = jnp.where(place < total, item_start - offset, local)
    carried_rows = jnp.sum((start < 0).astype(jnp.int32))
    scalars = jnp.concatenate(
        [
            start.reshape(steps, ROWS)[:, ROWS - TAIL - 1],
            carried_rows[None],
            start[rows - 1 :],
            (total - offset)[None],
            lax.axis_index("dp").astype(jnp.int32)[None],
            lax.axis_index("head").astype(jnp.int32)[None],
        ]
    )
    shards = jnp.concatenate([qkv_weight, out_weight.T[None]], axis=0)[None]
    feed = jnp.stack([in_weight, down_weight])
    shards = widen(shards, groups[0], 0)
    feed, late, _ = lax.optimization_barrier((feed, start, shards))
    start_wide = jnp.broadcast_to(late[:, None], (rows, PAIR))
    row_wide = jnp.broadcast_to(local[:, None], (rows, PAIR))
    bias, far, tally = masks(row_wide, start_wide, row_wide // ROWS * ROWS - TAIL)
    tables = (bias.astype(BF16), far.astype(BF16), tally)
    feed = widen(feed, groups[0][:1], 1)
    for group in groups[1:-1]:
        shards = widen(shards, group, 0)
    shards, feed, start_wide, tables = lax.optimization_barrier((shards, feed, start_wide, tables))
    others = peer(shards, groups[-1], 1)

    keep_all = (start[rows - 1] < 0).astype(F32)
    blend_wide = jnp.repeat(blend, HEAD_DIM, axis=1)

    spec = pair_specs(rows)
    wide = jax.ShapeDtypeStruct((rows, width), F32)
    states_shape = jax.ShapeDtypeStruct((pairs, steps * PAIR, 3 * PAIR), BF16)
    message_shape = jax.ShapeDtypeStruct((pairs, HEAD_DIM + TAIL, 3 * PAIR), BF16)
    big = rows * width
    part = rows // 3

    def whole_spec(shape):
        return pl.BlockSpec(shape, lambda p, s: (0,) * len(shape))

    qkv, normed_one, qkv_all, out_all, closing = call(
        functools.partial(project_kernel, flips=flips),
        [
            pl.BlockSpec((part, width), lambda p, s: (p, 0)),
            whole_spec((1, width)),
            whole_spec(shards.shape),
            whole_spec(shards.shape),
        ],
        [
            pl.BlockSpec((3, part, width), lambda p, s: (0, p, 0)),
            pl.BlockSpec((part, width), lambda p, s: (p, 0)),
            whole_spec((3, width, width)),
            whole_spec((width, width)),
            whole_spec(message_shape.shape),
        ],
        [
            jax.ShapeDtypeStruct((3, rows, width), BF16),
            jax.ShapeDtypeStruct((rows, width), BF16),
            jax.ShapeDtypeStruct((3, width, width), BF16),
            jax.ShapeDtypeStruct((width, width), BF16),
            message_shape,
        ],
        [
            pltpu.VMEM((pairs, PAIR, 3 * PAIR), F32),
            pltpu.VMEM((n_head, 4, n_dp, width // n_dp, width // n_head), BF16),
        ],
        3,
        "project",
        6 * big * width,
        12 * big,
    )(scalars, tokens, ln1_gain[None], shards, others)
    for pair in groups[0][1:]:
        feed, _ = widen(feed, [pair], 1, closing)
    message = pass_along(closing, keep_all, 1)

    key_scratch = pltpu.VMEM((rows + TAIL, PAIR), BF16)
    state_scratch = pltpu.VMEM((PAIR, 3 * PAIR), F32)
    tail_scratch = pltpu.VMEM((TAIL, PAIR), F32)
    results = ()
    most = pairs - pairs // 4
    for first, count in ((0, most), (most, pairs - most)):
        spec = pair_specs(rows, first)
        results = call(
            functools.partial(resume, forward_kernel, 7, len(results)),
            [spec["qkv"], spec["message"]]
            + [spec["start"]] * 3
            + [spec["blend"]]
            + [pl.BlockSpec(memory_space=pl.ANY)] * len(results),
            [spec["column"]] * 6 + [spec["states"]],
            [jax.ShapeDtypeStruct((rows, width), BF16)] + [wide] * 5 + [states_shape],
            [key_scratch, key_scratch, state_scratch],
            count,
            "forward",
            8000 * big * count // pairs,
            40 * big * count // pairs,
            {7 + i: i for i in range(len(results))},
        )(scalars, qkv, message, *tables, blend_wide, *results)
        if not first:
            feed, results = widen(feed, groups[1], 1, results)
            feed, message = lax.optimization_barrier((feed, message))
    for group in groups[2:-1]:
        feed = widen(feed, group, 1)
    feed_other = peer(feed, groups[-1], 1)
    mixed, near, far1, far2, inv_l, inv_d, states = results

    spec = pair_specs(rows)
    low = jax.ShapeDtypeStruct((rows, width), BF16)
    row_spec = pl.BlockSpec((part, width), lambda p, s: (p, 0))
    hidden_units = 2 * feed.shape[1]
    unit_spec = pl.BlockSpec((part, hidden_units), lambda p, s: (p, 0))
    unit_shape = jax.ShapeDtypeStruct((rows, hidden_units), BF16)
    sums_shape = jax.ShapeDtypeStruct((8, width), F32)
    layer_out, d_hidden, d_branch, d_mixed, normed_two, active, d_inner, gain_two_rows = call(
        feed_kernel,
        [row_spec] * 3
        + [
            whole_spec((width, width)),
            whole_spec((1, width)),
            whole_spec(feed.shape),
            whole_spec(feed.shape),
        ],
        [row_spec] * 5 + [unit_spec] * 2 + [whole_spec((8, width))],
        [low, wide, low, low, low, unit_shape, unit_shape, sums_shape],
        [],
        3,
        "feed",
        8 * big * hidden_units,
        32 * big,
    )(scalars, mixed, tokens, cotangent, out_all, ln2_gain[None], feed, feed_other)

    back = call(
        prologue_kernel,
        [
            spec["query"],
            pl.BlockSpec((1, ROWS, PAIR), lambda p, s: (1, 0, p)),
            pl.BlockSpec((1, ROWS, PAIR), lambda p, s: (2, 0, p)),
            spec["message"],
            spec["start"],
            spec["blend"],
            spec["column"],
            spec["head_rows"],
            spec["column"],
            spec["head_rows"],
            spec["column"],
        ],
        spec["message"],
        message_shape,
        [],
        pairs,
        "prologue",
        500 * big,
        20 * big,
    )(scalars, qkv, qkv, qkv, message, start_wide, blend_wide, d_mixed, near, far1, inv_l, inv_d)
    d_inner, _ = lax.optimization_barrier((d_inner, back))
    back_in = pass_along(back, keep_all, -1)

    unit = hidden_units // 4
    half_shape = (2, 2 * unit, width)
    whole_rows = whole_spec((rows, width))

    def feed_grad(place, kind, d_inner, more_ins, more_in_specs, more_outs, more_out_specs):
        columns = pl.BlockSpec((rows, unit), lambda p, s: (0, p + 2 * place))
        return call(
            feed_grad_kernel,
            [whole_rows] * 2 + [columns] * 2 + more_in_specs,
            more_out_specs + [pl.BlockSpec((2, unit, width), lambda p, s: (0, p, 0))],
            more_outs + [jax.ShapeDtypeStruct(half_shape, kind)],
            [],
            2,
            "feed_grad",
            2 * big * hidden_units,
            12 * big,
        )(scalars, normed_two, cotangent, active, d_inner, *more_ins)

    (give,) = feed_grad(1, BF16, d_inner, [], [], [], [])
    d_inner, _ = lax.optimization_barrier((d_inner, give))
    out_grad, keep = feed_grad(
        0,
        F32,
        d_inner,
        [mixed, d_branch],
        [whole_rows] * 2,
        [jax.ShapeDtypeStruct((width, width), F32)],
        [whole_spec((width, width))],
    )
    feed_share = narrow(keep, [give], groups[-1])
    left = list(reversed(groups[:-1]))
    _, back_in = lax.optimization_barrier((feed_share, back_in))
    feed_share = narrow_axis(feed_share, left.pop(0), 1)

    d_qkv = jnp.zeros((3, 8, PAIR), BF16)
    sums = []
    first = 0
    for count in (most, pairs - most):
        spec = pair_specs(rows, first)
        more = {15: 0} if first else {}
        d_qkv, part_sums = call(
            backward_kernel,
            [spec["qkv"], spec["message"]]
            + [spec["start"]] * 3
            + [spec["blend"]]
            + [spec["column"]] * 6
            + [spec["states"], spec["message"], pl.BlockSpec(memory_space=pl.ANY)],
            [spec["qkv"], spec["sums"]],
            [
                jax.ShapeDtypeStruct((3, rows, width), BF16),
                jax.ShapeDtypeStruct((24, count * PAIR), F32),
            ],
            [key_scratch, key_scratch, state_scratch, tail_scratch, tail_scratch],
            count,
            "backward",
            16000 * big * count // pairs,
            40 * big * count // pairs,
            more,
        )(
            scalars,
            qkv,
            message,
            *tables,
            blend_wide,
            d_mixed,
            near,
            far1,
            far2,
            inv_l,
            inv_d,
            states,
            back_in,
            d_qkv,
        )
        sums.append(part_sums)
        first += count
        if left and first < pairs:
            _, back_in = lax.optimization_barrier((feed_share, back_in))
            feed_share = narrow_axis(feed_share, left.pop(0), 1)
    for group in left:
        feed_share = narrow_axis(feed_share, group, 1)
    feed_share, d_qkv = lax.optimization_barrier((feed_share, d_qkv))
    sums = jnp.concatenate(sums, axis=1)
    blend_part = jnp.sum(sums.reshape(3, 8, blend.shape[1], HEAD_DIM), axis=(1, 3))

    shard_shape = (n_dp * n_head // 2, 4, width // n_dp, width // n_head)
    shard_spec = pl.BlockSpec((shard_shape[0], 1) + shard_shape[2:], lambda p, s: (0, p, 0, 0))
    keep, give, gain_one_rows = call(
        functools.partial(weight_grad_kernel, flips=flips),
        [
            whole_spec((rows, width)),
            pl.BlockSpec((1, rows, width), lambda p, s: (jnp.minimum(p, 2), 0, 0)),
            whole_spec((width, width)),
            pl.BlockSpec((1, width, width), lambda p, s: (jnp.minimum(p, 2), 0, 0)),
        ],
        [shard_spec, shard_spec, whole_spec((8, width))],
        [
            jax.ShapeDtypeStruct(shard_shape, F32),
            jax.ShapeDtypeStruct(shard_shape, BF16),
            sums_shape,
        ],
        [pltpu.VMEM((n_head, n_dp, width // n_dp, width // n_head), F32)],
        4,
        "weight_grad",
        6 * big * width,
        8 * big,
    )(scalars, normed_one, d_qkv, out_grad, qkv_all)
    parts = [gain_one_rows[0] / ln1_gain, jnp.sum(gain_two_rows, axis=0), blend_part.reshape(-1)]
    total_sums = jnp.concatenate(parts)[None]
    share = narrow(keep, [give], groups[-1])
    hops = list(reversed(relative_bits()))
    total_sums = total_sums + peer(total_sums, [hops[0]], 1)
    total_sums, d_qkv, _ = lax.optimization_barrier((total_sums, d_qkv, share))
    total_sums = total_sums + peer(total_sums, [hops[1]], 1)
    input_grad = call(
        input_kernel,
        [
            pl.BlockSpec((3, part, width), lambda p, s: (0, p, 0)),
            whole_spec((3, width, width)),
            row_spec,
            row_spec,
            whole_spec((1, width)),
        ],
        row_spec,
        wide,
        [],
        3,
        "input",
        6 * big * width,
        24 * big,
    )(scalars, d_qkv, qkv_all, tokens, d_hidden, ln1_gain[None])
    share = narrow_axis(share, groups[-2], 0, input_grad)
    total_sums, _ = lax.optimization_barrier((total_sums, input_grad))
    total_sums = total_sums + peer(total_sums, [hops[2]], 1)
    for group in reversed(groups[:-2]):
        parts = jnp.split(share, 1 << len(group), axis=0)
        arrived = [
            peer(part.astype(BF16), group, combo) for combo, part in enumerate(parts[1:], 1)
        ]
        total_sums, _ = lax.optimization_barrier((total_sums, arrived[0]))
        share = parts[0] + sum(part.astype(F32) for part in arrived)
    for place in range(3, len(hops), 2):
        group = hops[place : place + 2]
        arrived = [peer(total_sums, group, combo) for combo in range(1, 1 << len(group))]
        total_sums = total_sums + sum(arrived)
    total_sums = total_sums[0]
    gain_one, gain_two = total_sums[:width], total_sums[width : 2 * width]
    blend_sum = total_sums[2 * width :].reshape(blend.shape)
    qkv_share, out_share = share[0, :3], share[0, 3].T
    in_share, down_share = feed_share[0], feed_share[1]
    return (
        layer_out,
        input_grad,
        gain_one,
        qkv_share,
        out_share,
        blend_sum,
        gain_two,
        in_share,
        down_share,
    )


def solution(mesh):
    return jax.shard_map(
        per_device,
        mesh=mesh,
        in_specs=(
            P(("dp", "head"), None),
            P(),
            P(None, "dp", "head"),
            P("head", "dp"),
            P(),
            P(),
            P(("dp", "head"), None),
            P(("dp", "head"), None),
            P(("dp", "head"), None),
            P("dp", None),
        ),
        out_specs=(
            P(("dp", "head"), None),
            P(("dp", "head"), None),
            P(),
            P(None, "dp", "head"),
            P("head", "dp"),
            P(),
            P(),
            P(("dp", "head"), None),
            P(("dp", "head"), None),
        ),
        check_vma=False,
    )
```
